32 devices in a mesh: pair: 8 (over z, x), row: 4 (over y, core).
Axes of the slice: x: 2, y: 2, z: 4, core: 2. Of those that a mesh axis runs over, the one named last changes fastest.
Arguments:
- sector: float32 [8192, 2048], P('row', 'pair'), may hold values from -1.767767 to 1.767767
- block_label: int32 [16], replicated, may hold values from 0 to 15, each once
Outputs:
- rotated: float32 [8192, 2048], P('row', 'pair')
- vectors: float32 [2048, 2048], P('row', 'pair')
- singular: float32 [2048], P('pair')
The draws below stay inside these ranges and needn't reach their ends.
Inputs may be any that keep to these rules, and one draw needn't show every extreme that they name: `block_label`: each block number appears once.
All inputs are finite; a program needn't handle non-finite values.
Results may differ from the reference program's by a relative error of at most 0.0003.
Values sent between devices are 32-bit elements; how exact they have to be, the bound alone decides.
No kernel may reach another device: no remote copies, remote signals or barrier semaphores. Data moves between devices by JAX's collectives and lax.ppermute only.
A program may use at most 64 MiB of HBM per device.

```python
import jax
import jax.numpy as jnp
from jax import lax

BW = 128
ROWS = 8192
ROUNDS = 4
NEWTON = 16
BLOCKS = 16
COLS = 2048
N_PAIR = 8


def signed_coefficients(key):
    key_size = jax.random.fold_in(key, 3)
    key_sign = jax.random.fold_in(key, 5)
    magnitude = jax.random.uniform(key_size, (1, COLS), jnp.float32, 0.2, 0.45)
    signs = (2 * jax.random.randint(key_sign, (1, COLS), 0, 2) - 1).astype(jnp.float32)
    return magnitude * signs


def draw_sector(key, part):
    key_entries = jax.random.fold_in(key, 11)
    key_columns = jax.random.fold_in(key, 23)
    key_near = jax.random.fold_in(key, 41)
    key_far = jax.random.fold_in(key, 43)
    entries = jnp.clip(jax.random.normal(key_entries, (ROWS, COLS), jnp.float32), -5.0, 5.0)
    near_weight = signed_coefficients(key_near)
    far_weight = signed_coefficients(key_far)
    mixed = entries + near_weight * jnp.roll(entries, -1, axis=1) + far_weight * jnp.roll(entries, -BW, axis=1)
    col_scale = jnp.exp(jax.random.uniform(key_columns, (1, COLS), jnp.float32, 0.0, 2.302))
    return mixed * col_scale / jnp.sqrt(jnp.float32(ROWS))


def setup_inputs(seed: int = 0) -> dict:
    key_list = jax.random.split(jax.random.key(seed), 3)
    sector = draw_sector(jax.random.fold_in(key_list[2], 71), 0)
    block_label = jax.random.permutation(key_list[1], BLOCKS).astype(jnp.int32)
    return dict(sector=sector, block_label=block_label)


highest = lax.Precision.HIGHEST

def rotation_of(gram_matrix):
    size_two = gram_matrix.shape[0]
    diagonal = jnp.diagonal(gram_matrix)
    spread = diagonal[None, :] - diagonal[:, None]
    summed = diagonal[None, :] + diagonal[:, None]
    skewed = gram_matrix * spread / (spread * spread + 2.0 * gram_matrix * gram_matrix + 0.01 * summed * summed)
    identity = jnp.eye(size_two, dtype=jnp.float32)
    half_step = identity + 0.5 * skewed
    system = identity - 0.25 * jnp.dot(skewed, skewed, precision=highest)
    bound = 1.0 + 0.25 * jnp.sum(skewed * skewed)
    inverse = 2.0 / (1.0 + bound) * identity
    for newton_step in range(NEWTON):
        inverse = jnp.dot(inverse, 2.0 * identity - jnp.dot(system, inverse, precision=highest), precision=highest)
    return jnp.dot(inverse, jnp.dot(half_step, half_step, precision=highest), precision=highest)

def reference(sector, block_label):
    width_pair = 2 * BW
    total_cols = sector.shape[1]
    total_rows = sector.shape[0]
    slot_ids = jnp.arange(total_cols, dtype=jnp.int32)
    targets = block_label[slot_ids // BW] * BW + slot_ids % BW
    vectors = (slot_ids[:, None] == targets[None, :]).astype(jnp.float32)
    stacked = jnp.concatenate([sector, vectors], 0)
    all_rows = stacked.shape[0]
    stacked = jnp.transpose(stacked.reshape(all_rows, N_PAIR, width_pair), (1, 0, 2))

    def rotate_pair(pair_block):
        pair_rows = pair_block[:total_rows]
        gram_matrix = jnp.dot(pair_rows.T, pair_rows, precision=highest)
        return jnp.dot(pair_block, rotation_of(gram_matrix), precision=highest)
    for sweep_round in range(ROUNDS):
        stacked = lax.map(rotate_pair, stacked)
        if sweep_round < ROUNDS - 1:
            upper_half = stacked[:, :, :BW]
            lower_half = stacked[:, :, BW:]
            new_upper = jnp.concatenate([upper_half[:1], lower_half[:1], upper_half[1:N_PAIR - 1]], 0)
            new_lower = jnp.concatenate([lower_half[1:], upper_half[N_PAIR - 1:]], 0)
            stacked = jnp.concatenate([new_upper, new_lower], 2)
    stacked = jnp.transpose(stacked, (1, 0, 2)).reshape(all_rows, total_cols)
    rotated = stacked[:total_rows]
    vectors_out = stacked[total_rows:]
    singular = jnp.sqrt(lax.optimization_barrier(jnp.sum(rotated * rotated, axis=0)) + 1e-06)
    return (rotated, vectors_out, singular)
```

```python
import jax
import jax.numpy as jnp
from jax import lax
from jax.experimental import pallas as pl
from jax.experimental.pallas import tpu as pltpu
from jax.sharding import PartitionSpec as P

ROUNDS = 4
NEWTON = 16

highest = lax.Precision.HIGHEST

TARGET = 2.0**-12
BOUNDS = [
    (1.0 + TARGET ** (2.0**-j)) / (1.0 - TARGET ** (2.0**-j)) for j in range(NEWTON)
]

X, CORE, FIRST, LAST, VROW, LABEL = 0, 1, 2, 3, 4, 5


def dot(a, b, precision=highest):
    return lax.dot_general(
        a, b, (((1,), (0,)), ((), ())), precision=precision,
        preferred_element_type=jnp.float32,
    )


def dot_tn(a, b):
    return lax.dot_general(
        a, b, (((0,), (0,)), ((), ())), precision=highest,
        preferred_element_type=jnp.float32,
    )


def shape(*dims):
    return jax.ShapeDtypeStruct(dims, jnp.float32)


def call(body, facts, inputs, outs, scratch=(), limit=24):
    return pl.pallas_call(
        body,
        out_shape=outs,
        in_specs=[pl.BlockSpec(memory_space=pltpu.SMEM)]
        + [pl.BlockSpec(memory_space=pltpu.VMEM)] * len(inputs),
        out_specs=jax.tree.map(
            lambda _: pl.BlockSpec(memory_space=pltpu.VMEM), outs
        ),
        scratch_shapes=list(scratch),
        compiler_params=pltpu.CompilerParams(vmem_limit_bytes=limit << 20),
    )(facts, *inputs)


def first_gram(facts, sector, half):
    rows, width = sector.shape

    def body(f, x_ref, out_ref):
        x = x_ref[...]
        g = dot_tn(x, x)
        out_ref[:half] = g[:half, :half]
        out_ref[half : 2 * half] = g[:half, half:]
        out_ref[2 * half :] = g[half:, half:]

    return call(body, facts, [sector], shape(3 * half, half))


def rotate_of(gram, x_ref, e_ref):
    size = gram.shape[0]
    half = size // 2
    rows = lax.broadcasted_iota(jnp.int32, (size, size), 0)
    cols = lax.broadcasted_iota(jnp.int32, (size, size), 1)
    identity = (rows == cols).astype(jnp.float32)
    only = jnp.where(rows == cols, gram, 0.0)
    g_j = jnp.sum(only, axis=0, keepdims=True)
    g_i = jnp.sum(only, axis=1, keepdims=True)
    spread = g_j - g_i
    summed = g_j + g_i
    skew = gram * spread / (spread * spread + 2.0 * gram * gram + 0.01 * summed * summed)
    bound = 1.0 + 0.25 * jnp.sum(skew * skew)
    steps = jnp.int32(0)
    for limit in BOUNDS:
        steps = steps + (bound > limit).astype(jnp.int32)
    scale = 2.0 / (1.0 + jnp.full((size, size), bound, jnp.float32))
    system = identity - 0.25 * dot(skew, skew)
    residual = identity - scale * system
    x_ref[...] = scale * (identity + residual)
    e_ref[...] = dot(residual, residual)

    def step(_, carry):
        e = e_ref[...]
        x = x_ref[...]
        x_ref[...] = x + dot(x, e)
        e_ref[...] = dot(e, e)
        return carry

    lax.fori_loop(0, jnp.maximum(steps - 1, 0), step, jnp.int32(0))
    x = x_ref[...]
    half_inverse = x + 0.5 * dot(x, skew)
    missing = half_inverse - 0.5 * dot(skew, half_inverse)
    half_inverse = half_inverse + (half_inverse - dot(half_inverse, missing))
    rotation = 2.0 * half_inverse - identity
    turned = dot(gram, rotation)
    upper = dot_tn(rotation[:, :half], turned[:, :half])
    lower = dot_tn(rotation[:, half:], turned[:, half:])
    return rotation, upper, lower


def put_pack(pack_ref, rotation, upper, lower):
    size = rotation.shape[0]
    half = size // 2
    pack_ref[:size] = rotation
    pack_ref[size:, :half] = upper
    pack_ref[size:, half:] = lower


def first_rotation(facts, own, near, far, half):
    size = 2 * half

    def body(f, own_ref, near_ref, far_ref, pack_ref, g_ref, x_ref, e_ref):
        mine = f[X] == f[CORE]
        total = near_ref[...] + jnp.where(mine, own_ref[...], far_ref[...])
        g_ref[:half, :half] = total[:half]
        g_ref[:half, half:] = total[half : 2 * half]
        g_ref[half:, :half] = total[half : 2 * half].T
        g_ref[half:, half:] = total[2 * half :]
        put_pack(pack_ref, *rotate_of(g_ref[...], x_ref, e_ref))

    square = pltpu.VMEM((size, size), jnp.float32)
    return call(
        body, facts, [own, near, far], shape(3 * half, size), [square] * 3
    )


def later_rotation(facts, parts, tails, half):
    size = 2 * half
    top = tails[0].shape[0] - half

    def body(f, *refs):
        own, other_y, other_x, other_xy = [r[...] for r in refs[:4]]
        from_left, kept_left, nat_l, nat_u, from_right, kept_right = [
            r[top:] for r in refs[4:10]
        ]
        pack_ref, g_ref, x_ref, e_ref = refs[10:]
        cross = (own + other_y) + (other_x + other_xy)
        first, last, core = f[FIRST] == 1, f[LAST] == 1, f[CORE] == 0
        up_0 = jnp.where(first, kept_left, from_left)
        low_1 = jnp.where(last, kept_right, from_right)
        g_ref[:half, :half] = jnp.where(core, up_0, nat_u)
        g_ref[:half, half:] = cross
        g_ref[half:, :half] = cross.T
        g_ref[half:, half:] = jnp.where(core, nat_l, low_1)
        put_pack(pack_ref, *rotate_of(g_ref[...], x_ref, e_ref))

    square = pltpu.VMEM((size, size), jnp.float32)
    return call(
        body, facts, parts + tails, shape(3 * half, size), [square] * 3
    )


def two_packs(f, own, other):
    core = f[CORE] == 0
    return jnp.where(core, own, other), jnp.where(core, other, own)


def swapped(flag, matrix, axis):
    half = matrix.shape[axis] // 2
    a = lax.slice_in_dim(matrix, 0, half, axis=axis)
    b = lax.slice_in_dim(matrix, half, 2 * half, axis=axis)
    return jnp.where(flag, lax.concatenate([b, a], axis), matrix)


def blocks_of(f, refs, rows=None):
    vals = [r[...] if rows is None else r[:rows] for r in refs]
    from_left, kept_left, nat_l, nat_u, from_right, kept_right = vals
    up_0 = jnp.where(f[FIRST] == 1, kept_left, from_left)
    low_1 = jnp.where(f[LAST] == 1, kept_right, from_right)
    return up_0, nat_l, nat_u, low_1


def put_turned(f, refs, zero, one, half, swap_natives):
    to_left_ref, nat_l_ref, nat_u_ref, to_right_ref = refs
    to_left_ref[...] = zero[:, half:]
    to_right_ref[...] = one[:, :half]
    nat_u, nat_l = zero[:, :half], one[:, half:]
    if swap_natives:
        even = f[X] == 0
        nat_l, nat_u = jnp.where(even, nat_l, nat_u), jnp.where(even, nat_u, nat_l)
    nat_l_ref[...] = nat_l
    nat_u_ref[...] = nat_u


def turn(facts, packs, kept, got, blocks, half, swap_natives):
    size = 2 * half
    first_round = blocks is None
    inputs = packs + ([kept, got] if first_round else blocks)
    rows = kept.shape[0] if first_round else blocks[0].shape[0]

    def body(f, *refs):
        own, other = refs[0][:size], refs[1][:size]
        turn_0, turn_1 = two_packs(f, own, other)
        turn_0 = swapped(f[FIRST] == 1, turn_0, 1)
        outs = refs[2 + len(inputs) - 2 :]
        if first_round:
            even = f[X] == 0
            mine, theirs = refs[2][...], refs[3][...]
            zero, one = jnp.where(even, mine, theirs), jnp.where(even, theirs, mine)
        else:
            up_0, low_0, up_1, low_1 = blocks_of(f, refs[2:8])
            zero = lax.concatenate([up_0, low_0], 1)
            one = lax.concatenate([up_1, low_1], 1)
        put_turned(f, outs, dot(zero, turn_0), dot(one, turn_1), half, swap_natives)

    return call(body, facts, inputs, (shape(rows, half),) * 4)


def turn_tail(facts, packs, tails, vector_rows, half):
    size = 2 * half
    inputs = packs + (tails or [])

    def body(f, *refs):
        own, other = refs[0][...], refs[1][...]
        pack_0, pack_1 = two_packs(f, own, other)
        pack_0 = swapped(f[FIRST] == 1, pack_0, 1)
        outs = refs[len(inputs) :]
        if tails is None:
            rows = f[VROW] + lax.broadcasted_iota(jnp.int32, (vector_rows, half), 0)
            cols = lax.broadcasted_iota(jnp.int32, (vector_rows, half), 1)
            up_0, low_0, up_1, low_1 = [
                (rows == f[LABEL + k] * half + cols).astype(jnp.float32)
                for k in range(4)
            ]
        else:
            up_0, low_0, up_1, low_1 = blocks_of(f, refs[2:8], vector_rows)
        zero = dot(lax.concatenate([up_0, low_0], 1), pack_0[:size])
        one = dot(lax.concatenate([up_1, low_1], 1), pack_1[:size])
        to_left_ref, nat_l_ref, nat_u_ref, to_right_ref = outs
        for ref, matrix, pack, at in (
            (to_left_ref, zero, pack_0, half),
            (nat_l_ref, one, pack_1, half),
            (nat_u_ref, zero, pack_0, 0),
            (to_right_ref, one, pack_1, 0),
        ):
            ref[:vector_rows] = matrix[:, at : at + half]
            ref[vector_rows:] = pack[size:, at : at + half]

    return call(body, facts, inputs, (shape(vector_rows + half, half),) * 4)


def cross_gram(facts, blocks, half, last_round):
    rows = blocks[0].shape[0]

    def body(f, *refs):
        outs = refs[6:]
        vals = blocks_of(f, refs[:6])
        up_0, low_0, up_1, low_1 = vals
        if last_round:
            even = f[X] == 0
            low_0, up_1 = jnp.where(even, low_0, up_1), jnp.where(even, up_1, low_0)
            outs[2][...] = jnp.where(even, up_0, low_1)
            outs[3][...] = jnp.where(even, low_1, up_0)
        zero, one = dot_tn(up_0, low_0), dot_tn(up_1, low_1)
        core = f[CORE] == 0
        outs[0][...] = jnp.where(core, zero, one)
        outs[1][...] = jnp.where(core, one, zero)

    outs = (shape(half, half),) * 2
    if last_round:
        outs = outs + (shape(rows, half),) * 2
    return call(body, facts, blocks, outs)


def split_vectors(facts, tails, vector_rows, half):
    def body(f, *refs):
        up_0, low_0, up_1, low_1 = blocks_of(f, refs[:6], vector_rows)
        even = f[X] == 0
        keep_ref, send_ref = refs[6:]
        keep_ref[:, :half] = jnp.where(even, up_0, up_1)
        keep_ref[:, half:] = jnp.where(even, low_0, low_1)
        send_ref[:, :half] = jnp.where(even, up_1, up_0)
        send_ref[:, half:] = jnp.where(even, low_1, low_0)

    return call(body, facts, tails, (shape(vector_rows, 2 * half),) * 2)


def finish(facts, packs, moved, native, vectors, half):
    size = 2 * half
    part = moved[0].shape[0]
    vector_part = vectors[0].shape[0]

    def body(f, *refs):
        x = f[X]
        mine = f[CORE] == x
        pack = jnp.where(mine, refs[0][...], refs[1][...])
        rotation = pack[:size]
        turned = swapped(x == 1, rotation, 0)
        moved_keep, moved_got, native_keep, native_got, v_keep, v_got = refs[2:8]
        out_ref, vectors_ref, singular_ref = refs[8:]
        here = pl.multiple_of(x * part, part)
        there = pl.multiple_of((1 - x) * part, part)
        out_ref[pl.ds(here, part)] = dot(
            lax.concatenate([moved_keep[...], native_keep[...]], 1), turned
        )
        out_ref[pl.ds(there, part)] = dot(
            lax.concatenate([moved_got[...], native_got[...]], 1), turned
        )
        here = pl.multiple_of(x * vector_part, vector_part)
        there = pl.multiple_of((1 - x) * vector_part, vector_part)
        vectors_ref[pl.ds(here, vector_part)] = dot(v_keep[...], rotation)
        vectors_ref[pl.ds(there, vector_part)] = dot(v_got[...], rotation)
        rows = lax.broadcasted_iota(jnp.int32, (half, size), 0)
        cols = lax.broadcasted_iota(jnp.int32, (half, size), 1)
        diagonal = (rows == cols) | (rows + half == cols)
        squares = jnp.sum(jnp.where(diagonal, pack[size:], 0.0), axis=0, keepdims=True)
        singular_ref[...] = jnp.sqrt(jnp.maximum(squares, 0.0) + 1e-06)

    return call(
        body,
        facts,
        packs + moved + native + vectors,
        (shape(2 * part, size), shape(2 * vector_part, size), shape(1, size)),
    )


def per_device(sector, block_label):
    local_rows, size = sector.shape
    half = size // 2
    part = local_rows // 2
    pairs = lax.axis_size("pair")
    row_count = lax.axis_size("row")
    vector_rows = pairs * size // row_count // 2
    pair_index = lax.axis_index("pair")
    row_index = lax.axis_index("row")
    x = pair_index % 2
    group = pair_index // 2
    core = row_index % 2

    def permute(block, route):
        moves = [
            (a * row_count + b, c * row_count + d) for (a, b), (c, d) in route
        ]
        return lax.ppermute(block, ("pair", "row"), moves)

    devices = [(p, r) for p in range(pairs) for r in range(row_count)]

    def exchange(block, over_pair, over_row):
        return permute(
            block, [((p ^ over_pair, r ^ over_row), (p, r)) for p, r in devices]
        )

    def shift(block, by):
        return permute(
            block, [((p - by, r), (p, r)) for p, r in devices if 0 <= p - by < pairs]
        )

    def sum_rows(block):
        bit = 4
        while bit < row_count:
            block = block + exchange(block, 0, bit)
            bit *= 2
        return block

    names = jnp.arange(16, dtype=jnp.int32)
    facts = jnp.zeros((16,), jnp.int32)
    for name, value in (
        (X, x),
        (CORE, core),
        (FIRST, group == 0),
        (LAST, group == pairs // 2 - 1),
        (VROW, (row_index * 2 + x) * vector_rows),
    ):
        facts = jnp.where(names == name, value.astype(jnp.int32), facts)
    labels = lax.dynamic_slice_in_dim(block_label, 4 * group, 4)
    facts = lax.dynamic_update_slice_in_dim(facts, labels, LABEL, 0)

    give = lax.dynamic_slice_in_dim(sector, (1 - x) * part, part)
    kept = lax.dynamic_slice_in_dim(sector, x * part, part)
    got = exchange(give, 1, 0)

    own = first_gram(facts, sector, half)
    own = sum_rows(own + exchange(own, 0, 1))
    near = permute(
        own,
        [
            ((p, r ^ 2) if p % 2 == r % 2 else (p ^ 1, r ^ 1), (p, r))
            for p, r in devices
        ],
    )
    far = permute(
        own, [((p ^ 1, r ^ 2), (p, r)) for p, r in devices if p % 2 != r % 2]
    )
    pack = first_rotation(facts, own, near, far, half)

    blocks = tails = None
    for sweep_round in range(ROUNDS - 1):
        packs = [pack, exchange(pack, 0, 1)]
        last_move = sweep_round == ROUNDS - 2
        to_left, nat_l, nat_u, to_right = turn(
            facts, packs, kept, got, blocks, half, last_move
        )
        from_left, from_right = shift(to_right, 2), shift(to_left, -2)
        tail_left, tail_l, tail_u, tail_right = turn_tail(
            facts, packs, tails, vector_rows, half
        )
        tail_from_left, tail_from_right = shift(tail_right, 2), shift(tail_left, -2)
        if last_move:
            native = [nat_l, exchange(nat_u, 1, 0)]
        blocks = [from_left, to_left, nat_l, nat_u, from_right, to_right]
        tails = [tail_from_left, tail_left, tail_l, tail_u, tail_from_right, tail_right]
        grams = cross_gram(facts, blocks, half, last_move)
        own = sum_rows(grams[0] + exchange(grams[1], 0, 1))
        parts = [own, exchange(own, 0, 2), exchange(own, 1, 0), exchange(own, 1, 2)]
        if last_move:
            moved = [grams[2], exchange(grams[3], 1, 0)]
            v_keep, v_give = split_vectors(facts, tails, vector_rows, half)
            vectors = [v_keep, exchange(v_give, 1, 0)]
        pack = later_rotation(facts, parts, tails, half)
    packs = [pack, exchange(pack, 0, 1)]
    rotated, vectors_out, singular = finish(
        facts, packs, moved, native, vectors, half
    )
    return rotated, vectors_out, singular.reshape(size)


def solution(mesh):
    placed = (P("row", "pair"), P())
    return jax.shard_map(
        per_device,
        mesh=mesh,
        in_specs=placed,
        out_specs=(P("row", "pair"), P("row", "pair"), P("pair")),
        check_vma=False,
    )
```

```python
import jax
import jax.numpy as jnp
from jax import lax
from jax.experimental import pallas as pl
from jax.experimental.pallas import tpu as pltpu
from jax.sharding import PartitionSpec as P

ROUNDS = 4
NEWTON = 16

highest = lax.Precision.HIGHEST

TARGET = 2.0**-12
BOUNDS = [
    (1.0 + TARGET ** (2.0**-j)) / (1.0 - TARGET ** (2.0**-j)) for j in range(NEWTON)
]

X, CORE, FIRST, LAST, VROW, LABEL = 0, 1, 2, 3, 4, 5


def dot(a, b, precision=highest):
    return lax.dot_general(
        a, b, (((1,), (0,)), ((), ())), precision=precision,
        preferred_element_type=jnp.float32,
    )


def split(a):
    high = a.astype(jnp.bfloat16)
    return high, (a - high.astype(jnp.float32)).astype(jnp.bfloat16)


def dot3(a, b):
    a_high, a_low = a if isinstance(a, tuple) else split(a)
    b_high, b_low = b if isinstance(b, tuple) else split(b)
    small = dot(a_high, b_low, None) + dot(a_low, b_high, None)
    return dot(a_high, b_high, None) + small


def dot_tn(a, b):
    return lax.dot_general(
        a, b, (((0,), (0,)), ((), ())), precision=highest,
        preferred_element_type=jnp.float32,
    )


def shape(*dims):
    return jax.ShapeDtypeStruct(dims, jnp.float32)


def call(body, facts, inputs, outs, scratch=(), limit=24):
    return pl.pallas_call(
        body,
        out_shape=outs,
        in_specs=[pl.BlockSpec(memory_space=pltpu.SMEM)]
        + [pl.BlockSpec(memory_space=pltpu.VMEM)] * len(inputs),
        out_specs=jax.tree.map(
            lambda _: pl.BlockSpec(memory_space=pltpu.VMEM), outs
        ),
        scratch_shapes=list(scratch),
        compiler_params=pltpu.CompilerParams(vmem_limit_bytes=limit << 20),
    )(facts, *inputs)


def first_gram(facts, sector, half):
    rows, width = sector.shape
    part = rows // 2

    def body(f, x_ref, out_ref, give_ref):
        x = x_ref[...]
        g = dot_tn(x, x)
        out_ref[:half] = g[:half, :half]
        out_ref[half : 2 * half] = g[:half, half:]
        out_ref[2 * half :] = g[half:, half:]
        there = pl.multiple_of((1 - f[X]) * part, part)
        give_ref[...] = x_ref[pl.ds(there, part)]

    return call(
        body, facts, [sector], (shape(3 * half, half), shape(part, width))
    )


def rotate_of(gram, x_ref, e_ref):
    size = gram.shape[0]
    rows = lax.broadcasted_iota(jnp.int32, (size, size), 0)
    cols = lax.broadcasted_iota(jnp.int32, (size, size), 1)
    identity = (rows == cols).astype(jnp.float32)
    only = jnp.where(rows == cols, gram, 0.0)
    g_j = jnp.sum(only, axis=0, keepdims=True)
    g_i = jnp.sum(only, axis=1, keepdims=True)
    spread = g_j - g_i
    summed = g_j + g_i
    skew = gram * spread / (spread * spread + 2.0 * gram * gram + 0.01 * summed * summed)
    bound = 1.0 + 0.25 * jnp.sum(skew * skew)
    steps = jnp.int32(0)
    for limit in BOUNDS:
        steps = steps + (bound > limit).astype(jnp.int32)
    fixes = 1 + (steps > 7).astype(jnp.int32) + 2 * (steps > 9).astype(jnp.int32)
    scale = 2.0 / (1.0 + jnp.full((size, size), bound, jnp.float32))
    skew_parts = split(skew)
    residual = identity - scale * (identity - 0.25 * dot3(skew_parts, skew_parts))
    x_ref[...] = scale * (identity + residual)
    residual_parts = split(residual)
    e_ref[...] = dot3(residual_parts, residual_parts)

    def step(_, carry):
        e = split(e_ref[...])
        x = x_ref[...]
        x_ref[...] = x + dot3(x, e)
        e_ref[...] = dot3(e, e)
        return carry

    lax.fori_loop(0, jnp.maximum(steps - 1, 0), step, jnp.int32(0))
    x = x_ref[...]
    x_ref[...] = x + 0.5 * dot3(x, skew_parts)

    def fix(_, carry):
        x = x_ref[...]
        x_ref[...] = x + dot3(x, identity - (x - 0.5 * dot(skew, x)))
        return carry

    lax.fori_loop(0, fixes, fix, jnp.int32(0))
    return 2.0 * x_ref[...] - identity


def put_rotation(rotation_ref, gram, x_ref, e_ref, last_round):
    size = gram.shape[0]
    rotation = rotate_of(gram, x_ref, e_ref)
    rotation_ref[:size] = rotation
    if last_round:
        squares = jnp.sum(rotation * dot(gram, rotation), axis=0, keepdims=True)
        rotation_ref[size:] = jnp.broadcast_to(squares, (8, size))


def first_rotation(facts, own, near, far, half):
    size = 2 * half

    def body(f, own_ref, near_ref, far_ref, rotation_ref, g_ref, x_ref, e_ref):
        mine = f[X] == f[CORE]
        total = near_ref[...] + jnp.where(mine, own_ref[...], far_ref[...])
        g_ref[:half, :half] = total[:half]
        g_ref[:half, half:] = total[half : 2 * half]
        g_ref[half:, :half] = total[half : 2 * half].T
        g_ref[half:, half:] = total[2 * half :]
        put_rotation(rotation_ref, g_ref[...], x_ref, e_ref, False)

    square = pltpu.VMEM((size, size), jnp.float32)
    return call(
        body, facts, [own, near, far], (shape(size, size),) * 2, [square] * 2
    )


def later_rotation(facts, parts, tails, half, last_round):
    size = 2 * half
    top = tails[0].shape[0] - half

    def body(f, *refs):
        own, other_y, other_x, other_xy = [r[...] for r in refs[:4]]
        from_left, kept_left, nat_l, nat_u, from_right, kept_right = [
            r[top:] for r in refs[4:10]
        ]
        rotation_ref, g_ref, x_ref, e_ref = refs[10:]
        cross = (own + other_y) + (other_x + other_xy)
        first, last, core = f[FIRST] == 1, f[LAST] == 1, f[CORE] == 0
        up_0 = jnp.where(first, kept_left, from_left)
        low_1 = jnp.where(last, kept_right, from_right)
        g_ref[:half, :half] = jnp.where(core, up_0, nat_u)
        g_ref[:half, half:] = cross
        g_ref[half:, :half] = cross.T
        g_ref[half:, half:] = jnp.where(core, nat_l, low_1)
        put_rotation(rotation_ref, g_ref[...], x_ref, e_ref, last_round)

    square = pltpu.VMEM((size, size), jnp.float32)
    return call(
        body,
        facts,
        parts + tails,
        (shape(size + 8 if last_round else size, size), shape(size, size)),
        [square] * 2,
    )


def turned_gram(facts, gram, rotation):
    size = gram.shape[0]
    half = size // 2

    def body(f, gram_ref, rotation_ref, out_ref):
        rotation = rotation_ref[...]
        turned = dot(gram_ref[...], rotation)
        out_ref[:, :half] = dot_tn(rotation[:, :half], turned[:, :half])
        out_ref[:, half:] = dot_tn(rotation[:, half:], turned[:, half:])

    return call(body, facts, [gram, rotation], shape(half, size))


def two_packs(f, own, other):
    core = f[CORE] == 0
    return jnp.where(core, own, other), jnp.where(core, other, own)


def swapped(flag, matrix, axis):
    half = matrix.shape[axis] // 2
    a = lax.slice_in_dim(matrix, 0, half, axis=axis)
    b = lax.slice_in_dim(matrix, half, 2 * half, axis=axis)
    return jnp.where(flag, lax.concatenate([b, a], axis), matrix)


def blocks_of(f, refs, rows=None):
    vals = [r[...] if rows is None else r[:rows] for r in refs]
    from_left, kept_left, nat_l, nat_u, from_right, kept_right = vals
    up_0 = jnp.where(f[FIRST] == 1, kept_left, from_left)
    low_1 = jnp.where(f[LAST] == 1, kept_right, from_right)
    return up_0, nat_l, nat_u, low_1


def put_turned(f, refs, zero, one, half):
    to_left_ref, nat_l_ref, nat_u_ref, to_right_ref = refs[:4]
    rows = zero.shape[0]
    to_left_ref[:rows] = zero[:, half:]
    to_right_ref[:rows] = one[:, :half]
    nat_u_ref[:rows] = zero[:, :half]
    nat_l_ref[:rows] = one[:, half:]
    if len(refs) > 4:
        refs[4][...] = jnp.where(f[X] == 0, zero[:, :half], one[:, half:])


def turn(facts, packs, kept, got, blocks, half, last_move):
    size = 2 * half
    first_round = blocks is None
    inputs = packs + ([kept, got] if first_round else blocks)
    rows = got.shape[0] if first_round else blocks[0].shape[0]

    def body(f, *refs):
        own, other = refs[0][:size], refs[1][:size]
        turn_0, turn_1 = two_packs(f, own, other)
        turn_0 = swapped(f[FIRST] == 1, turn_0, 1)
        outs = refs[2 + len(inputs) - 2 :]
        if first_round:
            even = f[X] == 0
            here = pl.multiple_of(f[X] * rows, rows)
            mine, theirs = refs[2][pl.ds(here, rows)], refs[3][...]
            zero, one = jnp.where(even, mine, theirs), jnp.where(even, theirs, mine)
        else:
            up_0, low_0, up_1, low_1 = blocks_of(f, refs[2:8])
            zero = lax.concatenate([up_0, low_0], 1)
            one = lax.concatenate([up_1, low_1], 1)
        put_turned(f, outs, dot3(zero, turn_0), dot3(one, turn_1), half)

    return call(body, facts, inputs, (shape(rows, half),) * (5 if last_move else 4))


def turn_tail(facts, packs, grams, tails, vector_rows, half, last_move):
    size = 2 * half
    inputs = packs + grams + (tails or [])

    def body(f, *refs):
        pack_0, pack_1 = two_packs(f, refs[0][...], refs[1][...])
        gram_0, gram_1 = two_packs(f, refs[2][...], refs[3][...])
        pack_0 = swapped(f[FIRST] == 1, pack_0, 1)
        gram_0 = swapped(f[FIRST] == 1, gram_0, 1)
        outs = refs[len(inputs) :]
        if tails is None:
            rows = f[VROW] + lax.broadcasted_iota(jnp.int32, (vector_rows, half), 0)
            cols = lax.broadcasted_iota(jnp.int32, (vector_rows, half), 1)
            up_0, low_0, up_1, low_1 = [
                (rows == f[LABEL + k] * half + cols).astype(jnp.float32)
                for k in range(4)
            ]
        else:
            up_0, low_0, up_1, low_1 = blocks_of(f, refs[4:10], vector_rows)
        zero = dot3(lax.concatenate([up_0, low_0], 1), pack_0)
        one = dot3(lax.concatenate([up_1, low_1], 1), pack_1)
        put_turned(f, outs, zero, one, half)
        outs[0][vector_rows:] = gram_0[:, half:]
        outs[1][vector_rows:] = gram_1[:, half:]
        outs[2][vector_rows:] = gram_0[:, :half]
        outs[3][vector_rows:] = gram_1[:, :half]

    outs = (shape(vector_rows + half, half),) * 4
    if last_move:
        outs = outs + (shape(vector_rows, half),)
    return call(body, facts, inputs, outs)


def cross_gram(facts, blocks, half):
    def body(f, *refs):
        up_0, low_0, up_1, low_1 = blocks_of(f, refs[:6])
        zero, one = dot_tn(up_0, low_0), dot_tn(up_1, low_1)
        core = f[CORE] == 0
        refs[6][...] = jnp.where(core, zero, one)
        refs[7][...] = jnp.where(core, one, zero)

    return call(body, facts, blocks, (shape(half, half),) * 2)


def arrived(f, from_left_ref, kept_left_ref, from_right_ref, kept_right_ref, rows, other):
    up_0 = jnp.where(f[FIRST] == 1, kept_left_ref[rows], from_left_ref[rows])
    low_1 = jnp.where(f[LAST] == 1, kept_right_ref[rows], from_right_ref[rows])
    return jnp.where(f[X] == (1 if other else 0), up_0, low_1)


def ends(refs):
    return refs[0], refs[1], refs[4], refs[5]


def give_top(facts, blocks, rows, half):
    def body(f, *refs):
        refs[4][...] = arrived(f, *refs[:4], slice(0, rows), True)

    return call(body, facts, list(ends(blocks)), shape(rows, half))


def give_rest(facts, blocks, tails, top, vector_rows, half):
    rest = blocks[0].shape[0] - top

    def body(f, *refs):
        refs[8][:rest] = arrived(f, *refs[:4], slice(top, top + rest), True)
        refs[8][rest:] = arrived(f, *refs[4:8], slice(0, vector_rows), True)

    return call(
        body,
        facts,
        list(ends(blocks)) + list(ends(tails)),
        shape(rest + vector_rows, half),
    )


def finish(facts, packs, blocks, tails, got, vector_rows, half):
    size = 2 * half
    part = blocks[0].shape[0]
    top = got[2].shape[0]

    def body(f, *refs):
        x = f[X]
        mine = f[CORE] == x
        pack = jnp.where(mine, refs[0][...], refs[1][...])
        turned = split(swapped(x == 1, pack[:size], 0))
        block_refs, tail_refs = refs[2:8], refs[8:14]
        native_ref, native_tail_ref, top_ref, rest_ref = refs[14:18]
        out_ref, vectors_ref, singular_ref = refs[18:]

        def put(ref, at, rows, moved, native):
            here = pl.ds(pl.multiple_of(at, 8), rows)
            ref[here] = dot3(lax.concatenate([moved, native], 1), turned)

        def own(refs, rows):
            moved = arrived(f, *ends(refs), slice(0, rows), False)
            return moved, jnp.where(x == 0, refs[2][:rows], refs[3][:rows])

        put(out_ref, x * part, part, *own(block_refs, part))
        put(vectors_ref, x * vector_rows, vector_rows, *own(tail_refs, vector_rows))
        put(out_ref, (1 - x) * part, top, top_ref[...], native_ref[:top])
        put(
            out_ref, (1 - x) * part + top, part - top,
            rest_ref[: part - top], native_ref[top:],
        )
        put(
            vectors_ref, (1 - x) * vector_rows, vector_rows,
            rest_ref[part - top :], native_tail_ref[...],
        )
        squares = pack[size : size + 1]
        singular_ref[...] = jnp.sqrt(jnp.maximum(squares, 0.0) + 1e-06)

    return call(
        body,
        facts,
        packs + blocks + tails + got,
        (shape(2 * part, size), shape(2 * vector_rows, size), shape(1, size)),
    )


def per_device(sector, block_label):
    local_rows, size = sector.shape
    half = size // 2
    part = local_rows // 2
    pairs = lax.axis_size("pair")
    row_count = lax.axis_size("row")
    vector_rows = pairs * size // row_count // 2
    pair_index = lax.axis_index("pair")
    row_index = lax.axis_index("row")
    x = pair_index % 2
    group = pair_index // 2
    core = row_index % 2

    def permute(block, route):
        moves = [
            (a * row_count + b, c * row_count + d) for (a, b), (c, d) in route
        ]
        return lax.ppermute(block, ("pair", "row"), moves)

    devices = [(p, r) for p in range(pairs) for r in range(row_count)]

    def exchange(block, over_pair, over_row):
        return permute(
            block, [((p ^ over_pair, r ^ over_row), (p, r)) for p, r in devices]
        )

    def shift(block, by):
        return permute(
            block, [((p - by, r), (p, r)) for p, r in devices if 0 <= p - by < pairs]
        )

    def sum_rows(block):
        bit = 4
        while bit < row_count:
            block = block + exchange(block, 0, bit)
            bit *= 2
        return block

    names = jnp.arange(16, dtype=jnp.int32)
    facts = jnp.zeros((16,), jnp.int32)
    for name, value in (
        (X, x),
        (CORE, core),
        (FIRST, group == 0),
        (LAST, group == pairs // 2 - 1),
        (VROW, (row_index * 2 + x) * vector_rows),
    ):
        facts = jnp.where(names == name, value.astype(jnp.int32), facts)
    labels = lax.dynamic_slice_in_dim(block_label, 4 * group, 4)
    facts = lax.dynamic_update_slice_in_dim(facts, labels, LABEL, 0)

    def after(block, *others):
        return lax.optimization_barrier((block,) + others)[0]

    own, give = first_gram(facts, sector, half)
    own = sum_rows(own + exchange(own, 0, 1))
    near = permute(
        own,
        [
            ((p, r ^ 2) if p % 2 == r % 2 else (p ^ 1, r ^ 1), (p, r))
            for p, r in devices
        ],
    )
    far = permute(
        own, [((p ^ 1, r ^ 2), (p, r)) for p, r in devices if p % 2 != r % 2]
    )
    got = exchange(after(give, near, far), 1, 0)
    rotation, gram = first_rotation(facts, own, near, far, half)

    blocks = tails = None
    for sweep_round in range(ROUNDS - 1):
        packs = [rotation, exchange(rotation, 0, 1)]
        last_move = sweep_round == ROUNDS - 2
        to_left, nat_l, nat_u, to_right, *give = turn(
            facts, packs, sector, got, blocks, half, last_move
        )
        from_left, from_right = shift(to_right, 2), shift(to_left, -2)
        gram = turned_gram(facts, gram, rotation)
        tail_left, tail_l, tail_u, tail_right, *tail_give = turn_tail(
            facts, packs, [gram, exchange(gram, 0, 1)], tails, vector_rows, half,
            last_move,
        )
        tail_from_left, tail_from_right = shift(tail_right, 2), shift(tail_left, -2)
        blocks = [from_left, to_left, nat_l, nat_u, from_right, to_right]
        tails = [tail_from_left, tail_left, tail_l, tail_u, tail_from_right, tail_right]
        if last_move:
            native = exchange(give[0], 1, 0)
            native_tail = exchange(tail_give[0], 1, 0)
            top = part // 2
            top_give = give_top(facts, blocks, top, half)
            *blocks, native, native_tail, top_give = lax.optimization_barrier(
                tuple(blocks) + (native, native_tail, top_give)
            )
            got_top = exchange(top_give, 1, 0)
        grams = cross_gram(facts, blocks, half)
        own = sum_rows(grams[0] + exchange(grams[1], 0, 1))
        parts = [own, exchange(own, 0, 2), exchange(own, 1, 0), exchange(own, 1, 2)]
        if last_move:
            rest = give_rest(facts, blocks, tails, top, vector_rows, half)
            *parts, got_top, rest = lax.optimization_barrier(
                tuple(parts) + (got_top, rest)
            )
            got_rest = exchange(rest, 1, 0)
        rotation, gram = later_rotation(facts, parts, tails, half, last_move)
    packs = [rotation, exchange(rotation, 0, 1)]
    rotated, vectors_out, singular = finish(
        facts, packs, blocks, tails, [native, native_tail, got_top, got_rest],
        vector_rows, half,
    )
    return rotated, vectors_out, singular.reshape(size)


def solution(mesh):
    placed = (P("row", "pair"), P())
    return jax.shard_map(
        per_device,
        mesh=mesh,
        in_specs=placed,
        out_specs=(P("row", "pair"), P("row", "pair"), P("pair")),
        check_vma=False,
    )
```

```python
import jax
import jax.numpy as jnp
from jax import lax
from jax.experimental import pallas as pl
from jax.experimental.pallas import tpu as pltpu
from jax.sharding import PartitionSpec as P

ROUNDS = 4
NEWTON = 16

highest = lax.Precision.HIGHEST

TARGET = 2.0**-12
BOUNDS = [
    (1.0 + TARGET ** (2.0**-j)) / (1.0 - TARGET ** (2.0**-j)) for j in range(NEWTON)
]

X, CORE, FIRST, LAST, VROW, LABEL, EVEN = 0, 1, 2, 3, 4, 5, 9


def dot(a, b, precision=highest):
    return lax.dot_general(
        a, b, (((1,), (0,)), ((), ())), precision=precision,
        preferred_element_type=jnp.float32,
    )


def split(a):
    high = a.astype(jnp.bfloat16)
    return high, (a - high.astype(jnp.float32)).astype(jnp.bfloat16)


def dot3(a, b):
    a_high, a_low = a if isinstance(a, tuple) else split(a)
    b_high, b_low = b if isinstance(b, tuple) else split(b)
    small = dot(a_high, b_low, None) + dot(a_low, b_high, None)
    return dot(a_high, b_high, None) + small


def dot_tn(a, b):
    return lax.dot_general(
        a, b, (((0,), (0,)), ((), ())), precision=highest,
        preferred_element_type=jnp.float32,
    )


def shape(*dims):
    return jax.ShapeDtypeStruct(dims, jnp.float32)


def call(body, facts, inputs, outs, scratch=(), limit=24):
    return pl.pallas_call(
        body,
        out_shape=outs,
        in_specs=[pl.BlockSpec(memory_space=pltpu.SMEM)]
        + [pl.BlockSpec(memory_space=pltpu.VMEM)] * len(inputs),
        out_specs=jax.tree.map(
            lambda _: pl.BlockSpec(memory_space=pltpu.VMEM), outs
        ),
        scratch_shapes=list(scratch),
        compiler_params=pltpu.CompilerParams(vmem_limit_bytes=limit << 20),
    )(facts, *inputs)


def first_gram(facts, sector, half, top):
    rows, width = sector.shape
    part = rows // 2

    def body(f, x_ref, out_ref, give_ref):
        x = x_ref[...]
        g = dot_tn(x, x)
        out_ref[:half] = g[:half, :half]
        out_ref[half : 2 * half] = g[:half, half:]
        out_ref[2 * half :] = g[half:, half:]
        there = pl.multiple_of((1 - f[X]) * part + top, 8)
        give_ref[...] = x_ref[pl.ds(there, part - top)]

    return call(
        body, facts, [sector], (shape(3 * half, half), shape(part - top, width))
    )


def rotate_of(gram, x_ref, e_ref):
    size = gram.shape[0]
    rows = lax.broadcasted_iota(jnp.int32, (size, size), 0)
    cols = lax.broadcasted_iota(jnp.int32, (size, size), 1)
    identity = (rows == cols).astype(jnp.float32)
    only = jnp.where(rows == cols, gram, 0.0)
    g_j = jnp.sum(only, axis=0, keepdims=True)
    g_i = jnp.sum(only, axis=1, keepdims=True)
    spread = g_j - g_i
    summed = g_j + g_i
    skew = gram * spread / (spread * spread + 2.0 * gram * gram + 0.01 * summed * summed)
    bound = 1.0 + 0.25 * jnp.sum(skew * skew)
    steps = jnp.int32(0)
    for limit in BOUNDS:
        steps = steps + (bound > limit).astype(jnp.int32)
    fixes = 1 + (steps > 7).astype(jnp.int32) + 2 * (steps > 9).astype(jnp.int32)
    scale = 2.0 / (1.0 + jnp.full((size, size), bound, jnp.float32))
    skew_parts = split(skew)
    residual = identity - scale * (identity - 0.25 * dot3(skew_parts, skew_parts))
    x_ref[...] = scale * (identity + residual)
    residual_parts = split(residual)
    e_ref[...] = dot3(residual_parts, residual_parts)

    def step(_, carry):
        e = split(e_ref[...])
        x = x_ref[...]
        x_ref[...] = x + dot3(x, e)
        e_ref[...] = dot3(e, e)
        return carry

    lax.fori_loop(0, jnp.maximum(steps - 1, 0), step, jnp.int32(0))
    x = x_ref[...]
    x_ref[...] = x + 0.5 * dot3(x, skew_parts)

    def fix(_, carry):
        x = x_ref[...]
        x_ref[...] = x + dot3(x, identity - (x - 0.5 * dot(skew, x)))
        return carry

    lax.fori_loop(0, fixes, fix, jnp.int32(0))
    return 2.0 * x_ref[...] - identity


def put_rotation(rotation_ref, gram, x_ref, e_ref, last_round):
    size = gram.shape[0]
    rotation = rotate_of(gram, x_ref, e_ref)
    rotation_ref[:size] = rotation
    if last_round:
        squares = jnp.sum(rotation * dot(gram, rotation), axis=0, keepdims=True)
        rotation_ref[size:] = jnp.broadcast_to(squares, (8, size))


def first_rotation(facts, own, near, far, half):
    size = 2 * half

    def body(f, own_ref, near_ref, far_ref, rotation_ref, g_ref, x_ref, e_ref):
        mine = f[X] == f[CORE]
        total = near_ref[...] + jnp.where(mine, own_ref[...], far_ref[...])
        g_ref[:half, :half] = total[:half]
        g_ref[:half, half:] = total[half : 2 * half]
        g_ref[half:, :half] = total[half : 2 * half].T
        g_ref[half:, half:] = total[2 * half :]
        put_rotation(rotation_ref, g_ref[...], x_ref, e_ref, False)

    square = pltpu.VMEM((size, size), jnp.float32)
    return call(
        body, facts, [own, near, far], (shape(size, size),) * 2, [square] * 2
    )


def later_rotation(facts, parts, diagonals, half, last_round):
    size = 2 * half

    def body(f, *refs):
        own, other_y, other_x, other_xy, foreign, native = [r[...] for r in refs[:6]]
        rotation_ref, g_ref, x_ref, e_ref = refs[6:]
        cross = (own + other_y) + (other_x + other_xy)
        core = f[CORE] == 0
        g_ref[:half, :half] = jnp.where(core, foreign, native)
        g_ref[:half, half:] = cross
        g_ref[half:, :half] = cross.T
        g_ref[half:, half:] = jnp.where(core, native, foreign)
        put_rotation(rotation_ref, g_ref[...], x_ref, e_ref, last_round)

    square = pltpu.VMEM((size, size), jnp.float32)
    return call(
        body,
        facts,
        parts + diagonals,
        (shape(size + 8 if last_round else size, size), shape(size, size)),
        [square] * 2,
    )


def turned_gram(facts, gram, rotation):
    size = gram.shape[0]
    half = size // 2

    def body(f, gram_ref, rotation_ref, leave_ref, stay_ref):
        rotation = rotation_ref[...]
        turned = dot(gram_ref[...], rotation)
        upper = dot_tn(rotation[:, :half], turned[:, :half])
        lower = dot_tn(rotation[:, half:], turned[:, half:])
        lower_leaves = (f[CORE] == 0) & (f[FIRST] == 0)
        leave_ref[...] = jnp.where(lower_leaves, lower, upper)
        stay_ref[...] = jnp.where(lower_leaves, upper, lower)

    return call(body, facts, [gram, rotation], (shape(half, half),) * 2)


def two_packs(f, own, other):
    core = f[CORE] == 0
    return jnp.where(core, own, other), jnp.where(core, other, own)


def swapped(flag, matrix, axis):
    half = matrix.shape[axis] // 2
    a = lax.slice_in_dim(matrix, 0, half, axis=axis)
    b = lax.slice_in_dim(matrix, half, 2 * half, axis=axis)
    return jnp.where(flag, lax.concatenate([b, a], axis), matrix)


def blocks_of(f, got_a, got_b, low_0, up_1):
    even = f[EVEN] == 1
    return (
        jnp.where(even, got_b, got_a), low_0, up_1, jnp.where(even, got_a, got_b)
    )


def put_turned(f, refs, zero, one, half):
    a_ref, b_ref, nat_l_ref, nat_u_ref = refs[:4]
    even = f[EVEN] == 1
    to_left, to_right = zero[:, half:], one[:, :half]
    a_ref[...] = jnp.where(even, to_right, to_left)
    b_ref[...] = jnp.where(even, to_left, to_right)
    nat_l_ref[...] = one[:, half:]
    nat_u_ref[...] = zero[:, :half]
    if len(refs) > 4:
        refs[4][...] = jnp.where(f[X] == 0, zero[:, :half], one[:, half:])


def turns_of(f, own_ref, other_ref):
    size = other_ref.shape[1]
    turn_0, turn_1 = two_packs(f, own_ref[:size], other_ref[:size])
    return swapped(f[FIRST] == 1, turn_0, 1), turn_1


def turn_rows(facts, packs, rows_of, vector_rows, half, own):
    size = 2 * half
    rows = rows_of.shape[0] // 2 if own else rows_of.shape[0]

    def body(f, own_ref, other_ref, x_ref, stay_ref, leave_ref):
        turn_0, turn_1 = turns_of(f, own_ref, other_ref)
        zero = f[X] == (0 if own else 1)
        turn = split(jnp.where(zero, turn_0, swapped(True, turn_1, 1)))
        here = pl.multiple_of(f[X] * rows, 8)
        out = dot3(x_ref[pl.ds(here, rows)] if own else x_ref[...], turn)
        stay_ref[:rows] = out[:, :half]
        leave_ref[:rows] = out[:, half:]
        if vector_rows:
            ids = f[VROW] + lax.broadcasted_iota(jnp.int32, (vector_rows, half), 0)
            cols = lax.broadcasted_iota(jnp.int32, (vector_rows, half), 1)
            position = jnp.where(zero, 0, 2)
            vectors = [
                (ids == f[LABEL + position + k] * half + cols).astype(jnp.float32)
                for k in range(2)
            ]
            out = dot3(lax.concatenate(vectors, 1), turn)
            stay_ref[rows:] = out[:, :half]
            leave_ref[rows:] = out[:, half:]

    return call(
        body, facts, packs + [rows_of], (shape(rows + vector_rows, half),) * 2
    )


def turn(facts, packs, blocks, half, last_move):
    rows = blocks[0].shape[0]

    def body(f, own_ref, other_ref, *refs):
        turn_0, turn_1 = turns_of(f, own_ref, other_ref)
        up_0, low_0, up_1, low_1 = [r[...] for r in refs[:4]]
        zero = dot3(lax.concatenate([up_0, low_0], 1), turn_0)
        one = dot3(lax.concatenate([up_1, low_1], 1), turn_1)
        put_turned(f, refs[4:], zero, one, half)

    outs = (shape(rows, half),) * (5 if last_move else 4)
    return call(body, facts, packs + blocks, outs)


def put_cross(f, refs, zero, one):
    core = f[CORE] == 0
    refs[0][...] = jnp.where(core, zero, one)
    refs[1][...] = jnp.where(core, one, zero)


def first_cross_gram(facts, own, others, part, half):
    rows = own[0].shape[0]
    pieces = len(others)

    def body(f, *refs):
        own_refs = [[r] for r in refs[:3]]
        other_refs = [refs[3 + k : 3 + 3 * pieces : 3] for k in range(3)]
        up_0, low_0, up_1, low_1 = refs[5 + 3 * pieces :]

        def fill(target, sources):
            at = 0
            for ref in sources:
                target[at : at + ref.shape[0]] = ref[...]
                at += ref.shape[0]

        first, last = f[FIRST] == 1, f[LAST] == 1
        for x, near, far in ((0, own_refs, other_refs), (1, other_refs, own_refs)):
            here = f[X] == x

            @pl.when(here)
            def _():
                fill(up_1, near[0])
                fill(low_0, far[0])

            @pl.when(here & first)
            def _():
                fill(up_0, near[1])

            @pl.when(here & ~first)
            def _():
                fill(up_0, far[2])

            @pl.when(here & last)
            def _():
                fill(low_1, far[1])

            @pl.when(here & ~last)
            def _():
                fill(low_1, near[2])

        put_cross(
            f,
            refs[3 + 3 * pieces :],
            dot_tn(up_0[:part], low_0[:part]),
            dot_tn(up_1[:part], low_1[:part]),
        )

    outs = (shape(half, half),) * 2 + (shape(rows, half),) * 4
    return call(body, facts, own + sum(others, []), outs)


def cross_gram(facts, got, natives, part, half):
    rows = got[0].shape[0]

    def body(f, *refs):
        up_0, low_0, up_1, low_1 = blocks_of(f, *[r[...] for r in refs[:4]])
        put_cross(
            f,
            refs[4:],
            dot_tn(up_0[:part], low_0[:part]),
            dot_tn(up_1[:part], low_1[:part]),
        )
        refs[6][...] = up_0
        refs[7][...] = low_1

    outs = (shape(half, half),) * 2 + (shape(rows, half),) * 2
    return call(body, facts, got + natives, outs)


def give(facts, got, start, stop, half):
    def body(f, a_ref, b_ref, out_ref):
        mine = f[X] != f[EVEN]
        out_ref[...] = jnp.where(mine, a_ref[start:stop], b_ref[start:stop])

    return call(body, facts, got, shape(stop - start, half))


def finish(facts, packs, blocks, native, got_top, got_rest, part, half):
    size = 2 * half
    vector_rows = blocks[0].shape[0] - part
    top = got_top.shape[0]

    def body(f, *refs):
        x = f[X]
        mine = f[CORE] == x
        pack = jnp.where(mine, refs[0][...], refs[1][...])
        turned = split(swapped(x == 1, pack[:size], 0))
        native_ref, top_ref, rest_ref = refs[6:9]
        out_ref, vectors_ref, singular_ref = refs[9:]
        up_0, low_0, up_1, low_1 = [r[...] for r in refs[2:6]]

        def product(moved, native):
            return dot3(lax.concatenate([moved, native], 1), turned)

        def put(ref, at, value):
            ref[pl.ds(pl.multiple_of(at, 8), value.shape[0])] = value

        kept = product(jnp.where(x == 0, up_0, low_1), jnp.where(x == 0, low_0, up_1))
        put(out_ref, x * part, kept[:part])
        put(vectors_ref, x * vector_rows, kept[part:])
        there = (1 - x) * part
        put(out_ref, there, product(top_ref[...], native_ref[:top]))
        rest = product(rest_ref[...], native_ref[top:])
        put(out_ref, there + top, rest[: part - top])
        put(vectors_ref, (1 - x) * vector_rows, rest[part - top :])
        squares = pack[size : size + 1]
        singular_ref[...] = jnp.sqrt(jnp.maximum(squares, 0.0) + 1e-06)

    return call(
        body,
        facts,
        packs + blocks + [native, got_top, got_rest],
        (shape(2 * part, size), shape(2 * vector_rows, size), shape(1, size)),
    )


def per_device(sector, block_label):
    local_rows, size = sector.shape
    half = size // 2
    part = local_rows // 2
    pairs = lax.axis_size("pair")
    row_count = lax.axis_size("row")
    vector_rows = pairs * size // row_count // 2
    pair_index = lax.axis_index("pair")
    row_index = lax.axis_index("row")
    x = pair_index % 2
    group = pair_index // 2
    core = row_index % 2

    def permute(block, route):
        moves = [
            (a * row_count + b, c * row_count + d) for (a, b), (c, d) in route
        ]
        return lax.ppermute(block, ("pair", "row"), moves)

    devices = [(p, r) for p in range(pairs) for r in range(row_count)]

    def exchange(block, over_pair, over_row):
        return permute(
            block, [((p ^ over_pair, r ^ over_row), (p, r)) for p, r in devices]
        )

    def shift(block, even_by):
        moves = []
        for p, r in devices:
            source = p - even_by if p % 2 == 0 else p + even_by
            if 0 <= source < pairs:
                moves.append(((source, r), (p, r)))
        return permute(block, moves)

    def swap(block, odd):
        moves = []
        for p, r in devices:
            other = p + 2 if p // 2 % 2 == odd else p - 2
            moves.append(((other if 0 <= other < pairs else p, r), (p, r)))
        return permute(block, moves)

    def pass_diagonal(block):
        moves = []
        for p, r in devices:
            other = p + 2 if r % 2 else p - 2
            inside = 0 <= other < pairs
            moves.append(((other, r ^ 1) if inside else (p, r), (p, r)))
        return permute(block, [((a, b), c) for (a, b), c in moves])

    def sum_rows(block):
        bit = 4
        while bit < row_count:
            block = block + exchange(block, 0, bit)
            bit *= 2
        return block

    names = jnp.arange(16, dtype=jnp.int32)
    facts = jnp.zeros((16,), jnp.int32)
    for name, value in (
        (X, x),
        (CORE, core),
        (FIRST, group == 0),
        (LAST, group == pairs // 2 - 1),
        (VROW, (row_index * 2 + x) * vector_rows),
        (EVEN, group % 2 == 0),
    ):
        facts = jnp.where(names == name, value.astype(jnp.int32), facts)
    labels = lax.dynamic_slice_in_dim(block_label, 4 * group, 4)
    facts = lax.dynamic_update_slice_in_dim(facts, labels, LABEL, 0)

    def together(*arrays):
        return lax.optimization_barrier(arrays)

    top = part * 3 // 8
    got_top = exchange(
        lax.dynamic_slice_in_dim(sector, (1 - x) * part, top), 1, 0
    )
    own, rest = first_gram(facts, sector, half, top)
    own, got_top = together(sum_rows(own + exchange(own, 0, 1)), got_top)
    near = permute(
        own,
        [
            ((p, r ^ 2) if p % 2 == r % 2 else (p ^ 1, r ^ 1), (p, r))
            for p, r in devices
        ],
    )
    far = permute(
        own, [((p ^ 1, r ^ 2), (p, r)) for p, r in devices if p % 2 != r % 2]
    )
    got_rest = exchange(together(rest, own)[0], 1, 0)
    rotation, gram = first_rotation(facts, own, near, far, half)

    for sweep_round in range(ROUNDS - 1):
        packs = [rotation, exchange(rotation, 0, 1)]
        last_move = sweep_round == ROUNDS - 2
        if sweep_round == 0:
            stay, leave = turn_rows(facts, packs, sector, vector_rows, half, True)
            own_rows = [stay, leave, shift(leave, -2)]
            other_rows = []
            for got, below in ((got_top, 0), (got_rest, vector_rows)):
                got, leave = together(got, leave)
                stay, leave = turn_rows(facts, packs, got, below, half, False)
                other_rows.append([stay, leave, shift(leave, 2)])
        else:
            leave_a, leave_b, nat_l, nat_u, *native_give = turn(
                facts, packs, blocks, half, last_move
            )
            got = [swap(leave_a, 0), swap(leave_b, 1)]
        leave, stay = turned_gram(facts, gram, rotation)
        diagonals = [pass_diagonal(leave), exchange(stay, 0, 1)]
        if sweep_round == 0:
            own_rows[2], *diagonals = together(own_rows[2], *diagonals)
            *grams, up_0, nat_l, nat_u, low_1 = first_cross_gram(
                facts, own_rows, other_rows, part, half
            )
        else:
            *got, diagonals[0], diagonals[1] = together(*got, *diagonals)
            if last_move:
                native = exchange(native_give[0], 1, 0)
                top = part // 2
                top_give = give(facts, got, 0, top, half)
                *got, native, top_give = together(*got, native, top_give)
                got_top = exchange(top_give, 1, 0)
            *grams, up_0, low_1 = cross_gram(facts, got, [nat_l, nat_u], part, half)
        blocks = [up_0, nat_l, nat_u, low_1]
        own = sum_rows(grams[0] + exchange(grams[1], 0, 1))
        parts = [own, exchange(own, 0, 2), exchange(own, 1, 0), exchange(own, 1, 2)]
        if last_move:
            rest = give(facts, got, top, part + vector_rows, half)
            *parts, got_top, rest = together(*parts, got_top, rest)
            got_rest = exchange(rest, 1, 0)
        rotation, gram = later_rotation(facts, parts, diagonals, half, last_move)
    packs = [rotation, exchange(rotation, 0, 1)]
    rotated, vectors_out, singular = finish(
        facts, packs, blocks, native, got_top, got_rest, part, half
    )
    return rotated, vectors_out, singular.reshape(size)


def solution(mesh):
    placed = (P("row", "pair"), P())
    return jax.shard_map(
        per_device,
        mesh=mesh,
        in_specs=placed,
        out_specs=(P("row", "pair"), P("row", "pair"), P("pair")),
        check_vma=False,
    )
```

```python
import jax
import jax.numpy as jnp
from jax import lax
from jax.experimental import pallas as pl
from jax.experimental.pallas import tpu as pltpu
from jax.sharding import PartitionSpec as P

ROUNDS = 4
NEWTON = 16

highest = lax.Precision.HIGHEST

TARGET = 2.0**-12
REACHES = [
    (2.0 / (TARGET ** -(2.0**-j) - 1.0)) ** 2 for j in range(NEWTON)
]

X, CORE, FIRST, LAST, VROW, LABEL, EVEN = 0, 1, 2, 3, 4, 5, 9


def dot(a, b, precision=highest):
    return lax.dot_general(
        a, b, (((1,), (0,)), ((), ())), precision=precision,
        preferred_element_type=jnp.float32,
    )


def split(a):
    high = a.astype(jnp.bfloat16)
    return high, (a - high.astype(jnp.float32)).astype(jnp.bfloat16)


def dot3(a, b):
    a_high, a_low = a if isinstance(a, tuple) else split(a)
    b_high, b_low = b if isinstance(b, tuple) else split(b)
    small = dot(a_high, b_low, None) + dot(a_low, b_high, None)
    return dot(a_high, b_high, None) + small


def dot_tn(a, b):
    return lax.dot_general(
        a, b, (((0,), (0,)), ((), ())), precision=highest,
        preferred_element_type=jnp.float32,
    )


def shape(*dims):
    return jax.ShapeDtypeStruct(dims, jnp.float32)


def call(body, facts, inputs, outs, scratch=(), limit=24):
    return pl.pallas_call(
        body,
        out_shape=outs,
        in_specs=[pl.BlockSpec(memory_space=pltpu.SMEM)]
        + [pl.BlockSpec(memory_space=pltpu.VMEM)] * len(inputs),
        out_specs=jax.tree.map(
            lambda _: pl.BlockSpec(memory_space=pltpu.VMEM), outs
        ),
        scratch_shapes=list(scratch),
        compiler_params=pltpu.CompilerParams(vmem_limit_bytes=limit << 20),
    )(facts, *inputs)


def first_gram(facts, sector, half):
    def body(f, x_ref, out_ref):
        x = x_ref[...]
        g = dot_tn(x, x)
        out_ref[:half] = g[:half, :half]
        out_ref[half : 2 * half] = g[:half, half:]
        out_ref[2 * half :] = g[half:, half:]

    return call(body, facts, [sector], shape(3 * half, half))


def rotate_of(gram, x_ref, e_ref):
    size = gram.shape[0]
    rows = lax.broadcasted_iota(jnp.int32, (size, size), 0)
    cols = lax.broadcasted_iota(jnp.int32, (size, size), 1)
    identity = (rows == cols).astype(jnp.float32)
    only = jnp.where(rows == cols, gram, 0.0)
    g_j = jnp.sum(only, axis=0, keepdims=True)
    g_i = jnp.sum(only, axis=1, keepdims=True)
    spread = g_j - g_i
    summed = g_j + g_i
    skew = gram * spread / (spread * spread + 2.0 * gram * gram + 0.01 * summed * summed)
    skew_parts = split(skew)
    square = dot3(skew_parts, skew_parts)
    whole = 0.25 * jnp.sum(skew * skew)
    paired = 0.03125 * jnp.sum(square * square) * 1.001
    reach = jnp.minimum(whole * whole, paired)
    steps = jnp.int32(0)
    for limit in REACHES:
        steps = steps + (reach > limit).astype(jnp.int32)
    fixes = 1 + (steps > 7).astype(jnp.int32) + 2 * (steps > 9).astype(jnp.int32)
    scale = 2.0 / (2.0 + jnp.sqrt(jnp.full((size, size), reach, jnp.float32)))
    residual = identity - scale * (identity - 0.25 * square)
    x_ref[...] = scale * (identity + residual)
    residual_parts = split(residual)
    e_ref[...] = dot3(residual_parts, residual_parts)

    def step(_, carry):
        e = split(e_ref[...])
        x = x_ref[...]
        x_ref[...] = x + dot3(x, e)
        e_ref[...] = dot3(e, e)
        return carry

    lax.fori_loop(0, jnp.maximum(steps - 1, 0), step, jnp.int32(0))
    x = x_ref[...]
    x_ref[...] = x + 0.5 * dot3(x, skew_parts)

    def fix(_, carry):
        x = x_ref[...]
        x_ref[...] = x + dot3(x, identity - (x - 0.5 * dot(skew, x)))
        return carry

    lax.fori_loop(0, fixes, fix, jnp.int32(0))
    return 2.0 * x_ref[...] - identity


def put_rotation(rotation_ref, gram, x_ref, e_ref, last_round):
    size = gram.shape[0]
    rotation = rotate_of(gram, x_ref, e_ref)
    rotation_ref[:size] = rotation
    if last_round:
        squares = jnp.sum(rotation * dot(gram, rotation), axis=0, keepdims=True)
        rotation_ref[size:] = jnp.broadcast_to(squares, (8, size))


def first_rotation(facts, own, other_y, half):
    size = 2 * half

    def body(f, own_ref, other_ref, rotation_ref, g_ref, x_ref, e_ref):
        total = own_ref[...] + other_ref[...]
        g_ref[:half, :half] = total[:half]
        g_ref[:half, half:] = total[half : 2 * half]
        g_ref[half:, :half] = total[half : 2 * half].T
        g_ref[half:, half:] = total[2 * half :]
        put_rotation(rotation_ref, g_ref[...], x_ref, e_ref, False)

    square = pltpu.VMEM((size, size), jnp.float32)
    return call(body, facts, [own, other_y], (shape(size, size),) * 2, [square] * 2)


def later_rotation(facts, parts, diagonals, half, last_round):
    size = 2 * half

    def body(f, *refs):
        own, other_y, other_x, other_xy, foreign, native = [r[...] for r in refs[:6]]
        rotation_ref, g_ref, x_ref, e_ref = refs[6:]
        cross = (own + other_y) + (other_x + other_xy)
        core = f[CORE] == 0
        g_ref[:half, :half] = jnp.where(core, foreign, native)
        g_ref[:half, half:] = cross
        g_ref[half:, :half] = cross.T
        g_ref[half:, half:] = jnp.where(core, native, foreign)
        put_rotation(rotation_ref, g_ref[...], x_ref, e_ref, last_round)

    square = pltpu.VMEM((size, size), jnp.float32)
    return call(
        body,
        facts,
        parts + diagonals,
        (shape(size + 8 if last_round else size, size), shape(size, size)),
        [square] * 2,
    )


def turned_gram(facts, gram, rotation, position):
    size = gram.shape[0]
    half = size // 2

    def body(f, gram_ref, rotation_ref, leave_ref, stay_ref):
        rotation = rotation_ref[...]
        turned = dot(gram_ref[...], rotation)
        upper = dot_tn(rotation[:, :half], turned[:, :half])
        lower = dot_tn(rotation[:, half:], turned[:, half:])
        lower_leaves = (f[position] == 0) & (f[FIRST] == 0)
        leave_ref[...] = jnp.where(lower_leaves, lower, upper)
        stay_ref[...] = jnp.where(lower_leaves, upper, lower)

    return call(body, facts, [gram, rotation], (shape(half, half),) * 2)


def two_packs(f, own, other):
    core = f[CORE] == 0
    return jnp.where(core, own, other), jnp.where(core, other, own)


def swapped(flag, matrix, axis):
    half = matrix.shape[axis] // 2
    a = lax.slice_in_dim(matrix, 0, half, axis=axis)
    b = lax.slice_in_dim(matrix, half, 2 * half, axis=axis)
    return jnp.where(flag, lax.concatenate([b, a], axis), matrix)


def blocks_of(f, got_a, got_b, low_0, up_1):
    even = f[EVEN] == 1
    return (
        jnp.where(even, got_b, got_a), low_0, up_1, jnp.where(even, got_a, got_b)
    )


def put_turned(f, refs, zero, one, half):
    a_ref, b_ref, nat_l_ref, nat_u_ref = refs[:4]
    even = f[EVEN] == 1
    to_left, to_right = zero[:, half:], one[:, :half]
    a_ref[...] = jnp.where(even, to_right, to_left)
    b_ref[...] = jnp.where(even, to_left, to_right)
    nat_l_ref[...] = one[:, half:]
    nat_u_ref[...] = zero[:, :half]
    if len(refs) > 4:
        refs[4][...] = jnp.where(f[X] == 0, zero[:, :half], one[:, half:])


def turns_of(f, own_ref, other_ref):
    size = other_ref.shape[1]
    turn_0, turn_1 = two_packs(f, own_ref[:size], other_ref[:size])
    return swapped(f[FIRST] == 1, turn_0, 1), turn_1


def turn_rows(facts, rotation, rows_of, vector_rows, half, own):
    rows = rows_of.shape[0] // 2 if own else rows_of.shape[0]

    def body(f, rotation_ref, x_ref, stay_ref, leave_ref):
        zero = f[X] == (0 if own else 1)
        upper_leaves = jnp.where(zero, f[FIRST], 1) == 1
        turn = split(swapped(upper_leaves, rotation_ref[...], 1))
        here = pl.multiple_of(f[X] * rows, 8)
        out = dot3(x_ref[pl.ds(here, rows)] if own else x_ref[...], turn)
        stay_ref[:rows] = out[:, :half]
        leave_ref[:rows] = out[:, half:]
        ids = f[VROW] + lax.broadcasted_iota(jnp.int32, (vector_rows, half), 0)
        cols = lax.broadcasted_iota(jnp.int32, (vector_rows, half), 1)
        position = jnp.where(zero, 0, 2)
        vectors = [
            (ids == f[LABEL + position + k] * half + cols).astype(jnp.float32)
            for k in range(2)
        ]
        out = dot3(lax.concatenate(vectors, 1), turn)
        stay_ref[rows:] = out[:, :half]
        leave_ref[rows:] = out[:, half:]

    return call(
        body, facts, [rotation, rows_of], (shape(rows + vector_rows, half),) * 2
    )


def turn(facts, packs, blocks, half, last_move):
    rows = blocks[0].shape[0]

    def body(f, own_ref, other_ref, *refs):
        turn_0, turn_1 = turns_of(f, own_ref, other_ref)
        up_0, low_0, up_1, low_1 = [r[...] for r in refs[:4]]
        zero = dot3(lax.concatenate([up_0, low_0], 1), turn_0)
        one = dot3(lax.concatenate([up_1, low_1], 1), turn_1)
        put_turned(f, refs[4:], zero, one, half)

    outs = (shape(rows, half),) * (5 if last_move else 4)
    return call(body, facts, packs + blocks, outs)


def put_cross(f, refs, zero, one):
    core = f[CORE] == 0
    refs[0][...] = jnp.where(core, zero, one)
    refs[1][...] = jnp.where(core, one, zero)


def first_cross_gram(facts, own, other, part, half):
    rows = own[0].shape[0]

    def body(f, *refs):
        up_0, low_0, up_1, low_1 = refs[8:]
        first, last = f[FIRST] == 1, f[LAST] == 1
        for x, near, far in ((0, refs[:3], refs[3:6]), (1, refs[3:6], refs[:3])):
            here = f[X] == x

            @pl.when(here)
            def _():
                up_1[...] = near[0][...]
                low_0[...] = far[0][...]

            @pl.when(here & first)
            def _():
                up_0[...] = near[1][...]

            @pl.when(here & ~first)
            def _():
                up_0[...] = far[2][...]

            @pl.when(here & last)
            def _():
                low_1[...] = far[1][...]

            @pl.when(here & ~last)
            def _():
                low_1[...] = near[2][...]

        put_cross(
            f,
            refs[6:],
            dot_tn(up_0[:part], low_0[:part]),
            dot_tn(up_1[:part], low_1[:part]),
        )

    outs = (shape(half, half),) * 2 + (shape(rows, half),) * 4
    return call(body, facts, own + other, outs)


def cross_gram(facts, got, natives, part, half):
    rows = got[0].shape[0]

    def body(f, *refs):
        up_0, low_0, up_1, low_1 = blocks_of(f, *[r[...] for r in refs[:4]])
        put_cross(
            f,
            refs[4:],
            dot_tn(up_0[:part], low_0[:part]),
            dot_tn(up_1[:part], low_1[:part]),
        )
        refs[6][...] = up_0
        refs[7][...] = low_1

    outs = (shape(half, half),) * 2 + (shape(rows, half),) * 2
    return call(body, facts, got + natives, outs)


def give(facts, got, start, stop, half):
    def body(f, a_ref, b_ref, out_ref):
        mine = f[X] != f[EVEN]
        out_ref[...] = jnp.where(mine, a_ref[start:stop], b_ref[start:stop])

    return call(body, facts, got, shape(stop - start, half))


def finish(facts, packs, blocks, native, got_top, got_rest, part, half):
    size = 2 * half
    vector_rows = blocks[0].shape[0] - part
    top = got_top.shape[0]

    def body(f, *refs):
        x = f[X]
        mine = f[CORE] == x
        pack = jnp.where(mine, refs[0][...], refs[1][...])
        turned = split(swapped(x == 1, pack[:size], 0))
        native_ref, top_ref, rest_ref = refs[6:9]
        out_ref, vectors_ref, singular_ref = refs[9:]
        up_0, low_0, up_1, low_1 = [r[...] for r in refs[2:6]]

        def product(moved, native):
            return dot3(lax.concatenate([moved, native], 1), turned)

        def put(ref, at, value):
            ref[pl.ds(pl.multiple_of(at, 8), value.shape[0])] = value

        kept = product(jnp.where(x == 0, up_0, low_1), jnp.where(x == 0, low_0, up_1))
        put(out_ref, x * part, kept[:part])
        put(vectors_ref, x * vector_rows, kept[part:])
        there = (1 - x) * part
        put(out_ref, there, product(top_ref[...], native_ref[:top]))
        rest = product(rest_ref[...], native_ref[top:])
        put(out_ref, there + top, rest[: part - top])
        put(vectors_ref, (1 - x) * vector_rows, rest[part - top :])
        squares = pack[size : size + 1]
        singular_ref[...] = jnp.sqrt(jnp.maximum(squares, 0.0) + 1e-06)

    return call(
        body,
        facts,
        packs + blocks + [native, got_top, got_rest],
        (shape(2 * part, size), shape(2 * vector_rows, size), shape(1, size)),
    )


def per_device(sector, block_label):
    local_rows, size = sector.shape
    half = size // 2
    part = local_rows // 2
    pairs = lax.axis_size("pair")
    row_count = lax.axis_size("row")
    vector_rows = pairs * size // row_count // 2
    pair_index = lax.axis_index("pair")
    row_index = lax.axis_index("row")
    x = pair_index % 2
    group = pair_index // 2
    core = row_index % 2

    def permute(block, route):
        moves = [
            (a * row_count + b, c * row_count + d) for (a, b), (c, d) in route
        ]
        return lax.ppermute(block, ("pair", "row"), moves)

    devices = [(p, r) for p in range(pairs) for r in range(row_count)]

    def exchange(block, over_pair, over_row):
        return permute(
            block, [((p ^ over_pair, r ^ over_row), (p, r)) for p, r in devices]
        )

    def shift(block, even_by):
        moves = []
        for p, r in devices:
            source = p - even_by if p % 2 == 0 else p + even_by
            if 0 <= source < pairs:
                moves.append(((source, r), (p, r)))
        return permute(block, moves)

    def swap(block, odd):
        moves = []
        for p, r in devices:
            other = p + 2 if p // 2 % 2 == odd else p - 2
            moves.append(((other if 0 <= other < pairs else p, r), (p, r)))
        return permute(block, moves)

    def pass_diagonal(block):
        moves = []
        for p, r in devices:
            other = p + 2 if r % 2 else p - 2
            inside = 0 <= other < pairs
            moves.append(((other, r ^ 1) if inside else (p, r), (p, r)))
        return permute(block, [((a, b), c) for (a, b), c in moves])

    def first_diagonal(block, leaves):
        moves = []
        for p, r in devices:
            c, even = r % 2, p - p % 2
            if leaves:
                source = even - 1 if c == 0 else even + 2
                if not 0 <= source < pairs:
                    source = even + c
            else:
                source = even + 1 - c
            moves.append(((source, r - c + p % 2), (p, r)))
        return permute(block, moves)

    def sum_rows(block):
        bit = 4
        while bit < row_count:
            block = block + exchange(block, 0, bit)
            bit *= 2
        return block

    names = jnp.arange(16, dtype=jnp.int32)
    facts = jnp.zeros((16,), jnp.int32)
    for name, value in (
        (X, x),
        (CORE, core),
        (FIRST, group == 0),
        (LAST, group == pairs // 2 - 1),
        (VROW, (row_index * 2 + x) * vector_rows),
        (EVEN, group % 2 == 0),
    ):
        facts = jnp.where(names == name, value.astype(jnp.int32), facts)
    labels = lax.dynamic_slice_in_dim(block_label, 4 * group, 4)
    facts = lax.dynamic_update_slice_in_dim(facts, labels, LABEL, 0)

    def together(*arrays):
        return lax.optimization_barrier(arrays)

    got = exchange(lax.dynamic_slice_in_dim(sector, (1 - x) * part, part), 1, 0)
    own = first_gram(facts, sector, half)
    own = sum_rows(own + exchange(own, 0, 1))
    rotation, gram = first_rotation(facts, own, exchange(own, 0, 2), half)

    for sweep_round in range(ROUNDS - 1):
        last_move = sweep_round == ROUNDS - 2
        if sweep_round == 0:
            stay, leave = turn_rows(facts, rotation, sector, vector_rows, half, True)
            own_rows = [stay, leave, shift(leave, -2)]
            leave, stay = turned_gram(facts, gram, rotation, X)
            diagonals = [first_diagonal(leave, True), first_diagonal(stay, False)]
            other_rotation = exchange(rotation, 1, 0)
            stay, leave = turn_rows(
                facts, other_rotation, got, vector_rows, half, False
            )
            other_rows = [stay, leave, shift(leave, 2)]
        else:
            packs = [rotation, exchange(rotation, 0, 1)]
            leave_a, leave_b, nat_l, nat_u, *native_give = turn(
                facts, packs, blocks, half, last_move
            )
            got = [swap(leave_a, 0), swap(leave_b, 1)]
            leave, stay = turned_gram(facts, gram, rotation, CORE)
            diagonals = [pass_diagonal(leave), exchange(stay, 0, 1)]
        if sweep_round == 0:
            own_rows[2], *diagonals = together(own_rows[2], *diagonals)
            *grams, up_0, nat_l, nat_u, low_1 = first_cross_gram(
                facts, own_rows, other_rows, part, half
            )
        else:
            *got, diagonals[0], diagonals[1] = together(*got, *diagonals)
            if last_move:
                native = exchange(native_give[0], 1, 0)
                top = part // 2
                top_give = give(facts, got, 0, top, half)
                *got, native, top_give = together(*got, native, top_give)
                got_top = exchange(top_give, 1, 0)
            *grams, up_0, low_1 = cross_gram(facts, got, [nat_l, nat_u], part, half)
        blocks = [up_0, nat_l, nat_u, low_1]
        own = sum_rows(grams[0] + exchange(grams[1], 0, 1))
        parts = [own, exchange(own, 0, 2), exchange(own, 1, 0), exchange(own, 1, 2)]
        if last_move:
            rest = give(facts, got, top, part + vector_rows, half)
            *parts, got_top, rest = together(*parts, got_top, rest)
            got_rest = exchange(rest, 1, 0)
        rotation, gram = later_rotation(facts, parts, diagonals, half, last_move)
    packs = [rotation, exchange(rotation, 0, 1)]
    rotated, vectors_out, singular = finish(
        facts, packs, blocks, native, got_top, got_rest, part, half
    )
    return rotated, vectors_out, singular.reshape(size)


def solution(mesh):
    placed = (P("row", "pair"), P())
    return jax.shard_map(
        per_device,
        mesh=mesh,
        in_specs=placed,
        out_specs=(P("row", "pair"), P("row", "pair"), P("pair")),
        check_vma=False,
    )
```

```python
import jax
import jax.numpy as jnp
from jax import lax
from jax.experimental import pallas as pl
from jax.experimental.pallas import tpu as pltpu
from jax.sharding import PartitionSpec as P

ROUNDS = 4
NEWTON = 16

highest = lax.Precision.HIGHEST

TARGET = 2.0**-12
REACHES = [
    (2.0 / (TARGET ** -(2.0**-j) - 1.0)) ** 2 for j in range(NEWTON)
]

X, CORE, FIRST, LAST, VROW, LABEL, EVEN = 0, 1, 2, 3, 4, 5, 9


def dot(a, b, precision=highest):
    return lax.dot_general(
        a, b, (((1,), (0,)), ((), ())), precision=precision,
        preferred_element_type=jnp.float32,
    )


def split(a):
    high = a.astype(jnp.bfloat16)
    return high, (a - high.astype(jnp.float32)).astype(jnp.bfloat16)


def dot3(a, b):
    a_high, a_low = a if isinstance(a, tuple) else split(a)
    b_high, b_low = b if isinstance(b, tuple) else split(b)
    small = dot(a_high, b_low, None) + dot(a_low, b_high, None)
    return dot(a_high, b_high, None) + small


def dot_tn(a, b):
    return lax.dot_general(
        a, b, (((0,), (0,)), ((), ())), precision=highest,
        preferred_element_type=jnp.float32,
    )


def shape(*dims):
    return jax.ShapeDtypeStruct(dims, jnp.float32)


def call(body, facts, inputs, outs, scratch=(), limit=24):
    return pl.pallas_call(
        body,
        out_shape=outs,
        in_specs=[pl.BlockSpec(memory_space=pltpu.SMEM)]
        + [pl.BlockSpec(memory_space=pltpu.VMEM)] * len(inputs),
        out_specs=jax.tree.map(
            lambda _: pl.BlockSpec(memory_space=pltpu.VMEM), outs
        ),
        scratch_shapes=list(scratch),
        compiler_params=pltpu.CompilerParams(vmem_limit_bytes=limit << 20),
    )(facts, *inputs)


def first_gram(facts, sector, half):
    def body(f, x_ref, out_ref):
        x = x_ref[...]
        g = dot_tn(x, x)
        out_ref[:half] = g[:half, :half]
        out_ref[half : 2 * half] = g[:half, half:]
        out_ref[2 * half :] = g[half:, half:]

    return call(body, facts, [sector], shape(3 * half, half))


def rotate_of(gram, x_ref, e_ref):
    size = gram.shape[0]
    rows = lax.broadcasted_iota(jnp.int32, (size, size), 0)
    cols = lax.broadcasted_iota(jnp.int32, (size, size), 1)
    identity = (rows == cols).astype(jnp.float32)
    only = jnp.where(rows == cols, gram, 0.0)
    g_j = jnp.sum(only, axis=0, keepdims=True)
    g_i = jnp.sum(only, axis=1, keepdims=True)
    spread = g_j - g_i
    summed = g_j + g_i
    skew = gram * spread / (spread * spread + 2.0 * gram * gram + 0.01 * summed * summed)
    skew_parts = split(skew)
    square = dot3(skew_parts, skew_parts)
    whole = 0.25 * jnp.sum(skew * skew)
    paired = 0.03125 * jnp.sum(square * square) * 1.001
    reach = jnp.minimum(whole * whole, paired)
    steps = jnp.int32(0)
    for limit in REACHES:
        steps = steps + (reach > limit).astype(jnp.int32)
    fixes = 1 + (steps > 7).astype(jnp.int32) + 2 * (steps > 9).astype(jnp.int32)
    scale = 2.0 / (2.0 + jnp.sqrt(jnp.full((size, size), reach, jnp.float32)))
    residual = identity - scale * (identity - 0.25 * square)
    x_ref[...] = scale * (identity + residual)
    residual_parts = split(residual)
    e_ref[...] = dot3(residual_parts, residual_parts)

    def step(_, carry):
        e = split(e_ref[...])
        x = x_ref[...]
        x_ref[...] = x + dot3(x, e)
        e_ref[...] = dot3(e, e)
        return carry

    lax.fori_loop(0, jnp.maximum(steps - 1, 0), step, jnp.int32(0))
    x = x_ref[...]
    x_ref[...] = x + 0.5 * dot3(x, skew_parts)

    def fix(_, carry):
        x = x_ref[...]
        x_ref[...] = x + dot3(x, identity - (x - 0.5 * dot(skew, x)))
        return carry

    lax.fori_loop(0, fixes, fix, jnp.int32(0))
    return 2.0 * x_ref[...] - identity


def put_rotation(rotation_ref, gram, x_ref, e_ref, last_round):
    size = gram.shape[0]
    rotation = rotate_of(gram, x_ref, e_ref)
    rotation_ref[:size] = rotation
    if last_round:
        squares = jnp.sum(rotation * dot(gram, rotation), axis=0, keepdims=True)
        rotation_ref[size:] = jnp.broadcast_to(squares, (8, size))


def first_rotation(facts, own, other_y, half):
    size = 2 * half

    def body(f, own_ref, other_ref, rotation_ref, g_ref, x_ref, e_ref):
        total = own_ref[...] + other_ref[...]
        g_ref[:half, :half] = total[:half]
        g_ref[:half, half:] = total[half : 2 * half]
        g_ref[half:, :half] = total[half : 2 * half].T
        g_ref[half:, half:] = total[2 * half :]
        put_rotation(rotation_ref, g_ref[...], x_ref, e_ref, False)

    square = pltpu.VMEM((size, size), jnp.float32)
    return call(body, facts, [own, other_y], (shape(size, size),) * 2, [square] * 2)


def later_rotation(facts, parts, diagonals, half, last_round):
    size = 2 * half

    def body(f, *refs):
        own, other_y, other_x, other_xy, foreign, native = [r[...] for r in refs[:6]]
        rotation_ref, g_ref, x_ref, e_ref = refs[6:]
        cross = (own + other_y) + (other_x + other_xy)
        core = f[CORE] == 0
        g_ref[:half, :half] = jnp.where(core, foreign, native)
        g_ref[:half, half:] = cross
        g_ref[half:, :half] = cross.T
        g_ref[half:, half:] = jnp.where(core, native, foreign)
        put_rotation(rotation_ref, g_ref[...], x_ref, e_ref, last_round)

    square = pltpu.VMEM((size, size), jnp.float32)
    return call(
        body,
        facts,
        parts + diagonals,
        (shape(size + 8 if last_round else size, size), shape(size, size)),
        [square] * 2,
    )


def turned_gram(facts, gram, rotation, position):
    size = gram.shape[0]
    half = size // 2

    def body(f, gram_ref, rotation_ref, leave_ref, stay_ref):
        rotation = rotation_ref[...]
        turned = dot(gram_ref[...], rotation)
        upper = dot_tn(rotation[:, :half], turned[:, :half])
        lower = dot_tn(rotation[:, half:], turned[:, half:])
        lower_leaves = (f[position] == 0) & (f[FIRST] == 0)
        leave_ref[...] = jnp.where(lower_leaves, lower, upper)
        stay_ref[...] = jnp.where(lower_leaves, upper, lower)

    return call(body, facts, [gram, rotation], (shape(half, half),) * 2)


def two_packs(f, own, other):
    core = f[CORE] == 0
    return jnp.where(core, own, other), jnp.where(core, other, own)


def swapped(flag, matrix, axis):
    half = matrix.shape[axis] // 2
    a = lax.slice_in_dim(matrix, 0, half, axis=axis)
    b = lax.slice_in_dim(matrix, half, 2 * half, axis=axis)
    return jnp.where(flag, lax.concatenate([b, a], axis), matrix)


def blocks_of(f, got_a, got_b, low_0, up_1):
    even = f[EVEN] == 1
    return (
        jnp.where(even, got_b, got_a), low_0, up_1, jnp.where(even, got_a, got_b)
    )


def put_turned(f, refs, zero, one, half):
    a_ref, b_ref, nat_l_ref, nat_u_ref = refs
    even = f[EVEN] == 1
    to_left, to_right = zero[:, half:], one[:, :half]
    a_ref[...] = jnp.where(even, to_right, to_left)
    b_ref[...] = jnp.where(even, to_left, to_right)
    nat_l_ref[...] = one[:, half:]
    nat_u_ref[...] = zero[:, :half]


def turns_of(f, own_ref, other_ref):
    size = other_ref.shape[1]
    turn_0, turn_1 = two_packs(f, own_ref[:size], other_ref[:size])
    return swapped(f[FIRST] == 1, turn_0, 1), turn_1


def turn_rows(facts, rotation, rows_of, half, own):
    rows = rows_of.shape[0] // 2 if own else rows_of.shape[0]

    def body(f, rotation_ref, x_ref, stay_ref, leave_ref):
        zero = f[X] == (0 if own else 1)
        upper_leaves = jnp.where(zero, f[FIRST], 1) == 1
        turn = swapped(upper_leaves, rotation_ref[...], 1)
        here = pl.multiple_of(f[X] * rows, 8)
        out = dot3(x_ref[pl.ds(here, rows)] if own else x_ref[...], turn)
        stay_ref[...] = out[:, :half]
        leave_ref[...] = out[:, half:]

    return call(body, facts, [rotation, rows_of], (shape(rows, half),) * 2)


def first_vectors(facts, rotation, other_rotation, vector_rows, half):
    def body(f, own_ref, other_ref, *refs):
        even = f[X] == 0
        own, other = own_ref[...], other_ref[...]
        turn_0 = swapped(f[FIRST] == 1, jnp.where(even, own, other), 1)
        turn_1 = jnp.where(even, other, own)
        ids = f[VROW] + lax.broadcasted_iota(jnp.int32, (vector_rows, half), 0)
        cols = lax.broadcasted_iota(jnp.int32, (vector_rows, half), 1)
        up_0, low_0, up_1, low_1 = [
            (ids == f[LABEL + k] * half + cols).astype(jnp.float32) for k in range(4)
        ]
        zero = dot3(lax.concatenate([up_0, low_0], 1), turn_0)
        one = dot3(lax.concatenate([up_1, low_1], 1), turn_1)
        put_turned(f, refs, zero, one, half)

    return call(
        body, facts, [rotation, other_rotation], (shape(vector_rows, half),) * 4
    )


def turn(facts, packs, blocks, vectors, half, last_move):
    part, vector_rows = blocks[0].shape[0], vectors[0].shape[0]

    def body(f, own_ref, other_ref, *refs):
        turn_0, turn_1 = turns_of(f, own_ref, other_ref)
        turn_0, turn_1 = split(turn_0), split(turn_1)
        columns = [r[...] for r in refs[:4]]
        rows = blocks_of(f, *[r[...] for r in refs[4:8]])
        at = 0
        for (up_0, low_0, up_1, low_1), outs in (
            (columns, refs[8:12]), (rows, refs[12:16])
        ):
            zero = dot3(lax.concatenate([up_0, low_0], 1), turn_0)
            one = dot3(lax.concatenate([up_1, low_1], 1), turn_1)
            put_turned(f, outs, zero, one, half)
            if last_move:
                given = jnp.where(f[X] == 0, zero[:, :half], one[:, half:])
                refs[16][at : at + given.shape[0]] = given
                at += given.shape[0]

    outs = (shape(part, half),) * 4 + (shape(vector_rows, half),) * 4
    if last_move:
        outs = outs + (shape(part + vector_rows, half),)
    return call(body, facts, packs + blocks + vectors, outs)


def put_cross(f, refs, zero, one):
    core = f[CORE] == 0
    refs[0][...] = jnp.where(core, zero, one)
    refs[1][...] = jnp.where(core, one, zero)


def first_cross_gram(facts, own, other, half):
    rows = own[0].shape[0]

    def body(f, *refs):
        up_0, low_0, up_1, low_1 = refs[8:]
        first, last = f[FIRST] == 1, f[LAST] == 1
        for x, near, far in ((0, refs[:3], refs[3:6]), (1, refs[3:6], refs[:3])):
            here = f[X] == x

            @pl.when(here)
            def _():
                up_1[...] = near[0][...]
                low_0[...] = far[0][...]

            @pl.when(here & first)
            def _():
                up_0[...] = near[1][...]

            @pl.when(here & ~first)
            def _():
                up_0[...] = far[2][...]

            @pl.when(here & last)
            def _():
                low_1[...] = far[1][...]

            @pl.when(here & ~last)
            def _():
                low_1[...] = near[2][...]

        put_cross(
            f,
            refs[6:],
            dot_tn(up_0[...], low_0[...]),
            dot_tn(up_1[...], low_1[...]),
        )

    outs = (shape(half, half),) * 2 + (shape(rows, half),) * 4
    return call(body, facts, own + other, outs)


def cross_gram(facts, got, natives, half):
    rows = got[0].shape[0]

    def body(f, *refs):
        up_0, low_0, up_1, low_1 = blocks_of(f, *[r[...] for r in refs[:4]])
        put_cross(f, refs[4:], dot_tn(up_0, low_0), dot_tn(up_1, low_1))
        refs[6][...] = up_0
        refs[7][...] = low_1

    outs = (shape(half, half),) * 2 + (shape(rows, half),) * 2
    return call(body, facts, got + natives, outs)


def give(facts, pieces, half):
    total = sum(stop - start for _, start, stop in pieces)

    def body(f, *refs):
        mine = f[X] != f[EVEN]
        at = 0
        for k, (_, start, stop) in enumerate(pieces):
            a_ref, b_ref = refs[2 * k : 2 * k + 2]
            refs[-1][at : at + stop - start] = jnp.where(
                mine, a_ref[start:stop], b_ref[start:stop]
            )
            at += stop - start

    return call(
        body, facts, sum([list(got) for got, _, _ in pieces], []), shape(total, half)
    )


def finish(facts, packs, blocks, vectors, native, got_top, got_rest, half):
    size = 2 * half
    part, vector_rows = blocks[0].shape[0], vectors[0].shape[0]
    top = got_top.shape[0]

    def body(f, *refs):
        x = f[X]
        mine = f[CORE] == x
        pack = jnp.where(mine, refs[0][...], refs[1][...])
        turned = split(swapped(x == 1, pack[:size], 0))
        native_ref, top_ref, rest_ref = refs[10:13]
        out_ref, vectors_ref, singular_ref = refs[13:]

        def product(moved, native):
            return dot3(lax.concatenate([moved, native], 1), turned)

        def own(up_0, low_0, up_1, low_1):
            return product(
                jnp.where(x == 0, up_0, low_1), jnp.where(x == 0, low_0, up_1)
            )

        def put(ref, at, value):
            ref[pl.ds(pl.multiple_of(at, 8), value.shape[0])] = value

        put(out_ref, x * part, own(*[r[...] for r in refs[2:6]]))
        rows = blocks_of(f, *[r[...] for r in refs[6:10]])
        put(vectors_ref, x * vector_rows, own(*rows))
        there = (1 - x) * part
        put(out_ref, there, product(top_ref[...], native_ref[:top]))
        rest = product(rest_ref[...], native_ref[top:])
        put(out_ref, there + top, rest[: part - top])
        put(vectors_ref, (1 - x) * vector_rows, rest[part - top :])
        squares = pack[size : size + 1]
        singular_ref[...] = jnp.sqrt(jnp.maximum(squares, 0.0) + 1e-06)

    return call(
        body,
        facts,
        packs + blocks + vectors + [native, got_top, got_rest],
        (shape(2 * part, size), shape(2 * vector_rows, size), shape(1, size)),
    )


def per_device(sector, block_label):
    local_rows, size = sector.shape
    half = size // 2
    part = local_rows // 2
    pairs = lax.axis_size("pair")
    row_count = lax.axis_size("row")
    vector_rows = pairs * size // row_count // 2
    pair_index = lax.axis_index("pair")
    row_index = lax.axis_index("row")
    x = pair_index % 2
    group = pair_index // 2
    core = row_index % 2

    def permute(block, route):
        moves = [
            (a * row_count + b, c * row_count + d) for (a, b), (c, d) in route
        ]
        return lax.ppermute(block, ("pair", "row"), moves)

    devices = [(p, r) for p in range(pairs) for r in range(row_count)]

    def exchange(block, over_pair, over_row):
        return permute(
            block, [((p ^ over_pair, r ^ over_row), (p, r)) for p, r in devices]
        )

    def shift(block, even_by):
        moves = []
        for p, r in devices:
            source = p - even_by if p % 2 == 0 else p + even_by
            if 0 <= source < pairs:
                moves.append(((source, r), (p, r)))
        return permute(block, moves)

    def swap(block, odd):
        moves = []
        for p, r in devices:
            other = p + 2 if p // 2 % 2 == odd else p - 2
            moves.append(((other if 0 <= other < pairs else p, r), (p, r)))
        return permute(block, moves)

    def pass_diagonal(block):
        moves = []
        for p, r in devices:
            other = p + 2 if r % 2 else p - 2
            inside = 0 <= other < pairs
            moves.append(((other, r ^ 1) if inside else (p, r), (p, r)))
        return permute(block, [((a, b), c) for (a, b), c in moves])

    def first_diagonal(block, leaves):
        moves = []
        for p, r in devices:
            c, even = r % 2, p - p % 2
            if leaves:
                source = even - 1 if c == 0 else even + 2
                if not 0 <= source < pairs:
                    source = even + c
            else:
                source = even + 1 - c
            moves.append(((source, r - c + p % 2), (p, r)))
        return permute(block, moves)

    def sum_rows(block):
        bit = 4
        while bit < row_count:
            block = block + exchange(block, 0, bit)
            bit *= 2
        return block

    names = jnp.arange(16, dtype=jnp.int32)
    facts = jnp.zeros((16,), jnp.int32)
    for name, value in (
        (X, x),
        (CORE, core),
        (FIRST, group == 0),
        (LAST, group == pairs // 2 - 1),
        (VROW, (row_index * 2 + x) * vector_rows),
        (EVEN, group % 2 == 0),
    ):
        facts = jnp.where(names == name, value.astype(jnp.int32), facts)
    labels = lax.dynamic_slice_in_dim(block_label, 4 * group, 4)
    facts = lax.dynamic_update_slice_in_dim(facts, labels, LABEL, 0)

    def together(*arrays):
        return lax.optimization_barrier(arrays)

    got = exchange(lax.dynamic_slice_in_dim(sector, (1 - x) * part, part), 1, 0)
    own = first_gram(facts, sector, half)
    own = sum_rows(own + exchange(own, 0, 1))
    rotation, gram = first_rotation(facts, own, exchange(own, 0, 2), half)

    for sweep_round in range(ROUNDS - 1):
        last_move = sweep_round == ROUNDS - 2
        if sweep_round == 0:
            stay, leave = turn_rows(facts, rotation, sector, half, True)
            own_rows = [stay, leave, shift(leave, -2)]
            leave, stay = turned_gram(facts, gram, rotation, X)
            diagonals = [first_diagonal(leave, True), first_diagonal(stay, False)]
            other_rotation = exchange(rotation, 1, 0)
            stay, leave = turn_rows(facts, other_rotation, got, half, False)
            other_rows = [stay, leave, shift(leave, 2)]
            vectors = first_vectors(
                facts, rotation, other_rotation, vector_rows, half
            )
            own_rows[2], *diagonals = together(own_rows[2], *diagonals)
            *grams, up_0, nat_l, nat_u, low_1 = first_cross_gram(
                facts, own_rows, other_rows, half
            )
        else:
            packs = [rotation, exchange(rotation, 0, 1)]
            leave_a, leave_b, nat_l, nat_u, *vectors = turn(
                facts, packs, blocks, vectors, half, last_move
            )
            got = [swap(leave_a, 0), swap(leave_b, 1)]
            leave, stay = turned_gram(facts, gram, rotation, CORE)
            diagonals = [pass_diagonal(leave), exchange(stay, 0, 1)]
            *got, diagonals[0], diagonals[1] = together(*got, *diagonals)
            if last_move:
                native = exchange(vectors.pop(), 1, 0)
                top = part // 2
                top_give = give(facts, [(got, 0, top)], half)
                *got, native, top_give = together(*got, native, top_give)
                got_top = exchange(top_give, 1, 0)
            *grams, up_0, low_1 = cross_gram(facts, got, [nat_l, nat_u], half)
        blocks = [up_0, nat_l, nat_u, low_1]
        vector_a, vector_b, *kept = vectors
        vectors = [swap(vector_a, 0), swap(vector_b, 1)] + kept
        grams[1], vectors[0], vectors[1] = together(grams[1], *vectors[:2])
        own = sum_rows(grams[0] + exchange(grams[1], 0, 1))
        if last_move:
            rest = give(
                facts, [(got, top, part), (vectors[:2], 0, vector_rows)], half
            )
        parts = [own, exchange(own, 0, 2), exchange(own, 1, 0), exchange(own, 1, 2)]
        if last_move:
            parts[2], parts[3], got_top, rest = together(*parts[2:], got_top, rest)
            got_rest = exchange(rest, 1, 0)
        rotation, gram = later_rotation(facts, parts, diagonals, half, last_move)
    packs = [rotation, exchange(rotation, 0, 1)]
    rotated, vectors_out, singular = finish(
        facts, packs, blocks, vectors, native, got_top, got_rest, half
    )
    return rotated, vectors_out, singular.reshape(size)


def solution(mesh):
    placed = (P("row", "pair"), P())
    return jax.shard_map(
        per_device,
        mesh=mesh,
        in_specs=placed,
        out_specs=(P("row", "pair"), P("row", "pair"), P("pair")),
        check_vma=False,
    )
```

```python
import jax
import jax.numpy as jnp
from jax import lax
from jax.experimental import pallas as pl
from jax.experimental.pallas import tpu as pltpu
from jax.sharding import PartitionSpec as P

ROUNDS = 4
NEWTON = 16

highest = lax.Precision.HIGHEST

TARGET = 2.0**-12
REACHES = [
    (2.0 / (TARGET ** -(2.0**-j) - 1.0)) ** 2 for j in range(NEWTON)
]

X, CORE, FIRST, LAST, VROW, LABEL, EVEN = 0, 1, 2, 3, 4, 5, 9


def dot(a, b, precision=highest):
    return lax.dot_general(
        a, b, (((1,), (0,)), ((), ())), precision=precision,
        preferred_element_type=jnp.float32,
    )


def split(a):
    high = a.astype(jnp.bfloat16)
    return high, (a - high.astype(jnp.float32)).astype(jnp.bfloat16)


def dot3(a, b):
    a_high, a_low = a if isinstance(a, tuple) else split(a)
    b_high, b_low = b if isinstance(b, tuple) else split(b)
    small = dot(a_high, b_low, None) + dot(a_low, b_high, None)
    return dot(a_high, b_high, None) + small


def dot_tn(a, b):
    return lax.dot_general(
        a, b, (((0,), (0,)), ((), ())), precision=highest,
        preferred_element_type=jnp.float32,
    )


def shape(*dims):
    return jax.ShapeDtypeStruct(dims, jnp.float32)


def call(body, facts, inputs, outs, scratch=(), limit=24):
    return pl.pallas_call(
        body,
        out_shape=outs,
        in_specs=[pl.BlockSpec(memory_space=pltpu.SMEM)]
        + [pl.BlockSpec(memory_space=pltpu.VMEM)] * len(inputs),
        out_specs=jax.tree.map(
            lambda _: pl.BlockSpec(memory_space=pltpu.VMEM), outs
        ),
        scratch_shapes=list(scratch),
        compiler_params=pltpu.CompilerParams(vmem_limit_bytes=limit << 20),
    )(facts, *inputs)


def first_gram(facts, sector, half):
    def body(f, x_ref, out_ref):
        x = x_ref[...]
        g = dot_tn(x, x)
        out_ref[:half] = g[:half, :half]
        out_ref[half : 2 * half] = g[:half, half:]
        out_ref[2 * half :] = g[half:, half:]

    return call(body, facts, [sector], shape(3 * half, half))


def rotate_of(gram, x_ref, e_ref):
    size = gram.shape[0]
    rows = lax.broadcasted_iota(jnp.int32, (size, size), 0)
    cols = lax.broadcasted_iota(jnp.int32, (size, size), 1)
    identity = (rows == cols).astype(jnp.float32)
    only = jnp.where(rows == cols, gram, 0.0)
    g_j = jnp.sum(only, axis=0, keepdims=True)
    g_i = jnp.sum(only, axis=1, keepdims=True)
    spread = g_j - g_i
    summed = g_j + g_i
    skew = gram * spread / (spread * spread + 2.0 * gram * gram + 0.01 * summed * summed)
    skew_parts = split(skew)
    square = dot3(skew_parts, skew_parts)
    whole = 0.25 * jnp.sum(skew * skew)
    paired = 0.03125 * jnp.sum(square * square) * 1.001
    reach = jnp.minimum(whole * whole, paired)
    steps = jnp.int32(0)
    for limit in REACHES:
        steps = steps + (reach > limit).astype(jnp.int32)
    fixes = 1 + (steps > 7).astype(jnp.int32) + 2 * (steps > 9).astype(jnp.int32)
    scale = 2.0 / (2.0 + jnp.sqrt(jnp.full((size, size), reach, jnp.float32)))
    residual = identity - scale * (identity - 0.25 * square)
    x_ref[...] = scale * (identity + residual)
    residual_parts = split(residual)
    e_ref[...] = dot3(residual_parts, residual_parts)

    def step(_, carry):
        e = split(e_ref[...])
        x = x_ref[...]
        x_ref[...] = x + dot3(x, e)
        e_ref[...] = dot3(e, e)
        return carry

    lax.fori_loop(0, jnp.maximum(steps - 1, 0), step, jnp.int32(0))
    x = x_ref[...]
    x_ref[...] = x + 0.5 * dot3(x, skew_parts)

    def fix(_, carry):
        x = x_ref[...]
        x_ref[...] = x + dot3(x, identity - (x - 0.5 * dot(skew, x)))
        return carry

    lax.fori_loop(0, fixes, fix, jnp.int32(0))
    return 2.0 * x_ref[...] - identity


def put_rotation(rotation_ref, gram, x_ref, e_ref, last_round):
    size = gram.shape[0]
    rotation = rotate_of(gram, x_ref, e_ref)
    rotation_ref[:size] = rotation
    if last_round:
        squares = jnp.sum(rotation * dot(gram, rotation), axis=0, keepdims=True)
        rotation_ref[size:] = jnp.broadcast_to(squares, (8, size))


def first_rotation(facts, own, other_y, half):
    size = 2 * half

    def body(f, own_ref, other_ref, rotation_ref, g_ref, x_ref, e_ref):
        total = own_ref[...] + other_ref[...]
        g_ref[:half, :half] = total[:half]
        g_ref[:half, half:] = total[half : 2 * half]
        g_ref[half:, :half] = total[half : 2 * half].T
        g_ref[half:, half:] = total[2 * half :]
        put_rotation(rotation_ref, g_ref[...], x_ref, e_ref, False)

    square = pltpu.VMEM((size, size), jnp.float32)
    return call(body, facts, [own, other_y], (shape(size, size),) * 2, [square] * 2)


def later_rotation(facts, parts, diagonals, half, last_round):
    size = 2 * half

    def body(f, *refs):
        own, other_y, other_x, other_xy, foreign, native = [r[...] for r in refs[:6]]
        rotation_ref, g_ref, x_ref, e_ref = refs[6:]
        cross = (own + other_y) + (other_x + other_xy)
        core = f[CORE] == 0
        g_ref[:half, :half] = jnp.where(core, foreign, native)
        g_ref[:half, half:] = cross
        g_ref[half:, :half] = cross.T
        g_ref[half:, half:] = jnp.where(core, native, foreign)
        put_rotation(rotation_ref, g_ref[...], x_ref, e_ref, last_round)

    square = pltpu.VMEM((size, size), jnp.float32)
    return call(
        body,
        facts,
        parts + diagonals,
        (shape(size + 8 if last_round else size, size), shape(size, size)),
        [square] * 2,
    )


def turned_gram(facts, gram, rotation, position):
    size = gram.shape[0]
    half = size // 2

    def body(f, gram_ref, rotation_ref, leave_ref, stay_ref):
        rotation = rotation_ref[...]
        turned = dot(gram_ref[...], rotation)
        upper = dot_tn(rotation[:, :half], turned[:, :half])
        lower = dot_tn(rotation[:, half:], turned[:, half:])
        lower_leaves = (f[position] == 0) & (f[FIRST] == 0)
        leave_ref[...] = jnp.where(lower_leaves, lower, upper)
        stay_ref[...] = jnp.where(lower_leaves, upper, lower)

    return call(body, facts, [gram, rotation], (shape(half, half),) * 2)


def two_packs(f, own, other):
    core = f[CORE] == 0
    return jnp.where(core, own, other), jnp.where(core, other, own)


def swapped(flag, matrix, axis):
    half = matrix.shape[axis] // 2
    a = lax.slice_in_dim(matrix, 0, half, axis=axis)
    b = lax.slice_in_dim(matrix, half, 2 * half, axis=axis)
    return jnp.where(flag, lax.concatenate([b, a], axis), matrix)


def blocks_of(f, got_a, got_b, low_0, up_1):
    even = f[EVEN] == 1
    return (
        jnp.where(even, got_b, got_a), low_0, up_1, jnp.where(even, got_a, got_b)
    )


def put_turned(f, refs, zero, one, half):
    a_ref, b_ref, nat_l_ref, nat_u_ref = refs
    even = f[EVEN] == 1
    to_left, to_right = zero[:, half:], one[:, :half]
    a_ref[...] = jnp.where(even, to_right, to_left)
    b_ref[...] = jnp.where(even, to_left, to_right)
    nat_l_ref[...] = one[:, half:]
    nat_u_ref[...] = zero[:, :half]


def turns_of(f, own_ref, other_ref):
    size = other_ref.shape[1]
    turn_0, turn_1 = two_packs(f, own_ref[:size], other_ref[:size])
    return swapped(f[FIRST] == 1, turn_0, 1), turn_1


def turn_rows(facts, rotation, rows_of, half, own):
    rows = rows_of.shape[0] // 2 if own else rows_of.shape[0]

    def body(f, rotation_ref, x_ref, stay_ref, leave_ref):
        zero = f[X] == (0 if own else 1)
        upper_leaves = jnp.where(zero, f[FIRST], 1) == 1
        turn = swapped(upper_leaves, rotation_ref[...], 1)
        here = pl.multiple_of(f[X] * rows, 8)
        out = dot3(x_ref[pl.ds(here, rows)] if own else x_ref[...], turn)
        stay_ref[...] = out[:, :half]
        leave_ref[...] = out[:, half:]

    return call(body, facts, [rotation, rows_of], (shape(rows, half),) * 2)


def first_vectors(facts, rotation, other_rotation, vector_rows, half):
    def body(f, own_ref, other_ref, *refs):
        even = f[X] == 0
        own, other = own_ref[...], other_ref[...]
        turn_0 = swapped(f[FIRST] == 1, jnp.where(even, own, other), 1)
        turn_1 = jnp.where(even, other, own)
        ids = f[VROW] + lax.broadcasted_iota(jnp.int32, (vector_rows, half), 0)
        cols = lax.broadcasted_iota(jnp.int32, (vector_rows, half), 1)
        up_0, low_0, up_1, low_1 = [
            (ids == f[LABEL + k] * half + cols).astype(jnp.float32) for k in range(4)
        ]
        zero = dot3(lax.concatenate([up_0, low_0], 1), turn_0)
        one = dot3(lax.concatenate([up_1, low_1], 1), turn_1)
        put_turned(f, refs, zero, one, half)

    return call(
        body, facts, [rotation, other_rotation], (shape(vector_rows, half),) * 4
    )


def turn(facts, packs, blocks, vectors, half, last_move):
    part, vector_rows = blocks[0].shape[0], vectors[0].shape[0]

    def body(f, own_ref, other_ref, *refs):
        turn_0, turn_1 = turns_of(f, own_ref, other_ref)
        turn_0, turn_1 = split(turn_0), split(turn_1)
        columns = [r[...] for r in refs[:4]]
        rows = blocks_of(f, *[r[...] for r in refs[4:8]])
        at = 0
        for (up_0, low_0, up_1, low_1), outs in (
            (columns, refs[8:12]), (rows, refs[12:16])
        ):
            zero = dot3(lax.concatenate([up_0, low_0], 1), turn_0)
            one = dot3(lax.concatenate([up_1, low_1], 1), turn_1)
            put_turned(f, outs, zero, one, half)
            if last_move:
                given = jnp.where(f[X] == 0, zero[:, :half], one[:, half:])
                refs[16][at : at + given.shape[0]] = given
                at += given.shape[0]

    outs = (shape(part, half),) * 4 + (shape(vector_rows, half),) * 4
    if last_move:
        outs = outs + (shape(part + vector_rows, half),)
    return call(body, facts, packs + blocks + vectors, outs)


def put_cross(f, refs, zero, one):
    core = f[CORE] == 0
    refs[0][...] = jnp.where(core, zero, one)
    refs[1][...] = jnp.where(core, one, zero)


def first_cross_gram(facts, own, other, half):
    rows = own[0].shape[0]

    def body(f, *refs):
        up_0, low_0, up_1, low_1 = refs[8:]
        first, last = f[FIRST] == 1, f[LAST] == 1
        for x, near, far in ((0, refs[:3], refs[3:6]), (1, refs[3:6], refs[:3])):
            here = f[X] == x

            @pl.when(here)
            def _():
                up_1[...] = near[0][...]
                low_0[...] = far[0][...]

            @pl.when(here & first)
            def _():
                up_0[...] = near[1][...]

            @pl.when(here & ~first)
            def _():
                up_0[...] = far[2][...]

            @pl.when(here & last)
            def _():
                low_1[...] = far[1][...]

            @pl.when(here & ~last)
            def _():
                low_1[...] = near[2][...]

        put_cross(
            f,
            refs[6:],
            dot_tn(up_0[...], low_0[...]),
            dot_tn(up_1[...], low_1[...]),
        )

    outs = (shape(half, half),) * 2 + (shape(rows, half),) * 4
    return call(body, facts, own + other, outs)


def cross_gram(facts, got, natives, half):
    rows = got[0].shape[0]

    def body(f, *refs):
        up_0, low_0, up_1, low_1 = blocks_of(f, *[r[...] for r in refs[:4]])
        put_cross(f, refs[4:], dot_tn(up_0, low_0), dot_tn(up_1, low_1))
        refs[6][...] = up_0
        refs[7][...] = low_1

    outs = (shape(half, half),) * 2 + (shape(rows, half),) * 2
    return call(body, facts, got + natives, outs)


def give(facts, pieces, half):
    total = sum(stop - start for _, start, stop in pieces)

    def body(f, *refs):
        mine = f[X] != f[EVEN]
        at = 0
        for k, (_, start, stop) in enumerate(pieces):
            a_ref, b_ref = refs[2 * k : 2 * k + 2]
            refs[-1][at : at + stop - start] = jnp.where(
                mine, a_ref[start:stop], b_ref[start:stop]
            )
            at += stop - start

    return call(
        body, facts, sum([list(got) for got, _, _ in pieces], []), shape(total, half)
    )


def finish(facts, packs, blocks, vectors, native, got_top, got_rest, half):
    size = 2 * half
    part, vector_rows = blocks[0].shape[0], vectors[0].shape[0]
    top = got_top.shape[0]

    def body(f, *refs):
        x = f[X]
        mine = f[CORE] == x
        pack = jnp.where(mine, refs[0][...], refs[1][...])
        turned = split(swapped(x == 1, pack[:size], 0))
        native_ref, top_ref, rest_ref = refs[10:13]
        out_ref, vectors_ref, singular_ref = refs[13:]

        def product(moved, native):
            return dot3(lax.concatenate([moved, native], 1), turned)

        def own(up_0, low_0, up_1, low_1):
            return product(
                jnp.where(x == 0, up_0, low_1), jnp.where(x == 0, low_0, up_1)
            )

        def put(ref, at, value):
            ref[pl.ds(pl.multiple_of(at, 8), value.shape[0])] = value

        put(out_ref, x * part, own(*[r[...] for r in refs[2:6]]))
        rows = blocks_of(f, *[r[...] for r in refs[6:10]])
        put(vectors_ref, x * vector_rows, own(*rows))
        there = (1 - x) * part
        put(out_ref, there, product(top_ref[...], native_ref[:top]))
        rest = product(rest_ref[...], native_ref[top:])
        put(out_ref, there + top, rest[: part - top])
        put(vectors_ref, (1 - x) * vector_rows, rest[part - top :])
        squares = pack[size : size + 1]
        singular_ref[...] = jnp.sqrt(jnp.maximum(squares, 0.0) + 1e-06)

    return call(
        body,
        facts,
        packs + blocks + vectors + [native, got_top, got_rest],
        (shape(2 * part, size), shape(2 * vector_rows, size), shape(1, size)),
    )


def per_device(sector, block_label):
    local_rows, size = sector.shape
    half = size // 2
    part = local_rows // 2
    pairs = lax.axis_size("pair")
    row_count = lax.axis_size("row")
    vector_rows = pairs * size // row_count // 2
    pair_index = lax.axis_index("pair")
    row_index = lax.axis_index("row")
    x = pair_index % 2
    group = pair_index // 2
    core = row_index % 2

    def permute(block, route):
        moves = [
            (a * row_count + b, c * row_count + d) for (a, b), (c, d) in route
        ]
        return lax.ppermute(block, ("pair", "row"), moves)

    devices = [(p, r) for p in range(pairs) for r in range(row_count)]

    def exchange(block, over_pair, over_row):
        return permute(
            block, [((p ^ over_pair, r ^ over_row), (p, r)) for p, r in devices]
        )

    def shift(block, even_by):
        moves = []
        for p, r in devices:
            source = p - even_by if p % 2 == 0 else p + even_by
            if 0 <= source < pairs:
                moves.append(((source, r), (p, r)))
        return permute(block, moves)

    def swap(block, odd):
        moves = []
        for p, r in devices:
            other = p + 2 if p // 2 % 2 == odd else p - 2
            moves.append(((other if 0 <= other < pairs else p, r), (p, r)))
        return permute(block, moves)

    def pass_diagonal(block):
        moves = []
        for p, r in devices:
            other = p + 2 if r % 2 else p - 2
            inside = 0 <= other < pairs
            moves.append(((other, r ^ 1) if inside else (p, r), (p, r)))
        return permute(block, [((a, b), c) for (a, b), c in moves])

    def first_diagonal(block, leaves):
        moves = []
        for p, r in devices:
            c, even = r % 2, p - p % 2
            if leaves:
                source = even - 1 if c == 0 else even + 2
                if not 0 <= source < pairs:
                    source = even + c
            else:
                source = even + 1 - c
            moves.append(((source, r - c + p % 2), (p, r)))
        return permute(block, moves)

    def sum_rows(block):
        bit = 4
        while bit < row_count:
            block = block + exchange(block, 0, bit)
            bit *= 2
        return block

    names = jnp.arange(16, dtype=jnp.int32)
    facts = jnp.zeros((16,), jnp.int32)
    for name, value in (
        (X, x),
        (CORE, core),
        (FIRST, group == 0),
        (LAST, group == pairs // 2 - 1),
        (VROW, (row_index * 2 + x) * vector_rows),
        (EVEN, group % 2 == 0),
    ):
        facts = jnp.where(names == name, value.astype(jnp.int32), facts)
    labels = lax.dynamic_slice_in_dim(block_label, 4 * group, 4)
    facts = lax.dynamic_update_slice_in_dim(facts, labels, LABEL, 0)

    def together(*arrays):
        return lax.optimization_barrier(arrays)

    got = exchange(lax.dynamic_slice_in_dim(sector, (1 - x) * part, part), 1, 0)
    own = first_gram(facts, sector, half)
    own = sum_rows(own + exchange(own, 0, 1))
    rotation, gram = first_rotation(facts, own, exchange(own, 0, 2), half)

    for sweep_round in range(ROUNDS - 1):
        last_move = sweep_round == ROUNDS - 2
        if sweep_round == 0:
            stay, leave = turn_rows(facts, rotation, sector, half, True)
            own_rows = [stay, leave, shift(leave, -2)]
            leave, stay = turned_gram(facts, gram, rotation, X)
            diagonals = [first_diagonal(leave, True), first_diagonal(stay, False)]
            other_rotation = exchange(rotation, 1, 0)
            stay, leave = turn_rows(facts, other_rotation, got, half, False)
            other_rows = [stay, leave, shift(leave, 2)]
            vectors = list(
                first_vectors(facts, rotation, other_rotation, vector_rows, half)
            )
            vectors[0], vectors[1], diagonals[1] = together(
                vectors[0], vectors[1], diagonals[1]
            )
            *grams, up_0, nat_l, nat_u, low_1 = first_cross_gram(
                facts, own_rows, other_rows, half
            )
        else:
            packs = [rotation, exchange(rotation, 0, 1)]
            leave_a, leave_b, nat_l, nat_u, *vectors = turn(
                facts, packs, blocks, vectors, half, last_move
            )
            got = [swap(leave_a, 0), swap(leave_b, 1)]
            leave, stay = turned_gram(facts, gram, rotation, CORE)
            diagonals = [pass_diagonal(leave), exchange(stay, 0, 1)]
            vectors[0], vectors[1], diagonals[1] = together(
                vectors[0], vectors[1], diagonals[1]
            )
            if last_move:
                native = exchange(vectors.pop(), 1, 0)
                top = part // 2
                top_give = give(facts, [(got, 0, top)], half)
                *got, top_give = together(*got, top_give)
                got_top = exchange(top_give, 1, 0)
            *grams, up_0, low_1 = cross_gram(facts, got, [nat_l, nat_u], half)
            if last_move:
                grams[1], native = together(grams[1], native)
        blocks = [up_0, nat_l, nat_u, low_1]
        vector_a, vector_b, *kept = vectors
        vectors = [swap(vector_a, 0), swap(vector_b, 1)] + kept
        grams[1], vectors[0], vectors[1], diagonals[0] = together(
            grams[1], *vectors[:2], diagonals[0]
        )
        own = sum_rows(grams[0] + exchange(grams[1], 0, 1))
        if last_move:
            rest = give(
                facts, [(got, top, part), (vectors[:2], 0, vector_rows)], half
            )
        parts = [own, exchange(own, 0, 2), exchange(own, 1, 0), exchange(own, 1, 2)]
        if last_move:
            parts[2], parts[3], got_top, rest = together(*parts[2:], got_top, rest)
            got_rest = exchange(rest, 1, 0)
        rotation, gram = later_rotation(facts, parts, diagonals, half, last_move)
    packs = [rotation, exchange(rotation, 0, 1)]
    rotated, vectors_out, singular = finish(
        facts, packs, blocks, vectors, native, got_top, got_rest, half
    )
    return rotated, vectors_out, singular.reshape(size)


def solution(mesh):
    placed = (P("row", "pair"), P())
    return jax.shard_map(
        per_device,
        mesh=mesh,
        in_specs=placed,
        out_specs=(P("row", "pair"), P("row", "pair"), P("pair")),
        check_vma=False,
    )
```

```python
import jax
import jax.numpy as jnp
from jax import lax
from jax.experimental import pallas as pl
from jax.experimental.pallas import tpu as pltpu
from jax.sharding import PartitionSpec as P

ROUNDS = 4
NEWTON = 16

highest = lax.Precision.HIGHEST

TARGET = 2.0**-12
REACHES = [
    (2.0 / (TARGET ** -(2.0**-j) - 1.0)) ** 2 for j in range(NEWTON)
]

X, CORE, FIRST, LAST, VROW, LABEL, EVEN = 0, 1, 2, 3, 4, 5, 9


def dot(a, b, precision=highest):
    return lax.dot_general(
        a, b, (((1,), (0,)), ((), ())), precision=precision,
        preferred_element_type=jnp.float32,
    )


def split(a):
    high = a.astype(jnp.bfloat16)
    return high, (a - high.astype(jnp.float32)).astype(jnp.bfloat16)


def dot3(a, b):
    a_high, a_low = a if isinstance(a, tuple) else split(a)
    b_high, b_low = b if isinstance(b, tuple) else split(b)
    small = dot(a_high, b_low, None) + dot(a_low, b_high, None)
    return dot(a_high, b_high, None) + small


def dot_tn(a, b):
    return lax.dot_general(
        a, b, (((0,), (0,)), ((), ())), precision=highest,
        preferred_element_type=jnp.float32,
    )


def shape(*dims):
    return jax.ShapeDtypeStruct(dims, jnp.float32)


def call(body, facts, inputs, outs, scratch=(), limit=24):
    return pl.pallas_call(
        body,
        out_shape=outs,
        in_specs=[pl.BlockSpec(memory_space=pltpu.SMEM)]
        + [pl.BlockSpec(memory_space=pltpu.VMEM)] * len(inputs),
        out_specs=jax.tree.map(
            lambda _: pl.BlockSpec(memory_space=pltpu.VMEM), outs
        ),
        scratch_shapes=list(scratch),
        compiler_params=pltpu.CompilerParams(vmem_limit_bytes=limit << 20),
    )(facts, *inputs)


def first_gram(facts, sector, half):
    def body(f, x_ref, out_ref):
        x = x_ref[...]
        g = dot_tn(x, x)
        out_ref[:half] = g[:half, :half]
        out_ref[half : 2 * half] = g[:half, half:]
        out_ref[2 * half :] = g[half:, half:]

    return call(body, facts, [sector], shape(3 * half, half))


def give_rows(facts, sector, top):
    rows, width = sector.shape
    part = rows // 2

    def body(f, x_ref, top_ref, rest_ref, sems):
        start = pl.multiple_of((1 - f[X]) * part, 8)
        copies = [
            pltpu.make_async_copy(
                x_ref.at[pl.ds(start, top)], top_ref, sems.at[0]
            ),
            pltpu.make_async_copy(
                x_ref.at[pl.ds(start + top, part - top)], rest_ref, sems.at[1]
            ),
        ]
        for copy in copies:
            copy.start()
        for copy in copies:
            copy.wait()

    return pl.pallas_call(
        body,
        out_shape=(shape(top, width), shape(part - top, width)),
        in_specs=[
            pl.BlockSpec(memory_space=pltpu.SMEM), pl.BlockSpec(memory_space=pl.ANY)
        ],
        out_specs=(pl.BlockSpec(memory_space=pltpu.VMEM),) * 2,
        scratch_shapes=[pltpu.SemaphoreType.DMA((2,))],
    )(facts, sector)


def rotate_of(gram, x_ref, e_ref):
    size = gram.shape[0]
    rows = lax.broadcasted_iota(jnp.int32, (size, size), 0)
    cols = lax.broadcasted_iota(jnp.int32, (size, size), 1)
    identity = (rows == cols).astype(jnp.float32)
    only = jnp.where(rows == cols, gram, 0.0)
    g_j = jnp.sum(only, axis=0, keepdims=True)
    g_i = jnp.sum(only, axis=1, keepdims=True)
    spread = g_j - g_i
    summed = g_j + g_i
    skew = gram * spread / (spread * spread + 2.0 * gram * gram + 0.01 * summed * summed)
    skew_parts = split(skew)
    square = dot3(skew_parts, skew_parts)
    whole = 0.25 * jnp.sum(skew * skew)
    paired = 0.03125 * jnp.sum(square * square) * 1.001
    reach = jnp.minimum(whole * whole, paired)
    steps = jnp.int32(0)
    for limit in REACHES:
        steps = steps + (reach > limit).astype(jnp.int32)
    fixes = 1 + (steps > 7).astype(jnp.int32) + 2 * (steps > 9).astype(jnp.int32)
    scale = 2.0 / (2.0 + jnp.sqrt(jnp.full((size, size), reach, jnp.float32)))
    residual = identity - scale * (identity - 0.25 * square)
    x_ref[...] = scale * (identity + residual)
    residual_parts = split(residual)
    e_ref[...] = dot3(residual_parts, residual_parts)

    def step(_, carry):
        e = split(e_ref[...])
        x = x_ref[...]
        x_ref[...] = x + dot3(x, e)
        e_ref[...] = dot3(e, e)
        return carry

    lax.fori_loop(0, jnp.maximum(steps - 1, 0), step, jnp.int32(0))
    x = x_ref[...]
    x_ref[...] = x + 0.5 * dot3(x, skew_parts)

    def fix(_, carry):
        x = x_ref[...]
        x_ref[...] = x + dot3(x, identity - (x - 0.5 * dot(skew, x)))
        return carry

    lax.fori_loop(0, fixes, fix, jnp.int32(0))
    return 2.0 * x_ref[...] - identity


def put_rotation(rotation_ref, gram, x_ref, e_ref, last_round):
    size = gram.shape[0]
    rotation = rotate_of(gram, x_ref, e_ref)
    rotation_ref[:size] = rotation
    if last_round:
        squares = jnp.sum(rotation * dot(gram, rotation), axis=0, keepdims=True)
        rotation_ref[size:] = jnp.broadcast_to(squares, (8, size))


def first_rotation(facts, own, other_y, half):
    size = 2 * half

    def body(f, own_ref, other_ref, rotation_ref, g_ref, x_ref, e_ref):
        total = own_ref[...] + other_ref[...]
        g_ref[:half, :half] = total[:half]
        g_ref[:half, half:] = total[half : 2 * half]
        g_ref[half:, :half] = total[half : 2 * half].T
        g_ref[half:, half:] = total[2 * half :]
        put_rotation(rotation_ref, g_ref[...], x_ref, e_ref, False)

    square = pltpu.VMEM((size, size), jnp.float32)
    return call(body, facts, [own, other_y], (shape(size, size),) * 2, [square] * 2)


def later_rotation(facts, parts, diagonals, half, last_round):
    size = 2 * half

    def body(f, *refs):
        own, other_y, other_x, other_xy, foreign, native = [r[...] for r in refs[:6]]
        rotation_ref, g_ref, x_ref, e_ref = refs[6:]
        cross = (own + other_y) + (other_x + other_xy)
        core = f[CORE] == 0
        g_ref[:half, :half] = jnp.where(core, foreign, native)
        g_ref[:half, half:] = cross
        g_ref[half:, :half] = cross.T
        g_ref[half:, half:] = jnp.where(core, native, foreign)
        put_rotation(rotation_ref, g_ref[...], x_ref, e_ref, last_round)

    square = pltpu.VMEM((size, size), jnp.float32)
    return call(
        body,
        facts,
        parts + diagonals,
        (shape(size + 8 if last_round else size, size), shape(size, size)),
        [square] * 2,
    )


def turned_gram(facts, gram, rotation, position):
    size = gram.shape[0]
    half = size // 2

    def body(f, gram_ref, rotation_ref, leave_ref, stay_ref):
        rotation = rotation_ref[...]
        turned = dot(gram_ref[...], rotation)
        upper = dot_tn(rotation[:, :half], turned[:, :half])
        lower = dot_tn(rotation[:, half:], turned[:, half:])
        lower_leaves = (f[position] == 0) & (f[FIRST] == 0)
        leave_ref[...] = jnp.where(lower_leaves, lower, upper)
        stay_ref[...] = jnp.where(lower_leaves, upper, lower)

    return call(body, facts, [gram, rotation], (shape(half, half),) * 2)


def two_packs(f, own, other):
    core = f[CORE] == 0
    return jnp.where(core, own, other), jnp.where(core, other, own)


def swapped(flag, matrix, axis):
    half = matrix.shape[axis] // 2
    a = lax.slice_in_dim(matrix, 0, half, axis=axis)
    b = lax.slice_in_dim(matrix, half, 2 * half, axis=axis)
    return jnp.where(flag, lax.concatenate([b, a], axis), matrix)


def blocks_of(f, got_a, got_b, low_0, up_1):
    even = f[EVEN] == 1
    return (
        jnp.where(even, got_b, got_a), low_0, up_1, jnp.where(even, got_a, got_b)
    )


def put_turned(f, refs, zero, one, half, at=0):
    a_ref, b_ref, nat_l_ref, nat_u_ref = refs[:4]
    even = f[EVEN] == 1
    rows = slice(at, at + zero.shape[0])
    to_left, to_right = zero[:, half:], one[:, :half]
    a_ref[rows] = jnp.where(even, to_right, to_left)
    b_ref[rows] = jnp.where(even, to_left, to_right)
    nat_l_ref[rows] = one[:, half:]
    nat_u_ref[rows] = zero[:, :half]
    if len(refs) > 4:
        refs[4][rows] = jnp.where(f[X] == 0, zero[:, :half], one[:, half:])


def turns_of(f, own_ref, other_ref):
    size = other_ref.shape[1]
    turn_0, turn_1 = two_packs(f, own_ref[:size], other_ref[:size])
    return swapped(f[FIRST] == 1, turn_0, 1), turn_1


def turn_rows(facts, rotation, rows_of, half, own):
    rows = rows_of.shape[0] // 2 if own else rows_of.shape[0]

    def body(f, rotation_ref, x_ref, stay_ref, leave_ref):
        zero = f[X] == (0 if own else 1)
        upper_leaves = jnp.where(zero, f[FIRST], 1) == 1
        turn = swapped(upper_leaves, rotation_ref[...], 1)
        here = pl.multiple_of(f[X] * rows, 8)
        out = dot3(x_ref[pl.ds(here, rows)] if own else x_ref[...], turn)
        stay_ref[...] = out[:, :half]
        leave_ref[...] = out[:, half:]

    return call(body, facts, [rotation, rows_of], (shape(rows, half),) * 2)


def first_vectors(facts, rotation, other_rotation, vector_rows, half):
    def body(f, own_ref, other_ref, *refs):
        even = f[X] == 0
        own, other = own_ref[...], other_ref[...]
        turn_0 = swapped(f[FIRST] == 1, jnp.where(even, own, other), 1)
        turn_1 = jnp.where(even, other, own)
        ids = f[VROW] + lax.broadcasted_iota(jnp.int32, (vector_rows, half), 0)
        cols = lax.broadcasted_iota(jnp.int32, (vector_rows, half), 1)
        up_0, low_0, up_1, low_1 = [
            (ids == f[LABEL + k] * half + cols).astype(jnp.float32) for k in range(4)
        ]
        zero = dot3(lax.concatenate([up_0, low_0], 1), turn_0)
        one = dot3(lax.concatenate([up_1, low_1], 1), turn_1)
        put_turned(f, refs, zero, one, half)

    return call(
        body, facts, [rotation, other_rotation], (shape(vector_rows, half),) * 4
    )


def turn(facts, packs, blocks, vectors, half, last_move):
    part, vector_rows = blocks[0].shape[0], vectors[0].shape[0]

    def body(f, own_ref, other_ref, *refs):
        turn_0, turn_1 = turns_of(f, own_ref, other_ref)
        turn_0, turn_1 = split(turn_0), split(turn_1)
        columns = [r[...] for r in refs[:4]]
        rows = blocks_of(f, *[r[...] for r in refs[4:8]])
        outs = refs[8:]
        for (up_0, low_0, up_1, low_1), at in ((columns, 0), (rows, part)):
            zero = dot3(lax.concatenate([up_0, low_0], 1), turn_0)
            one = dot3(lax.concatenate([up_1, low_1], 1), turn_1)
            if last_move:
                put_turned(f, outs, zero, one, half, at)
            else:
                put_turned(f, outs[4 if at else 0 :][:4], zero, one, half)

    if last_move:
        outs = (shape(part + vector_rows, half),) * 5
    else:
        outs = (shape(part, half),) * 4 + (shape(vector_rows, half),) * 4
    return call(body, facts, packs + blocks + vectors, outs)


def put_cross(f, refs, zero, one):
    core = f[CORE] == 0
    refs[0][...] = jnp.where(core, zero, one)
    refs[1][...] = jnp.where(core, one, zero)


def first_cross_gram(facts, own, others, half):
    rows = own[0].shape[0]
    pieces = len(others)

    def body(f, *refs):
        own_refs = [[r] for r in refs[:3]]
        other_refs = [refs[3 + k : 3 + 3 * pieces : 3] for k in range(3)]
        up_0, low_0, up_1, low_1 = refs[5 + 3 * pieces :]

        def fill(target, sources):
            at = 0
            for ref in sources:
                target[at : at + ref.shape[0]] = ref[...]
                at += ref.shape[0]

        first, last = f[FIRST] == 1, f[LAST] == 1
        for x, near, far in ((0, own_refs, other_refs), (1, other_refs, own_refs)):
            here = f[X] == x

            @pl.when(here)
            def _():
                fill(up_1, near[0])
                fill(low_0, far[0])

            @pl.when(here & first)
            def _():
                fill(up_0, near[1])

            @pl.when(here & ~first)
            def _():
                fill(up_0, far[2])

            @pl.when(here & last)
            def _():
                fill(low_1, far[1])

            @pl.when(here & ~last)
            def _():
                fill(low_1, near[2])

        put_cross(
            f,
            refs[3 + 3 * pieces :],
            dot_tn(up_0[...], low_0[...]),
            dot_tn(up_1[...], low_1[...]),
        )

    outs = (shape(half, half),) * 2 + (shape(rows, half),) * 4
    return call(body, facts, own + sum(others, []), outs)


def cross_gram(facts, got, natives, part, half):
    rows = got[0].shape[0]

    def body(f, *refs):
        up_0, low_0, up_1, low_1 = blocks_of(f, *[r[...] for r in refs[:4]])
        put_cross(
            f,
            refs[4:],
            dot_tn(up_0[:part], low_0[:part]),
            dot_tn(up_1[:part], low_1[:part]),
        )
        refs[6][...] = up_0
        refs[7][...] = low_1

    outs = (shape(half, half),) * 2 + (shape(rows, half),) * 2
    return call(body, facts, got + natives, outs)


def give(facts, got, start, stop, half):
    def body(f, a_ref, b_ref, out_ref):
        mine = f[X] != f[EVEN]
        out_ref[...] = jnp.where(mine, a_ref[start:stop], b_ref[start:stop])

    return call(body, facts, got, shape(stop - start, half))


def finish(facts, packs, blocks, native, got_top, got_rest, part, half):
    size = 2 * half
    vector_rows = blocks[0].shape[0] - part
    top = got_top.shape[0]

    def body(f, *refs):
        x = f[X]
        mine = f[CORE] == x
        pack = jnp.where(mine, refs[0][...], refs[1][...])
        turned = split(swapped(x == 1, pack[:size], 0))
        native_ref, top_ref, rest_ref = refs[6:9]
        out_ref, vectors_ref, singular_ref, out, vectors, sems = refs[9:]
        copies = []

        def put(source, target, here, there, value):
            rows = value.shape[0]
            source[here : here + rows] = value
            there = pl.multiple_of(there, 8)
            copies.append(
                pltpu.make_async_copy(
                    source.at[here : here + rows],
                    target.at[pl.ds(there, rows)],
                    sems.at[len(copies)],
                )
            )
            copies[-1].start()

        def product(moved, native):
            return dot3(lax.concatenate([moved, native], 1), turned)

        def kept(rows):
            up_0, low_0, up_1, low_1 = [r[rows] for r in refs[2:6]]
            return product(
                jnp.where(x == 0, up_0, low_1), jnp.where(x == 0, low_0, up_1)
            )

        squares = pack[size : size + 1]
        singular_ref[...] = jnp.sqrt(jnp.maximum(squares, 0.0) + 1e-06)
        other = (1 - x) * part
        middle = part // 2
        put(out, out_ref, 0, x * part, kept(slice(0, middle)))
        put(out, out_ref, middle, x * part + middle, kept(slice(middle, part)))
        put(out, out_ref, part, other, product(top_ref[...], native_ref[:top]))
        put(
            out, out_ref, part + top, other + top,
            product(rest_ref[: part - top], native_ref[top:part]),
        )
        put(vectors, vectors_ref, 0, x * vector_rows, kept(slice(part, None)))
        put(
            vectors, vectors_ref, vector_rows, (1 - x) * vector_rows,
            product(rest_ref[part - top :], native_ref[part:]),
        )
        for copy in copies:
            copy.wait()

    vmem = pl.BlockSpec(memory_space=pltpu.VMEM)
    hbm = pl.BlockSpec(memory_space=pl.ANY)
    inputs = packs + blocks + [native, got_top, got_rest]
    return pl.pallas_call(
        body,
        out_shape=(
            shape(2 * part, size), shape(2 * vector_rows, size), shape(1, size)
        ),
        in_specs=[pl.BlockSpec(memory_space=pltpu.SMEM)] + [vmem] * len(inputs),
        out_specs=(hbm, hbm, vmem),
        scratch_shapes=[
            pltpu.VMEM((2 * part, size), jnp.float32),
            pltpu.VMEM((2 * vector_rows, size), jnp.float32),
            pltpu.SemaphoreType.DMA((6,)),
        ],
        compiler_params=pltpu.CompilerParams(vmem_limit_bytes=24 << 20),
    )(facts, *inputs)


def per_device(sector, block_label):
    local_rows, size = sector.shape
    half = size // 2
    part = local_rows // 2
    pairs = lax.axis_size("pair")
    row_count = lax.axis_size("row")
    vector_rows = pairs * size // row_count // 2
    pair_index = lax.axis_index("pair")
    row_index = lax.axis_index("row")
    x = pair_index % 2
    group = pair_index // 2
    core = row_index % 2

    def permute(block, route):
        moves = [
            (a * row_count + b, c * row_count + d) for (a, b), (c, d) in route
        ]
        return lax.ppermute(block, ("pair", "row"), moves)

    devices = [(p, r) for p in range(pairs) for r in range(row_count)]

    def exchange(block, over_pair, over_row):
        return permute(
            block, [((p ^ over_pair, r ^ over_row), (p, r)) for p, r in devices]
        )

    def shift(block, even_by):
        moves = []
        for p, r in devices:
            source = p - even_by if p % 2 == 0 else p + even_by
            if 0 <= source < pairs:
                moves.append(((source, r), (p, r)))
        return permute(block, moves)

    def swap(block, odd):
        moves = []
        for p, r in devices:
            other = p + 2 if p // 2 % 2 == odd else p - 2
            moves.append(((other if 0 <= other < pairs else p, r), (p, r)))
        return permute(block, moves)

    def pass_diagonal(block):
        moves = []
        for p, r in devices:
            other = p + 2 if r % 2 else p - 2
            inside = 0 <= other < pairs
            moves.append(((other, r ^ 1) if inside else (p, r), (p, r)))
        return permute(block, [((a, b), c) for (a, b), c in moves])

    def first_diagonal(block, leaves):
        moves = []
        for p, r in devices:
            c, even = r % 2, p - p % 2
            if leaves:
                source = even - 1 if c == 0 else even + 2
                if not 0 <= source < pairs:
                    source = even + c
            else:
                source = even + 1 - c
            moves.append(((source, r - c + p % 2), (p, r)))
        return permute(block, moves)

    def sum_rows(block):
        bit = 4
        while bit < row_count:
            block = block + exchange(block, 0, bit)
            bit *= 2
        return block

    names = jnp.arange(16, dtype=jnp.int32)
    facts = jnp.zeros((16,), jnp.int32)
    for name, value in (
        (X, x),
        (CORE, core),
        (FIRST, group == 0),
        (LAST, group == pairs // 2 - 1),
        (VROW, (row_index * 2 + x) * vector_rows),
        (EVEN, group % 2 == 0),
    ):
        facts = jnp.where(names == name, value.astype(jnp.int32), facts)
    labels = lax.dynamic_slice_in_dim(block_label, 4 * group, 4)
    facts = lax.dynamic_update_slice_in_dim(facts, labels, LABEL, 0)

    def together(*arrays):
        return lax.optimization_barrier(arrays)

    top_give, rest_give = give_rows(facts, sector, part * 3 // 4)
    got_top = exchange(top_give, 1, 0)
    own = first_gram(facts, sector, half)
    own = sum_rows(own + exchange(own, 0, 1))
    rotation, gram = first_rotation(facts, own, exchange(own, 0, 2), half)

    for sweep_round in range(ROUNDS - 1):
        last_move = sweep_round == ROUNDS - 2
        if sweep_round == 0:
            other_rotation = exchange(rotation, 1, 0)
            stay, leave = turn_rows(facts, rotation, sector, half, True)
            leave, rest_give = together(leave, rest_give)
            got_rest = exchange(rest_give, 1, 0)
            own_rows = [stay, leave, shift(leave, -2)]
            other_rows = []
            for got in (got_top, got_rest):
                stay, leave = turn_rows(facts, other_rotation, got, half, False)
                other_rows.append([stay, leave, shift(leave, 2)])
            leave, stay = turned_gram(facts, gram, rotation, X)
            diagonals = [first_diagonal(leave, True), first_diagonal(stay, False)]
            vectors = list(
                first_vectors(facts, rotation, other_rotation, vector_rows, half)
            )
            vectors[0], vectors[1], diagonals[1] = together(
                vectors[0], vectors[1], diagonals[1]
            )
            *grams, up_0, nat_l, nat_u, low_1 = first_cross_gram(
                facts, own_rows, other_rows, half
            )
        else:
            packs = [rotation, exchange(rotation, 0, 1)]
            leave_a, leave_b, nat_l, nat_u, *vectors = turn(
                facts, packs, blocks, vectors, half, last_move
            )
            got = [swap(leave_a, 0), swap(leave_b, 1)]
            leave, stay = turned_gram(facts, gram, rotation, CORE)
            diagonals = [pass_diagonal(leave), exchange(stay, 0, 1)]
            if last_move:
                native = exchange(vectors.pop(), 1, 0)
                top = part // 2
                top_give = give(facts, got, 0, top, half)
                *got, top_give, diagonals[0], diagonals[1] = together(
                    *got, top_give, *diagonals
                )
                got_top = exchange(top_give, 1, 0)
            else:
                vectors[0], vectors[1], diagonals[1] = together(
                    vectors[0], vectors[1], diagonals[1]
                )
            *grams, up_0, low_1 = cross_gram(facts, got, [nat_l, nat_u], part, half)
        blocks = [up_0, nat_l, nat_u, low_1]
        if last_move:
            grams[1], native = together(grams[1], native)
        else:
            vector_a, vector_b, *kept = vectors
            grams[1], vector_a, vector_b, diagonals[0] = together(
                grams[1], swap(vector_a, 0), swap(vector_b, 1), diagonals[0]
            )
            vectors = [vector_a, vector_b] + kept
        own = sum_rows(grams[0] + exchange(grams[1], 0, 1))
        parts = [own, exchange(own, 0, 2), exchange(own, 1, 0), exchange(own, 1, 2)]
        if last_move:
            rest_give = give(facts, got, top, part + vector_rows, half)
            parts[2], parts[3], got_top, rest_give = together(
                *parts[2:], got_top, rest_give
            )
            got_rest = exchange(rest_give, 1, 0)
        rotation, gram = later_rotation(facts, parts, diagonals, half, last_move)
    packs = [rotation, exchange(rotation, 0, 1)]
    rotated, vectors_out, singular = finish(
        facts, packs, blocks, native, got_top, got_rest, part, half
    )
    return rotated, vectors_out, singular.reshape(size)


def solution(mesh):
    placed = (P("row", "pair"), P())
    return jax.shard_map(
        per_device,
        mesh=mesh,
        in_specs=placed,
        out_specs=(P("row", "pair"), P("row", "pair"), P("pair")),
        check_vma=False,
    )
```

```python
import jax
import jax.numpy as jnp
from jax import lax
from jax.experimental import pallas as pl
from jax.experimental.pallas import tpu as pltpu
from jax.sharding import PartitionSpec as P

ROUNDS = 4
NEWTON = 16

highest = lax.Precision.HIGHEST

TARGET = 2.0**-12
REACHES = [
    (2.0 / (TARGET ** -(2.0**-j) - 1.0)) ** 2 for j in range(NEWTON)
]

X, CORE, FIRST, LAST, VROW, LABEL, EVEN = 0, 1, 2, 3, 4, 5, 9


def dot(a, b, precision=highest):
    return lax.dot_general(
        a, b, (((1,), (0,)), ((), ())), precision=precision,
        preferred_element_type=jnp.float32,
    )


def split(a):
    high = a.astype(jnp.bfloat16)
    return high, (a - high.astype(jnp.float32)).astype(jnp.bfloat16)


def dot3(a, b):
    a_high, a_low = a if isinstance(a, tuple) else split(a)
    b_high, b_low = b if isinstance(b, tuple) else split(b)
    small = dot(a_high, b_low, None) + dot(a_low, b_high, None)
    return dot(a_high, b_high, None) + small


def dot_tn(a, b):
    return lax.dot_general(
        a, b, (((0,), (0,)), ((), ())), precision=highest,
        preferred_element_type=jnp.float32,
    )


def shape(*dims):
    return jax.ShapeDtypeStruct(dims, jnp.float32)


def call(body, facts, inputs, outs, scratch=(), limit=24):
    return pl.pallas_call(
        body,
        out_shape=outs,
        in_specs=[pl.BlockSpec(memory_space=pltpu.SMEM)]
        + [pl.BlockSpec(memory_space=pltpu.VMEM)] * len(inputs),
        out_specs=jax.tree.map(
            lambda _: pl.BlockSpec(memory_space=pltpu.VMEM), outs
        ),
        scratch_shapes=list(scratch),
        compiler_params=pltpu.CompilerParams(vmem_limit_bytes=limit << 20),
    )(facts, *inputs)


def first_gram(facts, sector, half):
    def body(f, x_ref, out_ref):
        x = x_ref[...]
        g = dot_tn(x, x)
        out_ref[:half] = g[:half, :half]
        out_ref[half : 2 * half] = g[:half, half:]
        out_ref[2 * half :] = g[half:, half:]

    return call(body, facts, [sector], shape(3 * half, half))


def give_rows(facts, sector, top):
    rows, width = sector.shape
    part = rows // 2

    def body(f, x_ref, top_ref, rest_ref, sems):
        start = pl.multiple_of((1 - f[X]) * part, 8)
        copies = [
            pltpu.make_async_copy(
                x_ref.at[pl.ds(start, top)], top_ref, sems.at[0]
            ),
            pltpu.make_async_copy(
                x_ref.at[pl.ds(start + top, part - top)], rest_ref, sems.at[1]
            ),
        ]
        for copy in copies:
            copy.start()
        for copy in copies:
            copy.wait()

    return pl.pallas_call(
        body,
        out_shape=(shape(top, width), shape(part - top, width)),
        in_specs=[
            pl.BlockSpec(memory_space=pltpu.SMEM), pl.BlockSpec(memory_space=pl.ANY)
        ],
        out_specs=(pl.BlockSpec(memory_space=pltpu.VMEM),) * 2,
        scratch_shapes=[pltpu.SemaphoreType.DMA((2,))],
    )(facts, sector)


def rotate_of(gram, x_ref, e_ref):
    size = gram.shape[0]
    rows = lax.broadcasted_iota(jnp.int32, (size, size), 0)
    cols = lax.broadcasted_iota(jnp.int32, (size, size), 1)
    identity = (rows == cols).astype(jnp.float32)
    only = jnp.where(rows == cols, gram, 0.0)
    g_j = jnp.sum(only, axis=0, keepdims=True)
    g_i = jnp.sum(only, axis=1, keepdims=True)
    spread = g_j - g_i
    summed = g_j + g_i
    skew = gram * spread / (spread * spread + 2.0 * gram * gram + 0.01 * summed * summed)
    skew_parts = split(skew)
    square = dot3(skew_parts, skew_parts)
    whole = 0.25 * jnp.sum(skew * skew)
    paired = 0.03125 * jnp.sum(square * square) * 1.001
    reach = jnp.minimum(whole * whole, paired)
    steps = jnp.int32(0)
    for limit in REACHES:
        steps = steps + (reach > limit).astype(jnp.int32)
    fixes = 1 + (steps > 7).astype(jnp.int32) + 2 * (steps > 9).astype(jnp.int32)
    scale = 2.0 / (2.0 + jnp.sqrt(jnp.full((size, size), reach, jnp.float32)))
    residual = identity - scale * (identity - 0.25 * square)
    x_ref[...] = scale * (identity + residual)
    residual_parts = split(residual)
    e_ref[...] = dot3(residual_parts, residual_parts)

    def step(_, carry):
        e = split(e_ref[...])
        x = x_ref[...]
        x_ref[...] = x + dot3(x, e)
        e_ref[...] = dot3(e, e)
        return carry

    lax.fori_loop(0, jnp.maximum(steps - 1, 0), step, jnp.int32(0))
    x = x_ref[...]
    x_ref[...] = x + 0.5 * dot3(x, skew_parts)

    def fix(_, carry):
        x = x_ref[...]
        x_ref[...] = x + dot3(x, identity - (x - 0.5 * dot(skew, x)))
        return carry

    lax.fori_loop(0, fixes, fix, jnp.int32(0))
    return 2.0 * x_ref[...] - identity


def put_rotation(rotation_ref, gram, x_ref, e_ref, last_round):
    size = gram.shape[0]
    rotation = rotate_of(gram, x_ref, e_ref)
    rotation_ref[:size] = rotation
    if last_round:
        squares = jnp.sum(rotation * dot(gram, rotation), axis=0, keepdims=True)
        rotation_ref[size:] = jnp.broadcast_to(squares, (8, size))


def first_rotation(facts, own, other_y, half):
    size = 2 * half

    def body(f, own_ref, other_ref, rotation_ref, g_ref, x_ref, e_ref):
        total = own_ref[...] + other_ref[...]
        g_ref[:half, :half] = total[:half]
        g_ref[:half, half:] = total[half : 2 * half]
        g_ref[half:, :half] = total[half : 2 * half].T
        g_ref[half:, half:] = total[2 * half :]
        put_rotation(rotation_ref, g_ref[...], x_ref, e_ref, False)

    square = pltpu.VMEM((size, size), jnp.float32)
    return call(body, facts, [own, other_y], (shape(size, size),) * 2, [square] * 2)


def later_rotation(facts, parts, diagonals, half, last_round):
    size = 2 * half

    def body(f, *refs):
        own, other_y, other_x, other_xy, foreign, native = [r[...] for r in refs[:6]]
        rotation_ref, g_ref, x_ref, e_ref = refs[6:]
        cross = (own + other_y) + (other_x + other_xy)
        core = f[CORE] == 0
        g_ref[:half, :half] = jnp.where(core, foreign, native)
        g_ref[:half, half:] = cross
        g_ref[half:, :half] = cross.T
        g_ref[half:, half:] = jnp.where(core, native, foreign)
        put_rotation(rotation_ref, g_ref[...], x_ref, e_ref, last_round)

    square = pltpu.VMEM((size, size), jnp.float32)
    return call(
        body,
        facts,
        parts + diagonals,
        (shape(size + 8 if last_round else size, size), shape(size, size)),
        [square] * 2,
    )


def turned_gram(facts, gram, rotation, position):
    size = gram.shape[0]
    half = size // 2

    def body(f, gram_ref, rotation_ref, leave_ref, stay_ref):
        rotation = rotation_ref[...]
        turned = dot(gram_ref[...], rotation)
        upper = dot_tn(rotation[:, :half], turned[:, :half])
        lower = dot_tn(rotation[:, half:], turned[:, half:])
        lower_leaves = (f[position] == 0) & (f[FIRST] == 0)
        leave_ref[...] = jnp.where(lower_leaves, lower, upper)
        stay_ref[...] = jnp.where(lower_leaves, upper, lower)

    return call(body, facts, [gram, rotation], (shape(half, half),) * 2)


def two_packs(f, own, other):
    core = f[CORE] == 0
    return jnp.where(core, own, other), jnp.where(core, other, own)


def swapped(flag, matrix, axis):
    half = matrix.shape[axis] // 2
    a = lax.slice_in_dim(matrix, 0, half, axis=axis)
    b = lax.slice_in_dim(matrix, half, 2 * half, axis=axis)
    return jnp.where(flag, lax.concatenate([b, a], axis), matrix)


def blocks_of(f, got_a, got_b, low_0, up_1):
    even = f[EVEN] == 1
    return (
        jnp.where(even, got_b, got_a), low_0, up_1, jnp.where(even, got_a, got_b)
    )


def put_turned(f, refs, zero, one, half, at=0):
    a_ref, b_ref, nat_l_ref, nat_u_ref = refs[:4]
    even = f[EVEN] == 1
    rows = slice(at, at + zero.shape[0])
    to_left, to_right = zero[:, half:], one[:, :half]
    a_ref[rows] = jnp.where(even, to_right, to_left)
    b_ref[rows] = jnp.where(even, to_left, to_right)
    nat_l_ref[rows] = one[:, half:]
    nat_u_ref[rows] = zero[:, :half]
    if len(refs) > 4:
        refs[4][rows] = jnp.where(f[X] == 0, zero[:, :half], one[:, half:])


def turns_of(f, own_ref, other_ref):
    size = other_ref.shape[1]
    turn_0, turn_1 = two_packs(f, own_ref[:size], other_ref[:size])
    return swapped(f[FIRST] == 1, turn_0, 1), turn_1


def turn_rows(facts, rotation, rows_of, half, own):
    rows = rows_of.shape[0] // 2 if own else rows_of.shape[0]

    def body(f, rotation_ref, x_ref, stay_ref, leave_ref):
        zero = f[X] == (0 if own else 1)
        upper_leaves = jnp.where(zero, f[FIRST], 1) == 1
        turn = swapped(upper_leaves, rotation_ref[...], 1)
        here = pl.multiple_of(f[X] * rows, 8)
        out = dot3(x_ref[pl.ds(here, rows)] if own else x_ref[...], turn)
        stay_ref[...] = out[:, :half]
        leave_ref[...] = out[:, half:]

    return call(body, facts, [rotation, rows_of], (shape(rows, half),) * 2)


def first_vectors(facts, rotation, other_rotation, vector_rows, half):
    def body(f, own_ref, other_ref, *refs):
        even = f[X] == 0
        own, other = own_ref[...], other_ref[...]
        turn_0 = swapped(f[FIRST] == 1, jnp.where(even, own, other), 1)
        turn_1 = jnp.where(even, other, own)
        ids = f[VROW] + lax.broadcasted_iota(jnp.int32, (vector_rows, half), 0)
        cols = lax.broadcasted_iota(jnp.int32, (vector_rows, half), 1)
        up_0, low_0, up_1, low_1 = [
            (ids == f[LABEL + k] * half + cols).astype(jnp.float32) for k in range(4)
        ]
        zero = dot3(lax.concatenate([up_0, low_0], 1), turn_0)
        one = dot3(lax.concatenate([up_1, low_1], 1), turn_1)
        put_turned(f, refs, zero, one, half)

    return call(
        body, facts, [rotation, other_rotation], (shape(vector_rows, half),) * 4
    )


def turn(facts, packs, blocks, vectors, half, last_move):
    part, vector_rows = blocks[0].shape[0], vectors[0].shape[0]

    def body(f, own_ref, other_ref, *refs):
        turn_0, turn_1 = turns_of(f, own_ref, other_ref)
        turn_0, turn_1 = split(turn_0), split(turn_1)
        columns = [r[...] for r in refs[:4]]
        rows = blocks_of(f, *[r[...] for r in refs[4:8]])
        outs = refs[8:]
        for (up_0, low_0, up_1, low_1), at in ((columns, 0), (rows, part)):
            zero = dot3(lax.concatenate([up_0, low_0], 1), turn_0)
            one = dot3(lax.concatenate([up_1, low_1], 1), turn_1)
            if last_move:
                put_turned(f, outs, zero, one, half, at)
            else:
                put_turned(f, outs[4 if at else 0 :][:4], zero, one, half)

    if last_move:
        outs = (shape(part + vector_rows, half),) * 5
    else:
        outs = (shape(part, half),) * 4 + (shape(vector_rows, half),) * 4
    return call(body, facts, packs + blocks + vectors, outs)


def put_cross(f, refs, zero, one):
    core = f[CORE] == 0
    refs[0][...] = jnp.where(core, zero, one)
    refs[1][...] = jnp.where(core, one, zero)


def first_cross_gram(facts, own, others, half):
    rows = own[0].shape[0]
    pieces = len(others)

    def body(f, *refs):
        own_refs = [[r] for r in refs[:3]]
        other_refs = [refs[3 + k : 3 + 3 * pieces : 3] for k in range(3)]
        up_0, low_0, up_1, low_1 = refs[5 + 3 * pieces :]

        def fill(target, sources):
            at = 0
            for ref in sources:
                target[at : at + ref.shape[0]] = ref[...]
                at += ref.shape[0]

        first, last = f[FIRST] == 1, f[LAST] == 1
        for x, near, far in ((0, own_refs, other_refs), (1, other_refs, own_refs)):
            here = f[X] == x

            @pl.when(here)
            def _():
                fill(up_1, near[0])
                fill(low_0, far[0])

            @pl.when(here & first)
            def _():
                fill(up_0, near[1])

            @pl.when(here & ~first)
            def _():
                fill(up_0, far[2])

            @pl.when(here & last)
            def _():
                fill(low_1, far[1])

            @pl.when(here & ~last)
            def _():
                fill(low_1, near[2])

        put_cross(
            f,
            refs[3 + 3 * pieces :],
            dot_tn(up_0[...], low_0[...]),
            dot_tn(up_1[...], low_1[...]),
        )

    outs = (shape(half, half),) * 2 + (shape(rows, half),) * 4
    return call(body, facts, own + sum(others, []), outs)


def cross_gram(facts, got, natives, part, half):
    rows = got[0].shape[0]

    def body(f, *refs):
        up_0, low_0, up_1, low_1 = blocks_of(f, *[r[...] for r in refs[:4]])
        put_cross(
            f,
            refs[4:],
            dot_tn(up_0[:part], low_0[:part]),
            dot_tn(up_1[:part], low_1[:part]),
        )
        refs[6][...] = up_0
        refs[7][...] = low_1

    outs = (shape(half, half),) * 2 + (shape(rows, half),) * 2
    return call(body, facts, got + natives, outs)


def give(facts, got, start, stop, half):
    def body(f, a_ref, b_ref, out_ref):
        mine = f[X] != f[EVEN]
        out_ref[...] = jnp.where(mine, a_ref[start:stop], b_ref[start:stop])

    return call(body, facts, got, shape(stop - start, half))


def finish(facts, packs, blocks, native, got_top, got_rest, part, half):
    size = 2 * half
    vector_rows = blocks[0].shape[0] - part
    top = got_top.shape[0]

    def body(f, *refs):
        x = f[X]
        mine = f[CORE] == x
        pack = jnp.where(mine, refs[0][...], refs[1][...])
        turned = split(swapped(x == 1, pack[:size], 0))
        native_ref, top_ref, rest_ref = refs[6:9]
        out_ref, vectors_ref, singular_ref, out, vectors, sems = refs[9:]
        copies = []

        def put(source, target, here, there, value):
            rows = value.shape[0]
            source[here : here + rows] = value
            there = pl.multiple_of(there, 8)
            copies.append(
                pltpu.make_async_copy(
                    source.at[here : here + rows],
                    target.at[pl.ds(there, rows)],
                    sems.at[len(copies)],
                )
            )
            copies[-1].start()

        def product(moved, native):
            return dot3(lax.concatenate([moved, native], 1), turned)

        def kept(rows):
            up_0, low_0, up_1, low_1 = [r[rows] for r in refs[2:6]]
            return product(
                jnp.where(x == 0, up_0, low_1), jnp.where(x == 0, low_0, up_1)
            )

        squares = pack[size : size + 1]
        singular_ref[...] = jnp.sqrt(jnp.maximum(squares, 0.0) + 1e-06)
        other = (1 - x) * part
        middle = part // 2
        put(out, out_ref, 0, x * part, kept(slice(0, middle)))
        put(out, out_ref, middle, x * part + middle, kept(slice(middle, part)))
        put(out, out_ref, part, other, product(top_ref[...], native_ref[:top]))
        put(
            out, out_ref, part + top, other + top,
            product(rest_ref[: part - top], native_ref[top:part]),
        )
        put(vectors, vectors_ref, 0, x * vector_rows, kept(slice(part, None)))
        put(
            vectors, vectors_ref, vector_rows, (1 - x) * vector_rows,
            product(rest_ref[part - top :], native_ref[part:]),
        )
        for copy in copies:
            copy.wait()

    vmem = pl.BlockSpec(memory_space=pltpu.VMEM)
    hbm = pl.BlockSpec(memory_space=pl.ANY)
    inputs = packs + blocks + [native, got_top, got_rest]
    return pl.pallas_call(
        body,
        out_shape=(
            shape(2 * part, size), shape(2 * vector_rows, size), shape(1, size)
        ),
        in_specs=[pl.BlockSpec(memory_space=pltpu.SMEM)] + [vmem] * len(inputs),
        out_specs=(hbm, hbm, vmem),
        scratch_shapes=[
            pltpu.VMEM((2 * part, size), jnp.float32),
            pltpu.VMEM((2 * vector_rows, size), jnp.float32),
            pltpu.SemaphoreType.DMA((6,)),
        ],
        compiler_params=pltpu.CompilerParams(vmem_limit_bytes=24 << 20),
    )(facts, *inputs)


def per_device(sector, block_label):
    local_rows, size = sector.shape
    half = size // 2
    part = local_rows // 2
    pairs = lax.axis_size("pair")
    row_count = lax.axis_size("row")
    vector_rows = pairs * size // row_count // 2
    pair_index = lax.axis_index("pair")
    row_index = lax.axis_index("row")
    x = pair_index % 2
    group = pair_index // 2
    core = row_index % 2

    def permute(block, route):
        moves = [
            (a * row_count + b, c * row_count + d) for (a, b), (c, d) in route
        ]
        return lax.ppermute(block, ("pair", "row"), moves)

    devices = [(p, r) for p in range(pairs) for r in range(row_count)]

    def exchange(block, over_pair, over_row):
        return permute(
            block, [((p ^ over_pair, r ^ over_row), (p, r)) for p, r in devices]
        )

    def shift(block, even_by):
        moves = []
        for p, r in devices:
            source = p - even_by if p % 2 == 0 else p + even_by
            if 0 <= source < pairs:
                moves.append(((source, r), (p, r)))
        return permute(block, moves)

    def swap(block, odd):
        moves = []
        for p, r in devices:
            other = p + 2 if p // 2 % 2 == odd else p - 2
            moves.append(((other if 0 <= other < pairs else p, r), (p, r)))
        return permute(block, moves)

    def pass_diagonal(block):
        moves = []
        for p, r in devices:
            other = p + 2 if r % 2 else p - 2
            inside = 0 <= other < pairs
            moves.append(((other, r ^ 1) if inside else (p, r), (p, r)))
        return permute(block, [((a, b), c) for (a, b), c in moves])

    def first_diagonal(block, leaves):
        moves = []
        for p, r in devices:
            c, even = r % 2, p - p % 2
            if leaves:
                source = even - 1 if c == 0 else even + 2
                if not 0 <= source < pairs:
                    source = even + c
            else:
                source = even + 1 - c
            moves.append(((source, r - c + p % 2), (p, r)))
        return permute(block, moves)

    def sum_rows(block):
        bit = 4
        while bit < row_count:
            block = block + exchange(block, 0, bit)
            bit *= 2
        return block

    names = jnp.arange(16, dtype=jnp.int32)
    facts = jnp.zeros((16,), jnp.int32)
    for name, value in (
        (X, x),
        (CORE, core),
        (FIRST, group == 0),
        (LAST, group == pairs // 2 - 1),
        (VROW, (row_index * 2 + x) * vector_rows),
        (EVEN, group % 2 == 0),
    ):
        facts = jnp.where(names == name, value.astype(jnp.int32), facts)
    labels = lax.dynamic_slice_in_dim(block_label, 4 * group, 4)
    facts = lax.dynamic_update_slice_in_dim(facts, labels, LABEL, 0)

    def together(*arrays):
        return lax.optimization_barrier(arrays)

    top_give, rest_give = give_rows(facts, sector, part * 3 // 4)
    got_top = exchange(top_give, 1, 0)
    own = first_gram(facts, sector, half)
    own = sum_rows(own + exchange(own, 0, 1))
    rotation, gram = first_rotation(facts, own, exchange(own, 0, 2), half)

    for sweep_round in range(ROUNDS - 1):
        last_move = sweep_round == ROUNDS - 2
        if sweep_round == 0:
            other_rotation = exchange(rotation, 1, 0)
            stay, leave = turn_rows(facts, rotation, sector, half, True)
            leave, rest_give = together(leave, rest_give)
            got_rest = exchange(rest_give, 1, 0)
            own_rows = [stay, leave, shift(leave, -2)]
            other_rows = []
            for got in (got_top, got_rest):
                stay, leave = turn_rows(facts, other_rotation, got, half, False)
                other_rows.append([stay, leave, shift(leave, 2)])
            leave, stay = turned_gram(facts, gram, rotation, X)
            diagonals = [first_diagonal(leave, True), first_diagonal(stay, False)]
            vectors = list(
                first_vectors(facts, rotation, other_rotation, vector_rows, half)
            )
            vectors[0], vectors[1], diagonals[1] = together(
                vectors[0], vectors[1], diagonals[1]
            )
            *grams, up_0, nat_l, nat_u, low_1 = first_cross_gram(
                facts, own_rows, other_rows, half
            )
        else:
            packs = [rotation, exchange(rotation, 0, 1)]
            leave_a, leave_b, nat_l, nat_u, *vectors = turn(
                facts, packs, blocks, vectors, half, last_move
            )
            got = [swap(leave_a, 0), swap(leave_b, 1)]
            leave, stay = turned_gram(facts, gram, rotation, CORE)
            diagonals = [pass_diagonal(leave), exchange(stay, 0, 1)]
            if last_move:
                native = exchange(vectors.pop(), 1, 0)
                top = part * 3 // 4
                top_give = give(facts, got, 0, top, half)
                *got, top_give, diagonals[0], diagonals[1] = together(
                    *got, top_give, *diagonals
                )
                got_top = exchange(top_give, 1, 0)
            else:
                vectors[0], vectors[1], diagonals[1] = together(
                    vectors[0], vectors[1], diagonals[1]
                )
            *grams, up_0, low_1 = cross_gram(facts, got, [nat_l, nat_u], part, half)
        blocks = [up_0, nat_l, nat_u, low_1]
        if last_move:
            grams[1], native = together(grams[1], native)
        else:
            vector_a, vector_b, *kept = vectors
            grams[1], vector_a, vector_b, diagonals[0] = together(
                grams[1], swap(vector_a, 0), swap(vector_b, 1), diagonals[0]
            )
            vectors = [vector_a, vector_b] + kept
        own = sum_rows(grams[0] + exchange(grams[1], 0, 1))
        parts = [own, exchange(own, 0, 2), exchange(own, 1, 0), exchange(own, 1, 2)]
        if last_move:
            rest_give = give(facts, got, top, part + vector_rows, half)
            *parts, got_top, rest_give = together(*parts, got_top, rest_give)
            got_rest = exchange(rest_give, 1, 0)
        rotation, gram = later_rotation(facts, parts, diagonals, half, last_move)
    packs = [rotation, exchange(rotation, 0, 1)]
    rotated, vectors_out, singular = finish(
        facts, packs, blocks, native, got_top, got_rest, part, half
    )
    return rotated, vectors_out, singular.reshape(size)


def solution(mesh):
    placed = (P("row", "pair"), P())
    return jax.shard_map(
        per_device,
        mesh=mesh,
        in_specs=placed,
        out_specs=(P("row", "pair"), P("row", "pair"), P("pair")),
        check_vma=False,
    )
```

```python
import jax
import jax.numpy as jnp
from jax import lax
from jax.experimental import pallas as pl
from jax.experimental.pallas import tpu as pltpu
from jax.sharding import PartitionSpec as P

ROUNDS = 4
NEWTON = 16

highest = lax.Precision.HIGHEST

TARGET = 2.0**-12
REACHES = [
    (2.0 / (TARGET ** -(2.0**-j) - 1.0)) ** 2 for j in range(NEWTON)
]

X, CORE, FIRST, LAST, VROW, LABEL, EVEN = 0, 1, 2, 3, 4, 5, 9


def dot(a, b, precision=highest):
    return lax.dot_general(
        a, b, (((1,), (0,)), ((), ())), precision=precision,
        preferred_element_type=jnp.float32,
    )


def split(a):
    high = a.astype(jnp.bfloat16)
    return high, (a - high.astype(jnp.float32)).astype(jnp.bfloat16)


def dot3(a, b):
    a_high, a_low = a if isinstance(a, tuple) else split(a)
    b_high, b_low = b if isinstance(b, tuple) else split(b)
    small = dot(a_high, b_low, None) + dot(a_low, b_high, None)
    return dot(a_high, b_high, None) + small


def dot_tn(a, b):
    return lax.dot_general(
        a, b, (((0,), (0,)), ((), ())), precision=highest,
        preferred_element_type=jnp.float32,
    )


def shape(*dims):
    return jax.ShapeDtypeStruct(dims, jnp.float32)


def call(body, facts, inputs, outs, scratch=(), limit=24):
    return pl.pallas_call(
        body,
        out_shape=outs,
        in_specs=[pl.BlockSpec(memory_space=pltpu.SMEM)]
        + [pl.BlockSpec(memory_space=pltpu.VMEM)] * len(inputs),
        out_specs=jax.tree.map(
            lambda _: pl.BlockSpec(memory_space=pltpu.VMEM), outs
        ),
        scratch_shapes=list(scratch),
        compiler_params=pltpu.CompilerParams(vmem_limit_bytes=limit << 20),
    )(facts, *inputs)


def first_gram(facts, sector, half):
    def body(f, x_ref, out_ref):
        x = x_ref[...]
        g = dot_tn(x, x)
        out_ref[:half] = g[:half, :half]
        out_ref[half : 2 * half] = g[:half, half:]
        out_ref[2 * half :] = g[half:, half:]

    return call(body, facts, [sector], shape(3 * half, half))


def give_rows(facts, sector, top):
    rows, width = sector.shape
    part = rows // 2

    def body(f, x_ref, top_ref, rest_ref, sems):
        start = pl.multiple_of((1 - f[X]) * part, 8)
        copies = [
            pltpu.make_async_copy(
                x_ref.at[pl.ds(start, top)], top_ref, sems.at[0]
            ),
            pltpu.make_async_copy(
                x_ref.at[pl.ds(start + top, part - top)], rest_ref, sems.at[1]
            ),
        ]
        for copy in copies:
            copy.start()
        for copy in copies:
            copy.wait()

    return pl.pallas_call(
        body,
        out_shape=(shape(top, width), shape(part - top, width)),
        in_specs=[
            pl.BlockSpec(memory_space=pltpu.SMEM), pl.BlockSpec(memory_space=pl.ANY)
        ],
        out_specs=(pl.BlockSpec(memory_space=pltpu.VMEM),) * 2,
        scratch_shapes=[pltpu.SemaphoreType.DMA((2,))],
    )(facts, sector)


def rotate_of(gram, x_ref, e_ref):
    size = gram.shape[0]
    rows = lax.broadcasted_iota(jnp.int32, (size, size), 0)
    cols = lax.broadcasted_iota(jnp.int32, (size, size), 1)
    identity = (rows == cols).astype(jnp.float32)
    only = jnp.where(rows == cols, gram, 0.0)
    g_j = jnp.sum(only, axis=0, keepdims=True)
    g_i = jnp.sum(only, axis=1, keepdims=True)
    spread = g_j - g_i
    summed = g_j + g_i
    skew = gram * spread / (spread * spread + 2.0 * gram * gram + 0.01 * summed * summed)
    skew_parts = split(skew)
    square = dot3(skew_parts, skew_parts)
    whole = 0.25 * jnp.sum(skew * skew)
    paired = 0.03125 * jnp.sum(square * square) * 1.001
    reach = jnp.minimum(whole * whole, paired)
    steps = jnp.int32(0)
    for limit in REACHES:
        steps = steps + (reach > limit).astype(jnp.int32)
    fixes = 1 + (steps > 7).astype(jnp.int32) + 2 * (steps > 9).astype(jnp.int32)
    scale = 2.0 / (2.0 + jnp.sqrt(jnp.full((size, size), reach, jnp.float32)))
    residual = identity - scale * (identity - 0.25 * square)
    x_ref[...] = scale * (identity + residual)
    residual_parts = split(residual)
    e_ref[...] = dot3(residual_parts, residual_parts)

    def step(_, carry):
        e = split(e_ref[...])
        x = x_ref[...]
        x_ref[...] = x + dot3(x, e)
        e_ref[...] = dot3(e, e)
        return carry

    lax.fori_loop(0, jnp.maximum(steps - 1, 0), step, jnp.int32(0))
    x = x_ref[...]
    x_ref[...] = x + 0.5 * dot3(x, skew_parts)

    def fix(_, carry):
        x = x_ref[...]
        x_ref[...] = x + dot3(x, identity - (x - 0.5 * dot(skew, x)))
        return carry

    lax.fori_loop(0, fixes, fix, jnp.int32(0))
    return 2.0 * x_ref[...] - identity


def put_rotation(rotation_ref, gram, x_ref, e_ref, last_round):
    size = gram.shape[0]
    rotation = rotate_of(gram, x_ref, e_ref)
    rotation_ref[:size] = rotation
    if last_round:
        squares = jnp.sum(rotation * dot(gram, rotation), axis=0, keepdims=True)
        rotation_ref[size:] = jnp.broadcast_to(squares, (8, size))


def first_rotation(facts, own, other_y, half):
    size = 2 * half

    def body(f, own_ref, other_ref, rotation_ref, g_ref, x_ref, e_ref):
        total = own_ref[...] + other_ref[...]
        g_ref[:half, :half] = total[:half]
        g_ref[:half, half:] = total[half : 2 * half]
        g_ref[half:, :half] = total[half : 2 * half].T
        g_ref[half:, half:] = total[2 * half :]
        put_rotation(rotation_ref, g_ref[...], x_ref, e_ref, False)

    square = pltpu.VMEM((size, size), jnp.float32)
    return call(body, facts, [own, other_y], (shape(size, size),) * 2, [square] * 2)


def later_rotation(facts, parts, diagonals, half, last_round):
    size = 2 * half

    def body(f, *refs):
        own, other_y, other_x, other_xy, foreign, native = [r[...] for r in refs[:6]]
        rotation_ref, g_ref, x_ref, e_ref = refs[6:]
        cross = (own + other_y) + (other_x + other_xy)
        core = f[CORE] == 0
        g_ref[:half, :half] = jnp.where(core, foreign, native)
        g_ref[:half, half:] = cross
        g_ref[half:, :half] = cross.T
        g_ref[half:, half:] = jnp.where(core, native, foreign)
        put_rotation(rotation_ref, g_ref[...], x_ref, e_ref, last_round)

    square = pltpu.VMEM((size, size), jnp.float32)
    return call(
        body,
        facts,
        parts + diagonals,
        (shape(size + 8 if last_round else size, size), shape(size, size)),
        [square] * 2,
    )


def turned_gram(facts, gram, rotation, position):
    size = gram.shape[0]
    half = size // 2

    def body(f, gram_ref, rotation_ref, leave_ref, stay_ref):
        rotation = rotation_ref[...]
        turned = dot(gram_ref[...], rotation)
        upper = dot_tn(rotation[:, :half], turned[:, :half])
        lower = dot_tn(rotation[:, half:], turned[:, half:])
        lower_leaves = (f[position] == 0) & (f[FIRST] == 0)
        leave_ref[...] = jnp.where(lower_leaves, lower, upper)
        stay_ref[...] = jnp.where(lower_leaves, upper, lower)

    return call(body, facts, [gram, rotation], (shape(half, half),) * 2)


def two_packs(f, own, other):
    core = f[CORE] == 0
    return jnp.where(core, own, other), jnp.where(core, other, own)


def swapped(flag, matrix, axis):
    half = matrix.shape[axis] // 2
    a = lax.slice_in_dim(matrix, 0, half, axis=axis)
    b = lax.slice_in_dim(matrix, half, 2 * half, axis=axis)
    return jnp.where(flag, lax.concatenate([b, a], axis), matrix)


def blocks_of(f, got_a, got_b, low_0, up_1):
    even = f[EVEN] == 1
    return (
        jnp.where(even, got_b, got_a), low_0, up_1, jnp.where(even, got_a, got_b)
    )


def put_turned(f, refs, zero, one, half, at=0):
    a_ref, b_ref, nat_l_ref, nat_u_ref = refs[:4]
    even = f[EVEN] == 1
    rows = slice(at, at + zero.shape[0])
    to_left, to_right = zero[:, half:], one[:, :half]
    a_ref[rows] = jnp.where(even, to_right, to_left)
    b_ref[rows] = jnp.where(even, to_left, to_right)
    nat_l_ref[rows] = one[:, half:]
    nat_u_ref[rows] = zero[:, :half]
    if len(refs) > 4:
        refs[4][rows] = jnp.where(f[X] == 0, zero[:, :half], one[:, half:])


def turns_of(f, own_ref, other_ref):
    size = other_ref.shape[1]
    turn_0, turn_1 = two_packs(f, own_ref[:size], other_ref[:size])
    return swapped(f[FIRST] == 1, turn_0, 1), turn_1


def turn_rows(facts, rotation, rows_of, half, own):
    rows = rows_of.shape[0] // 2 if own else rows_of.shape[0]

    def body(f, rotation_ref, x_ref, stay_ref, leave_ref):
        zero = f[X] == (0 if own else 1)
        upper_leaves = jnp.where(zero, f[FIRST], 1) == 1
        turn = swapped(upper_leaves, rotation_ref[...], 1)
        here = pl.multiple_of(f[X] * rows, 8)
        out = dot3(x_ref[pl.ds(here, rows)] if own else x_ref[...], turn)
        stay_ref[...] = out[:, :half]
        leave_ref[...] = out[:, half:]

    return call(body, facts, [rotation, rows_of], (shape(rows, half),) * 2)


def first_vectors(facts, rotation, other_rotation, vector_rows, half):
    def body(f, own_ref, other_ref, *refs):
        even = f[X] == 0
        own, other = own_ref[...], other_ref[...]
        turn_0 = swapped(f[FIRST] == 1, jnp.where(even, own, other), 1)
        turn_1 = jnp.where(even, other, own)
        ids = f[VROW] + lax.broadcasted_iota(jnp.int32, (vector_rows, half), 0)
        cols = lax.broadcasted_iota(jnp.int32, (vector_rows, half), 1)
        up_0, low_0, up_1, low_1 = [
            (ids == f[LABEL + k] * half + cols).astype(jnp.float32) for k in range(4)
        ]
        zero = dot3(lax.concatenate([up_0, low_0], 1), turn_0)
        one = dot3(lax.concatenate([up_1, low_1], 1), turn_1)
        put_turned(f, refs, zero, one, half)

    return call(
        body, facts, [rotation, other_rotation], (shape(vector_rows, half),) * 4
    )


def turn(facts, packs, blocks, vectors, half, last_move):
    part, vector_rows = blocks[0].shape[0], vectors[0].shape[0]

    def body(f, own_ref, other_ref, *refs):
        turn_0, turn_1 = turns_of(f, own_ref, other_ref)
        turn_0, turn_1 = split(turn_0), split(turn_1)
        columns = [r[...] for r in refs[:4]]
        rows = blocks_of(f, *[r[...] for r in refs[4:8]])
        outs = refs[8:]
        for (up_0, low_0, up_1, low_1), at in ((columns, 0), (rows, part)):
            zero = dot3(lax.concatenate([up_0, low_0], 1), turn_0)
            one = dot3(lax.concatenate([up_1, low_1], 1), turn_1)
            if last_move:
                put_turned(f, outs, zero, one, half, at)
            else:
                put_turned(f, outs[4 if at else 0 :][:4], zero, one, half)

    if last_move:
        outs = (shape(part + vector_rows, half),) * 5
    else:
        outs = (shape(part, half),) * 4 + (shape(vector_rows, half),) * 4
    return call(body, facts, packs + blocks + vectors, outs)


def put_cross(f, refs, zero, one):
    core = f[CORE] == 0
    refs[0][...] = jnp.where(core, zero, one)
    refs[1][...] = jnp.where(core, one, zero)


def first_cross_gram(facts, own, others, half):
    rows = own[0].shape[0]
    pieces = len(others)

    def body(f, *refs):
        own_refs = [[r] for r in refs[:3]]
        other_refs = [refs[3 + k : 3 + 3 * pieces : 3] for k in range(3)]
        up_0, low_0, up_1, low_1 = refs[5 + 3 * pieces :]

        def fill(target, sources):
            at = 0
            for ref in sources:
                target[at : at + ref.shape[0]] = ref[...]
                at += ref.shape[0]

        first, last = f[FIRST] == 1, f[LAST] == 1
        for x, near, far in ((0, own_refs, other_refs), (1, other_refs, own_refs)):
            here = f[X] == x

            @pl.when(here)
            def _():
                fill(up_1, near[0])
                fill(low_0, far[0])

            @pl.when(here & first)
            def _():
                fill(up_0, near[1])

            @pl.when(here & ~first)
            def _():
                fill(up_0, far[2])

            @pl.when(here & last)
            def _():
                fill(low_1, far[1])

            @pl.when(here & ~last)
            def _():
                fill(low_1, near[2])

        put_cross(
            f,
            refs[3 + 3 * pieces :],
            dot_tn(up_0[...], low_0[...]),
            dot_tn(up_1[...], low_1[...]),
        )

    outs = (shape(half, half),) * 2 + (shape(rows, half),) * 4
    return call(body, facts, own + sum(others, []), outs)


def cross_gram(facts, got, natives, part, half):
    rows = got[0].shape[0]

    def body(f, *refs):
        up_0, low_0, up_1, low_1 = blocks_of(f, *[r[...] for r in refs[:4]])
        put_cross(
            f,
            refs[4:],
            dot_tn(up_0[:part], low_0[:part]),
            dot_tn(up_1[:part], low_1[:part]),
        )
        refs[6][...] = up_0
        refs[7][...] = low_1

    outs = (shape(half, half),) * 2 + (shape(rows, half),) * 2
    return call(body, facts, got + natives, outs)


def give(facts, got, start, stop, half):
    def body(f, a_ref, b_ref, out_ref):
        mine = f[X] != f[EVEN]
        out_ref[...] = jnp.where(mine, a_ref[start:stop], b_ref[start:stop])

    return call(body, facts, got, shape(stop - start, half))


def final_turn(f, own_ref, other_ref, size):
    pack = jnp.where(f[CORE] == f[X], own_ref[...], other_ref[...])
    return split(swapped(f[X] == 1, pack[:size], 0)), pack[size : size + 1]


def final_product(moved, native, turned):
    return dot3(lax.concatenate([moved, native], 1), turned)


def put_rows(copies, sems, source, target, here, there, value):
    rows = value.shape[0]
    source[here : here + rows] = value
    copy = pltpu.make_async_copy(
        source.at[here : here + rows],
        target.at[pl.ds(pl.multiple_of(there, 8), rows)],
        sems.at[len(copies)],
    )
    copies.append(copy)
    copy.start()


def finish_call(body, facts, inputs, outputs, outs, rows, vector_rows, size):
    vmem = pl.BlockSpec(memory_space=pltpu.VMEM)
    hbm = pl.BlockSpec(memory_space=pl.ANY)
    first = 1 + len(inputs)
    return pl.pallas_call(
        body,
        out_shape=outs,
        in_specs=[pl.BlockSpec(memory_space=pltpu.SMEM)]
        + [vmem] * len(inputs)
        + [hbm] * len(outputs),
        out_specs=(hbm, hbm, vmem)[: len(outs)],
        input_output_aliases={first + k: k for k in range(len(outputs))},
        cost_estimate=pl.CostEstimate(flops=1, transcendentals=0, bytes_accessed=1),
        scratch_shapes=[
            pltpu.VMEM((rows, size), jnp.float32),
            pltpu.VMEM((vector_rows, size), jnp.float32),
            pltpu.SemaphoreType.DMA((4,)),
        ],
        compiler_params=pltpu.CompilerParams(vmem_limit_bytes=24 << 20),
    )(facts, *inputs, *outputs)


def finish_kept(facts, packs, blocks, native, got_top, part, half):
    size = 2 * half
    vector_rows = blocks[0].shape[0] - part
    top = got_top.shape[0]

    def body(f, own_ref, other_ref, *refs):
        x = f[X]
        turned, squares = final_turn(f, own_ref, other_ref, size)
        native_ref, top_ref, out_ref, vectors_ref, singular_ref, out, vectors, sems = (
            refs[4:]
        )
        copies = []

        def kept(rows):
            up_0, low_0, up_1, low_1 = [r[rows] for r in refs[:4]]
            return final_product(
                jnp.where(x == 0, up_0, low_1),
                jnp.where(x == 0, low_0, up_1),
                turned,
            )

        def put(*args):
            put_rows(copies, sems, *args)

        middle = part // 2
        put(out, out_ref, 0, x * part, kept(slice(0, middle)))
        put(out, out_ref, middle, x * part + middle, kept(slice(middle, part)))
        value = final_product(top_ref[...], native_ref[:top], turned)
        put(out, out_ref, part, (1 - x) * part, value)
        put(vectors, vectors_ref, 0, x * vector_rows, kept(slice(part, None)))
        singular_ref[...] = jnp.sqrt(jnp.maximum(squares, 0.0) + 1e-06)
        for copy in copies:
            copy.wait()

    outs = (shape(2 * part, size), shape(2 * vector_rows, size), shape(1, size))
    inputs = packs + blocks + [native, got_top]
    return finish_call(
        body, facts, inputs, [], outs, part + top, vector_rows, size
    )


def finish_rest(facts, packs, outputs, native, got_rest, part, half):
    size = 2 * half
    vector_rows = native.shape[0] - part
    rest = got_rest.shape[0] - vector_rows
    top = part - rest

    def body(f, own_ref, other_ref, native_ref, rest_ref, *refs):
        x = f[X]
        turned, _ = final_turn(f, own_ref, other_ref, size)
        out_ref, vectors_ref, out, vectors, sems = refs[2:]
        copies = []
        value = final_product(rest_ref[:rest], native_ref[top:part], turned)
        put_rows(copies, sems, out, out_ref, 0, (1 - x) * part + top, value)
        value = final_product(rest_ref[rest:], native_ref[part:], turned)
        put_rows(copies, sems, vectors, vectors_ref, 0, (1 - x) * vector_rows, value)
        for copy in copies:
            copy.wait()

    outs = (shape(2 * part, size), shape(2 * vector_rows, size))
    inputs = packs + [native, got_rest]
    return finish_call(
        body, facts, inputs, outputs, outs, rest, vector_rows, size
    )


def per_device(sector, block_label):
    local_rows, size = sector.shape
    half = size // 2
    part = local_rows // 2
    pairs = lax.axis_size("pair")
    row_count = lax.axis_size("row")
    vector_rows = pairs * size // row_count // 2
    pair_index = lax.axis_index("pair")
    row_index = lax.axis_index("row")
    x = pair_index % 2
    group = pair_index // 2
    core = row_index % 2

    def permute(block, route):
        moves = [
            (a * row_count + b, c * row_count + d) for (a, b), (c, d) in route
        ]
        return lax.ppermute(block, ("pair", "row"), moves)

    devices = [(p, r) for p in range(pairs) for r in range(row_count)]

    def exchange(block, over_pair, over_row):
        return permute(
            block, [((p ^ over_pair, r ^ over_row), (p, r)) for p, r in devices]
        )

    def shift(block, even_by):
        moves = []
        for p, r in devices:
            source = p - even_by if p % 2 == 0 else p + even_by
            if 0 <= source < pairs:
                moves.append(((source, r), (p, r)))
        return permute(block, moves)

    def swap(block, odd):
        moves = []
        for p, r in devices:
            other = p + 2 if p // 2 % 2 == odd else p - 2
            moves.append(((other if 0 <= other < pairs else p, r), (p, r)))
        return permute(block, moves)

    def pass_diagonal(block):
        moves = []
        for p, r in devices:
            other = p + 2 if r % 2 else p - 2
            inside = 0 <= other < pairs
            moves.append(((other, r ^ 1) if inside else (p, r), (p, r)))
        return permute(block, [((a, b), c) for (a, b), c in moves])

    def first_diagonal(block, leaves):
        moves = []
        for p, r in devices:
            c, even = r % 2, p - p % 2
            if leaves:
                source = even - 1 if c == 0 else even + 2
                if not 0 <= source < pairs:
                    source = even + c
            else:
                source = even + 1 - c
            moves.append(((source, r - c + p % 2), (p, r)))
        return permute(block, moves)

    def sum_rows(block):
        bit = 4
        while bit < row_count:
            block = block + exchange(block, 0, bit)
            bit *= 2
        return block

    names = jnp.arange(16, dtype=jnp.int32)
    facts = jnp.zeros((16,), jnp.int32)
    for name, value in (
        (X, x),
        (CORE, core),
        (FIRST, group == 0),
        (LAST, group == pairs // 2 - 1),
        (VROW, (row_index * 2 + x) * vector_rows),
        (EVEN, group % 2 == 0),
    ):
        facts = jnp.where(names == name, value.astype(jnp.int32), facts)
    labels = lax.dynamic_slice_in_dim(block_label, 4 * group, 4)
    facts = lax.dynamic_update_slice_in_dim(facts, labels, LABEL, 0)

    def together(*arrays):
        return lax.optimization_barrier(arrays)

    top_give, rest_give = give_rows(facts, sector, part * 3 // 4)
    got_top = exchange(top_give, 1, 0)
    own = first_gram(facts, sector, half)
    own = sum_rows(own + exchange(own, 0, 1))
    rotation, gram = first_rotation(facts, own, exchange(own, 0, 2), half)

    for sweep_round in range(ROUNDS - 1):
        last_move = sweep_round == ROUNDS - 2
        if sweep_round == 0:
            other_rotation = exchange(rotation, 1, 0)
            stay, leave = turn_rows(facts, rotation, sector, half, True)
            leave, rest_give = together(leave, rest_give)
            got_rest = exchange(rest_give, 1, 0)
            own_rows = [stay, leave, shift(leave, -2)]
            other_rows = []
            for got in (got_top, got_rest):
                stay, leave = turn_rows(facts, other_rotation, got, half, False)
                other_rows.append([stay, leave, shift(leave, 2)])
            leave, stay = turned_gram(facts, gram, rotation, X)
            diagonals = [first_diagonal(leave, True), first_diagonal(stay, False)]
            vectors = list(
                first_vectors(facts, rotation, other_rotation, vector_rows, half)
            )
            vectors[0], vectors[1], diagonals[1] = together(
                vectors[0], vectors[1], diagonals[1]
            )
            *grams, up_0, nat_l, nat_u, low_1 = first_cross_gram(
                facts, own_rows, other_rows, half
            )
        else:
            packs = [rotation, exchange(rotation, 0, 1)]
            leave_a, leave_b, nat_l, nat_u, *vectors = turn(
                facts, packs, blocks, vectors, half, last_move
            )
            got = [swap(leave_a, 0), swap(leave_b, 1)]
            leave, stay = turned_gram(facts, gram, rotation, CORE)
            diagonals = [pass_diagonal(leave), exchange(stay, 0, 1)]
            if last_move:
                native = exchange(vectors.pop(), 1, 0)
                top = part // 2
                top_give = give(facts, got, 0, top, half)
                *got, top_give, diagonals[0], diagonals[1] = together(
                    *got, top_give, *diagonals
                )
                got_top = exchange(top_give, 1, 0)
            else:
                vectors[0], vectors[1], diagonals[1] = together(
                    vectors[0], vectors[1], diagonals[1]
                )
            *grams, up_0, low_1 = cross_gram(facts, got, [nat_l, nat_u], part, half)
        blocks = [up_0, nat_l, nat_u, low_1]
        if last_move:
            grams[1], native = together(grams[1], native)
        else:
            vector_a, vector_b, *kept = vectors
            grams[1], vector_a, vector_b, diagonals[0] = together(
                grams[1], swap(vector_a, 0), swap(vector_b, 1), diagonals[0]
            )
            vectors = [vector_a, vector_b] + kept
        own = sum_rows(grams[0] + exchange(grams[1], 0, 1))
        parts = [own, exchange(own, 0, 2), exchange(own, 1, 0), exchange(own, 1, 2)]
        if last_move:
            rest_give = give(facts, got, top, part + vector_rows, half)
            *parts, got_top, rest_give = together(*parts, got_top, rest_give)
            got_rest = exchange(rest_give, 1, 0)
        rotation, gram = later_rotation(facts, parts, diagonals, half, last_move)
    packs = [rotation, exchange(rotation, 0, 1)]
    *outputs, singular = finish_kept(
        facts, packs, blocks, native, got_top, part, half
    )
    rotated, vectors_out = finish_rest(
        facts, packs, outputs, native, got_rest, part, half
    )
    return rotated, vectors_out, singular.reshape(size)


def solution(mesh):
    placed = (P("row", "pair"), P())
    return jax.shard_map(
        per_device,
        mesh=mesh,
        in_specs=placed,
        out_specs=(P("row", "pair"), P("row", "pair"), P("pair")),
        check_vma=False,
    )
```

```python
import jax
import jax.numpy as jnp
from jax import lax
from jax.experimental import pallas as pl
from jax.experimental.pallas import tpu as pltpu
from jax.sharding import PartitionSpec as P

ROUNDS = 4
NEWTON = 16

highest = lax.Precision.HIGHEST

TARGET = 2.0**-12
REACHES = [
    (2.0 / (TARGET ** -(2.0**-j) - 1.0)) ** 2 for j in range(NEWTON)
]

X, CORE, FIRST, LAST, VROW, LABEL, EVEN = 0, 1, 2, 3, 4, 5, 9


def dot(a, b, precision=highest):
    return lax.dot_general(
        a, b, (((1,), (0,)), ((), ())), precision=precision,
        preferred_element_type=jnp.float32,
    )


def split(a):
    high = a.astype(jnp.bfloat16)
    return high, (a - high.astype(jnp.float32)).astype(jnp.bfloat16)


def dot3(a, b):
    a_high, a_low = a if isinstance(a, tuple) else split(a)
    b_high, b_low = b if isinstance(b, tuple) else split(b)
    small = dot(a_high, b_low, None) + dot(a_low, b_high, None)
    return dot(a_high, b_high, None) + small


def dot_tn(a, b):
    return lax.dot_general(
        a, b, (((0,), (0,)), ((), ())), precision=highest,
        preferred_element_type=jnp.float32,
    )


def shape(*dims):
    return jax.ShapeDtypeStruct(dims, jnp.float32)


def call(body, facts, inputs, outs, scratch=(), limit=24):
    return pl.pallas_call(
        body,
        out_shape=outs,
        in_specs=[pl.BlockSpec(memory_space=pltpu.SMEM)]
        + [pl.BlockSpec(memory_space=pltpu.VMEM)] * len(inputs),
        out_specs=jax.tree.map(
            lambda _: pl.BlockSpec(memory_space=pltpu.VMEM), outs
        ),
        scratch_shapes=list(scratch),
        compiler_params=pltpu.CompilerParams(vmem_limit_bytes=limit << 20),
    )(facts, *inputs)


def first_gram(sector, half):
    def body(x_ref, out_ref):
        x = x_ref[...]
        g = dot_tn(x, x)
        out_ref[:half] = g[:half, :half]
        out_ref[half : 2 * half] = g[:half, half:]
        out_ref[2 * half :] = g[half:, half:]

    vmem = pl.BlockSpec(memory_space=pltpu.VMEM)
    return pl.pallas_call(
        body,
        out_shape=shape(3 * half, half),
        in_specs=[vmem],
        out_specs=vmem,
        compiler_params=pltpu.CompilerParams(vmem_limit_bytes=24 << 20),
    )(sector)


def give_rows(sector, top, pieces=8):
    rows, width = sector.shape
    part = rows // 2
    step = part // pieces

    def body(x_ref, top_ref, rest_ref, sems):
        start = (1 - lax.axis_index("pair") % 2) * part
        copies = []
        for k in range(pieces):
            at = k * step
            target, here = (top_ref, at) if at < top else (rest_ref, at - top)
            source = x_ref.at[pl.ds(pl.multiple_of(start + at, 8), step)]
            copies.append(
                pltpu.make_async_copy(
                    source, target.at[here : here + step], sems.at[k]
                )
            )
            copies[-1].start()
        for copy in copies:
            copy.wait()

    return pl.pallas_call(
        body,
        out_shape=(shape(top, width), shape(part - top, width)),
        in_specs=[pl.BlockSpec(memory_space=pl.ANY)],
        out_specs=(pl.BlockSpec(memory_space=pltpu.VMEM),) * 2,
        scratch_shapes=[pltpu.SemaphoreType.DMA((pieces,))],
    )(sector)


def rotate_of(gram, x_ref, e_ref):
    size = gram.shape[0]
    rows = lax.broadcasted_iota(jnp.int32, (size, size), 0)
    cols = lax.broadcasted_iota(jnp.int32, (size, size), 1)
    identity = (rows == cols).astype(jnp.float32)
    only = jnp.where(rows == cols, gram, 0.0)
    g_j = jnp.sum(only, axis=0, keepdims=True)
    g_i = jnp.sum(only, axis=1, keepdims=True)
    spread = g_j - g_i
    summed = g_j + g_i
    skew = gram * spread / (spread * spread + 2.0 * gram * gram + 0.01 * summed * summed)
    skew_parts = split(skew)
    square = dot3(skew_parts, skew_parts)
    whole = 0.25 * jnp.sum(skew * skew)
    paired = 0.03125 * jnp.sum(square * square) * 1.001
    reach = jnp.minimum(whole * whole, paired)
    steps = jnp.int32(0)
    for limit in REACHES:
        steps = steps + (reach > limit).astype(jnp.int32)
    fixes = 1 + (steps > 7).astype(jnp.int32) + 2 * (steps > 9).astype(jnp.int32)
    scale = 2.0 / (2.0 + jnp.sqrt(jnp.full((size, size), reach, jnp.float32)))
    residual = identity - scale * (identity - 0.25 * square)
    x_ref[...] = scale * (identity + residual)
    residual_parts = split(residual)
    e_ref[...] = dot3(residual_parts, residual_parts)

    def step(_, carry):
        e = split(e_ref[...])
        x = x_ref[...]
        x_ref[...] = x + dot3(x, e)
        e_ref[...] = dot3(e, e)
        return carry

    lax.fori_loop(0, jnp.maximum(steps - 1, 0), step, jnp.int32(0))
    x = x_ref[...]
    x_ref[...] = x + 0.5 * dot3(x, skew_parts)

    def fix(_, carry):
        x = x_ref[...]
        x_ref[...] = x + dot3(x, identity - (x - 0.5 * dot(skew, x)))
        return carry

    lax.fori_loop(0, fixes, fix, jnp.int32(0))
    return 2.0 * x_ref[...] - identity


def put_rotation(rotation_ref, gram, x_ref, e_ref, last_round):
    size = gram.shape[0]
    rotation = rotate_of(gram, x_ref, e_ref)
    rotation_ref[:size] = rotation
    if last_round:
        squares = jnp.sum(rotation * dot(gram, rotation), axis=0, keepdims=True)
        rotation_ref[size:] = jnp.broadcast_to(squares, (8, size))


def first_rotation(facts, own, other_y, half):
    size = 2 * half

    def body(f, own_ref, other_ref, rotation_ref, g_ref, x_ref, e_ref):
        total = own_ref[...] + other_ref[...]
        g_ref[:half, :half] = total[:half]
        g_ref[:half, half:] = total[half : 2 * half]
        g_ref[half:, :half] = total[half : 2 * half].T
        g_ref[half:, half:] = total[2 * half :]
        put_rotation(rotation_ref, g_ref[...], x_ref, e_ref, False)

    square = pltpu.VMEM((size, size), jnp.float32)
    return call(body, facts, [own, other_y], (shape(size, size),) * 2, [square] * 2)


def later_rotation(facts, parts, diagonals, half, last_round):
    size = 2 * half

    def body(f, *refs):
        own, other_y, other_x, other_xy, foreign, native = [r[...] for r in refs[:6]]
        rotation_ref, g_ref, x_ref, e_ref = refs[6:]
        cross = (own + other_y) + (other_x + other_xy)
        core = f[CORE] == 0
        g_ref[:half, :half] = jnp.where(core, foreign, native)
        g_ref[:half, half:] = cross
        g_ref[half:, :half] = cross.T
        g_ref[half:, half:] = jnp.where(core, native, foreign)
        put_rotation(rotation_ref, g_ref[...], x_ref, e_ref, last_round)

    square = pltpu.VMEM((size, size), jnp.float32)
    return call(
        body,
        facts,
        parts + diagonals,
        (shape(size + 8 if last_round else size, size), shape(size, size)),
        [square] * 2,
    )


def turned_gram(facts, gram, rotation, position):
    size = gram.shape[0]
    half = size // 2

    def body(f, gram_ref, rotation_ref, leave_ref, stay_ref):
        rotation = rotation_ref[...]
        turned = dot(gram_ref[...], rotation)
        upper = dot_tn(rotation[:, :half], turned[:, :half])
        lower = dot_tn(rotation[:, half:], turned[:, half:])
        lower_leaves = (f[position] == 0) & (f[FIRST] == 0)
        leave_ref[...] = jnp.where(lower_leaves, lower, upper)
        stay_ref[...] = jnp.where(lower_leaves, upper, lower)

    return call(body, facts, [gram, rotation], (shape(half, half),) * 2)


def two_packs(f, own, other):
    core = f[CORE] == 0
    return jnp.where(core, own, other), jnp.where(core, other, own)


def swapped(flag, matrix, axis):
    half = matrix.shape[axis] // 2
    a = lax.slice_in_dim(matrix, 0, half, axis=axis)
    b = lax.slice_in_dim(matrix, half, 2 * half, axis=axis)
    return jnp.where(flag, lax.concatenate([b, a], axis), matrix)


def blocks_of(f, got_a, got_b, low_0, up_1):
    even = f[EVEN] == 1
    return (
        jnp.where(even, got_b, got_a), low_0, up_1, jnp.where(even, got_a, got_b)
    )


def put_turned(f, refs, zero, one, half, at=0):
    a_ref, b_ref, nat_l_ref, nat_u_ref = refs[:4]
    even = f[EVEN] == 1
    rows = slice(at, at + zero.shape[0])
    to_left, to_right = zero[:, half:], one[:, :half]
    a_ref[rows] = jnp.where(even, to_right, to_left)
    b_ref[rows] = jnp.where(even, to_left, to_right)
    nat_l_ref[rows] = one[:, half:]
    nat_u_ref[rows] = zero[:, :half]
    if len(refs) > 4:
        refs[4][rows] = jnp.where(f[X] == 0, zero[:, :half], one[:, half:])


def turns_of(f, own_ref, other_ref):
    size = other_ref.shape[1]
    turn_0, turn_1 = two_packs(f, own_ref[:size], other_ref[:size])
    return swapped(f[FIRST] == 1, turn_0, 1), turn_1


def turn_rows(facts, rotation, rows_of, half, own):
    rows = rows_of.shape[0] // 2 if own else rows_of.shape[0]

    def body(f, rotation_ref, x_ref, stay_ref, leave_ref):
        zero = f[X] == (0 if own else 1)
        upper_leaves = jnp.where(zero, f[FIRST], 1) == 1
        turn = swapped(upper_leaves, rotation_ref[...], 1)
        here = pl.multiple_of(f[X] * rows, 8)
        out = dot3(x_ref[pl.ds(here, rows)] if own else x_ref[...], turn)
        stay_ref[...] = out[:, :half]
        leave_ref[...] = out[:, half:]

    return call(body, facts, [rotation, rows_of], (shape(rows, half),) * 2)


def first_vectors(facts, rotation, other_rotation, vector_rows, half):
    def body(f, own_ref, other_ref, *refs):
        even = f[X] == 0
        own, other = own_ref[...], other_ref[...]
        turn_0 = swapped(f[FIRST] == 1, jnp.where(even, own, other), 1)
        turn_1 = jnp.where(even, other, own)
        ids = f[VROW] + lax.broadcasted_iota(jnp.int32, (vector_rows, half), 0)
        cols = lax.broadcasted_iota(jnp.int32, (vector_rows, half), 1)
        up_0, low_0, up_1, low_1 = [
            (ids == f[LABEL + k] * half + cols).astype(jnp.float32) for k in range(4)
        ]
        zero = dot3(lax.concatenate([up_0, low_0], 1), turn_0)
        one = dot3(lax.concatenate([up_1, low_1], 1), turn_1)
        put_turned(f, refs, zero, one, half)

    return call(
        body, facts, [rotation, other_rotation], (shape(vector_rows, half),) * 4
    )


def turn(facts, packs, blocks, vectors, half, last_move):
    part, vector_rows = blocks[0].shape[0], vectors[0].shape[0]

    def body(f, own_ref, other_ref, *refs):
        turn_0, turn_1 = turns_of(f, own_ref, other_ref)
        turn_0, turn_1 = split(turn_0), split(turn_1)
        columns = [r[...] for r in refs[:4]]
        rows = blocks_of(f, *[r[...] for r in refs[4:8]])
        outs = refs[8:]
        for (up_0, low_0, up_1, low_1), at in ((columns, 0), (rows, part)):
            zero = dot3(lax.concatenate([up_0, low_0], 1), turn_0)
            one = dot3(lax.concatenate([up_1, low_1], 1), turn_1)
            if last_move:
                put_turned(f, outs, zero, one, half, at)
            else:
                put_turned(f, outs[4 if at else 0 :][:4], zero, one, half)

    if last_move:
        outs = (shape(part + vector_rows, half),) * 5
    else:
        outs = (shape(part, half),) * 4 + (shape(vector_rows, half),) * 4
    return call(body, facts, packs + blocks + vectors, outs)


def put_cross(f, refs, zero, one):
    core = f[CORE] == 0
    refs[0][...] = jnp.where(core, zero, one)
    refs[1][...] = jnp.where(core, one, zero)


def first_cross_gram(facts, own, others, half):
    rows = own[0].shape[0]
    pieces = len(others)

    def body(f, *refs):
        own_refs = [[r] for r in refs[:3]]
        other_refs = [refs[3 + k : 3 + 3 * pieces : 3] for k in range(3)]
        up_0, low_0, up_1, low_1 = refs[5 + 3 * pieces :]

        def fill(target, sources):
            at = 0
            for ref in sources:
                target[at : at + ref.shape[0]] = ref[...]
                at += ref.shape[0]

        first, last = f[FIRST] == 1, f[LAST] == 1
        for x, near, far in ((0, own_refs, other_refs), (1, other_refs, own_refs)):
            here = f[X] == x

            @pl.when(here)
            def _():
                fill(up_1, near[0])
                fill(low_0, far[0])

            @pl.when(here & first)
            def _():
                fill(up_0, near[1])

            @pl.when(here & ~first)
            def _():
                fill(up_0, far[2])

            @pl.when(here & last)
            def _():
                fill(low_1, far[1])

            @pl.when(here & ~last)
            def _():
                fill(low_1, near[2])

        put_cross(
            f,
            refs[3 + 3 * pieces :],
            dot_tn(up_0[...], low_0[...]),
            dot_tn(up_1[...], low_1[...]),
        )

    outs = (shape(half, half),) * 2 + (shape(rows, half),) * 4
    return call(body, facts, own + sum(others, []), outs)


def cross_gram(facts, got, natives, part, half):
    rows = got[0].shape[0]

    def body(f, *refs):
        up_0, low_0, up_1, low_1 = blocks_of(f, *[r[...] for r in refs[:4]])
        put_cross(
            f,
            refs[4:],
            dot_tn(up_0[:part], low_0[:part]),
            dot_tn(up_1[:part], low_1[:part]),
        )
        refs[6][...] = up_0
        refs[7][...] = low_1

    outs = (shape(half, half),) * 2 + (shape(rows, half),) * 2
    return call(body, facts, got + natives, outs)


def give(facts, got, start, stop, half):
    def body(f, a_ref, b_ref, out_ref):
        mine = f[X] != f[EVEN]
        out_ref[...] = jnp.where(mine, a_ref[start:stop], b_ref[start:stop])

    return call(body, facts, got, shape(stop - start, half))


def final_turn(f, own_ref, other_ref, size):
    pack = jnp.where(f[CORE] == f[X], own_ref[...], other_ref[...])
    return split(swapped(f[X] == 1, pack[:size], 0)), pack[size : size + 1]


def final_product(moved, native, turned):
    return dot3(lax.concatenate([moved, native], 1), turned)


def put_rows(copies, sems, source, target, here, there, value):
    rows = value.shape[0]
    source[here : here + rows] = value
    copy = pltpu.make_async_copy(
        source.at[here : here + rows],
        target.at[pl.ds(pl.multiple_of(there, 8), rows)],
        sems.at[len(copies)],
    )
    copies.append(copy)
    copy.start()


def finish_call(body, facts, inputs, outputs, outs, rows, vector_rows, size):
    vmem = pl.BlockSpec(memory_space=pltpu.VMEM)
    hbm = pl.BlockSpec(memory_space=pl.ANY)
    first = 1 + len(inputs)
    return pl.pallas_call(
        body,
        out_shape=outs,
        in_specs=[pl.BlockSpec(memory_space=pltpu.SMEM)]
        + [vmem] * len(inputs)
        + [hbm] * len(outputs),
        out_specs=(hbm, hbm, vmem)[: len(outs)],
        input_output_aliases={first + k: k for k in range(len(outputs))},
        cost_estimate=pl.CostEstimate(flops=1, transcendentals=0, bytes_accessed=1),
        scratch_shapes=[
            pltpu.VMEM((rows, size), jnp.float32),
            pltpu.VMEM((vector_rows, size), jnp.float32),
            pltpu.SemaphoreType.DMA((4,)),
        ],
        compiler_params=pltpu.CompilerParams(vmem_limit_bytes=24 << 20),
    )(facts, *inputs, *outputs)


def finish_kept(facts, packs, blocks, native, got_top, part, half):
    size = 2 * half
    vector_rows = blocks[0].shape[0] - part
    top = got_top.shape[0]

    def body(f, own_ref, other_ref, *refs):
        x = f[X]
        turned, squares = final_turn(f, own_ref, other_ref, size)
        native_ref, top_ref, out_ref, vectors_ref, singular_ref, out, vectors, sems = (
            refs[4:]
        )
        copies = []

        def kept(rows):
            up_0, low_0, up_1, low_1 = [r[rows] for r in refs[:4]]
            return final_product(
                jnp.where(x == 0, up_0, low_1),
                jnp.where(x == 0, low_0, up_1),
                turned,
            )

        def put(*args):
            put_rows(copies, sems, *args)

        middle = part // 2
        put(out, out_ref, 0, x * part, kept(slice(0, middle)))
        put(out, out_ref, middle, x * part + middle, kept(slice(middle, part)))
        value = final_product(top_ref[...], native_ref[:top], turned)
        put(out, out_ref, part, (1 - x) * part, value)
        put(vectors, vectors_ref, 0, x * vector_rows, kept(slice(part, None)))
        singular_ref[...] = jnp.sqrt(jnp.maximum(squares, 0.0) + 1e-06)
        for copy in copies:
            copy.wait()

    outs = (shape(2 * part, size), shape(2 * vector_rows, size), shape(1, size))
    inputs = packs + blocks + [native, got_top]
    return finish_call(
        body, facts, inputs, [], outs, part + top, vector_rows, size
    )


def finish_rest(facts, packs, outputs, native, got_rest, part, half):
    size = 2 * half
    vector_rows = native.shape[0] - part
    rest = got_rest.shape[0] - vector_rows
    top = part - rest

    def body(f, own_ref, other_ref, native_ref, rest_ref, *refs):
        x = f[X]
        turned, _ = final_turn(f, own_ref, other_ref, size)
        out_ref, vectors_ref, out, vectors, sems = refs[2:]
        copies = []
        value = final_product(rest_ref[:rest], native_ref[top:part], turned)
        put_rows(copies, sems, out, out_ref, 0, (1 - x) * part + top, value)
        value = final_product(rest_ref[rest:], native_ref[part:], turned)
        put_rows(copies, sems, vectors, vectors_ref, 0, (1 - x) * vector_rows, value)
        for copy in copies:
            copy.wait()

    outs = (shape(2 * part, size), shape(2 * vector_rows, size))
    inputs = packs + [native, got_rest]
    return finish_call(
        body, facts, inputs, outputs, outs, rest, vector_rows, size
    )


def per_device(sector, block_label):
    local_rows, size = sector.shape
    half = size // 2
    part = local_rows // 2
    pairs = lax.axis_size("pair")
    row_count = lax.axis_size("row")
    vector_rows = pairs * size // row_count // 2
    pair_index = lax.axis_index("pair")
    row_index = lax.axis_index("row")
    x = pair_index % 2
    group = pair_index // 2
    core = row_index % 2

    def permute(block, route):
        moves = [
            (a * row_count + b, c * row_count + d) for (a, b), (c, d) in route
        ]
        return lax.ppermute(block, ("pair", "row"), moves)

    devices = [(p, r) for p in range(pairs) for r in range(row_count)]

    def exchange(block, over_pair, over_row):
        return permute(
            block, [((p ^ over_pair, r ^ over_row), (p, r)) for p, r in devices]
        )

    def shift(block, even_by):
        moves = []
        for p, r in devices:
            source = p - even_by if p % 2 == 0 else p + even_by
            if 0 <= source < pairs:
                moves.append(((source, r), (p, r)))
        return permute(block, moves)

    def swap(block, odd):
        moves = []
        for p, r in devices:
            other = p + 2 if p // 2 % 2 == odd else p - 2
            moves.append(((other if 0 <= other < pairs else p, r), (p, r)))
        return permute(block, moves)

    def pass_diagonal(block):
        moves = []
        for p, r in devices:
            other = p + 2 if r % 2 else p - 2
            inside = 0 <= other < pairs
            moves.append(((other, r ^ 1) if inside else (p, r), (p, r)))
        return permute(block, [((a, b), c) for (a, b), c in moves])

    def first_diagonal(block, leaves):
        moves = []
        for p, r in devices:
            c, even = r % 2, p - p % 2
            if leaves:
                source = even - 1 if c == 0 else even + 2
                if not 0 <= source < pairs:
                    source = even + c
            else:
                source = even + 1 - c
            moves.append(((source, r - c + p % 2), (p, r)))
        return permute(block, moves)

    def sum_rows(block):
        bit = 4
        while bit < row_count:
            block = block + exchange(block, 0, bit)
            bit *= 2
        return block

    names = jnp.arange(16, dtype=jnp.int32)
    facts = jnp.zeros((16,), jnp.int32)
    for name, value in (
        (X, x),
        (CORE, core),
        (FIRST, group == 0),
        (LAST, group == pairs // 2 - 1),
        (VROW, (row_index * 2 + x) * vector_rows),
        (EVEN, group % 2 == 0),
    ):
        facts = jnp.where(names == name, value.astype(jnp.int32), facts)
    labels = lax.dynamic_slice_in_dim(block_label, 4 * group, 4)
    facts = lax.dynamic_update_slice_in_dim(facts, labels, LABEL, 0)

    def together(*arrays):
        return lax.optimization_barrier(arrays)

    top_give, rest_give = give_rows(sector, part * 3 // 4)
    got_top = exchange(top_give, 1, 0)
    own = first_gram(sector, half)
    own = sum_rows(own + exchange(own, 0, 1))
    rotation, gram = first_rotation(facts, own, exchange(own, 0, 2), half)

    for sweep_round in range(ROUNDS - 1):
        last_move = sweep_round == ROUNDS - 2
        if sweep_round == 0:
            other_rotation = exchange(rotation, 1, 0)
            stay, leave = turn_rows(facts, rotation, sector, half, True)
            leave, rest_give = together(leave, rest_give)
            got_rest = exchange(rest_give, 1, 0)
            own_rows = [stay, leave, shift(leave, -2)]
            other_rows = []
            for got in (got_top, got_rest):
                stay, leave = turn_rows(facts, other_rotation, got, half, False)
                other_rows.append([stay, leave, shift(leave, 2)])
            leave, stay = turned_gram(facts, gram, rotation, X)
            diagonals = [first_diagonal(leave, True), first_diagonal(stay, False)]
            vectors = list(
                first_vectors(facts, rotation, other_rotation, vector_rows, half)
            )
            vectors[0], vectors[1], diagonals[1] = together(
                vectors[0], vectors[1], diagonals[1]
            )
            *grams, up_0, nat_l, nat_u, low_1 = first_cross_gram(
                facts, own_rows, other_rows, half
            )
        else:
            packs = [rotation, exchange(rotation, 0, 1)]
            leave_a, leave_b, nat_l, nat_u, *vectors = turn(
                facts, packs, blocks, vectors, half, last_move
            )
            got = [swap(leave_a, 0), swap(leave_b, 1)]
            leave, stay = turned_gram(facts, gram, rotation, CORE)
            diagonals = [pass_diagonal(leave), exchange(stay, 0, 1)]
            if last_move:
                native = exchange(vectors.pop(), 1, 0)
                top = part // 2
                top_give = give(facts, got, 0, top, half)
                *got, top_give, diagonals[0], diagonals[1] = together(
                    *got, top_give, *diagonals
                )
                got_top = exchange(top_give, 1, 0)
            else:
                vectors[0], vectors[1], diagonals[1] = together(
                    vectors[0], vectors[1], diagonals[1]
                )
            *grams, up_0, low_1 = cross_gram(facts, got, [nat_l, nat_u], part, half)
        blocks = [up_0, nat_l, nat_u, low_1]
        if last_move:
            grams[1], native = together(grams[1], native)
        else:
            vector_a, vector_b, *kept = vectors
            grams[1], vector_a, vector_b, diagonals[0] = together(
                grams[1], swap(vector_a, 0), swap(vector_b, 1), diagonals[0]
            )
            vectors = [vector_a, vector_b] + kept
        own = sum_rows(grams[0] + exchange(grams[1], 0, 1))
        parts = [own, exchange(own, 0, 2), exchange(own, 1, 0), exchange(own, 1, 2)]
        if last_move:
            rest_give = give(facts, got, top, part + vector_rows, half)
            *parts, got_top, rest_give = together(*parts, got_top, rest_give)
            got_rest = exchange(rest_give, 1, 0)
        rotation, gram = later_rotation(facts, parts, diagonals, half, last_move)
    packs = [rotation, exchange(rotation, 0, 1)]
    *outputs, singular = finish_kept(
        facts, packs, blocks, native, got_top, part, half
    )
    rotated, vectors_out = finish_rest(
        facts, packs, outputs, native, got_rest, part, half
    )
    return rotated, vectors_out, singular.reshape(size)


def solution(mesh):
    placed = (P("row", "pair"), P())
    return jax.shard_map(
        per_device,
        mesh=mesh,
        in_specs=placed,
        out_specs=(P("row", "pair"), P("row", "pair"), P("pair")),
        check_vma=False,
    )
```

```python
import jax
import jax.numpy as jnp
from jax import lax
from jax.experimental import pallas as pl
from jax.experimental.pallas import tpu as pltpu
from jax.sharding import PartitionSpec as P

ROUNDS = 4
NEWTON = 16

highest = lax.Precision.HIGHEST

TARGET = 2.0**-12
REACHES = [
    (2.0 / (TARGET ** -(2.0**-j) - 1.0)) ** 2 for j in range(NEWTON)
]

X, CORE, FIRST, LAST, VROW, LABEL, EVEN = 0, 1, 2, 3, 4, 5, 9


def dot(a, b, precision=highest):
    return lax.dot_general(
        a, b, (((1,), (0,)), ((), ())), precision=precision,
        preferred_element_type=jnp.float32,
    )


def split(a):
    high = a.astype(jnp.bfloat16)
    return high, (a - high.astype(jnp.float32)).astype(jnp.bfloat16)


def dot3(a, b):
    a_high, a_low = a if isinstance(a, tuple) else split(a)
    b_high, b_low = b if isinstance(b, tuple) else split(b)
    small = dot(a_high, b_low, None) + dot(a_low, b_high, None)
    return dot(a_high, b_high, None) + small


def dot_tn(a, b):
    return lax.dot_general(
        a, b, (((0,), (0,)), ((), ())), precision=highest,
        preferred_element_type=jnp.float32,
    )


def shape(*dims):
    return jax.ShapeDtypeStruct(dims, jnp.float32)


def call(body, facts, inputs, outs, scratch=(), limit=24):
    return pl.pallas_call(
        body,
        out_shape=outs,
        in_specs=[pl.BlockSpec(memory_space=pltpu.SMEM)]
        + [pl.BlockSpec(memory_space=pltpu.VMEM)] * len(inputs),
        out_specs=jax.tree.map(
            lambda _: pl.BlockSpec(memory_space=pltpu.VMEM), outs
        ),
        scratch_shapes=list(scratch),
        compiler_params=pltpu.CompilerParams(vmem_limit_bytes=limit << 20),
    )(facts, *inputs)


def first_gram(sector, half):
    def body(x_ref, out_ref):
        x = x_ref[...]
        g = dot_tn(x, x)
        out_ref[:half] = g[:half, :half]
        out_ref[half : 2 * half] = g[:half, half:]
        out_ref[2 * half :] = g[half:, half:]

    vmem = pl.BlockSpec(memory_space=pltpu.VMEM)
    return pl.pallas_call(
        body,
        out_shape=shape(3 * half, half),
        in_specs=[vmem],
        out_specs=vmem,
        compiler_params=pltpu.CompilerParams(vmem_limit_bytes=24 << 20),
    )(sector)


def give_rows(sector, top, pieces=8):
    rows, width = sector.shape
    part = rows // 2
    step = part // pieces

    def body(x_ref, top_ref, rest_ref, sems):
        start = (1 - lax.axis_index("pair") % 2) * part
        copies = []
        for k in range(pieces):
            at = k * step
            target, here = (top_ref, at) if at < top else (rest_ref, at - top)
            source = x_ref.at[pl.ds(pl.multiple_of(start + at, 8), step)]
            copies.append(
                pltpu.make_async_copy(
                    source, target.at[here : here + step], sems.at[k]
                )
            )
            copies[-1].start()
        for copy in copies:
            copy.wait()

    return pl.pallas_call(
        body,
        out_shape=(shape(top, width), shape(part - top, width)),
        in_specs=[pl.BlockSpec(memory_space=pl.ANY)],
        out_specs=(pl.BlockSpec(memory_space=pltpu.VMEM),) * 2,
        scratch_shapes=[pltpu.SemaphoreType.DMA((pieces,))],
    )(sector)


def rotate_of(gram, x_ref, e_ref):
    size = gram.shape[0]
    rows = lax.broadcasted_iota(jnp.int32, (size, size), 0)
    cols = lax.broadcasted_iota(jnp.int32, (size, size), 1)
    identity = (rows == cols).astype(jnp.float32)
    only = jnp.where(rows == cols, gram, 0.0)
    g_j = jnp.sum(only, axis=0, keepdims=True)
    g_i = jnp.sum(only, axis=1, keepdims=True)
    spread = g_j - g_i
    summed = g_j + g_i
    skew = gram * spread / (spread * spread + 2.0 * gram * gram + 0.01 * summed * summed)
    skew_parts = split(skew)
    square = dot3(skew_parts, skew_parts)
    whole = 0.25 * jnp.sum(skew * skew)
    paired = 0.03125 * jnp.sum(square * square) * 1.001
    reach = jnp.minimum(whole * whole, paired)
    steps = jnp.int32(0)
    for limit in REACHES:
        steps = steps + (reach > limit).astype(jnp.int32)
    fixes = 1 + (steps > 7).astype(jnp.int32) + 2 * (steps > 9).astype(jnp.int32)
    scale = 2.0 / (2.0 + jnp.sqrt(jnp.full((size, size), reach, jnp.float32)))
    residual = identity - scale * (identity - 0.25 * square)
    x_ref[...] = scale * (identity + residual)
    residual_parts = split(residual)
    e_ref[...] = dot3(residual_parts, residual_parts)

    def step(_, carry):
        e = split(e_ref[...])
        x = x_ref[...]
        x_ref[...] = x + dot3(x, e)
        e_ref[...] = dot3(e, e)
        return carry

    lax.fori_loop(0, jnp.maximum(steps - 1, 0), step, jnp.int32(0))
    x = x_ref[...]
    x_ref[...] = x + 0.5 * dot3(x, skew_parts)

    def fix(_, carry):
        x = x_ref[...]
        x_ref[...] = x + dot3(x, identity - (x - 0.5 * dot(skew, x)))
        return carry

    lax.fori_loop(0, fixes, fix, jnp.int32(0))
    return 2.0 * x_ref[...] - identity


def put_rotation(rotation_ref, gram, x_ref, e_ref, last_round):
    size = gram.shape[0]
    rotation = rotate_of(gram, x_ref, e_ref)
    rotation_ref[:size] = rotation
    if last_round:
        squares = jnp.sum(rotation * dot(gram, rotation), axis=0, keepdims=True)
        rotation_ref[size:] = jnp.broadcast_to(squares, (8, size))


def first_rotation(facts, own, other_y, half):
    size = 2 * half

    def body(f, own_ref, other_ref, rotation_ref, g_ref, x_ref, e_ref):
        total = own_ref[...] + other_ref[...]
        g_ref[:half, :half] = total[:half]
        g_ref[:half, half:] = total[half : 2 * half]
        g_ref[half:, :half] = total[half : 2 * half].T
        g_ref[half:, half:] = total[2 * half :]
        put_rotation(rotation_ref, g_ref[...], x_ref, e_ref, False)

    square = pltpu.VMEM((size, size), jnp.float32)
    return call(body, facts, [own, other_y], (shape(size, size),) * 2, [square] * 2)


def later_rotation(facts, parts, diagonals, half, last_round):
    size = 2 * half

    def body(f, *refs):
        own, other_y, other_x, other_xy, foreign, native = [r[...] for r in refs[:6]]
        rotation_ref, g_ref, x_ref, e_ref = refs[6:]
        cross = (own + other_y) + (other_x + other_xy)
        core = f[CORE] == 0
        g_ref[:half, :half] = jnp.where(core, foreign, native)
        g_ref[:half, half:] = cross
        g_ref[half:, :half] = cross.T
        g_ref[half:, half:] = jnp.where(core, native, foreign)
        put_rotation(rotation_ref, g_ref[...], x_ref, e_ref, last_round)

    square = pltpu.VMEM((size, size), jnp.float32)
    return call(
        body,
        facts,
        parts + diagonals,
        (shape(size + 8 if last_round else size, size), shape(size, size)),
        [square] * 2,
    )


def turned_gram(facts, gram, rotation, position):
    size = gram.shape[0]
    half = size // 2

    def body(f, gram_ref, rotation_ref, leave_ref, stay_ref):
        rotation = rotation_ref[...]
        turned = dot(gram_ref[...], rotation)
        upper = dot_tn(rotation[:, :half], turned[:, :half])
        lower = dot_tn(rotation[:, half:], turned[:, half:])
        lower_leaves = (f[position] == 0) & (f[FIRST] == 0)
        leave_ref[...] = jnp.where(lower_leaves, lower, upper)
        stay_ref[...] = jnp.where(lower_leaves, upper, lower)

    return call(body, facts, [gram, rotation], (shape(half, half),) * 2)


def two_packs(f, own, other):
    core = f[CORE] == 0
    return jnp.where(core, own, other), jnp.where(core, other, own)


def swapped(flag, matrix, axis):
    half = matrix.shape[axis] // 2
    a = lax.slice_in_dim(matrix, 0, half, axis=axis)
    b = lax.slice_in_dim(matrix, half, 2 * half, axis=axis)
    return jnp.where(flag, lax.concatenate([b, a], axis), matrix)


def blocks_of(f, got_a, got_b, low_0, up_1):
    even = f[EVEN] == 1
    return (
        jnp.where(even, got_b, got_a), low_0, up_1, jnp.where(even, got_a, got_b)
    )


def put_turned(f, refs, zero, one, half, at=0):
    a_ref, b_ref, nat_l_ref, nat_u_ref = refs[:4]
    even = f[EVEN] == 1
    rows = slice(at, at + zero.shape[0])
    to_left, to_right = zero[:, half:], one[:, :half]
    a_ref[rows] = jnp.where(even, to_right, to_left)
    b_ref[rows] = jnp.where(even, to_left, to_right)
    nat_l_ref[rows] = one[:, half:]
    nat_u_ref[rows] = zero[:, :half]
    if len(refs) > 4:
        refs[4][rows] = jnp.where(f[X] == 0, zero[:, :half], one[:, half:])


def turns_of(f, own_ref, other_ref):
    size = other_ref.shape[1]
    turn_0, turn_1 = two_packs(f, own_ref[:size], other_ref[:size])
    return swapped(f[FIRST] == 1, turn_0, 1), turn_1


def turn_rows(facts, rotation, rows_of, half, own):
    rows = rows_of.shape[0] // 2 if own else rows_of.shape[0]

    def body(f, rotation_ref, x_ref, stay_ref, leave_ref):
        zero = f[X] == (0 if own else 1)
        upper_leaves = jnp.where(zero, f[FIRST], 1) == 1
        turn = swapped(upper_leaves, rotation_ref[...], 1)
        here = pl.multiple_of(f[X] * rows, 8)
        out = dot3(x_ref[pl.ds(here, rows)] if own else x_ref[...], turn)
        stay_ref[...] = out[:, :half]
        leave_ref[...] = out[:, half:]

    return call(body, facts, [rotation, rows_of], (shape(rows, half),) * 2)


def first_vectors(facts, rotation, other_rotation, vector_rows, half):
    def body(f, own_ref, other_ref, *refs):
        even = f[X] == 0
        own, other = own_ref[...], other_ref[...]
        turn_0 = swapped(f[FIRST] == 1, jnp.where(even, own, other), 1)
        turn_1 = jnp.where(even, other, own)
        ids = f[VROW] + lax.broadcasted_iota(jnp.int32, (vector_rows, half), 0)
        cols = lax.broadcasted_iota(jnp.int32, (vector_rows, half), 1)
        up_0, low_0, up_1, low_1 = [
            (ids == f[LABEL + k] * half + cols).astype(jnp.float32) for k in range(4)
        ]
        zero = dot3(lax.concatenate([up_0, low_0], 1), turn_0)
        one = dot3(lax.concatenate([up_1, low_1], 1), turn_1)
        put_turned(f, refs, zero, one, half)

    return call(
        body, facts, [rotation, other_rotation], (shape(vector_rows, half),) * 4
    )


def turn(facts, packs, blocks, vectors, half, last_move):
    part, vector_rows = blocks[0].shape[0], vectors[0].shape[0]

    def body(f, own_ref, other_ref, *refs):
        turn_0, turn_1 = turns_of(f, own_ref, other_ref)
        turn_0, turn_1 = split(turn_0), split(turn_1)
        columns = [r[...] for r in refs[:4]]
        rows = blocks_of(f, *[r[...] for r in refs[4:8]])
        outs = refs[8:]
        for (up_0, low_0, up_1, low_1), at in ((columns, 0), (rows, part)):
            zero = dot3(lax.concatenate([up_0, low_0], 1), turn_0)
            one = dot3(lax.concatenate([up_1, low_1], 1), turn_1)
            if last_move:
                put_turned(f, outs, zero, one, half, at)
            else:
                put_turned(f, outs[4 if at else 0 :][:4], zero, one, half)

    if last_move:
        outs = (shape(part + vector_rows, half),) * 5
    else:
        outs = (shape(part, half),) * 4 + (shape(vector_rows, half),) * 4
    return call(body, facts, packs + blocks + vectors, outs)


def put_cross(f, refs, zero, one):
    core = f[CORE] == 0
    refs[0][...] = jnp.where(core, zero, one)
    refs[1][...] = jnp.where(core, one, zero)


def first_cross_gram(facts, own, others, half):
    rows = own[0].shape[0]
    pieces = len(others)

    def body(f, *refs):
        own_refs = [[r] for r in refs[:3]]
        other_refs = [refs[3 + k : 3 + 3 * pieces : 3] for k in range(3)]
        up_0, low_0, up_1, low_1 = refs[5 + 3 * pieces :]

        def fill(target, sources):
            at = 0
            for ref in sources:
                target[at : at + ref.shape[0]] = ref[...]
                at += ref.shape[0]

        first, last = f[FIRST] == 1, f[LAST] == 1
        for x, near, far in ((0, own_refs, other_refs), (1, other_refs, own_refs)):
            here = f[X] == x

            @pl.when(here)
            def _():
                fill(up_1, near[0])
                fill(low_0, far[0])

            @pl.when(here & first)
            def _():
                fill(up_0, near[1])

            @pl.when(here & ~first)
            def _():
                fill(up_0, far[2])

            @pl.when(here & last)
            def _():
                fill(low_1, far[1])

            @pl.when(here & ~last)
            def _():
                fill(low_1, near[2])

        put_cross(
            f,
            refs[3 + 3 * pieces :],
            dot_tn(up_0[...], low_0[...]),
            dot_tn(up_1[...], low_1[...]),
        )

    outs = (shape(half, half),) * 2 + (shape(rows, half),) * 4
    return call(body, facts, own + sum(others, []), outs)


def cross_gram(facts, got, natives, part, half):
    rows = got[0].shape[0]

    def body(f, *refs):
        up_0, low_0, up_1, low_1 = blocks_of(f, *[r[...] for r in refs[:4]])
        put_cross(
            f,
            refs[4:],
            dot_tn(up_0[:part], low_0[:part]),
            dot_tn(up_1[:part], low_1[:part]),
        )
        refs[6][...] = up_0
        refs[7][...] = low_1

    outs = (shape(half, half),) * 2 + (shape(rows, half),) * 2
    return call(body, facts, got + natives, outs)


def give(facts, got, start, stop, half):
    def body(f, a_ref, b_ref, out_ref):
        mine = f[X] != f[EVEN]
        out_ref[...] = jnp.where(mine, a_ref[start:stop], b_ref[start:stop])

    return call(body, facts, got, shape(stop - start, half))


def final_turn(f, own_ref, other_ref, size):
    pack = jnp.where(f[CORE] == f[X], own_ref[...], other_ref[...])
    return split(swapped(f[X] == 1, pack[:size], 0)), pack[size : size + 1]


def final_product(moved, native, turned):
    return dot3(lax.concatenate([moved, native], 1), turned)


def put_rows(copies, sems, source, target, here, there, value):
    rows = value.shape[0]
    source[here : here + rows] = value
    copy = pltpu.make_async_copy(
        source.at[here : here + rows],
        target.at[pl.ds(pl.multiple_of(there, 8), rows)],
        sems.at[len(copies)],
    )
    copies.append(copy)
    copy.start()


def finish_call(body, facts, inputs, outputs, outs, rows, vector_rows, size):
    vmem = pl.BlockSpec(memory_space=pltpu.VMEM)
    hbm = pl.BlockSpec(memory_space=pl.ANY)
    first = 1 + len(inputs)
    return pl.pallas_call(
        body,
        out_shape=outs,
        in_specs=[pl.BlockSpec(memory_space=pltpu.SMEM)]
        + [vmem] * len(inputs)
        + [hbm] * len(outputs),
        out_specs=(hbm, hbm, vmem)[: len(outs)],
        input_output_aliases={first + k: k for k in range(len(outputs))},
        cost_estimate=pl.CostEstimate(flops=1, transcendentals=0, bytes_accessed=1),
        scratch_shapes=[
            pltpu.VMEM((rows, size), jnp.float32),
            pltpu.VMEM((vector_rows, size), jnp.float32),
            pltpu.SemaphoreType.DMA((4,)),
        ],
        compiler_params=pltpu.CompilerParams(vmem_limit_bytes=24 << 20),
    )(facts, *inputs, *outputs)


def finish_kept(facts, packs, blocks, native, got_top, part, half):
    size = 2 * half
    vector_rows = blocks[0].shape[0] - part
    top = got_top.shape[0]

    def body(f, own_ref, other_ref, *refs):
        x = f[X]
        turned, squares = final_turn(f, own_ref, other_ref, size)
        native_ref, top_ref, out_ref, vectors_ref, singular_ref, out, vectors, sems = (
            refs[4:]
        )
        copies = []

        def kept(rows):
            up_0, low_0, up_1, low_1 = [r[rows] for r in refs[:4]]
            return final_product(
                jnp.where(x == 0, up_0, low_1),
                jnp.where(x == 0, low_0, up_1),
                turned,
            )

        def put(*args):
            put_rows(copies, sems, *args)

        middle = part // 2
        put(out, out_ref, 0, x * part, kept(slice(0, middle)))
        put(out, out_ref, middle, x * part + middle, kept(slice(middle, part)))
        value = final_product(top_ref[...], native_ref[:top], turned)
        put(out, out_ref, part, (1 - x) * part, value)
        put(vectors, vectors_ref, 0, x * vector_rows, kept(slice(part, None)))
        singular_ref[...] = jnp.sqrt(jnp.maximum(squares, 0.0) + 1e-06)
        for copy in copies:
            copy.wait()

    outs = (shape(2 * part, size), shape(2 * vector_rows, size), shape(1, size))
    inputs = packs + blocks + [native, got_top]
    return finish_call(
        body, facts, inputs, [], outs, part + top, vector_rows, size
    )


def finish_rest(facts, packs, outputs, native, got_rest, part, half):
    size = 2 * half
    vector_rows = native.shape[0] - part
    rest = got_rest.shape[0] - vector_rows
    top = part - rest

    def body(f, own_ref, other_ref, native_ref, rest_ref, *refs):
        x = f[X]
        turned, _ = final_turn(f, own_ref, other_ref, size)
        out_ref, vectors_ref, out, vectors, sems = refs[2:]
        copies = []
        value = final_product(rest_ref[:rest], native_ref[top:part], turned)
        put_rows(copies, sems, out, out_ref, 0, (1 - x) * part + top, value)
        value = final_product(rest_ref[rest:], native_ref[part:], turned)
        put_rows(copies, sems, vectors, vectors_ref, 0, (1 - x) * vector_rows, value)
        for copy in copies:
            copy.wait()

    outs = (shape(2 * part, size), shape(2 * vector_rows, size))
    inputs = packs + [native, got_rest]
    return finish_call(
        body, facts, inputs, outputs, outs, rest, vector_rows, size
    )


def per_device(sector, block_label):
    local_rows, size = sector.shape
    half = size // 2
    part = local_rows // 2
    pairs = lax.axis_size("pair")
    row_count = lax.axis_size("row")
    vector_rows = pairs * size // row_count // 2
    pair_index = lax.axis_index("pair")
    row_index = lax.axis_index("row")
    x = pair_index % 2
    group = pair_index // 2
    core = row_index % 2

    def permute(block, route):
        moves = [
            (a * row_count + b, c * row_count + d) for (a, b), (c, d) in route
        ]
        return lax.ppermute(block, ("pair", "row"), moves)

    devices = [(p, r) for p in range(pairs) for r in range(row_count)]

    def exchange(block, over_pair, over_row):
        return permute(
            block, [((p ^ over_pair, r ^ over_row), (p, r)) for p, r in devices]
        )

    def shift(block, even_by):
        moves = []
        for p, r in devices:
            source = p - even_by if p % 2 == 0 else p + even_by
            if 0 <= source < pairs:
                moves.append(((source, r), (p, r)))
        return permute(block, moves)

    def swap(block, odd):
        moves = []
        for p, r in devices:
            other = p + 2 if p // 2 % 2 == odd else p - 2
            moves.append(((other if 0 <= other < pairs else p, r), (p, r)))
        return permute(block, moves)

    def pass_diagonal(block):
        moves = []
        for p, r in devices:
            other = p + 2 if r % 2 else p - 2
            inside = 0 <= other < pairs
            moves.append(((other, r ^ 1) if inside else (p, r), (p, r)))
        return permute(block, [((a, b), c) for (a, b), c in moves])

    def first_diagonal(block, leaves):
        moves = []
        for p, r in devices:
            c, even = r % 2, p - p % 2
            if leaves:
                source = even - 1 if c == 0 else even + 2
                if not 0 <= source < pairs:
                    source = even + c
            else:
                source = even + 1 - c
            moves.append(((source, r - c + p % 2), (p, r)))
        return permute(block, moves)

    def sum_rows(block):
        bit = 4
        while bit < row_count:
            block = block + exchange(block, 0, bit)
            bit *= 2
        return block

    names = jnp.arange(16, dtype=jnp.int32)
    facts = jnp.zeros((16,), jnp.int32)
    for name, value in (
        (X, x),
        (CORE, core),
        (FIRST, group == 0),
        (LAST, group == pairs // 2 - 1),
        (VROW, (row_index * 2 + x) * vector_rows),
        (EVEN, group % 2 == 0),
    ):
        facts = jnp.where(names == name, value.astype(jnp.int32), facts)
    labels = lax.dynamic_slice_in_dim(block_label, 4 * group, 4)
    facts = lax.dynamic_update_slice_in_dim(facts, labels, LABEL, 0)

    def together(*arrays):
        return lax.optimization_barrier(arrays)

    top_give, rest_give = give_rows(sector, part * 3 // 4)
    got_top = exchange(top_give, 1, 0)
    own = first_gram(sector, half)
    own = sum_rows(own + exchange(own, 0, 1))
    rotation, gram = first_rotation(facts, own, exchange(own, 0, 2), half)

    for sweep_round in range(ROUNDS - 1):
        last_move = sweep_round == ROUNDS - 2
        if sweep_round == 0:
            other_rotation = exchange(rotation, 1, 0)
            stay, leave = turn_rows(facts, rotation, sector, half, True)
            leave, rest_give = together(leave, rest_give)
            got_rest = exchange(rest_give, 1, 0)
            own_rows = [stay, leave, shift(leave, -2)]
            other_rows = []
            for got in (got_top, got_rest):
                stay, leave = turn_rows(facts, other_rotation, got, half, False)
                other_rows.append([stay, leave, shift(leave, 2)])
            leave, stay = turned_gram(facts, gram, rotation, X)
            diagonals = [first_diagonal(leave, True), first_diagonal(stay, False)]
            vectors = list(
                first_vectors(facts, rotation, other_rotation, vector_rows, half)
            )
            own_rows[2], *diagonals = together(own_rows[2], *diagonals)
            *grams, up_0, nat_l, nat_u, low_1 = first_cross_gram(
                facts, own_rows, other_rows, half
            )
        else:
            packs = [rotation, exchange(rotation, 0, 1)]
            leave_a, leave_b, nat_l, nat_u, *vectors = turn(
                facts, packs, blocks, vectors, half, last_move
            )
            got = [swap(leave_a, 0), swap(leave_b, 1)]
            leave, stay = turned_gram(facts, gram, rotation, CORE)
            diagonals = [pass_diagonal(leave), exchange(stay, 0, 1)]
            if last_move:
                native = exchange(vectors.pop(), 1, 0)
                top = part // 2
                top_give = give(facts, got, 0, top, half)
                *got, top_give, diagonals[0], diagonals[1] = together(
                    *got, top_give, *diagonals
                )
                got_top = exchange(top_give, 1, 0)
            else:
                *got, diagonals[0], diagonals[1] = together(*got, *diagonals)
            *grams, up_0, low_1 = cross_gram(facts, got, [nat_l, nat_u], part, half)
        blocks = [up_0, nat_l, nat_u, low_1]
        if last_move:
            grams[1], native = together(grams[1], native)
        else:
            vector_a, vector_b, *kept = vectors
            vectors = [swap(vector_a, 0), swap(vector_b, 1)] + kept
        own = sum_rows(grams[0] + exchange(grams[1], 0, 1))
        if not last_move:
            own, vectors[0], vectors[1] = together(own, vectors[0], vectors[1])
        parts = [own, exchange(own, 0, 2), exchange(own, 1, 0), exchange(own, 1, 2)]
        if last_move:
            rest_give = give(facts, got, top, part + vector_rows, half)
            *parts, got_top, rest_give = together(*parts, got_top, rest_give)
            got_rest = exchange(rest_give, 1, 0)
        rotation, gram = later_rotation(facts, parts, diagonals, half, last_move)
    packs = [rotation, exchange(rotation, 0, 1)]
    *outputs, singular = finish_kept(
        facts, packs, blocks, native, got_top, part, half
    )
    rotated, vectors_out = finish_rest(
        facts, packs, outputs, native, got_rest, part, half
    )
    return rotated, vectors_out, singular.reshape(size)


def solution(mesh):
    placed = (P("row", "pair"), P())
    return jax.shard_map(
        per_device,
        mesh=mesh,
        in_specs=placed,
        out_specs=(P("row", "pair"), P("row", "pair"), P("pair")),
        check_vma=False,
    )
```

```python
import jax
import jax.numpy as jnp
from jax import lax
from jax.experimental import pallas as pl
from jax.experimental.pallas import tpu as pltpu
from jax.sharding import PartitionSpec as P

ROUNDS = 4
NEWTON = 16

highest = lax.Precision.HIGHEST

TARGET = 2.0**-12
REACHES = [
    (2.0 / (TARGET ** -(2.0**-j) - 1.0)) ** 2 for j in range(NEWTON)
]

X, CORE, FIRST, LAST, VROW, LABEL, EVEN = 0, 1, 2, 3, 4, 5, 9


def dot(a, b, precision=highest):
    return lax.dot_general(
        a, b, (((1,), (0,)), ((), ())), precision=precision,
        preferred_element_type=jnp.float32,
    )


def split(a):
    high = a.astype(jnp.bfloat16)
    return high, (a - high.astype(jnp.float32)).astype(jnp.bfloat16)


def dot3(a, b):
    a_high, a_low = a if isinstance(a, tuple) else split(a)
    b_high, b_low = b if isinstance(b, tuple) else split(b)
    small = dot(a_high, b_low, None) + dot(a_low, b_high, None)
    return dot(a_high, b_high, None) + small


def dot_tn(a, b):
    return lax.dot_general(
        a, b, (((0,), (0,)), ((), ())), precision=highest,
        preferred_element_type=jnp.float32,
    )


def shape(*dims):
    return jax.ShapeDtypeStruct(dims, jnp.float32)


def call(body, facts, inputs, outs, scratch=(), limit=24):
    return pl.pallas_call(
        body,
        out_shape=outs,
        in_specs=[pl.BlockSpec(memory_space=pltpu.SMEM)]
        + [pl.BlockSpec(memory_space=pltpu.VMEM)] * len(inputs),
        out_specs=jax.tree.map(
            lambda _: pl.BlockSpec(memory_space=pltpu.VMEM), outs
        ),
        scratch_shapes=list(scratch),
        compiler_params=pltpu.CompilerParams(vmem_limit_bytes=limit << 20),
    )(facts, *inputs)


def first_gram(sector, half):
    def body(x_ref, out_ref):
        x = x_ref[...]
        g = dot_tn(x, x)
        out_ref[:half] = g[:half, :half]
        out_ref[half : 2 * half] = g[:half, half:]
        out_ref[2 * half :] = g[half:, half:]

    vmem = pl.BlockSpec(memory_space=pltpu.VMEM)
    return pl.pallas_call(
        body,
        out_shape=shape(3 * half, half),
        in_specs=[vmem],
        out_specs=vmem,
        compiler_params=pltpu.CompilerParams(vmem_limit_bytes=24 << 20),
    )(sector)


def give_rows(sector, top, pieces=8):
    rows, width = sector.shape
    part = rows // 2
    step = part // pieces

    def body(x_ref, top_ref, rest_ref, sems):
        start = (1 - lax.axis_index("pair") % 2) * part
        copies = []
        for k in range(pieces):
            at = k * step
            target, here = (top_ref, at) if at < top else (rest_ref, at - top)
            source = x_ref.at[pl.ds(pl.multiple_of(start + at, 8), step)]
            copies.append(
                pltpu.make_async_copy(
                    source, target.at[here : here + step], sems.at[k]
                )
            )
            copies[-1].start()
        for copy in copies:
            copy.wait()

    return pl.pallas_call(
        body,
        out_shape=(shape(top, width), shape(part - top, width)),
        in_specs=[pl.BlockSpec(memory_space=pl.ANY)],
        out_specs=(pl.BlockSpec(memory_space=pltpu.VMEM),) * 2,
        scratch_shapes=[pltpu.SemaphoreType.DMA((pieces,))],
    )(sector)


def rotate_of(gram, x_ref, e_ref):
    size = gram.shape[0]
    rows = lax.broadcasted_iota(jnp.int32, (size, size), 0)
    cols = lax.broadcasted_iota(jnp.int32, (size, size), 1)
    identity = (rows == cols).astype(jnp.float32)
    only = jnp.where(rows == cols, gram, 0.0)
    g_j = jnp.sum(only, axis=0, keepdims=True)
    g_i = jnp.sum(only, axis=1, keepdims=True)
    spread = g_j - g_i
    summed = g_j + g_i
    skew = gram * spread / (spread * spread + 2.0 * gram * gram + 0.01 * summed * summed)
    skew_parts = split(skew)
    square = dot3(skew_parts, skew_parts)
    whole = 0.25 * jnp.sum(skew * skew)
    paired = 0.03125 * jnp.sum(square * square) * 1.001
    reach = jnp.minimum(whole * whole, paired)
    steps = jnp.int32(0)
    for limit in REACHES:
        steps = steps + (reach > limit).astype(jnp.int32)
    fixes = 1 + (steps > 7).astype(jnp.int32) + 2 * (steps > 9).astype(jnp.int32)
    scale = 2.0 / (2.0 + jnp.sqrt(jnp.full((size, size), reach, jnp.float32)))
    residual = identity - scale * (identity - 0.25 * square)
    x_ref[...] = scale * (identity + residual)
    residual_parts = split(residual)
    e_ref[...] = dot3(residual_parts, residual_parts)

    def step(_, carry):
        e = split(e_ref[...])
        x = x_ref[...]
        x_ref[...] = x + dot3(x, e)
        e_ref[...] = dot3(e, e)
        return carry

    lax.fori_loop(0, jnp.maximum(steps - 1, 0), step, jnp.int32(0))
    x = x_ref[...]
    x_ref[...] = x + 0.5 * dot3(x, skew_parts)

    def fix(_, carry):
        x = x_ref[...]
        x_ref[...] = x + dot3(x, identity - (x - 0.5 * dot(skew, x)))
        return carry

    lax.fori_loop(0, fixes, fix, jnp.int32(0))
    return 2.0 * x_ref[...] - identity


def put_rotation(rotation_ref, gram, x_ref, e_ref, last_round):
    size = gram.shape[0]
    rotation = rotate_of(gram, x_ref, e_ref)
    rotation_ref[:size] = rotation
    if last_round:
        squares = jnp.sum(rotation * dot(gram, rotation), axis=0, keepdims=True)
        rotation_ref[size:] = jnp.broadcast_to(squares, (8, size))


def first_rotation(facts, own, other_y, half):
    size = 2 * half

    def body(f, own_ref, other_ref, rotation_ref, g_ref, x_ref, e_ref):
        total = own_ref[...] + other_ref[...]
        g_ref[:half, :half] = total[:half]
        g_ref[:half, half:] = total[half : 2 * half]
        g_ref[half:, :half] = total[half : 2 * half].T
        g_ref[half:, half:] = total[2 * half :]
        put_rotation(rotation_ref, g_ref[...], x_ref, e_ref, False)

    square = pltpu.VMEM((size, size), jnp.float32)
    return call(body, facts, [own, other_y], (shape(size, size),) * 2, [square] * 2)


def later_rotation(facts, parts, diagonals, half, last_round):
    size = 2 * half

    def body(f, *refs):
        own, other_y, other_x, other_xy, foreign, native = [r[...] for r in refs[:6]]
        rotation_ref, g_ref, x_ref, e_ref = refs[6:]
        cross = (own + other_y) + (other_x + other_xy)
        core = f[CORE] == 0
        g_ref[:half, :half] = jnp.where(core, foreign, native)
        g_ref[:half, half:] = cross
        g_ref[half:, :half] = cross.T
        g_ref[half:, half:] = jnp.where(core, native, foreign)
        put_rotation(rotation_ref, g_ref[...], x_ref, e_ref, last_round)

    square = pltpu.VMEM((size, size), jnp.float32)
    return call(
        body,
        facts,
        parts + diagonals,
        (shape(size + 8 if last_round else size, size), shape(size, size)),
        [square] * 2,
    )


def turned_gram(facts, gram, rotation, position):
    size = gram.shape[0]
    half = size // 2

    def body(f, gram_ref, rotation_ref, leave_ref, stay_ref):
        rotation = rotation_ref[...]
        turned = dot(gram_ref[...], rotation)
        upper = dot_tn(rotation[:, :half], turned[:, :half])
        lower = dot_tn(rotation[:, half:], turned[:, half:])
        lower_leaves = (f[position] == 0) & (f[FIRST] == 0)
        leave_ref[...] = jnp.where(lower_leaves, lower, upper)
        stay_ref[...] = jnp.where(lower_leaves, upper, lower)

    return call(body, facts, [gram, rotation], (shape(half, half),) * 2)


def two_packs(f, own, other):
    core = f[CORE] == 0
    return jnp.where(core, own, other), jnp.where(core, other, own)


def swapped(flag, matrix, axis):
    half = matrix.shape[axis] // 2
    a = lax.slice_in_dim(matrix, 0, half, axis=axis)
    b = lax.slice_in_dim(matrix, half, 2 * half, axis=axis)
    return jnp.where(flag, lax.concatenate([b, a], axis), matrix)


def blocks_of(f, got_a, got_b, low_0, up_1):
    even = f[EVEN] == 1
    return (
        jnp.where(even, got_b, got_a), low_0, up_1, jnp.where(even, got_a, got_b)
    )


def put_turned(f, refs, zero, one, half, at=0):
    a_ref, b_ref, nat_l_ref, nat_u_ref = refs[:4]
    even = f[EVEN] == 1
    rows = slice(at, at + zero.shape[0])
    to_left, to_right = zero[:, half:], one[:, :half]
    a_ref[rows] = jnp.where(even, to_right, to_left)
    b_ref[rows] = jnp.where(even, to_left, to_right)
    nat_l_ref[rows] = one[:, half:]
    nat_u_ref[rows] = zero[:, :half]
    if len(refs) > 4:
        refs[4][rows] = jnp.where(f[X] == 0, zero[:, :half], one[:, half:])


def turns_of(f, own_ref, other_ref):
    size = other_ref.shape[1]
    turn_0, turn_1 = two_packs(f, own_ref[:size], other_ref[:size])
    return swapped(f[FIRST] == 1, turn_0, 1), turn_1


def turn_rows(facts, rotation, rows_of, vector_rows, half, own):
    rows = rows_of.shape[0] // 2 if own else rows_of.shape[0]

    def body(f, rotation_ref, x_ref, stay_ref, leave_ref):
        zero = f[X] == (0 if own else 1)
        upper_leaves = jnp.where(zero, f[FIRST], 1) == 1
        turn = split(swapped(upper_leaves, rotation_ref[...], 1))
        here = pl.multiple_of(f[X] * rows, 8)
        out = dot3(x_ref[pl.ds(here, rows)] if own else x_ref[...], turn)
        stay_ref[:rows] = out[:, :half]
        leave_ref[:rows] = out[:, half:]
        if vector_rows:
            ids = f[VROW] + lax.broadcasted_iota(jnp.int32, (vector_rows, half), 0)
            cols = lax.broadcasted_iota(jnp.int32, (vector_rows, half), 1)
            position = jnp.where(zero, 0, 2)
            vectors = [
                (ids == f[LABEL + position + k] * half + cols).astype(jnp.float32)
                for k in range(2)
            ]
            out = dot3(lax.concatenate(vectors, 1), turn)
            stay_ref[rows:] = out[:, :half]
            leave_ref[rows:] = out[:, half:]

    return call(
        body, facts, [rotation, rows_of], (shape(rows + vector_rows, half),) * 2
    )


def turn(facts, packs, blocks, vectors, part, vector_rows, half, last_move):
    inputs = packs + blocks + vectors

    def body(f, own_ref, other_ref, *refs):
        turn_0, turn_1 = turns_of(f, own_ref, other_ref)
        turn_0, turn_1 = split(turn_0), split(turn_1)
        columns = [r[:part] for r in refs[:4]]
        if vectors:
            rows = blocks_of(f, *[r[...] for r in refs[4:8]])
        else:
            rows = [r[part:] for r in refs[:4]]
        outs = refs[len(inputs) - 2 :]
        for (up_0, low_0, up_1, low_1), at in ((columns, 0), (rows, part)):
            zero = dot3(lax.concatenate([up_0, low_0], 1), turn_0)
            one = dot3(lax.concatenate([up_1, low_1], 1), turn_1)
            if last_move:
                put_turned(f, outs, zero, one, half, at)
            else:
                put_turned(f, outs[4 if at else 0 :][:4], zero, one, half)

    if last_move:
        outs = (shape(part + vector_rows, half),) * 5
    else:
        outs = (shape(part, half),) * 4 + (shape(vector_rows, half),) * 4
    return call(body, facts, inputs, outs)


def put_cross(f, refs, zero, one):
    core = f[CORE] == 0
    refs[0][...] = jnp.where(core, zero, one)
    refs[1][...] = jnp.where(core, one, zero)


def first_cross_gram(facts, own, others, part, half):
    rows = own[0].shape[0]
    pieces = len(others)

    def body(f, *refs):
        own_refs = [[r] for r in refs[:3]]
        other_refs = [refs[3 + k : 3 + 3 * pieces : 3] for k in range(3)]
        up_0, low_0, up_1, low_1 = refs[5 + 3 * pieces :]

        def fill(target, sources):
            at = 0
            for ref in sources:
                target[at : at + ref.shape[0]] = ref[...]
                at += ref.shape[0]

        first, last = f[FIRST] == 1, f[LAST] == 1
        for x, near, far in ((0, own_refs, other_refs), (1, other_refs, own_refs)):
            here = f[X] == x

            @pl.when(here)
            def _():
                fill(up_1, near[0])
                fill(low_0, far[0])

            @pl.when(here & first)
            def _():
                fill(up_0, near[1])

            @pl.when(here & ~first)
            def _():
                fill(up_0, far[2])

            @pl.when(here & last)
            def _():
                fill(low_1, far[1])

            @pl.when(here & ~last)
            def _():
                fill(low_1, near[2])

        put_cross(
            f,
            refs[3 + 3 * pieces :],
            dot_tn(up_0[:part], low_0[:part]),
            dot_tn(up_1[:part], low_1[:part]),
        )

    outs = (shape(half, half),) * 2 + (shape(rows, half),) * 4
    return call(body, facts, own + sum(others, []), outs)


def cross_gram(facts, got, natives, part, half):
    rows = got[0].shape[0]

    def body(f, *refs):
        up_0, low_0, up_1, low_1 = blocks_of(f, *[r[...] for r in refs[:4]])
        put_cross(
            f,
            refs[4:],
            dot_tn(up_0[:part], low_0[:part]),
            dot_tn(up_1[:part], low_1[:part]),
        )
        refs[6][...] = up_0
        refs[7][...] = low_1

    outs = (shape(half, half),) * 2 + (shape(rows, half),) * 2
    return call(body, facts, got + natives, outs)


def give(facts, got, start, stop, half):
    def body(f, a_ref, b_ref, out_ref):
        mine = f[X] != f[EVEN]
        out_ref[...] = jnp.where(mine, a_ref[start:stop], b_ref[start:stop])

    return call(body, facts, got, shape(stop - start, half))


def final_turn(f, own_ref, other_ref, size):
    pack = jnp.where(f[CORE] == f[X], own_ref[...], other_ref[...])
    return split(swapped(f[X] == 1, pack[:size], 0)), pack[size : size + 1]


def final_product(moved, native, turned):
    return dot3(lax.concatenate([moved, native], 1), turned)


def put_rows(copies, sems, source, target, here, there, value):
    rows = value.shape[0]
    source[here : here + rows] = value
    copy = pltpu.make_async_copy(
        source.at[here : here + rows],
        target.at[pl.ds(pl.multiple_of(there, 8), rows)],
        sems.at[len(copies)],
    )
    copies.append(copy)
    copy.start()


def finish_call(body, facts, inputs, outputs, outs, rows, vector_rows, size):
    vmem = pl.BlockSpec(memory_space=pltpu.VMEM)
    hbm = pl.BlockSpec(memory_space=pl.ANY)
    first = 1 + len(inputs)
    return pl.pallas_call(
        body,
        out_shape=outs,
        in_specs=[pl.BlockSpec(memory_space=pltpu.SMEM)]
        + [vmem] * len(inputs)
        + [hbm] * len(outputs),
        out_specs=(hbm, hbm, vmem)[: len(outs)],
        input_output_aliases={first + k: k for k in range(len(outputs))},
        cost_estimate=pl.CostEstimate(flops=1, transcendentals=0, bytes_accessed=1),
        scratch_shapes=[
            pltpu.VMEM((rows, size), jnp.float32),
            pltpu.VMEM((vector_rows, size), jnp.float32),
            pltpu.SemaphoreType.DMA((4,)),
        ],
        compiler_params=pltpu.CompilerParams(vmem_limit_bytes=24 << 20),
    )(facts, *inputs, *outputs)


def finish_kept(facts, packs, blocks, native, got_top, part, half):
    size = 2 * half
    vector_rows = blocks[0].shape[0] - part
    top = got_top.shape[0]

    def body(f, own_ref, other_ref, *refs):
        x = f[X]
        turned, squares = final_turn(f, own_ref, other_ref, size)
        native_ref, top_ref, out_ref, vectors_ref, singular_ref, out, vectors, sems = (
            refs[4:]
        )
        copies = []

        def kept(rows):
            up_0, low_0, up_1, low_1 = [r[rows] for r in refs[:4]]
            return final_product(
                jnp.where(x == 0, up_0, low_1),
                jnp.where(x == 0, low_0, up_1),
                turned,
            )

        def put(*args):
            put_rows(copies, sems, *args)

        middle = part // 2
        put(out, out_ref, 0, x * part, kept(slice(0, middle)))
        put(out, out_ref, middle, x * part + middle, kept(slice(middle, part)))
        value = final_product(top_ref[...], native_ref[:top], turned)
        put(out, out_ref, part, (1 - x) * part, value)
        put(vectors, vectors_ref, 0, x * vector_rows, kept(slice(part, None)))
        singular_ref[...] = jnp.sqrt(jnp.maximum(squares, 0.0) + 1e-06)
        for copy in copies:
            copy.wait()

    outs = (shape(2 * part, size), shape(2 * vector_rows, size), shape(1, size))
    inputs = packs + blocks + [native, got_top]
    return finish_call(
        body, facts, inputs, [], outs, part + top, vector_rows, size
    )


def finish_rest(facts, packs, outputs, native, got_rest, part, half):
    size = 2 * half
    vector_rows = native.shape[0] - part
    rest = got_rest.shape[0] - vector_rows
    top = part - rest

    def body(f, own_ref, other_ref, native_ref, rest_ref, *refs):
        x = f[X]
        turned, _ = final_turn(f, own_ref, other_ref, size)
        out_ref, vectors_ref, out, vectors, sems = refs[2:]
        copies = []
        value = final_product(rest_ref[:rest], native_ref[top:part], turned)
        put_rows(copies, sems, out, out_ref, 0, (1 - x) * part + top, value)
        value = final_product(rest_ref[rest:], native_ref[part:], turned)
        put_rows(copies, sems, vectors, vectors_ref, 0, (1 - x) * vector_rows, value)
        for copy in copies:
            copy.wait()

    outs = (shape(2 * part, size), shape(2 * vector_rows, size))
    inputs = packs + [native, got_rest]
    return finish_call(
        body, facts, inputs, outputs, outs, rest, vector_rows, size
    )


def per_device(sector, block_label):
    local_rows, size = sector.shape
    half = size // 2
    part = local_rows // 2
    pairs = lax.axis_size("pair")
    row_count = lax.axis_size("row")
    vector_rows = pairs * size // row_count // 2
    pair_index = lax.axis_index("pair")
    row_index = lax.axis_index("row")
    x = pair_index % 2
    group = pair_index // 2
    core = row_index % 2

    def permute(block, route):
        moves = [
            (a * row_count + b, c * row_count + d) for (a, b), (c, d) in route
        ]
        return lax.ppermute(block, ("pair", "row"), moves)

    devices = [(p, r) for p in range(pairs) for r in range(row_count)]

    def exchange(block, over_pair, over_row):
        return permute(
            block, [((p ^ over_pair, r ^ over_row), (p, r)) for p, r in devices]
        )

    def shift(block, even_by):
        moves = []
        for p, r in devices:
            source = p - even_by if p % 2 == 0 else p + even_by
            if 0 <= source < pairs:
                moves.append(((source, r), (p, r)))
        return permute(block, moves)

    def swap(block, odd):
        moves = []
        for p, r in devices:
            other = p + 2 if p // 2 % 2 == odd else p - 2
            moves.append(((other if 0 <= other < pairs else p, r), (p, r)))
        return permute(block, moves)

    def pass_diagonal(block):
        moves = []
        for p, r in devices:
            other = p + 2 if r % 2 else p - 2
            inside = 0 <= other < pairs
            moves.append(((other, r ^ 1) if inside else (p, r), (p, r)))
        return permute(block, [((a, b), c) for (a, b), c in moves])

    def first_diagonal(block, leaves):
        moves = []
        for p, r in devices:
            c, even = r % 2, p - p % 2
            if leaves:
                source = even - 1 if c == 0 else even + 2
                if not 0 <= source < pairs:
                    source = even + c
            else:
                source = even + 1 - c
            moves.append(((source, r - c + p % 2), (p, r)))
        return permute(block, moves)

    def sum_rows(block):
        bit = 4
        while bit < row_count:
            block = block + exchange(block, 0, bit)
            bit *= 2
        return block

    names = jnp.arange(16, dtype=jnp.int32)
    facts = jnp.zeros((16,), jnp.int32)
    for name, value in (
        (X, x),
        (CORE, core),
        (FIRST, group == 0),
        (LAST, group == pairs // 2 - 1),
        (VROW, (row_index * 2 + x) * vector_rows),
        (EVEN, group % 2 == 0),
    ):
        facts = jnp.where(names == name, value.astype(jnp.int32), facts)
    labels = lax.dynamic_slice_in_dim(block_label, 4 * group, 4)
    facts = lax.dynamic_update_slice_in_dim(facts, labels, LABEL, 0)

    def together(*arrays):
        return lax.optimization_barrier(arrays)

    top_give, rest_give = give_rows(sector, part * 3 // 4)
    got_top = exchange(top_give, 1, 0)
    own = first_gram(sector, half)
    own = sum_rows(own + exchange(own, 0, 1))
    rotation, gram = first_rotation(facts, own, exchange(own, 0, 2), half)

    vectors = []
    for sweep_round in range(ROUNDS - 1):
        last_move = sweep_round == ROUNDS - 2
        if sweep_round == 0:
            other_rotation = exchange(rotation, 1, 0)
            stay, leave = turn_rows(facts, rotation, sector, vector_rows, half, True)
            leave, rest_give = together(leave, rest_give)
            got_rest = exchange(rest_give, 1, 0)
            own_rows = [stay, leave, shift(leave, -2)]
            other_rows = []
            for got, below in ((got_top, 0), (got_rest, vector_rows)):
                stay, leave = turn_rows(facts, other_rotation, got, below, half, False)
                other_rows.append([stay, leave, shift(leave, 2)])
            leave, stay = turned_gram(facts, gram, rotation, X)
            diagonals = [first_diagonal(leave, True), first_diagonal(stay, False)]
            *grams, up_0, nat_l, nat_u, low_1 = first_cross_gram(
                facts, own_rows, other_rows, part, half
            )
        else:
            packs = [rotation, exchange(rotation, 0, 1)]
            leave_a, leave_b, nat_l, nat_u, *vectors = turn(
                facts, packs, blocks, vectors, part, vector_rows, half, last_move
            )
            got = [swap(leave_a, 0), swap(leave_b, 1)]
            leave, stay = turned_gram(facts, gram, rotation, CORE)
            diagonals = [pass_diagonal(leave), exchange(stay, 0, 1)]
            if last_move:
                native = exchange(vectors.pop(), 1, 0)
                top = part // 2
                top_give = give(facts, got, 0, top, half)
                *got, top_give, diagonals[0], diagonals[1] = together(
                    *got, top_give, *diagonals
                )
                got_top = exchange(top_give, 1, 0)
            else:
                vectors[0], vectors[1], diagonals[1] = together(
                    vectors[0], vectors[1], diagonals[1]
                )
            *grams, up_0, low_1 = cross_gram(facts, got, [nat_l, nat_u], part, half)
        blocks = [up_0, nat_l, nat_u, low_1]
        if last_move:
            grams[1], native = together(grams[1], native)
        elif sweep_round == 0:
            grams[1], *diagonals = together(grams[1], *diagonals)
        else:
            vector_a, vector_b, *kept = vectors
            grams[1], vector_a, vector_b, diagonals[0] = together(
                grams[1], swap(vector_a, 0), swap(vector_b, 1), diagonals[0]
            )
            vectors = [vector_a, vector_b] + kept
        own = sum_rows(grams[0] + exchange(grams[1], 0, 1))
        parts = [own, exchange(own, 0, 2), exchange(own, 1, 0), exchange(own, 1, 2)]
        if last_move:
            rest_give = give(facts, got, top, part + vector_rows, half)
            *parts, got_top, rest_give = together(*parts, got_top, rest_give)
            got_rest = exchange(rest_give, 1, 0)
        rotation, gram = later_rotation(facts, parts, diagonals, half, last_move)
    packs = [rotation, exchange(rotation, 0, 1)]
    *outputs, singular = finish_kept(
        facts, packs, blocks, native, got_top, part, half
    )
    rotated, vectors_out = finish_rest(
        facts, packs, outputs, native, got_rest, part, half
    )
    return rotated, vectors_out, singular.reshape(size)


def solution(mesh):
    placed = (P("row", "pair"), P())
    return jax.shard_map(
        per_device,
        mesh=mesh,
        in_specs=placed,
        out_specs=(P("row", "pair"), P("row", "pair"), P("pair")),
        check_vma=False,
    )
```

```python
import jax
import jax.numpy as jnp
from jax import lax
from jax.experimental import pallas as pl
from jax.experimental.pallas import tpu as pltpu
from jax.sharding import PartitionSpec as P

ROUNDS = 4
NEWTON = 16

highest = lax.Precision.HIGHEST

TARGET = 2.0**-12
REACHES = [
    (2.0 / (TARGET ** -(2.0**-j) - 1.0)) ** 2 for j in range(NEWTON)
]

X, CORE, FIRST, LAST, VROW, LABEL, EVEN = 0, 1, 2, 3, 4, 5, 9


def dot(a, b, precision=highest):
    return lax.dot_general(
        a, b, (((1,), (0,)), ((), ())), precision=precision,
        preferred_element_type=jnp.float32,
    )


def split(a):
    high = a.astype(jnp.bfloat16)
    return high, (a - high.astype(jnp.float32)).astype(jnp.bfloat16)


def dot3(a, b):
    a_high, a_low = a if isinstance(a, tuple) else split(a)
    b_high, b_low = b if isinstance(b, tuple) else split(b)
    small = dot(a_high, b_low, None) + dot(a_low, b_high, None)
    return dot(a_high, b_high, None) + small


def dot_tn(a, b):
    return lax.dot_general(
        a, b, (((0,), (0,)), ((), ())), precision=highest,
        preferred_element_type=jnp.float32,
    )


def shape(*dims):
    return jax.ShapeDtypeStruct(dims, jnp.float32)


def call(body, facts, inputs, outs, scratch=(), limit=24):
    return pl.pallas_call(
        body,
        out_shape=outs,
        in_specs=[pl.BlockSpec(memory_space=pltpu.SMEM)]
        + [pl.BlockSpec(memory_space=pltpu.VMEM)] * len(inputs),
        out_specs=jax.tree.map(
            lambda _: pl.BlockSpec(memory_space=pltpu.VMEM), outs
        ),
        scratch_shapes=list(scratch),
        compiler_params=pltpu.CompilerParams(vmem_limit_bytes=limit << 20),
    )(facts, *inputs)


def first_gram(sector, half):
    def body(x_ref, out_ref):
        x = x_ref[...]
        g = dot_tn(x, x)
        out_ref[:half] = g[:half, :half]
        out_ref[half : 2 * half] = g[:half, half:]
        out_ref[2 * half :] = g[half:, half:]

    vmem = pl.BlockSpec(memory_space=pltpu.VMEM)
    return pl.pallas_call(
        body,
        out_shape=shape(3 * half, half),
        in_specs=[vmem],
        out_specs=vmem,
        compiler_params=pltpu.CompilerParams(vmem_limit_bytes=24 << 20),
    )(sector)


def give_rows(sector, top, pieces=8):
    rows, width = sector.shape
    part = rows // 2
    step = part // pieces

    def body(x_ref, top_ref, rest_ref, sems):
        start = (1 - lax.axis_index("pair") % 2) * part
        copies = []
        for k in range(pieces):
            at = k * step
            target, here = (top_ref, at) if at < top else (rest_ref, at - top)
            source = x_ref.at[pl.ds(pl.multiple_of(start + at, 8), step)]
            copies.append(
                pltpu.make_async_copy(
                    source, target.at[here : here + step], sems.at[k]
                )
            )
            copies[-1].start()
        for copy in copies:
            copy.wait()

    return pl.pallas_call(
        body,
        out_shape=(shape(top, width), shape(part - top, width)),
        in_specs=[pl.BlockSpec(memory_space=pl.ANY)],
        out_specs=(pl.BlockSpec(memory_space=pltpu.VMEM),) * 2,
        scratch_shapes=[pltpu.SemaphoreType.DMA((pieces,))],
    )(sector)


def rotate_of(gram, x_ref, e_ref):
    size = gram.shape[0]
    rows = lax.broadcasted_iota(jnp.int32, (size, size), 0)
    cols = lax.broadcasted_iota(jnp.int32, (size, size), 1)
    identity = (rows == cols).astype(jnp.float32)
    only = jnp.where(rows == cols, gram, 0.0)
    g_j = jnp.sum(only, axis=0, keepdims=True)
    g_i = jnp.sum(only, axis=1, keepdims=True)
    spread = g_j - g_i
    summed = g_j + g_i
    skew = gram * spread / (spread * spread + 2.0 * gram * gram + 0.01 * summed * summed)
    skew_parts = split(skew)
    square = dot3(skew_parts, skew_parts)
    whole = 0.25 * jnp.sum(skew * skew)
    paired = 0.03125 * jnp.sum(square * square) * 1.001
    reach = jnp.minimum(whole * whole, paired)
    steps = jnp.int32(0)
    for limit in REACHES:
        steps = steps + (reach > limit).astype(jnp.int32)
    fixes = 1 + (steps > 7).astype(jnp.int32) + 2 * (steps > 9).astype(jnp.int32)
    scale = 2.0 / (2.0 + jnp.sqrt(jnp.full((size, size), reach, jnp.float32)))
    residual = identity - scale * (identity - 0.25 * square)
    x_ref[...] = scale * (identity + residual)
    residual_parts = split(residual)
    e_ref[...] = dot3(residual_parts, residual_parts)

    def step(_, carry):
        e = split(e_ref[...])
        x = x_ref[...]
        x_ref[...] = x + dot3(x, e)
        e_ref[...] = dot3(e, e)
        return carry

    lax.fori_loop(0, jnp.maximum(steps - 1, 0), step, jnp.int32(0))
    x = x_ref[...]
    x_ref[...] = x + 0.5 * dot3(x, skew_parts)

    def fix(_, carry):
        x = x_ref[...]
        x_ref[...] = x + dot3(x, identity - (x - 0.5 * dot(skew, x)))
        return carry

    lax.fori_loop(0, fixes, fix, jnp.int32(0))
    return 2.0 * x_ref[...] - identity


def put_rotation(rotation_ref, gram, x_ref, e_ref, last_round):
    size = gram.shape[0]
    rotation = rotate_of(gram, x_ref, e_ref)
    rotation_ref[:size] = rotation
    if last_round:
        squares = jnp.sum(rotation * dot(gram, rotation), axis=0, keepdims=True)
        rotation_ref[size:] = jnp.broadcast_to(squares, (8, size))


def first_rotation(facts, own, other_y, half):
    size = 2 * half

    def body(f, own_ref, other_ref, rotation_ref, g_ref, x_ref, e_ref):
        total = own_ref[...] + other_ref[...]
        g_ref[:half, :half] = total[:half]
        g_ref[:half, half:] = total[half : 2 * half]
        g_ref[half:, :half] = total[half : 2 * half].T
        g_ref[half:, half:] = total[2 * half :]
        put_rotation(rotation_ref, g_ref[...], x_ref, e_ref, False)

    square = pltpu.VMEM((size, size), jnp.float32)
    return call(body, facts, [own, other_y], (shape(size, size),) * 2, [square] * 2)


def later_rotation(facts, parts, diagonals, half, last_round):
    size = 2 * half

    def body(f, *refs):
        own, other_y, other_x, other_xy, foreign, native = [r[...] for r in refs[:6]]
        rotation_ref, g_ref, x_ref, e_ref = refs[6:]
        cross = (own + other_y) + (other_x + other_xy)
        core = f[CORE] == 0
        g_ref[:half, :half] = jnp.where(core, foreign, native)
        g_ref[:half, half:] = cross
        g_ref[half:, :half] = cross.T
        g_ref[half:, half:] = jnp.where(core, native, foreign)
        put_rotation(rotation_ref, g_ref[...], x_ref, e_ref, last_round)

    square = pltpu.VMEM((size, size), jnp.float32)
    return call(
        body,
        facts,
        parts + diagonals,
        (shape(size + 8 if last_round else size, size), shape(size, size)),
        [square] * 2,
    )


def turned_gram(facts, gram, rotation, position):
    size = gram.shape[0]
    half = size // 2

    def body(f, gram_ref, rotation_ref, leave_ref, stay_ref):
        rotation = rotation_ref[...]
        turned = dot(gram_ref[...], rotation)
        upper = dot_tn(rotation[:, :half], turned[:, :half])
        lower = dot_tn(rotation[:, half:], turned[:, half:])
        lower_leaves = (f[position] == 0) & (f[FIRST] == 0)
        leave_ref[...] = jnp.where(lower_leaves, lower, upper)
        stay_ref[...] = jnp.where(lower_leaves, upper, lower)

    return call(body, facts, [gram, rotation], (shape(half, half),) * 2)


def swapped(flag, matrix, axis):
    half = matrix.shape[axis] // 2
    a = lax.slice_in_dim(matrix, 0, half, axis=axis)
    b = lax.slice_in_dim(matrix, half, 2 * half, axis=axis)
    return jnp.where(flag, lax.concatenate([b, a], axis), matrix)


def turn_rows(facts, rotation, rows_of, vector_rows, half, own):
    rows = rows_of.shape[0] // 2 if own else rows_of.shape[0]

    def body(f, rotation_ref, x_ref, stay_ref, leave_ref):
        zero = f[X] == (0 if own else 1)
        upper_leaves = jnp.where(zero, f[FIRST], 1) == 1
        turn = split(swapped(upper_leaves, rotation_ref[...], 1))
        here = pl.multiple_of(f[X] * rows, 8)
        out = dot3(x_ref[pl.ds(here, rows)] if own else x_ref[...], turn)
        stay_ref[:rows] = out[:, :half]
        leave_ref[:rows] = out[:, half:]
        if vector_rows:
            ids = f[VROW] + lax.broadcasted_iota(jnp.int32, (vector_rows, half), 0)
            cols = lax.broadcasted_iota(jnp.int32, (vector_rows, half), 1)
            position = jnp.where(zero, 0, 2)
            vectors = [
                (ids == f[LABEL + position + k] * half + cols).astype(jnp.float32)
                for k in range(2)
            ]
            out = dot3(lax.concatenate(vectors, 1), turn)
            stay_ref[rows:] = out[:, :half]
            leave_ref[rows:] = out[:, half:]

    return call(
        body, facts, [rotation, rows_of], (shape(rows + vector_rows, half),) * 2
    )


def turn(facts, rotation, blocks, own, own_stay=None):
    rows, half = blocks[0].shape
    size = 2 * half
    extra = [] if own_stay is None else [own_stay]

    def body(f, rotation_ref, *refs):
        up_0, low_0, up_1, low_1 = [r[...] for r in refs[:4]]
        zero = f[CORE] == (0 if own else 1)
        upper_leaves = jnp.where(zero, f[FIRST], 1) == 1
        turned = swapped(upper_leaves, rotation_ref[:size], 1)
        columns = lax.concatenate(
            [jnp.where(zero, up_0, up_1), jnp.where(zero, low_0, low_1)], 1
        )
        out = dot3(columns, turned)
        outs = refs[4 + len(extra) :]
        outs[0][...] = out[:, :half]
        outs[1][...] = out[:, half:]
        if extra:
            outs[2][...] = jnp.where(f[CORE] == f[X], refs[4][...], out[:, :half])

    return call(
        body, facts, [rotation] + blocks + extra,
        (shape(rows, half),) * (2 + len(extra)),
    )


def put_cross(f, refs, zero, one):
    core = f[CORE] == 0
    refs[0][...] = jnp.where(core, zero, one)
    refs[1][...] = jnp.where(core, one, zero)


def cross_gram(facts, own, others, position, part, half):
    rows = own[0].shape[0]
    pieces = len(others)

    def body(f, *refs):
        own_refs = [[r] for r in refs[:3]]
        other_refs = [refs[3 + k : 3 + 3 * pieces : 3] for k in range(3)]
        up_0, low_0, up_1, low_1 = refs[5 + 3 * pieces :]

        def fill(target, sources):
            at = 0
            for ref in sources:
                target[at : at + ref.shape[0]] = ref[...]
                at += ref.shape[0]

        first, last = f[FIRST] == 1, f[LAST] == 1
        for x, near, far in ((0, own_refs, other_refs), (1, other_refs, own_refs)):
            here = f[position] == x

            @pl.when(here)
            def _():
                fill(up_1, near[0])
                fill(low_0, far[0])

            @pl.when(here & first)
            def _():
                fill(up_0, near[1])

            @pl.when(here & ~first)
            def _():
                fill(up_0, far[2])

            @pl.when(here & last)
            def _():
                fill(low_1, far[1])

            @pl.when(here & ~last)
            def _():
                fill(low_1, near[2])

        put_cross(
            f,
            refs[3 + 3 * pieces :],
            dot_tn(up_0[:part], low_0[:part]),
            dot_tn(up_1[:part], low_1[:part]),
        )

    outs = (shape(half, half),) * 2 + (shape(rows, half),) * 4
    return call(body, facts, own + sum(others, []), outs)


def give(facts, blocks, start, stop, half):
    def body(f, up_0_ref, low_1_ref, out_ref):
        out_ref[...] = jnp.where(
            f[X] == 0, low_1_ref[start:stop], up_0_ref[start:stop]
        )

    return call(
        body, facts, [blocks[0], blocks[3]], shape(stop - start, half)
    )


def final_turn(f, own_ref, other_ref, size):
    pack = jnp.where(f[CORE] == f[X], own_ref[...], other_ref[...])
    return split(swapped(f[X] == 1, pack[:size], 0)), pack[size : size + 1]


def final_product(moved, native, turned):
    return dot3(lax.concatenate([moved, native], 1), turned)


def put_rows(copies, sems, source, target, here, there, value):
    rows = value.shape[0]
    source[here : here + rows] = value
    copy = pltpu.make_async_copy(
        source.at[here : here + rows],
        target.at[pl.ds(pl.multiple_of(there, 8), rows)],
        sems.at[len(copies)],
    )
    copies.append(copy)
    copy.start()


def finish_call(body, facts, inputs, outputs, outs, rows, vector_rows, size):
    vmem = pl.BlockSpec(memory_space=pltpu.VMEM)
    hbm = pl.BlockSpec(memory_space=pl.ANY)
    first = 1 + len(inputs)
    return pl.pallas_call(
        body,
        out_shape=outs,
        in_specs=[pl.BlockSpec(memory_space=pltpu.SMEM)]
        + [vmem] * len(inputs)
        + [hbm] * len(outputs),
        out_specs=(hbm, hbm, vmem)[: len(outs)],
        input_output_aliases={first + k: k for k in range(len(outputs))},
        cost_estimate=pl.CostEstimate(flops=1, transcendentals=0, bytes_accessed=1),
        scratch_shapes=[
            pltpu.VMEM((rows, size), jnp.float32),
            pltpu.VMEM((vector_rows, size), jnp.float32),
            pltpu.SemaphoreType.DMA((4,)),
        ],
        compiler_params=pltpu.CompilerParams(vmem_limit_bytes=24 << 20),
    )(facts, *inputs, *outputs)


def finish_kept(facts, packs, blocks, native, got_top, part, half):
    size = 2 * half
    vector_rows = blocks[0].shape[0] - part
    top = got_top.shape[0]

    def body(f, own_ref, other_ref, *refs):
        x = f[X]
        turned, squares = final_turn(f, own_ref, other_ref, size)
        native_ref, top_ref, out_ref, vectors_ref, singular_ref, out, vectors, sems = (
            refs[4:]
        )
        copies = []

        def kept(rows):
            up_0, low_0, up_1, low_1 = [r[rows] for r in refs[:4]]
            return final_product(
                jnp.where(x == 0, up_0, low_1),
                jnp.where(x == 0, low_0, up_1),
                turned,
            )

        def put(*args):
            put_rows(copies, sems, *args)

        middle = part // 2
        put(out, out_ref, 0, x * part, kept(slice(0, middle)))
        put(out, out_ref, middle, x * part + middle, kept(slice(middle, part)))
        value = final_product(top_ref[...], native_ref[:top], turned)
        put(out, out_ref, part, (1 - x) * part, value)
        put(vectors, vectors_ref, 0, x * vector_rows, kept(slice(part, None)))
        singular_ref[...] = jnp.sqrt(jnp.maximum(squares, 0.0) + 1e-06)
        for copy in copies:
            copy.wait()

    outs = (shape(2 * part, size), shape(2 * vector_rows, size), shape(1, size))
    inputs = packs + blocks + [native, got_top]
    return finish_call(
        body, facts, inputs, [], outs, part + top, vector_rows, size
    )


def finish_rest(facts, packs, outputs, native, got_rest, part, half):
    size = 2 * half
    vector_rows = native.shape[0] - part
    rest = got_rest.shape[0] - vector_rows
    top = part - rest

    def body(f, own_ref, other_ref, native_ref, rest_ref, *refs):
        x = f[X]
        turned, _ = final_turn(f, own_ref, other_ref, size)
        out_ref, vectors_ref, out, vectors, sems = refs[2:]
        copies = []
        value = final_product(rest_ref[:rest], native_ref[top:part], turned)
        put_rows(copies, sems, out, out_ref, 0, (1 - x) * part + top, value)
        value = final_product(rest_ref[rest:], native_ref[part:], turned)
        put_rows(copies, sems, vectors, vectors_ref, 0, (1 - x) * vector_rows, value)
        for copy in copies:
            copy.wait()

    outs = (shape(2 * part, size), shape(2 * vector_rows, size))
    inputs = packs + [native, got_rest]
    return finish_call(
        body, facts, inputs, outputs, outs, rest, vector_rows, size
    )


def per_device(sector, block_label):
    local_rows, size = sector.shape
    half = size // 2
    part = local_rows // 2
    pairs = lax.axis_size("pair")
    row_count = lax.axis_size("row")
    vector_rows = pairs * size // row_count // 2
    pair_index = lax.axis_index("pair")
    row_index = lax.axis_index("row")
    x = pair_index % 2
    group = pair_index // 2
    core = row_index % 2

    def permute(block, route):
        moves = [
            (a * row_count + b, c * row_count + d) for (a, b), (c, d) in route
        ]
        return lax.ppermute(block, ("pair", "row"), moves)

    devices = [(p, r) for p in range(pairs) for r in range(row_count)]

    def exchange(block, over_pair, over_row):
        return permute(
            block, [((p ^ over_pair, r ^ over_row), (p, r)) for p, r in devices]
        )

    def shift(block, leftward):
        moves = []
        for p, r in devices:
            source = p + 2 if leftward(p, r) else p - 2
            if 0 <= source < pairs:
                moves.append(((source, r), (p, r)))
        return permute(block, moves)

    def pass_diagonal(block):
        moves = []
        for p, r in devices:
            other = p + 2 if r % 2 else p - 2
            inside = 0 <= other < pairs
            moves.append(((other, r ^ 1) if inside else (p, r), (p, r)))
        return permute(block, [((a, b), c) for (a, b), c in moves])

    def first_diagonal(block, leaves):
        moves = []
        for p, r in devices:
            c, even = r % 2, p - p % 2
            if leaves:
                source = even - 1 if c == 0 else even + 2
                if not 0 <= source < pairs:
                    source = even + c
            else:
                source = even + 1 - c
            moves.append(((source, r - c + p % 2), (p, r)))
        return permute(block, moves)

    def sum_rows(block):
        bit = 4
        while bit < row_count:
            block = block + exchange(block, 0, bit)
            bit *= 2
        return block

    names = jnp.arange(16, dtype=jnp.int32)
    facts = jnp.zeros((16,), jnp.int32)
    for name, value in (
        (X, x),
        (CORE, core),
        (FIRST, group == 0),
        (LAST, group == pairs // 2 - 1),
        (VROW, (row_index * 2 + x) * vector_rows),
        (EVEN, group % 2 == 0),
    ):
        facts = jnp.where(names == name, value.astype(jnp.int32), facts)
    labels = lax.dynamic_slice_in_dim(block_label, 4 * group, 4)
    facts = lax.dynamic_update_slice_in_dim(facts, labels, LABEL, 0)

    def together(*arrays):
        return lax.optimization_barrier(arrays)

    top_give, rest_give = give_rows(sector, part * 3 // 4)
    got_top = exchange(top_give, 1, 0)
    own = first_gram(sector, half)
    own = sum_rows(own + exchange(own, 0, 1))
    rotation, gram = first_rotation(facts, own, exchange(own, 0, 2), half)

    for sweep_round in range(ROUNDS - 1):
        last_move = sweep_round == ROUNDS - 2
        if sweep_round == 0:
            other_rotation = exchange(rotation, 1, 0)
            stay, leave = turn_rows(facts, rotation, sector, vector_rows, half, True)
            leave, rest_give = together(leave, rest_give)
            got_rest = exchange(rest_give, 1, 0)
            own = [stay, leave, shift(leave, lambda p, r: p % 2 == 0)]
            others = []
            for got, below in ((got_top, 0), (got_rest, vector_rows)):
                stay, leave = turn_rows(facts, other_rotation, got, below, half, False)
                others.append([stay, leave, shift(leave, lambda p, r: p % 2 == 1)])
            leave, stay = turned_gram(facts, gram, rotation, X)
            diagonals = [first_diagonal(leave, True), first_diagonal(stay, False)]
            *grams, up_0, low_0, up_1, low_1 = cross_gram(
                facts, own, others, X, part, half
            )
        else:
            other_rotation = exchange(rotation, 0, 1)
            stay, leave = turn(facts, rotation, blocks, True)
            own = [stay, leave, shift(leave, lambda p, r: r % 2 == 0)]
            stay, leave, *native = turn(
                facts, other_rotation, blocks, False, stay if last_move else None
            )
            others = [[stay, leave, shift(leave, lambda p, r: r % 2 == 1)]]
            leave, stay = turned_gram(facts, gram, rotation, CORE)
            diagonals = [pass_diagonal(leave), exchange(stay, 0, 1)]
            if last_move:
                native = exchange(native[0], 1, 0)
            *grams, up_0, low_0, up_1, low_1 = cross_gram(
                facts, own, others, CORE, part, half
            )
        blocks = [up_0, low_0, up_1, low_1]
        grams[1], *diagonals = together(grams[1], *diagonals)
        own = sum_rows(grams[0] + exchange(grams[1], 0, 1))
        if last_move:
            top = part // 2
            top_give = give(facts, blocks, 0, top, half)
            own, native, top_give = together(own, native, top_give)
            got_top = exchange(top_give, 1, 0)
        parts = [own, exchange(own, 0, 2), exchange(own, 1, 0), exchange(own, 1, 2)]
        if last_move:
            rest_give = give(facts, blocks, top, part + vector_rows, half)
            *parts, got_top, rest_give = together(*parts, got_top, rest_give)
            got_rest = exchange(rest_give, 1, 0)
        rotation, gram = later_rotation(facts, parts, diagonals, half, last_move)
    packs = [rotation, exchange(rotation, 0, 1)]
    *outputs, singular = finish_kept(
        facts, packs, blocks, native, got_top, part, half
    )
    rotated, vectors_out = finish_rest(
        facts, packs, outputs, native, got_rest, part, half
    )
    return rotated, vectors_out, singular.reshape(size)


def solution(mesh):
    placed = (P("row", "pair"), P())
    return jax.shard_map(
        per_device,
        mesh=mesh,
        in_specs=placed,
        out_specs=(P("row", "pair"), P("row", "pair"), P("pair")),
        check_vma=False,
    )
```

```python
import jax
import jax.numpy as jnp
from jax import lax
from jax.experimental import pallas as pl
from jax.experimental.pallas import tpu as pltpu
from jax.sharding import PartitionSpec as P

ROUNDS = 4
NEWTON = 16

highest = lax.Precision.HIGHEST

TARGET = 2.0**-12
REACHES = [
    (2.0 / (TARGET ** -(2.0**-j) - 1.0)) ** 2 for j in range(NEWTON)
]

X, CORE, FIRST, LAST, VROW, LABEL, EVEN = 0, 1, 2, 3, 4, 5, 9


def dot(a, b, precision=highest):
    return lax.dot_general(
        a, b, (((1,), (0,)), ((), ())), precision=precision,
        preferred_element_type=jnp.float32,
    )


def split(a):
    high = a.astype(jnp.bfloat16)
    return high, (a - high.astype(jnp.float32)).astype(jnp.bfloat16)


def dot3(a, b):
    a_high, a_low = a if isinstance(a, tuple) else split(a)
    b_high, b_low = b if isinstance(b, tuple) else split(b)
    small = dot(a_high, b_low, None) + dot(a_low, b_high, None)
    return dot(a_high, b_high, None) + small


def dot_tn(a, b):
    return lax.dot_general(
        a, b, (((0,), (0,)), ((), ())), precision=highest,
        preferred_element_type=jnp.float32,
    )


def shape(*dims):
    return jax.ShapeDtypeStruct(dims, jnp.float32)


def call(body, facts, inputs, outs, scratch=(), limit=24):
    return pl.pallas_call(
        body,
        out_shape=outs,
        in_specs=[pl.BlockSpec(memory_space=pltpu.SMEM)]
        + [pl.BlockSpec(memory_space=pltpu.VMEM)] * len(inputs),
        out_specs=jax.tree.map(
            lambda _: pl.BlockSpec(memory_space=pltpu.VMEM), outs
        ),
        scratch_shapes=list(scratch),
        compiler_params=pltpu.CompilerParams(vmem_limit_bytes=limit << 20),
    )(facts, *inputs)


def first_gram(sector, half):
    def body(x_ref, out_ref):
        x = x_ref[...]
        g = dot_tn(x, x)
        out_ref[:half] = g[:half, :half]
        out_ref[half : 2 * half] = g[:half, half:]
        out_ref[2 * half :] = g[half:, half:]

    vmem = pl.BlockSpec(memory_space=pltpu.VMEM)
    return pl.pallas_call(
        body,
        out_shape=shape(3 * half, half),
        in_specs=[vmem],
        out_specs=vmem,
        compiler_params=pltpu.CompilerParams(vmem_limit_bytes=24 << 20),
    )(sector)


def give_rows(sector, top, pieces=8):
    rows, width = sector.shape
    part = rows // 2
    step = part // pieces

    def body(x_ref, top_ref, rest_ref, sems):
        start = (1 - lax.axis_index("pair") % 2) * part
        copies = []
        for k in range(pieces):
            at = k * step
            target, here = (top_ref, at) if at < top else (rest_ref, at - top)
            source = x_ref.at[pl.ds(pl.multiple_of(start + at, 8), step)]
            copies.append(
                pltpu.make_async_copy(
                    source, target.at[here : here + step], sems.at[k]
                )
            )
            copies[-1].start()
        for copy in copies:
            copy.wait()

    return pl.pallas_call(
        body,
        out_shape=(shape(top, width), shape(part - top, width)),
        in_specs=[pl.BlockSpec(memory_space=pl.ANY)],
        out_specs=(pl.BlockSpec(memory_space=pltpu.VMEM),) * 2,
        scratch_shapes=[pltpu.SemaphoreType.DMA((pieces,))],
    )(sector)


def rotate_of(gram, x_ref, e_ref):
    size = gram.shape[0]
    rows = lax.broadcasted_iota(jnp.int32, (size, size), 0)
    cols = lax.broadcasted_iota(jnp.int32, (size, size), 1)
    identity = (rows == cols).astype(jnp.float32)
    only = jnp.where(rows == cols, gram, 0.0)
    g_j = jnp.sum(only, axis=0, keepdims=True)
    g_i = jnp.sum(only, axis=1, keepdims=True)
    spread = g_j - g_i
    summed = g_j + g_i
    skew = gram * spread / (spread * spread + 2.0 * gram * gram + 0.01 * summed * summed)
    skew_parts = split(skew)
    square = dot3(skew_parts, skew_parts)
    whole = 0.25 * jnp.sum(skew * skew)
    paired = 0.03125 * jnp.sum(square * square) * 1.001
    reach = jnp.minimum(whole * whole, paired)
    steps = jnp.int32(0)
    for limit in REACHES:
        steps = steps + (reach > limit).astype(jnp.int32)
    fixes = 1 + (steps > 7).astype(jnp.int32) + 2 * (steps > 9).astype(jnp.int32)
    scale = 2.0 / (2.0 + jnp.sqrt(jnp.full((size, size), reach, jnp.float32)))
    residual = identity - scale * (identity - 0.25 * square)
    x_ref[...] = scale * (identity + residual)
    residual_parts = split(residual)
    e_ref[...] = dot3(residual_parts, residual_parts)

    def step(_, carry):
        e = split(e_ref[...])
        x = x_ref[...]
        x_ref[...] = x + dot3(x, e)
        e_ref[...] = dot3(e, e)
        return carry

    lax.fori_loop(0, jnp.maximum(steps - 1, 0), step, jnp.int32(0))
    x = x_ref[...]
    x_ref[...] = x + 0.5 * dot3(x, skew_parts)

    def fix(_, carry):
        x = x_ref[...]
        x_ref[...] = x + dot3(x, identity - (x - 0.5 * dot(skew, x)))
        return carry

    lax.fori_loop(0, fixes, fix, jnp.int32(0))
    return 2.0 * x_ref[...] - identity


def put_rotation(rotation_ref, gram, x_ref, e_ref, last_round):
    size = gram.shape[0]
    rotation = rotate_of(gram, x_ref, e_ref)
    rotation_ref[:size] = rotation
    if last_round:
        squares = jnp.sum(rotation * dot(gram, rotation), axis=0, keepdims=True)
        rotation_ref[size:] = jnp.broadcast_to(squares, (8, size))


def first_rotation(facts, own, other_y, half):
    size = 2 * half

    def body(f, own_ref, other_ref, rotation_ref, g_ref, x_ref, e_ref):
        total = own_ref[...] + other_ref[...]
        g_ref[:half, :half] = total[:half]
        g_ref[:half, half:] = total[half : 2 * half]
        g_ref[half:, :half] = total[half : 2 * half].T
        g_ref[half:, half:] = total[2 * half :]
        put_rotation(rotation_ref, g_ref[...], x_ref, e_ref, False)

    square = pltpu.VMEM((size, size), jnp.float32)
    return call(body, facts, [own, other_y], (shape(size, size),) * 2, [square] * 2)


def later_rotation(facts, parts, diagonals, half, last_round):
    size = 2 * half

    def body(f, *refs):
        own, other_y, other_x, other_xy, foreign, native = [r[...] for r in refs[:6]]
        rotation_ref, g_ref, x_ref, e_ref = refs[6:]
        cross = (own + other_y) + (other_x + other_xy)
        core = f[CORE] == 0
        g_ref[:half, :half] = jnp.where(core, foreign, native)
        g_ref[:half, half:] = cross
        g_ref[half:, :half] = cross.T
        g_ref[half:, half:] = jnp.where(core, native, foreign)
        put_rotation(rotation_ref, g_ref[...], x_ref, e_ref, last_round)

    square = pltpu.VMEM((size, size), jnp.float32)
    return call(
        body,
        facts,
        parts + diagonals,
        (shape(size + 8 if last_round else size, size), shape(size, size)),
        [square] * 2,
    )


def turned_gram(facts, gram, rotation, position):
    size = gram.shape[0]
    half = size // 2

    def body(f, gram_ref, rotation_ref, leave_ref, stay_ref):
        rotation = rotation_ref[...]
        turned = dot(gram_ref[...], rotation)
        upper = dot_tn(rotation[:, :half], turned[:, :half])
        lower = dot_tn(rotation[:, half:], turned[:, half:])
        lower_leaves = (f[position] == 0) & (f[FIRST] == 0)
        leave_ref[...] = jnp.where(lower_leaves, lower, upper)
        stay_ref[...] = jnp.where(lower_leaves, upper, lower)

    return call(body, facts, [gram, rotation], (shape(half, half),) * 2)


def swapped(flag, matrix, axis):
    half = matrix.shape[axis] // 2
    a = lax.slice_in_dim(matrix, 0, half, axis=axis)
    b = lax.slice_in_dim(matrix, half, 2 * half, axis=axis)
    return jnp.where(flag, lax.concatenate([b, a], axis), matrix)


def turn_rows(facts, rotation, rows_of, vector_rows, half, own):
    rows = rows_of.shape[0] // 2 if own else rows_of.shape[0]

    def body(f, rotation_ref, x_ref, stay_ref, leave_ref):
        zero = f[X] == (0 if own else 1)
        upper_leaves = jnp.where(zero, f[FIRST], 1) == 1
        turn = split(swapped(upper_leaves, rotation_ref[...], 1))
        here = pl.multiple_of(f[X] * rows, 8)
        out = dot3(x_ref[pl.ds(here, rows)] if own else x_ref[...], turn)
        stay_ref[:rows] = out[:, :half]
        leave_ref[:rows] = out[:, half:]
        if vector_rows:
            ids = f[VROW] + lax.broadcasted_iota(jnp.int32, (vector_rows, half), 0)
            cols = lax.broadcasted_iota(jnp.int32, (vector_rows, half), 1)
            position = jnp.where(zero, 0, 2)
            vectors = [
                (ids == f[LABEL + position + k] * half + cols).astype(jnp.float32)
                for k in range(2)
            ]
            out = dot3(lax.concatenate(vectors, 1), turn)
            stay_ref[rows:] = out[:, :half]
            leave_ref[rows:] = out[:, half:]

    return call(
        body, facts, [rotation, rows_of], (shape(rows + vector_rows, half),) * 2
    )


def turn(facts, rotation, blocks, own, own_stay=None):
    rows, half = blocks[0].shape
    size = 2 * half
    extra = [] if own_stay is None else [own_stay]

    def body(f, rotation_ref, *refs):
        up_0, low_0, up_1, low_1 = [r[...] for r in refs[:4]]
        zero = f[CORE] == (0 if own else 1)
        upper_leaves = jnp.where(zero, f[FIRST], 1) == 1
        turned = swapped(upper_leaves, rotation_ref[:size], 1)
        columns = lax.concatenate(
            [jnp.where(zero, up_0, up_1), jnp.where(zero, low_0, low_1)], 1
        )
        out = dot3(columns, turned)
        outs = refs[4 + len(extra) :]
        outs[0][...] = out[:, :half]
        outs[1][...] = out[:, half:]
        if extra:
            outs[2][...] = jnp.where(f[CORE] == f[X], refs[4][...], out[:, :half])

    return call(
        body, facts, [rotation] + blocks + extra,
        (shape(rows, half),) * (2 + len(extra)),
    )


def put_cross(f, refs, zero, one):
    core = f[CORE] == 0
    refs[0][...] = jnp.where(core, zero, one)
    refs[1][...] = jnp.where(core, one, zero)


def cross_gram(facts, own, others, position, part, half):
    rows = own[0].shape[0]
    pieces = len(others)

    def body(f, *refs):
        own_refs = [[r] for r in refs[:3]]
        other_refs = [refs[3 + k : 3 + 3 * pieces : 3] for k in range(3)]
        up_0, low_0, up_1, low_1 = refs[5 + 3 * pieces :]

        def fill(target, sources):
            at = 0
            for ref in sources:
                target[at : at + ref.shape[0]] = ref[...]
                at += ref.shape[0]

        first, last = f[FIRST] == 1, f[LAST] == 1
        for x, near, far in ((0, own_refs, other_refs), (1, other_refs, own_refs)):
            here = f[position] == x

            @pl.when(here)
            def _():
                fill(up_1, near[0])
                fill(low_0, far[0])

            @pl.when(here & first)
            def _():
                fill(up_0, near[1])

            @pl.when(here & ~first)
            def _():
                fill(up_0, far[2])

            @pl.when(here & last)
            def _():
                fill(low_1, far[1])

            @pl.when(here & ~last)
            def _():
                fill(low_1, near[2])

        put_cross(
            f,
            refs[3 + 3 * pieces :],
            dot_tn(up_0[:part], low_0[:part]),
            dot_tn(up_1[:part], low_1[:part]),
        )

    outs = (shape(half, half),) * 2 + (shape(rows, half),) * 4
    return call(body, facts, own + sum(others, []), outs)


def give_arrived(facts, own, other, rows, half):
    def body(f, *refs):
        out_ref = refs[4]
        near = f[CORE] == f[X]
        edge = jnp.where(f[X] == 0, f[LAST], f[FIRST]) == 1
        for ref, here in zip(
            refs, (~near & edge, near & ~edge, near & edge, ~near & ~edge)
        ):

            @pl.when(here)
            def _():
                out_ref[...] = ref[:rows]

    return call(body, facts, own[1:] + other[1:], shape(rows, half))


def give(facts, blocks, start, stop, half):
    def body(f, up_0_ref, low_1_ref, out_ref):
        out_ref[...] = jnp.where(
            f[X] == 0, low_1_ref[start:stop], up_0_ref[start:stop]
        )

    return call(
        body, facts, [blocks[0], blocks[3]], shape(stop - start, half)
    )


def final_turn(f, own_ref, other_ref, size):
    pack = jnp.where(f[CORE] == f[X], own_ref[...], other_ref[...])
    return split(swapped(f[X] == 1, pack[:size], 0)), pack[size : size + 1]


def final_product(moved, native, turned):
    return dot3(lax.concatenate([moved, native], 1), turned)


def put_rows(copies, sems, source, target, here, there, value):
    rows = value.shape[0]
    source[here : here + rows] = value
    copy = pltpu.make_async_copy(
        source.at[here : here + rows],
        target.at[pl.ds(pl.multiple_of(there, 8), rows)],
        sems.at[len(copies)],
    )
    copies.append(copy)
    copy.start()


def finish_call(body, facts, inputs, outputs, outs, rows, vector_rows, size):
    vmem = pl.BlockSpec(memory_space=pltpu.VMEM)
    hbm = pl.BlockSpec(memory_space=pl.ANY)
    first = 1 + len(inputs)
    return pl.pallas_call(
        body,
        out_shape=outs,
        in_specs=[pl.BlockSpec(memory_space=pltpu.SMEM)]
        + [vmem] * len(inputs)
        + [hbm] * len(outputs),
        out_specs=(hbm, hbm, vmem)[: len(outs)],
        input_output_aliases={first + k: k for k in range(len(outputs))},
        cost_estimate=pl.CostEstimate(flops=1, transcendentals=0, bytes_accessed=1),
        scratch_shapes=[
            pltpu.VMEM((rows, size), jnp.float32),
            pltpu.VMEM((vector_rows, size), jnp.float32),
            pltpu.SemaphoreType.DMA((4,)),
        ],
        compiler_params=pltpu.CompilerParams(vmem_limit_bytes=24 << 20),
    )(facts, *inputs, *outputs)


def finish_kept(facts, packs, blocks, native, got_top, part, half):
    size = 2 * half
    vector_rows = blocks[0].shape[0] - part
    top = got_top.shape[0]

    def body(f, own_ref, other_ref, *refs):
        x = f[X]
        turned, squares = final_turn(f, own_ref, other_ref, size)
        native_ref, top_ref, out_ref, vectors_ref, singular_ref, out, vectors, sems = (
            refs[4:]
        )
        copies = []

        def kept(rows):
            up_0, low_0, up_1, low_1 = [r[rows] for r in refs[:4]]
            return final_product(
                jnp.where(x == 0, up_0, low_1),
                jnp.where(x == 0, low_0, up_1),
                turned,
            )

        def put(*args):
            put_rows(copies, sems, *args)

        middle = part // 2
        put(out, out_ref, 0, x * part, kept(slice(0, middle)))
        put(out, out_ref, middle, x * part + middle, kept(slice(middle, part)))
        value = final_product(top_ref[...], native_ref[:top], turned)
        put(out, out_ref, part, (1 - x) * part, value)
        put(vectors, vectors_ref, 0, x * vector_rows, kept(slice(part, None)))
        singular_ref[...] = jnp.sqrt(jnp.maximum(squares, 0.0) + 1e-06)
        for copy in copies:
            copy.wait()

    outs = (shape(2 * part, size), shape(2 * vector_rows, size), shape(1, size))
    inputs = packs + blocks + [native, got_top]
    return finish_call(
        body, facts, inputs, [], outs, part + top, vector_rows, size
    )


def finish_rest(facts, packs, outputs, native, got_rest, part, half):
    size = 2 * half
    vector_rows = native.shape[0] - part
    rest = got_rest.shape[0] - vector_rows
    top = part - rest

    def body(f, own_ref, other_ref, native_ref, rest_ref, *refs):
        x = f[X]
        turned, _ = final_turn(f, own_ref, other_ref, size)
        out_ref, vectors_ref, out, vectors, sems = refs[2:]
        copies = []
        value = final_product(rest_ref[:rest], native_ref[top:part], turned)
        put_rows(copies, sems, out, out_ref, 0, (1 - x) * part + top, value)
        value = final_product(rest_ref[rest:], native_ref[part:], turned)
        put_rows(copies, sems, vectors, vectors_ref, 0, (1 - x) * vector_rows, value)
        for copy in copies:
            copy.wait()

    outs = (shape(2 * part, size), shape(2 * vector_rows, size))
    inputs = packs + [native, got_rest]
    return finish_call(
        body, facts, inputs, outputs, outs, rest, vector_rows, size
    )


def per_device(sector, block_label):
    local_rows, size = sector.shape
    half = size // 2
    part = local_rows // 2
    pairs = lax.axis_size("pair")
    row_count = lax.axis_size("row")
    vector_rows = pairs * size // row_count // 2
    pair_index = lax.axis_index("pair")
    row_index = lax.axis_index("row")
    x = pair_index % 2
    group = pair_index // 2
    core = row_index % 2

    def permute(block, route):
        moves = [
            (a * row_count + b, c * row_count + d) for (a, b), (c, d) in route
        ]
        return lax.ppermute(block, ("pair", "row"), moves)

    devices = [(p, r) for p in range(pairs) for r in range(row_count)]

    def exchange(block, over_pair, over_row):
        return permute(
            block, [((p ^ over_pair, r ^ over_row), (p, r)) for p, r in devices]
        )

    def shift(block, leftward):
        moves = []
        for p, r in devices:
            source = p + 2 if leftward(p, r) else p - 2
            if 0 <= source < pairs:
                moves.append(((source, r), (p, r)))
        return permute(block, moves)

    def pass_diagonal(block):
        moves = []
        for p, r in devices:
            other = p + 2 if r % 2 else p - 2
            inside = 0 <= other < pairs
            moves.append(((other, r ^ 1) if inside else (p, r), (p, r)))
        return permute(block, [((a, b), c) for (a, b), c in moves])

    def first_diagonal(block, leaves):
        moves = []
        for p, r in devices:
            c, even = r % 2, p - p % 2
            if leaves:
                source = even - 1 if c == 0 else even + 2
                if not 0 <= source < pairs:
                    source = even + c
            else:
                source = even + 1 - c
            moves.append(((source, r - c + p % 2), (p, r)))
        return permute(block, moves)

    def sum_rows(block):
        bit = 4
        while bit < row_count:
            block = block + exchange(block, 0, bit)
            bit *= 2
        return block

    names = jnp.arange(16, dtype=jnp.int32)
    facts = jnp.zeros((16,), jnp.int32)
    for name, value in (
        (X, x),
        (CORE, core),
        (FIRST, group == 0),
        (LAST, group == pairs // 2 - 1),
        (VROW, (row_index * 2 + x) * vector_rows),
        (EVEN, group % 2 == 0),
    ):
        facts = jnp.where(names == name, value.astype(jnp.int32), facts)
    labels = lax.dynamic_slice_in_dim(block_label, 4 * group, 4)
    facts = lax.dynamic_update_slice_in_dim(facts, labels, LABEL, 0)

    def together(*arrays):
        return lax.optimization_barrier(arrays)

    top_give, rest_give = give_rows(sector, part * 3 // 4)
    got_top = exchange(top_give, 1, 0)
    own = first_gram(sector, half)
    own = sum_rows(own + exchange(own, 0, 1))
    rotation, gram = first_rotation(facts, own, exchange(own, 0, 2), half)

    for sweep_round in range(ROUNDS - 1):
        last_move = sweep_round == ROUNDS - 2
        if sweep_round == 0:
            other_rotation = exchange(rotation, 1, 0)
            stay, leave = turn_rows(facts, rotation, sector, vector_rows, half, True)
            leave, rest_give = together(leave, rest_give)
            got_rest = exchange(rest_give, 1, 0)
            own = [stay, leave, shift(leave, lambda p, r: p % 2 == 0)]
            others = []
            for got, below in ((got_top, 0), (got_rest, vector_rows)):
                stay, leave = turn_rows(facts, other_rotation, got, below, half, False)
                others.append([stay, leave, shift(leave, lambda p, r: p % 2 == 1)])
            leave, stay = turned_gram(facts, gram, rotation, X)
            diagonals = [first_diagonal(leave, True), first_diagonal(stay, False)]
            *grams, up_0, low_0, up_1, low_1 = cross_gram(
                facts, own, others, X, part, half
            )
        else:
            other_rotation = exchange(rotation, 0, 1)
            stay, leave = turn(facts, rotation, blocks, True)
            own = [stay, leave, shift(leave, lambda p, r: r % 2 == 0)]
            stay, leave, *native = turn(
                facts, other_rotation, blocks, False, stay if last_move else None
            )
            others = [[stay, leave, shift(leave, lambda p, r: r % 2 == 1)]]
            leave, stay = turned_gram(facts, gram, rotation, CORE)
            diagonals = [pass_diagonal(leave), exchange(stay, 0, 1)]
            if last_move:
                native = exchange(native[0], 1, 0)
                top = part // 2
                top_give = give_arrived(facts, own, others[0], top, half)
                own[2], others[0][2], top_give, *diagonals = together(
                    own[2], others[0][2], top_give, *diagonals
                )
                got_top = exchange(top_give, 1, 0)
            *grams, up_0, low_0, up_1, low_1 = cross_gram(
                facts, own, others, CORE, part, half
            )
        blocks = [up_0, low_0, up_1, low_1]
        if last_move:
            grams[1], native = together(grams[1], native)
        else:
            grams[1], *diagonals = together(grams[1], *diagonals)
        own = sum_rows(grams[0] + exchange(grams[1], 0, 1))
        parts = [own, exchange(own, 0, 2), exchange(own, 1, 0), exchange(own, 1, 2)]
        if last_move:
            rest_give = give(facts, blocks, top, part + vector_rows, half)
            *parts, got_top, rest_give = together(*parts, got_top, rest_give)
            got_rest = exchange(rest_give, 1, 0)
        rotation, gram = later_rotation(facts, parts, diagonals, half, last_move)
    packs = [rotation, exchange(rotation, 0, 1)]
    *outputs, singular = finish_kept(
        facts, packs, blocks, native, got_top, part, half
    )
    rotated, vectors_out = finish_rest(
        facts, packs, outputs, native, got_rest, part, half
    )
    return rotated, vectors_out, singular.reshape(size)


def solution(mesh):
    placed = (P("row", "pair"), P())
    return jax.shard_map(
        per_device,
        mesh=mesh,
        in_specs=placed,
        out_specs=(P("row", "pair"), P("row", "pair"), P("pair")),
        check_vma=False,
    )
```

```python
import jax
import jax.numpy as jnp
from jax import lax
from jax.experimental import pallas as pl
from jax.experimental.pallas import tpu as pltpu
from jax.sharding import PartitionSpec as P

ROUNDS = 4
NEWTON = 16

highest = lax.Precision.HIGHEST

TARGET = 2.0**-12
REACHES = [
    (2.0 / (TARGET ** -(2.0**-j) - 1.0)) ** 2 for j in range(NEWTON)
]

X, CORE, FIRST, LAST, VROW, LABEL, EVEN = 0, 1, 2, 3, 4, 5, 9


def dot(a, b, precision=highest):
    return lax.dot_general(
        a, b, (((1,), (0,)), ((), ())), precision=precision,
        preferred_element_type=jnp.float32,
    )


def split(a):
    high = a.astype(jnp.bfloat16)
    return high, (a - high.astype(jnp.float32)).astype(jnp.bfloat16)


def dot3(a, b):
    a_high, a_low = a if isinstance(a, tuple) else split(a)
    b_high, b_low = b if isinstance(b, tuple) else split(b)
    small = dot(a_high, b_low, None) + dot(a_low, b_high, None)
    return dot(a_high, b_high, None) + small


def dot_tn(a, b):
    return lax.dot_general(
        a, b, (((0,), (0,)), ((), ())), precision=highest,
        preferred_element_type=jnp.float32,
    )


def shape(*dims):
    return jax.ShapeDtypeStruct(dims, jnp.float32)


def call(body, facts, inputs, outs, scratch=(), limit=24):
    return pl.pallas_call(
        body,
        out_shape=outs,
        in_specs=[pl.BlockSpec(memory_space=pltpu.SMEM)]
        + [pl.BlockSpec(memory_space=pltpu.VMEM)] * len(inputs),
        out_specs=jax.tree.map(
            lambda _: pl.BlockSpec(memory_space=pltpu.VMEM), outs
        ),
        scratch_shapes=list(scratch),
        compiler_params=pltpu.CompilerParams(vmem_limit_bytes=limit << 20),
    )(facts, *inputs)


def first_gram(sector, half):
    def body(x_ref, out_ref):
        x = x_ref[...]
        g = dot_tn(x, x)
        out_ref[:half] = g[:half, :half]
        out_ref[half : 2 * half] = g[:half, half:]
        out_ref[2 * half :] = g[half:, half:]

    vmem = pl.BlockSpec(memory_space=pltpu.VMEM)
    return pl.pallas_call(
        body,
        out_shape=shape(3 * half, half),
        in_specs=[vmem],
        out_specs=vmem,
        compiler_params=pltpu.CompilerParams(vmem_limit_bytes=24 << 20),
    )(sector)


def give_rows(sector, top, pieces=8):
    rows, width = sector.shape
    part = rows // 2
    step = part // pieces

    def body(x_ref, top_ref, rest_ref, sems):
        start = (1 - lax.axis_index("pair") % 2) * part
        copies = []
        for k in range(pieces):
            at = k * step
            target, here = (top_ref, at) if at < top else (rest_ref, at - top)
            source = x_ref.at[pl.ds(pl.multiple_of(start + at, 8), step)]
            copies.append(
                pltpu.make_async_copy(
                    source, target.at[here : here + step], sems.at[k]
                )
            )
            copies[-1].start()
        for copy in copies:
            copy.wait()

    return pl.pallas_call(
        body,
        out_shape=(shape(top, width), shape(part - top, width)),
        in_specs=[pl.BlockSpec(memory_space=pl.ANY)],
        out_specs=(pl.BlockSpec(memory_space=pltpu.VMEM),) * 2,
        scratch_shapes=[pltpu.SemaphoreType.DMA((pieces,))],
    )(sector)


def rotate_of(gram, x_ref, e_ref):
    size = gram.shape[0]
    rows = lax.broadcasted_iota(jnp.int32, (size, size), 0)
    cols = lax.broadcasted_iota(jnp.int32, (size, size), 1)
    identity = (rows == cols).astype(jnp.float32)
    only = jnp.where(rows == cols, gram, 0.0)
    g_j = jnp.sum(only, axis=0, keepdims=True)
    g_i = jnp.sum(only, axis=1, keepdims=True)
    spread = g_j - g_i
    summed = g_j + g_i
    skew = gram * spread / (spread * spread + 2.0 * gram * gram + 0.01 * summed * summed)
    skew_parts = split(skew)
    square = dot3(skew_parts, skew_parts)
    whole = 0.25 * jnp.sum(skew * skew)
    paired = 0.03125 * jnp.sum(square * square) * 1.001
    reach = jnp.minimum(whole * whole, paired)
    steps = jnp.int32(0)
    for limit in REACHES:
        steps = steps + (reach > limit).astype(jnp.int32)
    fixes = 1 + (steps > 7).astype(jnp.int32) + 2 * (steps > 9).astype(jnp.int32)
    scale = 2.0 / (2.0 + jnp.sqrt(jnp.full((size, size), reach, jnp.float32)))
    residual = identity - scale * (identity - 0.25 * square)
    x_ref[...] = scale * (identity + residual)
    residual_parts = split(residual)
    e_ref[...] = dot3(residual_parts, residual_parts)

    def step(_, carry):
        e = split(e_ref[...])
        x = x_ref[...]
        x_ref[...] = x + dot3(x, e)
        e_ref[...] = dot3(e, e)
        return carry

    lax.fori_loop(0, jnp.maximum(steps - 1, 0), step, jnp.int32(0))
    x = x_ref[...]
    x_ref[...] = x + 0.5 * dot3(x, skew_parts)

    def fix(_, carry):
        x = x_ref[...]
        x_ref[...] = x + dot3(x, identity - (x - 0.5 * dot(skew, x)))
        return carry

    lax.fori_loop(0, fixes, fix, jnp.int32(0))
    return 2.0 * x_ref[...] - identity


def put_rotation(rotation_ref, gram, x_ref, e_ref, last_round):
    size = gram.shape[0]
    rotation = rotate_of(gram, x_ref, e_ref)
    rotation_ref[:size] = rotation
    if last_round:
        squares = jnp.sum(rotation * dot(gram, rotation), axis=0, keepdims=True)
        rotation_ref[size:] = jnp.broadcast_to(squares, (8, size))


def first_rotation(facts, own, other_y, half):
    size = 2 * half

    def body(f, own_ref, other_ref, rotation_ref, g_ref, half_ref, x_ref, e_ref):
        total = own_ref[...] + other_ref[...]
        g_ref[:half, :half] = total[:half]
        g_ref[:half, half:] = total[half : 2 * half]
        g_ref[half:, :half] = total[half : 2 * half].T
        g_ref[half:, half:] = total[2 * half :]
        put_rotation(rotation_ref, g_ref[...], x_ref, e_ref, False)
        rotation = rotation_ref[...]
        half_ref[...] = jnp.where(f[CORE] == 0, rotation[:half], rotation[half:])

    square = pltpu.VMEM((size, size), jnp.float32)
    outs = (shape(size, size),) * 2 + (shape(half, size),)
    return call(body, facts, [own, other_y], outs, [square] * 2)


def later_rotation(facts, parts, diagonals, half, last_round):
    size = 2 * half

    def body(f, *refs):
        own, other_y, other_x, other_xy, foreign, native = [r[...] for r in refs[:6]]
        rotation_ref, g_ref, x_ref, e_ref = refs[6:]
        cross = (own + other_y) + (other_x + other_xy)
        core = f[CORE] == 0
        g_ref[:half, :half] = jnp.where(core, foreign, native)
        g_ref[:half, half:] = cross
        g_ref[half:, :half] = cross.T
        g_ref[half:, half:] = jnp.where(core, native, foreign)
        put_rotation(rotation_ref, g_ref[...], x_ref, e_ref, last_round)

    square = pltpu.VMEM((size, size), jnp.float32)
    return call(
        body,
        facts,
        parts + diagonals,
        (shape(size + 8 if last_round else size, size), shape(size, size)),
        [square] * 2,
    )


def turned_gram(facts, gram, rotation, position):
    size = gram.shape[0]
    half = size // 2

    def body(f, gram_ref, rotation_ref, leave_ref, stay_ref):
        rotation = rotation_ref[...]
        turned = dot(gram_ref[...], rotation)
        upper = dot_tn(rotation[:, :half], turned[:, :half])
        lower = dot_tn(rotation[:, half:], turned[:, half:])
        lower_leaves = (f[position] == 0) & (f[FIRST] == 0)
        leave_ref[...] = jnp.where(lower_leaves, lower, upper)
        stay_ref[...] = jnp.where(lower_leaves, upper, lower)

    return call(body, facts, [gram, rotation], (shape(half, half),) * 2)


def swapped(flag, matrix, axis):
    half = matrix.shape[axis] // 2
    a = lax.slice_in_dim(matrix, 0, half, axis=axis)
    b = lax.slice_in_dim(matrix, half, 2 * half, axis=axis)
    return jnp.where(flag, lax.concatenate([b, a], axis), matrix)


def turn_rows(facts, rotation, rows_of, vector_rows, half, own):
    rows = rows_of.shape[0] // 2 if own else rows_of.shape[0]

    def body(f, *refs):
        x_ref, stay_ref, leave_ref = refs[-3:]
        matrix = lax.concatenate([r[...] for r in refs[:-3]], 0)
        if not own:
            matrix = swapped(f[CORE] == 1, matrix, 0)
        zero = f[X] == (0 if own else 1)
        upper_leaves = jnp.where(zero, f[FIRST], 1) == 1
        turn = split(swapped(upper_leaves, matrix, 1))
        here = pl.multiple_of(f[X] * rows, 8)
        out = dot3(x_ref[pl.ds(here, rows)] if own else x_ref[...], turn)
        stay_ref[:rows] = out[:, :half]
        leave_ref[:rows] = out[:, half:]
        if vector_rows:
            ids = f[VROW] + lax.broadcasted_iota(jnp.int32, (vector_rows, half), 0)
            cols = lax.broadcasted_iota(jnp.int32, (vector_rows, half), 1)
            position = jnp.where(zero, 0, 2)
            vectors = [
                (ids == f[LABEL + position + k] * half + cols).astype(jnp.float32)
                for k in range(2)
            ]
            out = dot3(lax.concatenate(vectors, 1), turn)
            stay_ref[rows:] = out[:, :half]
            leave_ref[rows:] = out[:, half:]

    return call(
        body, facts, rotation + [rows_of], (shape(rows + vector_rows, half),) * 2
    )


def turn(facts, rotation, blocks, own, own_stay=None):
    rows, half = blocks[0].shape
    size = 2 * half
    extra = [] if own_stay is None else [own_stay]

    def body(f, rotation_ref, *refs):
        up_0, low_0, up_1, low_1 = [r[...] for r in refs[:4]]
        zero = f[CORE] == (0 if own else 1)
        upper_leaves = jnp.where(zero, f[FIRST], 1) == 1
        turned = swapped(upper_leaves, rotation_ref[:size], 1)
        columns = lax.concatenate(
            [jnp.where(zero, up_0, up_1), jnp.where(zero, low_0, low_1)], 1
        )
        out = dot3(columns, turned)
        outs = refs[4 + len(extra) :]
        outs[0][...] = out[:, :half]
        outs[1][...] = out[:, half:]
        if extra:
            outs[2][...] = jnp.where(f[CORE] == f[X], refs[4][...], out[:, :half])

    return call(
        body, facts, [rotation] + blocks + extra,
        (shape(rows, half),) * (2 + len(extra)),
    )


def put_cross(f, refs, zero, one):
    core = f[CORE] == 0
    refs[0][...] = jnp.where(core, zero, one)
    refs[1][...] = jnp.where(core, one, zero)


def cross_gram(facts, own, others, position, part, half):
    rows = own[0].shape[0]
    pieces = len(others)

    def body(f, *refs):
        own_refs = [[r] for r in refs[:3]]
        other_refs = [refs[3 + k : 3 + 3 * pieces : 3] for k in range(3)]
        up_0, low_0, up_1, low_1 = refs[5 + 3 * pieces :]

        def fill(target, sources):
            at = 0
            for ref in sources:
                target[at : at + ref.shape[0]] = ref[...]
                at += ref.shape[0]

        first, last = f[FIRST] == 1, f[LAST] == 1
        for x, near, far in ((0, own_refs, other_refs), (1, other_refs, own_refs)):
            here = f[position] == x

            @pl.when(here)
            def _():
                fill(up_1, near[0])
                fill(low_0, far[0])

            @pl.when(here & first)
            def _():
                fill(up_0, near[1])

            @pl.when(here & ~first)
            def _():
                fill(up_0, far[2])

            @pl.when(here & last)
            def _():
                fill(low_1, far[1])

            @pl.when(here & ~last)
            def _():
                fill(low_1, near[2])

        put_cross(
            f,
            refs[3 + 3 * pieces :],
            dot_tn(up_0[:part], low_0[:part]),
            dot_tn(up_1[:part], low_1[:part]),
        )

    outs = (shape(half, half),) * 2 + (shape(rows, half),) * 4
    return call(body, facts, own + sum(others, []), outs)


def give_arrived(facts, own, other, rows, half):
    def body(f, *refs):
        out_ref = refs[4]
        near = f[CORE] == f[X]
        edge = jnp.where(f[X] == 0, f[LAST], f[FIRST]) == 1
        for ref, here in zip(
            refs, (~near & edge, near & ~edge, near & edge, ~near & ~edge)
        ):

            @pl.when(here)
            def _():
                out_ref[...] = ref[:rows]

    return call(body, facts, own[1:] + other[1:], shape(rows, half))


def give(facts, blocks, start, stop, half):
    def body(f, up_0_ref, low_1_ref, out_ref):
        out_ref[...] = jnp.where(
            f[X] == 0, low_1_ref[start:stop], up_0_ref[start:stop]
        )

    return call(
        body, facts, [blocks[0], blocks[3]], shape(stop - start, half)
    )


def final_turn(f, own_ref, other_ref, size):
    pack = jnp.where(f[CORE] == f[X], own_ref[...], other_ref[...])
    return split(swapped(f[X] == 1, pack[:size], 0)), pack[size : size + 1]


def final_product(moved, native, turned):
    return dot3(lax.concatenate([moved, native], 1), turned)


def put_rows(copies, sems, source, target, here, there, value):
    rows = value.shape[0]
    source[here : here + rows] = value
    copy = pltpu.make_async_copy(
        source.at[here : here + rows],
        target.at[pl.ds(pl.multiple_of(there, 8), rows)],
        sems.at[len(copies)],
    )
    copies.append(copy)
    copy.start()


def finish_call(body, facts, inputs, outputs, outs, rows, vector_rows, size):
    vmem = pl.BlockSpec(memory_space=pltpu.VMEM)
    hbm = pl.BlockSpec(memory_space=pl.ANY)
    first = 1 + len(inputs)
    return pl.pallas_call(
        body,
        out_shape=outs,
        in_specs=[pl.BlockSpec(memory_space=pltpu.SMEM)]
        + [vmem] * len(inputs)
        + [hbm] * len(outputs),
        out_specs=(hbm, hbm, vmem)[: len(outs)],
        input_output_aliases={first + k: k for k in range(len(outputs))},
        cost_estimate=pl.CostEstimate(flops=1, transcendentals=0, bytes_accessed=1),
        scratch_shapes=[
            pltpu.VMEM((rows, size), jnp.float32),
            pltpu.VMEM((vector_rows, size), jnp.float32),
            pltpu.SemaphoreType.DMA((4,)),
        ],
        compiler_params=pltpu.CompilerParams(vmem_limit_bytes=24 << 20),
    )(facts, *inputs, *outputs)


def finish_kept(facts, packs, blocks, native, got_top, part, half):
    size = 2 * half
    vector_rows = blocks[0].shape[0] - part
    top = got_top.shape[0]

    def body(f, own_ref, other_ref, *refs):
        x = f[X]
        turned, squares = final_turn(f, own_ref, other_ref, size)
        native_ref, top_ref, out_ref, vectors_ref, singular_ref, out, vectors, sems = (
            refs[4:]
        )
        copies = []

        def kept(rows):
            up_0, low_0, up_1, low_1 = [r[rows] for r in refs[:4]]
            return final_product(
                jnp.where(x == 0, up_0, low_1),
                jnp.where(x == 0, low_0, up_1),
                turned,
            )

        def put(*args):
            put_rows(copies, sems, *args)

        middle = part // 2
        put(out, out_ref, 0, x * part, kept(slice(0, middle)))
        put(out, out_ref, middle, x * part + middle, kept(slice(middle, part)))
        value = final_product(top_ref[...], native_ref[:top], turned)
        put(out, out_ref, part, (1 - x) * part, value)
        put(vectors, vectors_ref, 0, x * vector_rows, kept(slice(part, None)))
        singular_ref[...] = jnp.sqrt(jnp.maximum(squares, 0.0) + 1e-06)
        for copy in copies:
            copy.wait()

    outs = (shape(2 * part, size), shape(2 * vector_rows, size), shape(1, size))
    inputs = packs + blocks + [native, got_top]
    return finish_call(
        body, facts, inputs, [], outs, part + top, vector_rows, size
    )


def finish_rest(facts, packs, outputs, native, got_rest, part, half):
    size = 2 * half
    vector_rows = native.shape[0] - part
    rest = got_rest.shape[0] - vector_rows
    top = part - rest

    def body(f, own_ref, other_ref, native_ref, rest_ref, *refs):
        x = f[X]
        turned, _ = final_turn(f, own_ref, other_ref, size)
        out_ref, vectors_ref, out, vectors, sems = refs[2:]
        copies = []
        value = final_product(rest_ref[:rest], native_ref[top:part], turned)
        put_rows(copies, sems, out, out_ref, 0, (1 - x) * part + top, value)
        value = final_product(rest_ref[rest:], native_ref[part:], turned)
        put_rows(copies, sems, vectors, vectors_ref, 0, (1 - x) * vector_rows, value)
        for copy in copies:
            copy.wait()

    outs = (shape(2 * part, size), shape(2 * vector_rows, size))
    inputs = packs + [native, got_rest]
    return finish_call(
        body, facts, inputs, outputs, outs, rest, vector_rows, size
    )


def per_device(sector, block_label):
    local_rows, size = sector.shape
    half = size // 2
    part = local_rows // 2
    pairs = lax.axis_size("pair")
    row_count = lax.axis_size("row")
    vector_rows = pairs * size // row_count // 2
    pair_index = lax.axis_index("pair")
    row_index = lax.axis_index("row")
    x = pair_index % 2
    group = pair_index // 2
    core = row_index % 2

    def permute(block, route):
        moves = [
            (a * row_count + b, c * row_count + d) for (a, b), (c, d) in route
        ]
        return lax.ppermute(block, ("pair", "row"), moves)

    devices = [(p, r) for p in range(pairs) for r in range(row_count)]

    def exchange(block, over_pair, over_row):
        return permute(
            block, [((p ^ over_pair, r ^ over_row), (p, r)) for p, r in devices]
        )

    def shift(block, leftward):
        moves = []
        for p, r in devices:
            source = p + 2 if leftward(p, r) else p - 2
            if 0 <= source < pairs:
                moves.append(((source, r), (p, r)))
        return permute(block, moves)

    def pass_diagonal(block):
        moves = []
        for p, r in devices:
            other = p + 2 if r % 2 else p - 2
            inside = 0 <= other < pairs
            moves.append(((other, r ^ 1) if inside else (p, r), (p, r)))
        return permute(block, [((a, b), c) for (a, b), c in moves])

    def first_diagonal(block, leaves):
        moves = []
        for p, r in devices:
            c, even = r % 2, p - p % 2
            if leaves:
                source = even - 1 if c == 0 else even + 2
                if not 0 <= source < pairs:
                    source = even + c
            else:
                source = even + 1 - c
            moves.append(((source, r - c + p % 2), (p, r)))
        return permute(block, moves)

    def sum_rows(block):
        bit = 4
        while bit < row_count:
            block = block + exchange(block, 0, bit)
            bit *= 2
        return block

    names = jnp.arange(16, dtype=jnp.int32)
    facts = jnp.zeros((16,), jnp.int32)
    for name, value in (
        (X, x),
        (CORE, core),
        (FIRST, group == 0),
        (LAST, group == pairs // 2 - 1),
        (VROW, (row_index * 2 + x) * vector_rows),
        (EVEN, group % 2 == 0),
    ):
        facts = jnp.where(names == name, value.astype(jnp.int32), facts)
    labels = lax.dynamic_slice_in_dim(block_label, 4 * group, 4)
    facts = lax.dynamic_update_slice_in_dim(facts, labels, LABEL, 0)

    def together(*arrays):
        return lax.optimization_barrier(arrays)

    top_give, rest_give = give_rows(sector, part * 3 // 4)
    got_top = exchange(top_give, 1, 0)
    own = first_gram(sector, half)
    own = sum_rows(own + exchange(own, 0, 1))
    rotation, gram, rotation_half = first_rotation(facts, own, exchange(own, 0, 2), half)

    for sweep_round in range(ROUNDS - 1):
        last_move = sweep_round == ROUNDS - 2
        if sweep_round == 0:
            other_half = exchange(rotation_half, 1, 0)
            other_rotation = [other_half, exchange(other_half, 0, 1)]
            stay, leave = turn_rows(
                facts, [rotation], sector, vector_rows, half, True
            )
            leave, rest_give = together(leave, rest_give)
            got_rest = exchange(rest_give, 1, 0)
            own = [stay, leave, shift(leave, lambda p, r: p % 2 == 0)]
            others = []
            for got, below in ((got_top, 0), (got_rest, vector_rows)):
                stay, leave = turn_rows(facts, other_rotation, got, below, half, False)
                others.append([stay, leave, shift(leave, lambda p, r: p % 2 == 1)])
            leave, stay = turned_gram(facts, gram, rotation, X)
            diagonals = [first_diagonal(leave, True), first_diagonal(stay, False)]
            *grams, up_0, low_0, up_1, low_1 = cross_gram(
                facts, own, others, X, part, half
            )
        else:
            other_rotation = exchange(rotation, 0, 1)
            stay, leave = turn(facts, rotation, blocks, True)
            own = [stay, leave, shift(leave, lambda p, r: r % 2 == 0)]
            stay, leave, *native = turn(
                facts, other_rotation, blocks, False, stay if last_move else None
            )
            others = [[stay, leave, shift(leave, lambda p, r: r % 2 == 1)]]
            leave, stay = turned_gram(facts, gram, rotation, CORE)
            diagonals = [pass_diagonal(leave), exchange(stay, 0, 1)]
            if last_move:
                native = exchange(native[0], 1, 0)
                top = part * 5 // 8
                top_give = give_arrived(facts, own, others[0], top, half)
                own[2], others[0][2], top_give, *diagonals = together(
                    own[2], others[0][2], top_give, *diagonals
                )
                got_top = exchange(top_give, 1, 0)
            *grams, up_0, low_0, up_1, low_1 = cross_gram(
                facts, own, others, CORE, part, half
            )
        blocks = [up_0, low_0, up_1, low_1]
        if last_move:
            grams[1], native = together(grams[1], native)
        else:
            grams[1], *diagonals = together(grams[1], *diagonals)
        own = sum_rows(grams[0] + exchange(grams[1], 0, 1))
        parts = [own, exchange(own, 0, 2), exchange(own, 1, 0), exchange(own, 1, 2)]
        if last_move:
            rest_give = give(facts, blocks, top, part + vector_rows, half)
            *parts, got_top, rest_give = together(*parts, got_top, rest_give)
            got_rest = exchange(rest_give, 1, 0)
        rotation, gram = later_rotation(facts, parts, diagonals, half, last_move)
    packs = [rotation, exchange(rotation, 0, 1)]
    *outputs, singular = finish_kept(
        facts, packs, blocks, native, got_top, part, half
    )
    rotated, vectors_out = finish_rest(
        facts, packs, outputs, native, got_rest, part, half
    )
    return rotated, vectors_out, singular.reshape(size)


def solution(mesh):
    placed = (P("row", "pair"), P())
    return jax.shard_map(
        per_device,
        mesh=mesh,
        in_specs=placed,
        out_specs=(P("row", "pair"), P("row", "pair"), P("pair")),
        check_vma=False,
    )
```

```python
import jax
import jax.numpy as jnp
from jax import lax
from jax.experimental import pallas as pl
from jax.experimental.pallas import tpu as pltpu
from jax.sharding import PartitionSpec as P

ROUNDS = 4
NEWTON = 16

highest = lax.Precision.HIGHEST

TARGET = 2.0**-12
REACHES = [
    (2.0 / (TARGET ** -(2.0**-j) - 1.0)) ** 2 for j in range(NEWTON)
]

X, CORE, FIRST, LAST, VROW, LABEL, EVEN = 0, 1, 2, 3, 4, 5, 9


def dot(a, b, precision=highest):
    return lax.dot_general(
        a, b, (((1,), (0,)), ((), ())), precision=precision,
        preferred_element_type=jnp.float32,
    )


def split(a):
    high = a.astype(jnp.bfloat16)
    return high, (a - high.astype(jnp.float32)).astype(jnp.bfloat16)


def dot3(a, b):
    a_high, a_low = a if isinstance(a, tuple) else split(a)
    b_high, b_low = b if isinstance(b, tuple) else split(b)
    small = dot(a_high, b_low, None) + dot(a_low, b_high, None)
    return dot(a_high, b_high, None) + small


def dot_tn(a, b):
    return lax.dot_general(
        a, b, (((0,), (0,)), ((), ())), precision=highest,
        preferred_element_type=jnp.float32,
    )


def dot3_tn(a, b):
    def product(left, right):
        return lax.dot_general(
            left, right, (((0,), (0,)), ((), ())),
            preferred_element_type=jnp.float32,
        )

    a_high, a_low = split(a)
    b_high, b_low = split(b)
    small = product(a_high, b_low) + product(a_low, b_high)
    return product(a_high, b_high) + small


def shape(*dims):
    return jax.ShapeDtypeStruct(dims, jnp.float32)


def call(body, facts, inputs, outs, scratch=(), limit=24):
    return pl.pallas_call(
        body,
        out_shape=outs,
        in_specs=[pl.BlockSpec(memory_space=pltpu.SMEM)]
        + [pl.BlockSpec(memory_space=pltpu.VMEM)] * len(inputs),
        out_specs=jax.tree.map(
            lambda _: pl.BlockSpec(memory_space=pltpu.VMEM), outs
        ),
        scratch_shapes=list(scratch),
        compiler_params=pltpu.CompilerParams(vmem_limit_bytes=limit << 20),
    )(facts, *inputs)


def first_gram(sector, half):
    def body(x_ref, out_ref):
        x = x_ref[...]
        g = dot3_tn(x, x)
        out_ref[:half] = g[:half, :half]
        out_ref[half : 2 * half] = g[:half, half:]
        out_ref[2 * half :] = g[half:, half:]

    vmem = pl.BlockSpec(memory_space=pltpu.VMEM)
    return pl.pallas_call(
        body,
        out_shape=shape(3 * half, half),
        in_specs=[vmem],
        out_specs=vmem,
        compiler_params=pltpu.CompilerParams(vmem_limit_bytes=24 << 20),
    )(sector)


def give_rows(sector, top, pieces=8):
    rows, width = sector.shape
    part = rows // 2
    step = part // pieces

    def body(x_ref, top_ref, rest_ref, sems):
        start = (1 - lax.axis_index("pair") % 2) * part
        copies = []
        for k in range(pieces):
            at = k * step
            target, here = (top_ref, at) if at < top else (rest_ref, at - top)
            source = x_ref.at[pl.ds(pl.multiple_of(start + at, 8), step)]
            copies.append(
                pltpu.make_async_copy(
                    source, target.at[here : here + step], sems.at[k]
                )
            )
            copies[-1].start()
        for copy in copies:
            copy.wait()

    return pl.pallas_call(
        body,
        out_shape=(shape(top, width), shape(part - top, width)),
        in_specs=[pl.BlockSpec(memory_space=pl.ANY)],
        out_specs=(pl.BlockSpec(memory_space=pltpu.VMEM),) * 2,
        scratch_shapes=[pltpu.SemaphoreType.DMA((pieces,))],
    )(sector)


def rotate_of(gram, x_ref, e_ref):
    size = gram.shape[0]
    rows = lax.broadcasted_iota(jnp.int32, (size, size), 0)
    cols = lax.broadcasted_iota(jnp.int32, (size, size), 1)
    identity = (rows == cols).astype(jnp.float32)
    only = jnp.where(rows == cols, gram, 0.0)
    g_j = jnp.sum(only, axis=0, keepdims=True)
    g_i = jnp.sum(only, axis=1, keepdims=True)
    spread = g_j - g_i
    summed = g_j + g_i
    skew = gram * spread / (spread * spread + 2.0 * gram * gram + 0.01 * summed * summed)
    skew_parts = split(skew)
    square = dot3(skew_parts, skew_parts)
    whole = 0.25 * jnp.sum(skew * skew)
    paired = 0.03125 * jnp.sum(square * square) * 1.001
    reach = jnp.minimum(whole * whole, paired)
    steps = jnp.int32(0)
    for limit in REACHES:
        steps = steps + (reach > limit).astype(jnp.int32)
    fixes = 1 + (steps > 7).astype(jnp.int32) + 2 * (steps > 9).astype(jnp.int32)
    scale = 2.0 / (2.0 + jnp.sqrt(jnp.full((size, size), reach, jnp.float32)))
    residual = identity - scale * (identity - 0.25 * square)
    x_ref[...] = scale * (identity + residual)
    residual_parts = split(residual)
    e_ref[...] = dot3(residual_parts, residual_parts)

    def step(_, carry):
        e = split(e_ref[...])
        x = x_ref[...]
        x_ref[...] = x + dot3(x, e)
        e_ref[...] = dot3(e, e)
        return carry

    lax.fori_loop(0, jnp.maximum(steps - 1, 0), step, jnp.int32(0))
    x = x_ref[...]
    x_ref[...] = x + 0.5 * dot3(x, skew_parts)

    def fix(_, carry):
        x = x_ref[...]
        x_ref[...] = x + dot3(x, identity - (x - 0.5 * dot(skew, x)))
        return carry

    lax.fori_loop(0, fixes, fix, jnp.int32(0))
    return 2.0 * x_ref[...] - identity


def squares_of(facts, gram, rotation):
    size = gram.shape[0]

    def body(f, gram_ref, rotation_ref, out_ref):
        rotation = rotation_ref[...]
        squares = rotation * dot(gram_ref[...], rotation)
        out_ref[...] = jnp.broadcast_to(
            jnp.sum(squares, axis=0, keepdims=True), (8, size)
        )

    return call(body, facts, [gram, rotation], shape(8, size))


def first_rotation(facts, own, other_y, half):
    size = 2 * half

    def body(f, own_ref, other_ref, rotation_ref, g_ref, half_ref, x_ref, e_ref):
        total = own_ref[...] + other_ref[...]
        g_ref[:half, :half] = total[:half]
        g_ref[:half, half:] = total[half : 2 * half]
        g_ref[half:, :half] = total[half : 2 * half].T
        g_ref[half:, half:] = total[2 * half :]
        rotation_ref[...] = rotate_of(g_ref[...], x_ref, e_ref)
        rotation = rotation_ref[...]
        half_ref[...] = jnp.where(f[CORE] == 0, rotation[:half], rotation[half:])

    square = pltpu.VMEM((size, size), jnp.float32)
    outs = (shape(size, size),) * 2 + (shape(half, size),)
    return call(body, facts, [own, other_y], outs, [square] * 2)


def later_rotation(facts, parts, diagonals, half):
    size = 2 * half

    def body(f, *refs):
        own, other_y, other_x, other_xy, foreign, native = [r[...] for r in refs[:6]]
        rotation_ref, g_ref, x_ref, e_ref = refs[6:]
        cross = (own + other_y) + (other_x + other_xy)
        core = f[CORE] == 0
        g_ref[:half, :half] = jnp.where(core, foreign, native)
        g_ref[:half, half:] = cross
        g_ref[half:, :half] = cross.T
        g_ref[half:, half:] = jnp.where(core, native, foreign)
        rotation_ref[...] = rotate_of(g_ref[...], x_ref, e_ref)

    square = pltpu.VMEM((size, size), jnp.float32)
    return call(
        body,
        facts,
        parts + diagonals,
        (shape(size, size),) * 2,
        [square] * 2,
    )


def turned_gram(facts, gram, rotation, position):
    size = gram.shape[0]
    half = size // 2

    def body(f, gram_ref, rotation_ref, leave_ref, stay_ref):
        rotation = rotation_ref[...]
        turned = dot(gram_ref[...], rotation)
        upper = dot_tn(rotation[:, :half], turned[:, :half])
        lower = dot_tn(rotation[:, half:], turned[:, half:])
        lower_leaves = (f[position] == 0) & (f[FIRST] == 0)
        leave_ref[...] = jnp.where(lower_leaves, lower, upper)
        stay_ref[...] = jnp.where(lower_leaves, upper, lower)

    return call(body, facts, [gram, rotation], (shape(half, half),) * 2)


def swapped(flag, matrix, axis):
    half = matrix.shape[axis] // 2
    a = lax.slice_in_dim(matrix, 0, half, axis=axis)
    b = lax.slice_in_dim(matrix, half, 2 * half, axis=axis)
    return jnp.where(flag, lax.concatenate([b, a], axis), matrix)


def turn_rows(facts, rotation, rows_of, vector_rows, half, own):
    rows = rows_of.shape[0] // 2 if own else rows_of.shape[0]

    def body(f, *refs):
        x_ref, stay_ref, leave_ref = refs[-3:]
        matrix = lax.concatenate([r[...] for r in refs[:-3]], 0)
        if not own:
            matrix = swapped(f[CORE] == 1, matrix, 0)
        zero = f[X] == (0 if own else 1)
        upper_leaves = jnp.where(zero, f[FIRST], 1) == 1
        turn = split(swapped(upper_leaves, matrix, 1))
        here = pl.multiple_of(f[X] * rows, 8)
        out = dot3(x_ref[pl.ds(here, rows)] if own else x_ref[...], turn)
        stay_ref[:rows] = out[:, :half]
        leave_ref[:rows] = out[:, half:]
        if vector_rows:
            ids = f[VROW] + lax.broadcasted_iota(jnp.int32, (vector_rows, half), 0)
            cols = lax.broadcasted_iota(jnp.int32, (vector_rows, half), 1)
            position = jnp.where(zero, 0, 2)
            vectors = [
                (ids == f[LABEL + position + k] * half + cols).astype(jnp.float32)
                for k in range(2)
            ]
            out = dot3(lax.concatenate(vectors, 1), turn)
            stay_ref[rows:] = out[:, :half]
            leave_ref[rows:] = out[:, half:]

    return call(
        body, facts, rotation + [rows_of], (shape(rows + vector_rows, half),) * 2
    )


def turn(facts, rotation, blocks, own, own_stay=None):
    rows, half = blocks[0].shape
    size = 2 * half
    extra = [] if own_stay is None else [own_stay]

    def body(f, rotation_ref, *refs):
        up_0, low_0, up_1, low_1 = [r[...] for r in refs[:4]]
        zero = f[CORE] == (0 if own else 1)
        upper_leaves = jnp.where(zero, f[FIRST], 1) == 1
        turned = swapped(upper_leaves, rotation_ref[:size], 1)
        columns = lax.concatenate(
            [jnp.where(zero, up_0, up_1), jnp.where(zero, low_0, low_1)], 1
        )
        out = dot3(columns, turned)
        outs = refs[4 + len(extra) :]
        outs[0][...] = out[:, :half]
        outs[1][...] = out[:, half:]
        if extra:
            outs[2][...] = jnp.where(f[CORE] == f[X], refs[4][...], out[:, :half])

    return call(
        body, facts, [rotation] + blocks + extra,
        (shape(rows, half),) * (2 + len(extra)),
    )


def put_cross(f, refs, zero, one):
    core = f[CORE] == 0
    refs[0][...] = jnp.where(core, zero, one)
    refs[1][...] = jnp.where(core, one, zero)


def cross_gram(facts, own, others, position, part, half):
    rows = own[0].shape[0]
    pieces = len(others)

    def body(f, *refs):
        own_refs = [[r] for r in refs[:3]]
        other_refs = [refs[3 + k : 3 + 3 * pieces : 3] for k in range(3)]
        up_0, low_0, up_1, low_1 = refs[5 + 3 * pieces :]

        def fill(target, sources):
            at = 0
            for ref in sources:
                target[at : at + ref.shape[0]] = ref[...]
                at += ref.shape[0]

        first, last = f[FIRST] == 1, f[LAST] == 1
        for x, near, far in ((0, own_refs, other_refs), (1, other_refs, own_refs)):
            here = f[position] == x

            @pl.when(here)
            def _():
                fill(up_1, near[0])
                fill(low_0, far[0])

            @pl.when(here & first)
            def _():
                fill(up_0, near[1])

            @pl.when(here & ~first)
            def _():
                fill(up_0, far[2])

            @pl.when(here & last)
            def _():
                fill(low_1, far[1])

            @pl.when(here & ~last)
            def _():
                fill(low_1, near[2])

        put_cross(
            f,
            refs[3 + 3 * pieces :],
            dot3_tn(up_0[:part], low_0[:part]),
            dot3_tn(up_1[:part], low_1[:part]),
        )

    outs = (shape(half, half),) * 2 + (shape(rows, half),) * 4
    return call(body, facts, own + sum(others, []), outs)


def give_arrived(facts, own, other, rows, half):
    def body(f, *refs):
        out_ref = refs[4]
        near = f[CORE] == f[X]
        edge = jnp.where(f[X] == 0, f[LAST], f[FIRST]) == 1
        for ref, here in zip(
            refs, (~near & edge, near & ~edge, near & edge, ~near & ~edge)
        ):

            @pl.when(here)
            def _():
                out_ref[...] = ref[:rows]

    return call(body, facts, own[1:] + other[1:], shape(rows, half))


def give(facts, blocks, start, stop, half):
    def body(f, up_0_ref, low_1_ref, out_ref):
        out_ref[...] = jnp.where(
            f[X] == 0, low_1_ref[start:stop], up_0_ref[start:stop]
        )

    return call(
        body, facts, [blocks[0], blocks[3]], shape(stop - start, half)
    )


def final_turn(f, own_ref, other_ref):
    rotation = jnp.where(f[CORE] == f[X], own_ref[...], other_ref[...])
    return split(swapped(f[X] == 1, rotation, 0))


def final_product(moved, native, turned):
    return dot3(lax.concatenate([moved, native], 1), turned)


def put_rows(copies, sems, source, target, here, there, value):
    rows = value.shape[0]
    source[here : here + rows] = value
    copy = pltpu.make_async_copy(
        source.at[here : here + rows],
        target.at[pl.ds(pl.multiple_of(there, 8), rows)],
        sems.at[len(copies)],
    )
    copies.append(copy)
    copy.start()


def finish_call(body, facts, inputs, outputs, outs, rows, vector_rows, size):
    vmem = pl.BlockSpec(memory_space=pltpu.VMEM)
    hbm = pl.BlockSpec(memory_space=pl.ANY)
    first = 1 + len(inputs)
    return pl.pallas_call(
        body,
        out_shape=outs,
        in_specs=[pl.BlockSpec(memory_space=pltpu.SMEM)]
        + [vmem] * len(inputs)
        + [hbm] * len(outputs),
        out_specs=(hbm, hbm, vmem)[: len(outs)],
        input_output_aliases={first + k: k for k in range(len(outputs))},
        cost_estimate=pl.CostEstimate(flops=1, transcendentals=0, bytes_accessed=1),
        scratch_shapes=[
            pltpu.VMEM((rows, size), jnp.float32),
            pltpu.VMEM((vector_rows, size), jnp.float32),
            pltpu.SemaphoreType.DMA((4,)),
        ],
        compiler_params=pltpu.CompilerParams(vmem_limit_bytes=24 << 20),
    )(facts, *inputs, *outputs)


def finish_kept(facts, packs, blocks, native, got_top, part, half):
    size = 2 * half
    vector_rows = blocks[0].shape[0] - part
    top = got_top.shape[0]

    def body(f, own_ref, other_ref, *refs):
        x = f[X]
        turned = final_turn(f, own_ref, other_ref)
        native_ref, top_ref, out_ref, vectors_ref, out, vectors, sems = refs[4:]
        copies = []

        def kept(rows):
            up_0, low_0, up_1, low_1 = [r[rows] for r in refs[:4]]
            return final_product(
                jnp.where(x == 0, up_0, low_1),
                jnp.where(x == 0, low_0, up_1),
                turned,
            )

        def put(*args):
            put_rows(copies, sems, *args)

        middle = part // 2
        put(out, out_ref, 0, x * part, kept(slice(0, middle)))
        put(out, out_ref, middle, x * part + middle, kept(slice(middle, part)))
        value = final_product(top_ref[...], native_ref[:top], turned)
        put(out, out_ref, part, (1 - x) * part, value)
        put(vectors, vectors_ref, 0, x * vector_rows, kept(slice(part, None)))
        for copy in copies:
            copy.wait()

    outs = (shape(2 * part, size), shape(2 * vector_rows, size))
    inputs = packs + blocks + [native, got_top]
    return finish_call(
        body, facts, inputs, [], outs, part + top, vector_rows, size
    )


def finish_rest(facts, packs, squares, outputs, native, got_rest, part, half):
    size = 2 * half
    vector_rows = native.shape[0] - part
    rest = got_rest.shape[0] - vector_rows
    top = part - rest

    def body(f, own_ref, other_ref, native_ref, rest_ref, *refs):
        x = f[X]
        turned = final_turn(f, own_ref, other_ref)
        total = jnp.where(f[CORE] == x, refs[0][:1], refs[1][:1])
        out_ref, vectors_ref, singular_ref, out, vectors, sems = refs[4:]
        singular_ref[...] = jnp.sqrt(jnp.maximum(total, 0.0) + 1e-06)
        copies = []
        value = final_product(rest_ref[:rest], native_ref[top:part], turned)
        put_rows(copies, sems, out, out_ref, 0, (1 - x) * part + top, value)
        value = final_product(rest_ref[rest:], native_ref[part:], turned)
        put_rows(copies, sems, vectors, vectors_ref, 0, (1 - x) * vector_rows, value)
        for copy in copies:
            copy.wait()

    outs = (shape(2 * part, size), shape(2 * vector_rows, size), shape(1, size))
    inputs = packs + [native, got_rest] + squares
    return finish_call(
        body, facts, inputs, outputs, outs, rest, vector_rows, size
    )


def per_device(sector, block_label):
    local_rows, size = sector.shape
    half = size // 2
    part = local_rows // 2
    pairs = lax.axis_size("pair")
    row_count = lax.axis_size("row")
    vector_rows = pairs * size // row_count // 2
    pair_index = lax.axis_index("pair")
    row_index = lax.axis_index("row")
    x = pair_index % 2
    group = pair_index // 2
    core = row_index % 2

    def permute(block, route):
        moves = [
            (a * row_count + b, c * row_count + d) for (a, b), (c, d) in route
        ]
        return lax.ppermute(block, ("pair", "row"), moves)

    devices = [(p, r) for p in range(pairs) for r in range(row_count)]

    def exchange(block, over_pair, over_row):
        return permute(
            block, [((p ^ over_pair, r ^ over_row), (p, r)) for p, r in devices]
        )

    def shift(block, leftward):
        moves = []
        for p, r in devices:
            source = p + 2 if leftward(p, r) else p - 2
            if 0 <= source < pairs:
                moves.append(((source, r), (p, r)))
        return permute(block, moves)

    def pass_diagonal(block):
        moves = []
        for p, r in devices:
            other = p + 2 if r % 2 else p - 2
            inside = 0 <= other < pairs
            moves.append(((other, r ^ 1) if inside else (p, r), (p, r)))
        return permute(block, [((a, b), c) for (a, b), c in moves])

    def first_diagonal(block, leaves):
        moves = []
        for p, r in devices:
            c, even = r % 2, p - p % 2
            if leaves:
                source = even - 1 if c == 0 else even + 2
                if not 0 <= source < pairs:
                    source = even + c
            else:
                source = even + 1 - c
            moves.append(((source, r - c + p % 2), (p, r)))
        return permute(block, moves)

    def sum_rows(block):
        bit = 4
        while bit < row_count:
            block = block + exchange(block, 0, bit)
            bit *= 2
        return block

    names = jnp.arange(16, dtype=jnp.int32)
    facts = jnp.zeros((16,), jnp.int32)
    for name, value in (
        (X, x),
        (CORE, core),
        (FIRST, group == 0),
        (LAST, group == pairs // 2 - 1),
        (VROW, (row_index * 2 + x) * vector_rows),
        (EVEN, group % 2 == 0),
    ):
        facts = jnp.where(names == name, value.astype(jnp.int32), facts)
    labels = lax.dynamic_slice_in_dim(block_label, 4 * group, 4)
    facts = lax.dynamic_update_slice_in_dim(facts, labels, LABEL, 0)

    def together(*arrays):
        return lax.optimization_barrier(arrays)

    top_give, rest_give = give_rows(sector, part * 3 // 4)
    got_top = exchange(top_give, 1, 0)
    own = first_gram(sector, half)
    own = sum_rows(own + exchange(own, 0, 1))
    rotation, gram, rotation_half = first_rotation(facts, own, exchange(own, 0, 2), half)

    for sweep_round in range(ROUNDS - 1):
        last_move = sweep_round == ROUNDS - 2
        if sweep_round == 0:
            other_half = exchange(rotation_half, 1, 0)
            other_rotation = [other_half, exchange(other_half, 0, 1)]
            stay, leave = turn_rows(
                facts, [rotation], sector, vector_rows, half, True
            )
            leave, rest_give = together(leave, rest_give)
            got_rest = exchange(rest_give, 1, 0)
            own = [stay, leave, shift(leave, lambda p, r: p % 2 == 0)]
            others = []
            for got, below in ((got_top, 0), (got_rest, vector_rows)):
                stay, leave = turn_rows(facts, other_rotation, got, below, half, False)
                others.append([stay, leave, shift(leave, lambda p, r: p % 2 == 1)])
            leave, stay = turned_gram(facts, gram, rotation, X)
            diagonals = [first_diagonal(leave, True), first_diagonal(stay, False)]
            *grams, up_0, low_0, up_1, low_1 = cross_gram(
                facts, own, others, X, part, half
            )
        else:
            other_rotation = exchange(rotation, 0, 1)
            stay, leave = turn(facts, rotation, blocks, True)
            own = [stay, leave, shift(leave, lambda p, r: r % 2 == 0)]
            stay, leave, *native = turn(
                facts, other_rotation, blocks, False, stay if last_move else None
            )
            others = [[stay, leave, shift(leave, lambda p, r: r % 2 == 1)]]
            leave, stay = turned_gram(facts, gram, rotation, CORE)
            diagonals = [pass_diagonal(leave), exchange(stay, 0, 1)]
            if last_move:
                native = exchange(native[0], 1, 0)
                top = part * 5 // 8
                top_give = give_arrived(facts, own, others[0], top, half)
                own[2], others[0][2], top_give, *diagonals = together(
                    own[2], others[0][2], top_give, *diagonals
                )
                got_top = exchange(top_give, 1, 0)
            *grams, up_0, low_0, up_1, low_1 = cross_gram(
                facts, own, others, CORE, part, half
            )
        blocks = [up_0, low_0, up_1, low_1]
        if last_move:
            grams[1], native = together(grams[1], native)
        else:
            grams[1], *diagonals = together(grams[1], *diagonals)
        own = sum_rows(grams[0] + exchange(grams[1], 0, 1))
        parts = [own, exchange(own, 0, 2), exchange(own, 1, 0), exchange(own, 1, 2)]
        if last_move:
            rest_give = give(facts, blocks, top, part + vector_rows, half)
            *parts, got_top, rest_give = together(*parts, got_top, rest_give)
            got_rest = exchange(rest_give, 1, 0)
        rotation, gram = later_rotation(facts, parts, diagonals, half)
    packs = [rotation, exchange(rotation, 0, 1)]
    squares = squares_of(facts, gram, rotation)
    squares = [squares, exchange(squares, 0, 1)]
    outputs = list(finish_kept(facts, packs, blocks, native, got_top, part, half))
    rotated, vectors_out, singular = finish_rest(
        facts, packs, squares, outputs, native, got_rest, part, half
    )
    return rotated, vectors_out, singular.reshape(size)


def solution(mesh):
    placed = (P("row", "pair"), P())
    return jax.shard_map(
        per_device,
        mesh=mesh,
        in_specs=placed,
        out_specs=(P("row", "pair"), P("row", "pair"), P("pair")),
        check_vma=False,
    )
```

```python
import jax
import jax.numpy as jnp
from jax import lax
from jax.experimental import pallas as pl
from jax.experimental.pallas import tpu as pltpu
from jax.sharding import PartitionSpec as P

ROUNDS = 4
NEWTON = 16

highest = lax.Precision.HIGHEST

TARGET = 2.0**-12
REACHES = [
    (2.0 / (TARGET ** -(2.0**-j) - 1.0)) ** 2 for j in range(NEWTON)
]

X, CORE, FIRST, LAST, VROW, LABEL, EVEN = 0, 1, 2, 3, 4, 5, 9


def dot(a, b, precision=highest):
    return lax.dot_general(
        a, b, (((1,), (0,)), ((), ())), precision=precision,
        preferred_element_type=jnp.float32,
    )


def split(a):
    high = a.astype(jnp.bfloat16)
    return high, (a - high.astype(jnp.float32)).astype(jnp.bfloat16)


def dot3(a, b):
    a_high, a_low = a if isinstance(a, tuple) else split(a)
    b_high, b_low = b if isinstance(b, tuple) else split(b)
    small = dot(a_high, b_low, None) + dot(a_low, b_high, None)
    return dot(a_high, b_high, None) + small


def dot_tn(a, b):
    return lax.dot_general(
        a, b, (((0,), (0,)), ((), ())), precision=highest,
        preferred_element_type=jnp.float32,
    )


def dot3_tn(a, b):
    def product(left, right):
        return lax.dot_general(
            left, right, (((0,), (0,)), ((), ())),
            preferred_element_type=jnp.float32,
        )

    a_high, a_low = split(a)
    b_high, b_low = split(b)
    small = product(a_high, b_low) + product(a_low, b_high)
    return product(a_high, b_high) + small


def shape(*dims):
    return jax.ShapeDtypeStruct(dims, jnp.float32)


def call(body, facts, inputs, outs, scratch=(), limit=24):
    return pl.pallas_call(
        body,
        out_shape=outs,
        in_specs=[pl.BlockSpec(memory_space=pltpu.SMEM)]
        + [pl.BlockSpec(memory_space=pltpu.VMEM)] * len(inputs),
        out_specs=jax.tree.map(
            lambda _: pl.BlockSpec(memory_space=pltpu.VMEM), outs
        ),
        scratch_shapes=list(scratch),
        compiler_params=pltpu.CompilerParams(vmem_limit_bytes=limit << 20),
    )(facts, *inputs)


def first_gram(sector, half):
    def body(x_ref, out_ref):
        x = x_ref[...]
        g = dot3_tn(x, x)
        out_ref[:half] = g[:half, :half]
        out_ref[half : 2 * half] = g[:half, half:]
        out_ref[2 * half :] = g[half:, half:]

    vmem = pl.BlockSpec(memory_space=pltpu.VMEM)
    return pl.pallas_call(
        body,
        out_shape=shape(3 * half, half),
        in_specs=[vmem],
        out_specs=vmem,
        compiler_params=pltpu.CompilerParams(vmem_limit_bytes=24 << 20),
    )(sector)


def give_rows(sector, top, pieces=8):
    rows, width = sector.shape
    part = rows // 2
    step = part // pieces

    def body(x_ref, top_ref, rest_ref, sems):
        start = (1 - lax.axis_index("pair") % 2) * part
        copies = []
        for k in range(pieces):
            at = k * step
            target, here = (top_ref, at) if at < top else (rest_ref, at - top)
            source = x_ref.at[pl.ds(pl.multiple_of(start + at, 8), step)]
            copies.append(
                pltpu.make_async_copy(
                    source, target.at[here : here + step], sems.at[k]
                )
            )
            copies[-1].start()
        for copy in copies:
            copy.wait()

    return pl.pallas_call(
        body,
        out_shape=(shape(top, width), shape(part - top, width)),
        in_specs=[pl.BlockSpec(memory_space=pl.ANY)],
        out_specs=(pl.BlockSpec(memory_space=pltpu.VMEM),) * 2,
        scratch_shapes=[pltpu.SemaphoreType.DMA((pieces,))],
    )(sector)


def rotate_of(gram, x_ref, e_ref):
    size = gram.shape[0]
    rows = lax.broadcasted_iota(jnp.int32, (size, size), 0)
    cols = lax.broadcasted_iota(jnp.int32, (size, size), 1)
    identity = (rows == cols).astype(jnp.float32)
    only = jnp.where(rows == cols, gram, 0.0)
    g_j = jnp.sum(only, axis=0, keepdims=True)
    g_i = jnp.sum(only, axis=1, keepdims=True)
    spread = g_j - g_i
    summed = g_j + g_i
    skew = gram * spread / (spread * spread + 2.0 * gram * gram + 0.01 * summed * summed)
    skew_parts = split(skew)
    square = dot3(skew_parts, skew_parts)
    whole = 0.25 * jnp.sum(skew * skew)
    paired = 0.03125 * jnp.sum(square * square) * 1.001
    reach = jnp.minimum(whole * whole, paired)
    steps = jnp.int32(0)
    for limit in REACHES:
        steps = steps + (reach > limit).astype(jnp.int32)
    fixes = 1 + (steps > 7).astype(jnp.int32) + 2 * (steps > 9).astype(jnp.int32)
    scale = 2.0 / (2.0 + jnp.sqrt(jnp.full((size, size), reach, jnp.float32)))
    residual = identity - scale * (identity - 0.25 * square)
    x_ref[...] = scale * (identity + residual)
    residual_parts = split(residual)
    e_ref[...] = dot3(residual_parts, residual_parts)

    def step(_, carry):
        e = split(e_ref[...])
        x = x_ref[...]
        x_ref[...] = x + dot3(x, e)
        e_ref[...] = dot3(e, e)
        return carry

    lax.fori_loop(0, jnp.maximum(steps - 1, 0), step, jnp.int32(0))
    x = x_ref[...]
    x_ref[...] = x + 0.5 * dot3(x, skew_parts)

    def fix(_, carry):
        x = x_ref[...]
        x_ref[...] = x + dot3(x, identity - (x - 0.5 * dot(skew, x)))
        return carry

    lax.fori_loop(0, fixes, fix, jnp.int32(0))
    return 2.0 * x_ref[...] - identity


def squares_of(facts, gram, rotation):
    size = gram.shape[0]

    def body(f, gram_ref, rotation_ref, out_ref):
        rotation = rotation_ref[...]
        squares = rotation * dot(gram_ref[...], rotation)
        out_ref[...] = jnp.broadcast_to(
            jnp.sum(squares, axis=0, keepdims=True), (8, size)
        )

    return call(body, facts, [gram, rotation], shape(8, size))


def first_rotation(facts, own, other_y, half):
    size = 2 * half

    def body(f, own_ref, other_ref, rotation_ref, g_ref, half_ref, x_ref, e_ref):
        total = own_ref[...] + other_ref[...]
        g_ref[:half, :half] = total[:half]
        g_ref[:half, half:] = total[half : 2 * half]
        g_ref[half:, :half] = total[half : 2 * half].T
        g_ref[half:, half:] = total[2 * half :]
        rotation_ref[...] = rotate_of(g_ref[...], x_ref, e_ref)
        rotation = rotation_ref[...]
        half_ref[...] = jnp.where(f[CORE] == 0, rotation[:half], rotation[half:])

    square = pltpu.VMEM((size, size), jnp.float32)
    outs = (shape(size, size),) * 2 + (shape(half, size),)
    return call(body, facts, [own, other_y], outs, [square] * 2)


def later_rotation(facts, parts, diagonals, half):
    size = 2 * half

    def body(f, *refs):
        own, other_y, other_x, other_xy, foreign, native = [r[...] for r in refs[:6]]
        rotation_ref, g_ref, x_ref, e_ref = refs[6:]
        cross = (own + other_y) + (other_x + other_xy)
        core = f[CORE] == 0
        g_ref[:half, :half] = jnp.where(core, foreign, native)
        g_ref[:half, half:] = cross
        g_ref[half:, :half] = cross.T
        g_ref[half:, half:] = jnp.where(core, native, foreign)
        rotation_ref[...] = rotate_of(g_ref[...], x_ref, e_ref)

    square = pltpu.VMEM((size, size), jnp.float32)
    return call(
        body,
        facts,
        parts + diagonals,
        (shape(size, size),) * 2,
        [square] * 2,
    )


def turned_gram(facts, gram, rotation, position):
    size = gram.shape[0]
    half = size // 2

    def body(f, gram_ref, rotation_ref, leave_ref, stay_ref):
        rotation = rotation_ref[...]
        turned = dot(gram_ref[...], rotation)
        upper = dot_tn(rotation[:, :half], turned[:, :half])
        lower = dot_tn(rotation[:, half:], turned[:, half:])
        lower_leaves = (f[position] == 0) & (f[FIRST] == 0)
        leave_ref[...] = jnp.where(lower_leaves, lower, upper)
        stay_ref[...] = jnp.where(lower_leaves, upper, lower)

    return call(body, facts, [gram, rotation], (shape(half, half),) * 2)


def swapped(flag, matrix, axis):
    half = matrix.shape[axis] // 2
    a = lax.slice_in_dim(matrix, 0, half, axis=axis)
    b = lax.slice_in_dim(matrix, half, 2 * half, axis=axis)
    return jnp.where(flag, lax.concatenate([b, a], axis), matrix)


def turn_rows(facts, rotation, rows_of, vector_rows, half, own):
    rows = rows_of.shape[0] // 2 if own else rows_of.shape[0]

    def body(f, *refs):
        x_ref, stay_ref, leave_ref = refs[-3:]
        matrix = lax.concatenate([r[...] for r in refs[:-3]], 0)
        if not own:
            matrix = swapped(f[CORE] == 1, matrix, 0)
        zero = f[X] == (0 if own else 1)
        upper_leaves = jnp.where(zero, f[FIRST], 1) == 1
        turn = split(swapped(upper_leaves, matrix, 1))
        here = pl.multiple_of(f[X] * rows, 8)
        out = dot3(x_ref[pl.ds(here, rows)] if own else x_ref[...], turn)
        stay_ref[:rows] = out[:, :half]
        leave_ref[:rows] = out[:, half:]
        if vector_rows:
            ids = f[VROW] + lax.broadcasted_iota(jnp.int32, (vector_rows, half), 0)
            cols = lax.broadcasted_iota(jnp.int32, (vector_rows, half), 1)
            position = jnp.where(zero, 0, 2)
            vectors = [
                (ids == f[LABEL + position + k] * half + cols).astype(jnp.float32)
                for k in range(2)
            ]
            out = dot3(lax.concatenate(vectors, 1), turn)
            stay_ref[rows:] = out[:, :half]
            leave_ref[rows:] = out[:, half:]

    return call(
        body, facts, rotation + [rows_of], (shape(rows + vector_rows, half),) * 2
    )


def turn(facts, rotation, blocks, own, own_stay=None):
    rows, half = blocks[0].shape
    size = 2 * half
    extra = [] if own_stay is None else [own_stay]

    def body(f, rotation_ref, *refs):
        up_0, low_0, up_1, low_1 = [r[...] for r in refs[:4]]
        zero = f[CORE] == (0 if own else 1)
        upper_leaves = jnp.where(zero, f[FIRST], 1) == 1
        turned = swapped(upper_leaves, rotation_ref[:size], 1)
        columns = lax.concatenate(
            [jnp.where(zero, up_0, up_1), jnp.where(zero, low_0, low_1)], 1
        )
        out = dot3(columns, turned)
        outs = refs[4 + len(extra) :]
        outs[0][...] = out[:, :half]
        outs[1][...] = out[:, half:]
        if extra:
            outs[2][...] = jnp.where(f[CORE] == f[X], refs[4][...], out[:, :half])

    return call(
        body, facts, [rotation] + blocks + extra,
        (shape(rows, half),) * (2 + len(extra)),
    )


def put_cross(f, refs, zero, one):
    core = f[CORE] == 0
    refs[0][...] = jnp.where(core, zero, one)
    refs[1][...] = jnp.where(core, one, zero)


def cross_gram(facts, own, others, position, part, half):
    rows = own[0].shape[0]
    pieces = len(others)

    def body(f, *refs):
        own_refs = [[r] for r in refs[:3]]
        other_refs = [refs[3 + k : 3 + 3 * pieces : 3] for k in range(3)]
        up_0, low_0, up_1, low_1 = refs[5 + 3 * pieces :]

        def fill(target, sources):
            at = 0
            for ref in sources:
                target[at : at + ref.shape[0]] = ref[...]
                at += ref.shape[0]

        first, last = f[FIRST] == 1, f[LAST] == 1
        for x, near, far in ((0, own_refs, other_refs), (1, other_refs, own_refs)):
            here = f[position] == x

            @pl.when(here)
            def _():
                fill(up_1, near[0])
                fill(low_0, far[0])

            @pl.when(here & first)
            def _():
                fill(up_0, near[1])

            @pl.when(here & ~first)
            def _():
                fill(up_0, far[2])

            @pl.when(here & last)
            def _():
                fill(low_1, far[1])

            @pl.when(here & ~last)
            def _():
                fill(low_1, near[2])

        put_cross(
            f,
            refs[3 + 3 * pieces :],
            dot3_tn(up_0[:part], low_0[:part]),
            dot3_tn(up_1[:part], low_1[:part]),
        )

    outs = (shape(half, half),) * 2 + (shape(rows, half),) * 4
    return call(body, facts, own + sum(others, []), outs)


def give_arrived(facts, own, other, rows, half):
    def body(f, *refs):
        out_ref = refs[4]
        near = f[CORE] == f[X]
        edge = jnp.where(f[X] == 0, f[LAST], f[FIRST]) == 1
        for ref, here in zip(
            refs, (~near & edge, near & ~edge, near & edge, ~near & ~edge)
        ):

            @pl.when(here)
            def _():
                out_ref[...] = ref[:rows]

    return call(body, facts, own[1:] + other[1:], shape(rows, half))


def give(facts, blocks, start, stop, half):
    def body(f, up_0_ref, low_1_ref, out_ref):
        out_ref[...] = jnp.where(
            f[X] == 0, low_1_ref[start:stop], up_0_ref[start:stop]
        )

    return call(
        body, facts, [blocks[0], blocks[3]], shape(stop - start, half)
    )


def final_turn(f, own_ref, other_ref):
    rotation = jnp.where(f[CORE] == f[X], own_ref[...], other_ref[...])
    return split(swapped(f[X] == 1, rotation, 0))


def final_product(moved, native, turned):
    return dot3(lax.concatenate([moved, native], 1), turned)


def put_rows(copies, sems, source, target, here, there, value):
    rows = value.shape[0]
    source[here : here + rows] = value
    copy = pltpu.make_async_copy(
        source.at[here : here + rows],
        target.at[pl.ds(pl.multiple_of(there, 8), rows)],
        sems.at[len(copies)],
    )
    copies.append(copy)
    copy.start()


def finish_call(body, facts, inputs, outputs, outs, rows, vector_rows, size):
    vmem = pl.BlockSpec(memory_space=pltpu.VMEM)
    hbm = pl.BlockSpec(memory_space=pl.ANY)
    first = 1 + len(inputs)
    return pl.pallas_call(
        body,
        out_shape=outs,
        in_specs=[pl.BlockSpec(memory_space=pltpu.SMEM)]
        + [vmem] * len(inputs)
        + [hbm] * len(outputs),
        out_specs=(hbm, hbm, vmem)[: len(outs)],
        input_output_aliases={first + k: k for k in range(len(outputs))},
        cost_estimate=pl.CostEstimate(flops=1, transcendentals=0, bytes_accessed=1),
        scratch_shapes=[
            pltpu.VMEM((rows, size), jnp.float32),
            pltpu.VMEM((vector_rows, size), jnp.float32),
            pltpu.SemaphoreType.DMA((4,)),
        ],
        compiler_params=pltpu.CompilerParams(vmem_limit_bytes=24 << 20),
    )(facts, *inputs, *outputs)


def finish_kept(facts, packs, squares, blocks, native, got_top, part, half):
    size = 2 * half
    vector_rows = blocks[0].shape[0] - part
    top = got_top.shape[0]

    def body(f, own_ref, other_ref, *refs):
        x = f[X]
        turned = final_turn(f, own_ref, other_ref)
        native_ref, top_ref = refs[4:6]
        total = jnp.where(f[CORE] == x, refs[6][:1], refs[7][:1])
        out_ref, vectors_ref, singular_ref, out, vectors, sems = refs[8:]
        singular_ref[...] = jnp.sqrt(jnp.maximum(total, 0.0) + 1e-06)
        copies = []

        def kept(rows):
            up_0, low_0, up_1, low_1 = [r[rows] for r in refs[:4]]
            return final_product(
                jnp.where(x == 0, up_0, low_1),
                jnp.where(x == 0, low_0, up_1),
                turned,
            )

        def put(*args):
            put_rows(copies, sems, *args)

        middle = part // 2
        put(out, out_ref, 0, x * part, kept(slice(0, middle)))
        put(out, out_ref, middle, x * part + middle, kept(slice(middle, part)))
        value = final_product(top_ref[...], native_ref[:top], turned)
        put(out, out_ref, part, (1 - x) * part, value)
        put(vectors, vectors_ref, 0, x * vector_rows, kept(slice(part, None)))
        for copy in copies:
            copy.wait()

    outs = (shape(2 * part, size), shape(2 * vector_rows, size), shape(1, size))
    inputs = packs + blocks + [native, got_top] + squares
    return finish_call(
        body, facts, inputs, [], outs, part + top, vector_rows, size
    )


def finish_rest(facts, packs, outputs, native, got_rest, part, half):
    size = 2 * half
    vector_rows = native.shape[0] - part
    rest = got_rest.shape[0] - vector_rows
    top = part - rest

    def body(f, own_ref, other_ref, native_ref, rest_ref, *refs):
        x = f[X]
        turned = final_turn(f, own_ref, other_ref)
        out_ref, vectors_ref, out, vectors, sems = refs[2:]
        copies = []
        value = final_product(rest_ref[:rest], native_ref[top:part], turned)
        put_rows(copies, sems, out, out_ref, 0, (1 - x) * part + top, value)
        value = final_product(rest_ref[rest:], native_ref[part:], turned)
        put_rows(copies, sems, vectors, vectors_ref, 0, (1 - x) * vector_rows, value)
        for copy in copies:
            copy.wait()

    outs = (shape(2 * part, size), shape(2 * vector_rows, size))
    inputs = packs + [native, got_rest]
    return finish_call(
        body, facts, inputs, outputs, outs, rest, vector_rows, size
    )


def per_device(sector, block_label):
    local_rows, size = sector.shape
    half = size // 2
    part = local_rows // 2
    pairs = lax.axis_size("pair")
    row_count = lax.axis_size("row")
    vector_rows = pairs * size // row_count // 2
    pair_index = lax.axis_index("pair")
    row_index = lax.axis_index("row")
    x = pair_index % 2
    group = pair_index // 2
    core = row_index % 2

    def permute(block, route):
        moves = [
            (a * row_count + b, c * row_count + d) for (a, b), (c, d) in route
        ]
        return lax.ppermute(block, ("pair", "row"), moves)

    devices = [(p, r) for p in range(pairs) for r in range(row_count)]

    def exchange(block, over_pair, over_row):
        return permute(
            block, [((p ^ over_pair, r ^ over_row), (p, r)) for p, r in devices]
        )

    def shift(block, leftward):
        moves = []
        for p, r in devices:
            source = p + 2 if leftward(p, r) else p - 2
            if 0 <= source < pairs:
                moves.append(((source, r), (p, r)))
        return permute(block, moves)

    def pass_diagonal(block):
        moves = []
        for p, r in devices:
            other = p + 2 if r % 2 else p - 2
            inside = 0 <= other < pairs
            moves.append(((other, r ^ 1) if inside else (p, r), (p, r)))
        return permute(block, [((a, b), c) for (a, b), c in moves])

    def first_diagonal(block, leaves):
        moves = []
        for p, r in devices:
            c, even = r % 2, p - p % 2
            if leaves:
                source = even - 1 if c == 0 else even + 2
                if not 0 <= source < pairs:
                    source = even + c
            else:
                source = even + 1 - c
            moves.append(((source, r - c + p % 2), (p, r)))
        return permute(block, moves)

    def sum_rows(block):
        bit = 4
        while bit < row_count:
            block = block + exchange(block, 0, bit)
            bit *= 2
        return block

    names = jnp.arange(16, dtype=jnp.int32)
    facts = jnp.zeros((16,), jnp.int32)
    for name, value in (
        (X, x),
        (CORE, core),
        (FIRST, group == 0),
        (LAST, group == pairs // 2 - 1),
        (VROW, (row_index * 2 + x) * vector_rows),
        (EVEN, group % 2 == 0),
    ):
        facts = jnp.where(names == name, value.astype(jnp.int32), facts)
    labels = lax.dynamic_slice_in_dim(block_label, 4 * group, 4)
    facts = lax.dynamic_update_slice_in_dim(facts, labels, LABEL, 0)

    def together(*arrays):
        return lax.optimization_barrier(arrays)

    top_give, rest_give = give_rows(sector, part * 3 // 4)
    got_top = exchange(top_give, 1, 0)
    own = first_gram(sector, half)
    own = sum_rows(own + exchange(own, 0, 1))
    rotation, gram, rotation_half = first_rotation(facts, own, exchange(own, 0, 2), half)

    for sweep_round in range(ROUNDS - 1):
        last_move = sweep_round == ROUNDS - 2
        if sweep_round == 0:
            other_half = exchange(rotation_half, 1, 0)
            other_rotation = [other_half, exchange(other_half, 0, 1)]
            stay, leave = turn_rows(
                facts, [rotation], sector, vector_rows, half, True
            )
            leave, rest_give = together(leave, rest_give)
            got_rest = exchange(rest_give, 1, 0)
            own = [stay, leave, shift(leave, lambda p, r: p % 2 == 0)]
            others = []
            for got, below in ((got_top, 0), (got_rest, vector_rows)):
                stay, leave = turn_rows(facts, other_rotation, got, below, half, False)
                others.append([stay, leave, shift(leave, lambda p, r: p % 2 == 1)])
            leave, stay = turned_gram(facts, gram, rotation, X)
            diagonals = [first_diagonal(leave, True), first_diagonal(stay, False)]
            *grams, up_0, low_0, up_1, low_1 = cross_gram(
                facts, own, others, X, part, half
            )
        else:
            other_rotation = exchange(rotation, 0, 1)
            stay, leave = turn(facts, rotation, blocks, True)
            own = [stay, leave, shift(leave, lambda p, r: r % 2 == 0)]
            stay, leave, *native = turn(
                facts, other_rotation, blocks, False, stay if last_move else None
            )
            others = [[stay, leave, shift(leave, lambda p, r: r % 2 == 1)]]
            leave, stay = turned_gram(facts, gram, rotation, CORE)
            diagonals = [pass_diagonal(leave), exchange(stay, 0, 1)]
            if last_move:
                native = exchange(native[0], 1, 0)
                top = part * 5 // 8
                top_give = give_arrived(facts, own, others[0], top, half)
                own[2], others[0][2], top_give, *diagonals = together(
                    own[2], others[0][2], top_give, *diagonals
                )
                got_top = exchange(top_give, 1, 0)
            *grams, up_0, low_0, up_1, low_1 = cross_gram(
                facts, own, others, CORE, part, half
            )
        blocks = [up_0, low_0, up_1, low_1]
        if last_move:
            grams[1], native = together(grams[1], native)
        else:
            grams[1], *diagonals = together(grams[1], *diagonals)
        own = sum_rows(grams[0] + exchange(grams[1], 0, 1))
        parts = [own, exchange(own, 0, 2), exchange(own, 1, 0), exchange(own, 1, 2)]
        if last_move:
            rest_give = give(facts, blocks, top, part + vector_rows, half)
            *parts, got_top, rest_give = together(*parts, got_top, rest_give)
            got_rest = exchange(rest_give, 1, 0)
        rotation, gram = later_rotation(facts, parts, diagonals, half)
    packs = [rotation, exchange(rotation, 0, 1)]
    squares = squares_of(facts, gram, rotation)
    squares = [squares, exchange(squares, 0, 1)]
    *outputs, singular = finish_kept(
        facts, packs, squares, blocks, native, got_top, part, half
    )
    rotated, vectors_out = finish_rest(
        facts, packs, outputs, native, got_rest, part, half
    )
    return rotated, vectors_out, singular.reshape(size)


def solution(mesh):
    placed = (P("row", "pair"), P())
    return jax.shard_map(
        per_device,
        mesh=mesh,
        in_specs=placed,
        out_specs=(P("row", "pair"), P("row", "pair"), P("pair")),
        check_vma=False,
    )
```

```python
import jax
import jax.numpy as jnp
from jax import lax
from jax.experimental import pallas as pl
from jax.experimental.pallas import tpu as pltpu
from jax.sharding import PartitionSpec as P

ROUNDS = 4
NEWTON = 16

highest = lax.Precision.HIGHEST

TARGET = 2.0**-12
REACHES = [
    (2.0 / (TARGET ** -(2.0**-j) - 1.0)) ** 2 for j in range(NEWTON)
]

X, CORE, FIRST, LAST, VROW, LABEL, EVEN = 0, 1, 2, 3, 4, 5, 9


def dot(a, b, precision=highest):
    return lax.dot_general(
        a, b, (((1,), (0,)), ((), ())), precision=precision,
        preferred_element_type=jnp.float32,
    )


def split(a):
    high = a.astype(jnp.bfloat16)
    return high, (a - high.astype(jnp.float32)).astype(jnp.bfloat16)


def dot3(a, b):
    a_high, a_low = a if isinstance(a, tuple) else split(a)
    b_high, b_low = b if isinstance(b, tuple) else split(b)
    small = dot(a_high, b_low, None) + dot(a_low, b_high, None)
    return dot(a_high, b_high, None) + small


def dot_tn(a, b):
    return lax.dot_general(
        a, b, (((0,), (0,)), ((), ())), precision=highest,
        preferred_element_type=jnp.float32,
    )


def dot3_tn(a, b):
    def product(left, right):
        return lax.dot_general(
            left, right, (((0,), (0,)), ((), ())),
            preferred_element_type=jnp.float32,
        )

    a_high, a_low = split(a)
    b_high, b_low = split(b)
    small = product(a_high, b_low) + product(a_low, b_high)
    return product(a_high, b_high) + small


def shape(*dims):
    return jax.ShapeDtypeStruct(dims, jnp.float32)


def call(body, facts, inputs, outs, scratch=(), limit=24):
    return pl.pallas_call(
        body,
        out_shape=outs,
        in_specs=[pl.BlockSpec(memory_space=pltpu.SMEM)]
        + [pl.BlockSpec(memory_space=pltpu.VMEM)] * len(inputs),
        out_specs=jax.tree.map(
            lambda _: pl.BlockSpec(memory_space=pltpu.VMEM), outs
        ),
        scratch_shapes=list(scratch),
        compiler_params=pltpu.CompilerParams(vmem_limit_bytes=limit << 20),
    )(facts, *inputs)


def first_gram(sector, half):
    def body(x_ref, out_ref):
        x = x_ref[...]
        g = dot3_tn(x, x)
        out_ref[:half] = g[:half, :half]
        out_ref[half : 2 * half] = g[:half, half:]
        out_ref[2 * half :] = g[half:, half:]

    vmem = pl.BlockSpec(memory_space=pltpu.VMEM)
    return pl.pallas_call(
        body,
        out_shape=shape(3 * half, half),
        in_specs=[vmem],
        out_specs=vmem,
        compiler_params=pltpu.CompilerParams(vmem_limit_bytes=24 << 20),
    )(sector)


def give_rows(sector, top, pieces=8):
    rows, width = sector.shape
    part = rows // 2
    step = part // pieces

    def body(x_ref, top_ref, rest_ref, sems):
        start = (1 - lax.axis_index("pair") % 2) * part
        copies = []
        for k in range(pieces):
            at = k * step
            target, here = (top_ref, at) if at < top else (rest_ref, at - top)
            source = x_ref.at[pl.ds(pl.multiple_of(start + at, 8), step)]
            copies.append(
                pltpu.make_async_copy(
                    source, target.at[here : here + step], sems.at[k]
                )
            )
            copies[-1].start()
        for copy in copies:
            copy.wait()

    return pl.pallas_call(
        body,
        out_shape=(shape(top, width), shape(part - top, width)),
        in_specs=[pl.BlockSpec(memory_space=pl.ANY)],
        out_specs=(pl.BlockSpec(memory_space=pltpu.VMEM),) * 2,
        scratch_shapes=[pltpu.SemaphoreType.DMA((pieces,))],
    )(sector)


def rotate_of(gram, x_ref, e_ref):
    size = gram.shape[0]
    rows = lax.broadcasted_iota(jnp.int32, (size, size), 0)
    cols = lax.broadcasted_iota(jnp.int32, (size, size), 1)
    identity = (rows == cols).astype(jnp.float32)
    only = jnp.where(rows == cols, gram, 0.0)
    g_j = jnp.sum(only, axis=0, keepdims=True)
    g_i = jnp.sum(only, axis=1, keepdims=True)
    spread = g_j - g_i
    summed = g_j + g_i
    skew = gram * spread / (spread * spread + 2.0 * gram * gram + 0.01 * summed * summed)
    skew_parts = split(skew)
    square = dot3(skew_parts, skew_parts)
    whole = 0.25 * jnp.sum(skew * skew)
    paired = 0.03125 * jnp.sum(square * square) * 1.001
    reach = jnp.minimum(whole * whole, paired)
    steps = jnp.int32(0)
    for limit in REACHES:
        steps = steps + (reach > limit).astype(jnp.int32)
    fixes = 1 + (steps > 7).astype(jnp.int32) + 2 * (steps > 9).astype(jnp.int32)
    scale = 2.0 / (2.0 + jnp.sqrt(jnp.full((size, size), reach, jnp.float32)))
    residual = identity - scale * (identity - 0.25 * square)
    x_ref[...] = scale * (identity + residual)
    residual_parts = split(residual)
    e_ref[...] = dot3(residual_parts, residual_parts)

    def step(_, carry):
        e = split(e_ref[...])
        x = x_ref[...]
        x_ref[...] = x + dot3(x, e)
        e_ref[...] = dot3(e, e)
        return carry

    lax.fori_loop(0, jnp.maximum(steps - 1, 0), step, jnp.int32(0))
    x = x_ref[...]
    x_ref[...] = x + 0.5 * dot3(x, skew_parts)

    def fix(_, carry):
        x = x_ref[...]
        x_ref[...] = x + dot3(x, identity - (x - 0.5 * dot(skew, x)))
        return carry

    lax.fori_loop(0, fixes, fix, jnp.int32(0))
    return 2.0 * x_ref[...] - identity


def squares_of(facts, gram, rotation):
    size = gram.shape[0]

    def body(f, gram_ref, rotation_ref, out_ref):
        rotation = rotation_ref[...]
        squares = rotation * dot(gram_ref[...], rotation)
        out_ref[...] = jnp.broadcast_to(
            jnp.sum(squares, axis=0, keepdims=True), (8, size)
        )

    return call(body, facts, [gram, rotation], shape(8, size))


def first_rotation(facts, own, other_y, half):
    size = 2 * half

    def body(f, own_ref, other_ref, rotation_ref, g_ref, half_ref, x_ref, e_ref):
        total = own_ref[...] + other_ref[...]
        g_ref[:half, :half] = total[:half]
        g_ref[:half, half:] = total[half : 2 * half]
        g_ref[half:, :half] = total[half : 2 * half].T
        g_ref[half:, half:] = total[2 * half :]
        rotation_ref[...] = rotate_of(g_ref[...], x_ref, e_ref)
        rotation = rotation_ref[...]
        half_ref[...] = jnp.where(f[CORE] == 0, rotation[:half], rotation[half:])

    square = pltpu.VMEM((size, size), jnp.float32)
    outs = (shape(size, size),) * 2 + (shape(half, size),)
    return call(body, facts, [own, other_y], outs, [square] * 2)


def later_rotation(facts, parts, diagonals, half):
    size = 2 * half

    def body(f, *refs):
        own, other_y, other_x, other_xy, foreign, native = [r[...] for r in refs[:6]]
        rotation_ref, g_ref, x_ref, e_ref = refs[6:]
        cross = (own + other_y) + (other_x + other_xy)
        core = f[CORE] == 0
        g_ref[:half, :half] = jnp.where(core, foreign, native)
        g_ref[:half, half:] = cross
        g_ref[half:, :half] = cross.T
        g_ref[half:, half:] = jnp.where(core, native, foreign)
        rotation_ref[...] = rotate_of(g_ref[...], x_ref, e_ref)

    square = pltpu.VMEM((size, size), jnp.float32)
    return call(
        body,
        facts,
        parts + diagonals,
        (shape(size, size),) * 2,
        [square] * 2,
    )


def turned_gram(facts, gram, rotation, position):
    size = gram.shape[0]
    half = size // 2

    def body(f, gram_ref, rotation_ref, leave_ref, stay_ref):
        rotation = rotation_ref[...]
        turned = dot(gram_ref[...], rotation)
        upper = dot_tn(rotation[:, :half], turned[:, :half])
        lower = dot_tn(rotation[:, half:], turned[:, half:])
        lower_leaves = (f[position] == 0) & (f[FIRST] == 0)
        leave_ref[...] = jnp.where(lower_leaves, lower, upper)
        stay_ref[...] = jnp.where(lower_leaves, upper, lower)

    return call(body, facts, [gram, rotation], (shape(half, half),) * 2)


def swapped(flag, matrix, axis):
    half = matrix.shape[axis] // 2
    a = lax.slice_in_dim(matrix, 0, half, axis=axis)
    b = lax.slice_in_dim(matrix, half, 2 * half, axis=axis)
    return jnp.where(flag, lax.concatenate([b, a], axis), matrix)


def turn_rows(facts, rotation, rows_of, vector_rows, half, own):
    rows = rows_of.shape[0] // 2 if own else rows_of.shape[0]

    def body(f, *refs):
        x_ref, stay_ref, leave_ref = refs[-3:]
        matrix = lax.concatenate([r[...] for r in refs[:-3]], 0)
        if not own:
            matrix = swapped(f[CORE] == 1, matrix, 0)
        zero = f[X] == (0 if own else 1)
        upper_leaves = jnp.where(zero, f[FIRST], 1) == 1
        turn = split(swapped(upper_leaves, matrix, 1))
        here = pl.multiple_of(f[X] * rows, 8)
        out = dot3(x_ref[pl.ds(here, rows)] if own else x_ref[...], turn)
        stay_ref[:rows] = out[:, :half]
        leave_ref[:rows] = out[:, half:]
        if vector_rows:
            ids = f[VROW] + lax.broadcasted_iota(jnp.int32, (vector_rows, half), 0)
            cols = lax.broadcasted_iota(jnp.int32, (vector_rows, half), 1)
            position = jnp.where(zero, 0, 2)
            vectors = [
                (ids == f[LABEL + position + k] * half + cols).astype(jnp.float32)
                for k in range(2)
            ]
            out = dot3(lax.concatenate(vectors, 1), turn)
            stay_ref[rows:] = out[:, :half]
            leave_ref[rows:] = out[:, half:]

    return call(
        body, facts, rotation + [rows_of], (shape(rows + vector_rows, half),) * 2
    )


def turn(facts, rotation, blocks, own, own_stay=None):
    rows, half = blocks[0].shape
    size = 2 * half
    extra = [] if own_stay is None else [own_stay]

    def body(f, rotation_ref, *refs):
        up_0, low_0, up_1, low_1 = [r[...] for r in refs[:4]]
        zero = f[CORE] == (0 if own else 1)
        upper_leaves = jnp.where(zero, f[FIRST], 1) == 1
        turned = swapped(upper_leaves, rotation_ref[:size], 1)
        columns = lax.concatenate(
            [jnp.where(zero, up_0, up_1), jnp.where(zero, low_0, low_1)], 1
        )
        out = dot3(columns, turned)
        outs = refs[4 + len(extra) :]
        outs[0][...] = out[:, :half]
        outs[1][...] = out[:, half:]
        if extra:
            outs[2][...] = jnp.where(f[CORE] == f[X], refs[4][...], out[:, :half])

    return call(
        body, facts, [rotation] + blocks + extra,
        (shape(rows, half),) * (2 + len(extra)),
    )


def put_cross(f, refs, zero, one):
    core = f[CORE] == 0
    refs[0][...] = jnp.where(core, zero, one)
    refs[1][...] = jnp.where(core, one, zero)


def cross_gram(facts, own, others, position, part, half):
    rows = own[0].shape[0]
    pieces = len(others)

    def body(f, *refs):
        own_refs = [[r] for r in refs[:3]]
        other_refs = [refs[3 + k : 3 + 3 * pieces : 3] for k in range(3)]
        up_0, low_0, up_1, low_1 = refs[5 + 3 * pieces :]

        def fill(target, sources):
            at = 0
            for ref in sources:
                target[at : at + ref.shape[0]] = ref[...]
                at += ref.shape[0]

        first, last = f[FIRST] == 1, f[LAST] == 1
        for x, near, far in ((0, own_refs, other_refs), (1, other_refs, own_refs)):
            here = f[position] == x

            @pl.when(here)
            def _():
                fill(up_1, near[0])
                fill(low_0, far[0])

            @pl.when(here & first)
            def _():
                fill(up_0, near[1])

            @pl.when(here & ~first)
            def _():
                fill(up_0, far[2])

            @pl.when(here & last)
            def _():
                fill(low_1, far[1])

            @pl.when(here & ~last)
            def _():
                fill(low_1, near[2])

        put_cross(
            f,
            refs[3 + 3 * pieces :],
            dot3_tn(up_0[:part], low_0[:part]),
            dot3_tn(up_1[:part], low_1[:part]),
        )

    outs = (shape(half, half),) * 2 + (shape(rows, half),) * 4
    return call(body, facts, own + sum(others, []), outs)


def give_arrived(facts, own, other, rows, half):
    def body(f, *refs):
        out_ref = refs[4]
        near = f[CORE] == f[X]
        edge = jnp.where(f[X] == 0, f[LAST], f[FIRST]) == 1
        for ref, here in zip(
            refs, (~near & edge, near & ~edge, near & edge, ~near & ~edge)
        ):

            @pl.when(here)
            def _():
                out_ref[...] = ref[:rows]

    return call(body, facts, own[1:] + other[1:], shape(rows, half))


def give(facts, blocks, start, stop, half):
    def body(f, up_0_ref, low_1_ref, out_ref):
        out_ref[...] = jnp.where(
            f[X] == 0, low_1_ref[start:stop], up_0_ref[start:stop]
        )

    return call(
        body, facts, [blocks[0], blocks[3]], shape(stop - start, half)
    )


def final_turn(f, own_ref, other_ref):
    rotation = jnp.where(f[CORE] == f[X], own_ref[...], other_ref[...])
    return split(swapped(f[X] == 1, rotation, 0))


def final_product(moved, native, turned):
    return dot3(lax.concatenate([moved, native], 1), turned)


def put_rows(copies, sems, source, target, here, there, value):
    rows = value.shape[0]
    source[here : here + rows] = value
    copy = pltpu.make_async_copy(
        source.at[here : here + rows],
        target.at[pl.ds(pl.multiple_of(there, 8), rows)],
        sems.at[len(copies)],
    )
    copies.append(copy)
    copy.start()


def finish_call(body, facts, inputs, outputs, outs, rows, vector_rows, size):
    vmem = pl.BlockSpec(memory_space=pltpu.VMEM)
    hbm = pl.BlockSpec(memory_space=pl.ANY)
    first = 1 + len(inputs)
    return pl.pallas_call(
        body,
        out_shape=outs,
        in_specs=[pl.BlockSpec(memory_space=pltpu.SMEM)]
        + [vmem] * len(inputs)
        + [hbm] * len(outputs),
        out_specs=(hbm, hbm, vmem)[: len(outs)],
        input_output_aliases={first + k: k for k in range(len(outputs))},
        cost_estimate=pl.CostEstimate(flops=1, transcendentals=0, bytes_accessed=1),
        scratch_shapes=[
            pltpu.VMEM((rows, size), jnp.float32),
            pltpu.VMEM((vector_rows, size), jnp.float32),
            pltpu.SemaphoreType.DMA((4,)),
        ],
        compiler_params=pltpu.CompilerParams(vmem_limit_bytes=24 << 20),
    )(facts, *inputs, *outputs)


def finish_kept(facts, packs, squares, blocks, native, got_top, part, half):
    size = 2 * half
    vector_rows = blocks[0].shape[0] - part
    top = got_top.shape[0]

    def body(f, own_ref, other_ref, *refs):
        x = f[X]
        turned = final_turn(f, own_ref, other_ref)
        native_ref, top_ref = refs[4:6]
        total = jnp.where(f[CORE] == x, refs[6][:1], refs[7][:1])
        out_ref, vectors_ref, singular_ref, out, vectors, sems = refs[8:]
        singular_ref[...] = jnp.sqrt(jnp.maximum(total, 0.0) + 1e-06)
        copies = []

        def kept(rows):
            up_0, low_0, up_1, low_1 = [r[rows] for r in refs[:4]]
            return final_product(
                jnp.where(x == 0, up_0, low_1),
                jnp.where(x == 0, low_0, up_1),
                turned,
            )

        def put(*args):
            put_rows(copies, sems, *args)

        middle = part // 2
        put(out, out_ref, 0, x * part, kept(slice(0, middle)))
        put(out, out_ref, middle, x * part + middle, kept(slice(middle, part)))
        value = final_product(top_ref[...], native_ref[:top], turned)
        put(out, out_ref, part, (1 - x) * part, value)
        put(vectors, vectors_ref, 0, x * vector_rows, kept(slice(part, None)))
        for copy in copies:
            copy.wait()

    outs = (shape(2 * part, size), shape(2 * vector_rows, size), shape(1, size))
    inputs = packs + blocks + [native, got_top] + squares
    return finish_call(
        body, facts, inputs, [], outs, part + top, vector_rows, size
    )


def finish_rest(facts, packs, outputs, native, got_rest, part, half):
    size = 2 * half
    vector_rows = native.shape[0] - part
    rest = got_rest.shape[0] - vector_rows
    top = part - rest

    def body(f, own_ref, other_ref, native_ref, rest_ref, *refs):
        x = f[X]
        turned = final_turn(f, own_ref, other_ref)
        out_ref, vectors_ref, out, vectors, sems = refs[2:]
        copies = []
        value = final_product(rest_ref[:rest], native_ref[top:part], turned)
        put_rows(copies, sems, out, out_ref, 0, (1 - x) * part + top, value)
        value = final_product(rest_ref[rest:], native_ref[part:], turned)
        put_rows(copies, sems, vectors, vectors_ref, 0, (1 - x) * vector_rows, value)
        for copy in copies:
            copy.wait()

    outs = (shape(2 * part, size), shape(2 * vector_rows, size))
    inputs = packs + [native, got_rest]
    return finish_call(
        body, facts, inputs, outputs, outs, rest, vector_rows, size
    )


def per_device(sector, block_label):
    local_rows, size = sector.shape
    half = size // 2
    part = local_rows // 2
    pairs = lax.axis_size("pair")
    row_count = lax.axis_size("row")
    vector_rows = pairs * size // row_count // 2
    pair_index = lax.axis_index("pair")
    row_index = lax.axis_index("row")
    x = pair_index % 2
    group = pair_index // 2
    core = row_index % 2

    def permute(block, route):
        moves = [
            (a * row_count + b, c * row_count + d) for (a, b), (c, d) in route
        ]
        return lax.ppermute(block, ("pair", "row"), moves)

    devices = [(p, r) for p in range(pairs) for r in range(row_count)]

    def exchange(block, over_pair, over_row):
        return permute(
            block, [((p ^ over_pair, r ^ over_row), (p, r)) for p, r in devices]
        )

    def shift(block, leftward):
        moves = []
        for p, r in devices:
            source = p + 2 if leftward(p, r) else p - 2
            if 0 <= source < pairs:
                moves.append(((source, r), (p, r)))
        return permute(block, moves)

    def pass_diagonal(block):
        moves = []
        for p, r in devices:
            other = p + 2 if r % 2 else p - 2
            inside = 0 <= other < pairs
            moves.append(((other, r ^ 1) if inside else (p, r), (p, r)))
        return permute(block, [((a, b), c) for (a, b), c in moves])

    def first_diagonal(block, leaves):
        moves = []
        for p, r in devices:
            c, even = r % 2, p - p % 2
            if leaves:
                source = even - 1 if c == 0 else even + 2
                if not 0 <= source < pairs:
                    source = even + c
            else:
                source = even + 1 - c
            moves.append(((source, r - c + p % 2), (p, r)))
        return permute(block, moves)

    def sum_rows(block):
        bit = 4
        while bit < row_count:
            block = block + exchange(block, 0, bit)
            bit *= 2
        return block

    names = jnp.arange(16, dtype=jnp.int32)
    facts = jnp.zeros((16,), jnp.int32)
    for name, value in (
        (X, x),
        (CORE, core),
        (FIRST, group == 0),
        (LAST, group == pairs // 2 - 1),
        (VROW, (row_index * 2 + x) * vector_rows),
        (EVEN, group % 2 == 0),
    ):
        facts = jnp.where(names == name, value.astype(jnp.int32), facts)
    labels = lax.dynamic_slice_in_dim(block_label, 4 * group, 4)
    facts = lax.dynamic_update_slice_in_dim(facts, labels, LABEL, 0)

    def together(*arrays):
        return lax.optimization_barrier(arrays)

    top_give, rest_give = give_rows(sector, part * 3 // 4)
    got_top = exchange(top_give, 1, 0)
    own = first_gram(sector, half)
    own = sum_rows(own + exchange(own, 0, 1))
    rotation, gram, rotation_half = first_rotation(facts, own, exchange(own, 0, 2), half)

    for sweep_round in range(ROUNDS - 1):
        last_move = sweep_round == ROUNDS - 2
        if sweep_round == 0:
            other_half = exchange(rotation_half, 1, 0)
            other_rotation = [other_half, exchange(other_half, 0, 1)]
            stay, leave = turn_rows(
                facts, [rotation], sector, vector_rows, half, True
            )
            leave, rest_give = together(leave, rest_give)
            got_rest = exchange(rest_give, 1, 0)
            own = [stay, leave, shift(leave, lambda p, r: p % 2 == 0)]
            others = []
            for got, below in ((got_top, 0), (got_rest, vector_rows)):
                stay, leave = turn_rows(facts, other_rotation, got, below, half, False)
                others.append([stay, leave, shift(leave, lambda p, r: p % 2 == 1)])
            leave, stay = turned_gram(facts, gram, rotation, X)
            diagonals = [first_diagonal(leave, True), first_diagonal(stay, False)]
            *grams, up_0, low_0, up_1, low_1 = cross_gram(
                facts, own, others, X, part, half
            )
        else:
            other_rotation = exchange(rotation, 0, 1)
            stay, leave = turn(facts, rotation, blocks, True)
            own = [stay, leave, shift(leave, lambda p, r: r % 2 == 0)]
            stay, leave, *native = turn(
                facts, other_rotation, blocks, False, stay if last_move else None
            )
            others = [[stay, leave, shift(leave, lambda p, r: r % 2 == 1)]]
            leave, stay = turned_gram(facts, gram, rotation, CORE)
            diagonals = [pass_diagonal(leave), exchange(stay, 0, 1)]
            if last_move:
                native = exchange(native[0], 1, 0)
                top = part // 2
                top_give = give_arrived(facts, own, others[0], top, half)
                own[2], others[0][2], top_give, *diagonals = together(
                    own[2], others[0][2], top_give, *diagonals
                )
                got_top = exchange(top_give, 1, 0)
            *grams, up_0, low_0, up_1, low_1 = cross_gram(
                facts, own, others, CORE, part, half
            )
        blocks = [up_0, low_0, up_1, low_1]
        if last_move:
            grams[1], native = together(grams[1], native)
        else:
            grams[1], *diagonals = together(grams[1], *diagonals)
        own = sum_rows(grams[0] + exchange(grams[1], 0, 1))
        parts = [own, exchange(own, 0, 2), exchange(own, 1, 0), exchange(own, 1, 2)]
        if last_move:
            rest_give = give(facts, blocks, top, part + vector_rows, half)
            *parts, got_top, rest_give = together(*parts, got_top, rest_give)
            got_rest = exchange(rest_give, 1, 0)
        rotation, gram = later_rotation(facts, parts, diagonals, half)
    packs = [rotation, exchange(rotation, 0, 1)]
    squares = squares_of(facts, gram, rotation)
    squares = [squares, exchange(squares, 0, 1)]
    *outputs, singular = finish_kept(
        facts, packs, squares, blocks, native, got_top, part, half
    )
    rotated, vectors_out = finish_rest(
        facts, packs, outputs, native, got_rest, part, half
    )
    return rotated, vectors_out, singular.reshape(size)


def solution(mesh):
    placed = (P("row", "pair"), P())
    return jax.shard_map(
        per_device,
        mesh=mesh,
        in_specs=placed,
        out_specs=(P("row", "pair"), P("row", "pair"), P("pair")),
        check_vma=False,
    )
```

```python
import jax
import jax.numpy as jnp
from jax import lax
from jax.experimental import pallas as pl
from jax.experimental.pallas import tpu as pltpu
from jax.sharding import PartitionSpec as P

ROUNDS = 4
NEWTON = 16

highest = lax.Precision.HIGHEST

TARGET = 2.0**-12
REACHES = [
    (2.0 / (TARGET ** -(2.0**-j) - 1.0)) ** 2 for j in range(NEWTON)
]

X, CORE, FIRST, LAST, VROW, LABEL, EVEN = 0, 1, 2, 3, 4, 5, 9


def dot(a, b, precision=highest):
    return lax.dot_general(
        a, b, (((1,), (0,)), ((), ())), precision=precision,
        preferred_element_type=jnp.float32,
    )


def split(a):
    high = a.astype(jnp.bfloat16)
    return high, (a - high.astype(jnp.float32)).astype(jnp.bfloat16)


def dot3(a, b):
    a_high, a_low = a if isinstance(a, tuple) else split(a)
    b_high, b_low = b if isinstance(b, tuple) else split(b)
    small = dot(a_high, b_low, None) + dot(a_low, b_high, None)
    return dot(a_high, b_high, None) + small


def dot_tn(a, b):
    return lax.dot_general(
        a, b, (((0,), (0,)), ((), ())), precision=highest,
        preferred_element_type=jnp.float32,
    )


def shape(*dims):
    return jax.ShapeDtypeStruct(dims, jnp.float32)


def call(body, facts, inputs, outs, scratch=(), limit=24):
    return pl.pallas_call(
        body,
        out_shape=outs,
        in_specs=[pl.BlockSpec(memory_space=pltpu.SMEM)]
        + [pl.BlockSpec(memory_space=pltpu.VMEM)] * len(inputs),
        out_specs=jax.tree.map(
            lambda _: pl.BlockSpec(memory_space=pltpu.VMEM), outs
        ),
        scratch_shapes=list(scratch),
        compiler_params=pltpu.CompilerParams(vmem_limit_bytes=limit << 20),
    )(facts, *inputs)


def first_gram(sector, half):
    def body(x_ref, out_ref):
        x = x_ref[...]
        g = dot_tn(x, x)
        out_ref[:half] = g[:half, :half]
        out_ref[half : 2 * half] = g[:half, half:]
        out_ref[2 * half :] = g[half:, half:]

    vmem = pl.BlockSpec(memory_space=pltpu.VMEM)
    return pl.pallas_call(
        body,
        out_shape=shape(3 * half, half),
        in_specs=[vmem],
        out_specs=vmem,
        compiler_params=pltpu.CompilerParams(vmem_limit_bytes=24 << 20),
    )(sector)


def give_rows(sector, top, pieces=8):
    rows, width = sector.shape
    part = rows // 2
    step = part // pieces

    def body(x_ref, top_ref, rest_ref, sems):
        start = (1 - lax.axis_index("pair") % 2) * part
        copies = []
        for k in range(pieces):
            at = k * step
            target, here = (top_ref, at) if at < top else (rest_ref, at - top)
            source = x_ref.at[pl.ds(pl.multiple_of(start + at, 8), step)]
            copies.append(
                pltpu.make_async_copy(
                    source, target.at[here : here + step], sems.at[k]
                )
            )
            copies[-1].start()
        for copy in copies:
            copy.wait()

    return pl.pallas_call(
        body,
        out_shape=(shape(top, width), shape(part - top, width)),
        in_specs=[pl.BlockSpec(memory_space=pl.ANY)],
        out_specs=(pl.BlockSpec(memory_space=pltpu.VMEM),) * 2,
        scratch_shapes=[pltpu.SemaphoreType.DMA((pieces,))],
    )(sector)


def rotate_of(gram, x_ref, e_ref):
    size = gram.shape[0]
    rows = lax.broadcasted_iota(jnp.int32, (size, size), 0)
    cols = lax.broadcasted_iota(jnp.int32, (size, size), 1)
    identity = (rows == cols).astype(jnp.float32)
    only = jnp.where(rows == cols, gram, 0.0)
    g_j = jnp.sum(only, axis=0, keepdims=True)
    g_i = jnp.sum(only, axis=1, keepdims=True)
    spread = g_j - g_i
    summed = g_j + g_i
    skew = gram * spread / (spread * spread + 2.0 * gram * gram + 0.01 * summed * summed)
    skew_parts = split(skew)
    square = dot3(skew_parts, skew_parts)
    whole = 0.25 * jnp.sum(skew * skew)
    paired = 0.03125 * jnp.sum(square * square) * 1.001
    reach = jnp.minimum(whole * whole, paired)
    steps = jnp.int32(0)
    for limit in REACHES:
        steps = steps + (reach > limit).astype(jnp.int32)
    fixes = 1 + (steps > 7).astype(jnp.int32) + 2 * (steps > 9).astype(jnp.int32)
    scale = 2.0 / (2.0 + jnp.sqrt(jnp.full((size, size), reach, jnp.float32)))
    residual = identity - scale * (identity - 0.25 * square)
    x_ref[...] = scale * (identity + residual)
    residual_parts = split(residual)
    e_ref[...] = dot3(residual_parts, residual_parts)

    def step(_, carry):
        e = split(e_ref[...])
        x = x_ref[...]
        x_ref[...] = x + dot3(x, e)
        e_ref[...] = dot3(e, e)
        return carry

    lax.fori_loop(0, jnp.maximum(steps - 1, 0), step, jnp.int32(0))
    x = x_ref[...]
    x_ref[...] = x + 0.5 * dot3(x, skew_parts)

    def fix(_, carry):
        x = x_ref[...]
        x_ref[...] = x + dot3(x, identity - (x - 0.5 * dot(skew, x)))
        return carry

    lax.fori_loop(0, fixes, fix, jnp.int32(0))
    return 2.0 * x_ref[...] - identity


def squares_of(facts, gram, rotation):
    size = gram.shape[0]

    def body(f, gram_ref, rotation_ref, out_ref):
        rotation = rotation_ref[...]
        squares = rotation * dot(gram_ref[...], rotation)
        out_ref[...] = jnp.broadcast_to(
            jnp.sum(squares, axis=0, keepdims=True), (8, size)
        )

    return call(body, facts, [gram, rotation], shape(8, size))


def first_rotation(facts, own, other_y, half):
    size = 2 * half

    def body(f, own_ref, other_ref, rotation_ref, g_ref, half_ref, x_ref, e_ref):
        total = own_ref[...] + other_ref[...]
        g_ref[:half, :half] = total[:half]
        g_ref[:half, half:] = total[half : 2 * half]
        g_ref[half:, :half] = total[half : 2 * half].T
        g_ref[half:, half:] = total[2 * half :]
        rotation_ref[...] = rotate_of(g_ref[...], x_ref, e_ref)
        rotation = rotation_ref[...]
        half_ref[...] = jnp.where(f[CORE] == 0, rotation[:half], rotation[half:])

    square = pltpu.VMEM((size, size), jnp.float32)
    outs = (shape(size, size),) * 2 + (shape(half, size),)
    return call(body, facts, [own, other_y], outs, [square] * 2)


def later_rotation(facts, parts, diagonals, half):
    size = 2 * half

    def body(f, *refs):
        own, other_y, other_x, other_xy, foreign, native = [r[...] for r in refs[:6]]
        rotation_ref, g_ref, x_ref, e_ref = refs[6:]
        cross = (own + other_y) + (other_x + other_xy)
        core = f[CORE] == 0
        g_ref[:half, :half] = jnp.where(core, foreign, native)
        g_ref[:half, half:] = cross
        g_ref[half:, :half] = cross.T
        g_ref[half:, half:] = jnp.where(core, native, foreign)
        rotation_ref[...] = rotate_of(g_ref[...], x_ref, e_ref)

    square = pltpu.VMEM((size, size), jnp.float32)
    return call(
        body,
        facts,
        parts + diagonals,
        (shape(size, size),) * 2,
        [square] * 2,
    )


def turned_gram(facts, gram, rotation, position):
    size = gram.shape[0]
    half = size // 2

    def body(f, gram_ref, rotation_ref, leave_ref, stay_ref):
        rotation = rotation_ref[...]
        turned = dot(gram_ref[...], rotation)
        upper = dot_tn(rotation[:, :half], turned[:, :half])
        lower = dot_tn(rotation[:, half:], turned[:, half:])
        lower_leaves = (f[position] == 0) & (f[FIRST] == 0)
        leave_ref[...] = jnp.where(lower_leaves, lower, upper)
        stay_ref[...] = jnp.where(lower_leaves, upper, lower)

    return call(body, facts, [gram, rotation], (shape(half, half),) * 2)


def swapped(flag, matrix, axis):
    half = matrix.shape[axis] // 2
    a = lax.slice_in_dim(matrix, 0, half, axis=axis)
    b = lax.slice_in_dim(matrix, half, 2 * half, axis=axis)
    return jnp.where(flag, lax.concatenate([b, a], axis), matrix)


def turn_rows(facts, rotation, rows_of, vector_rows, half, own):
    rows = rows_of.shape[0] // 2 if own else rows_of.shape[0]

    def body(f, *refs):
        x_ref, stay_ref, leave_ref = refs[-3:]
        matrix = lax.concatenate([r[...] for r in refs[:-3]], 0)
        if not own:
            matrix = swapped(f[CORE] == 1, matrix, 0)
        zero = f[X] == (0 if own else 1)
        upper_leaves = jnp.where(zero, f[FIRST], 1) == 1
        turn = split(swapped(upper_leaves, matrix, 1))
        here = pl.multiple_of(f[X] * rows, 8)
        out = dot3(x_ref[pl.ds(here, rows)] if own else x_ref[...], turn)
        stay_ref[:rows] = out[:, :half]
        leave_ref[:rows] = out[:, half:]
        if vector_rows:
            ids = f[VROW] + lax.broadcasted_iota(jnp.int32, (vector_rows, half), 0)
            cols = lax.broadcasted_iota(jnp.int32, (vector_rows, half), 1)
            position = jnp.where(zero, 0, 2)
            vectors = [
                (ids == f[LABEL + position + k] * half + cols).astype(jnp.float32)
                for k in range(2)
            ]
            out = dot3(lax.concatenate(vectors, 1), turn)
            stay_ref[rows:] = out[:, :half]
            leave_ref[rows:] = out[:, half:]

    return call(
        body, facts, rotation + [rows_of], (shape(rows + vector_rows, half),) * 2
    )


def turn(facts, rotation, blocks, own, own_stay=None):
    rows, half = blocks[0].shape
    size = 2 * half
    extra = [] if own_stay is None else [own_stay]

    def body(f, rotation_ref, *refs):
        up_0, low_0, up_1, low_1 = [r[...] for r in refs[:4]]
        zero = f[CORE] == (0 if own else 1)
        upper_leaves = jnp.where(zero, f[FIRST], 1) == 1
        turned = swapped(upper_leaves, rotation_ref[:size], 1)
        columns = lax.concatenate(
            [jnp.where(zero, up_0, up_1), jnp.where(zero, low_0, low_1)], 1
        )
        out = dot3(columns, turned)
        outs = refs[4 + len(extra) :]
        outs[0][...] = out[:, :half]
        outs[1][...] = out[:, half:]
        if extra:
            outs[2][...] = jnp.where(f[CORE] == f[X], refs[4][...], out[:, :half])

    return call(
        body, facts, [rotation] + blocks + extra,
        (shape(rows, half),) * (2 + len(extra)),
    )


def put_cross(f, refs, zero, one):
    core = f[CORE] == 0
    refs[0][...] = jnp.where(core, zero, one)
    refs[1][...] = jnp.where(core, one, zero)


def cross_gram(facts, own, others, position, part, half):
    rows = own[0].shape[0]
    pieces = len(others)

    def body(f, *refs):
        own_refs = [[r] for r in refs[:3]]
        other_refs = [refs[3 + k : 3 + 3 * pieces : 3] for k in range(3)]
        up_0, low_0, up_1, low_1 = refs[5 + 3 * pieces :]

        def fill(target, sources):
            at = 0
            for ref in sources:
                target[at : at + ref.shape[0]] = ref[...]
                at += ref.shape[0]

        first, last = f[FIRST] == 1, f[LAST] == 1
        for x, near, far in ((0, own_refs, other_refs), (1, other_refs, own_refs)):
            here = f[position] == x

            @pl.when(here)
            def _():
                fill(up_1, near[0])
                fill(low_0, far[0])

            @pl.when(here & first)
            def _():
                fill(up_0, near[1])

            @pl.when(here & ~first)
            def _():
                fill(up_0, far[2])

            @pl.when(here & last)
            def _():
                fill(low_1, far[1])

            @pl.when(here & ~last)
            def _():
                fill(low_1, near[2])

        put_cross(
            f,
            refs[3 + 3 * pieces :],
            dot_tn(up_0[:part], low_0[:part]),
            dot_tn(up_1[:part], low_1[:part]),
        )

    outs = (shape(half, half),) * 2 + (shape(rows, half),) * 4
    return call(body, facts, own + sum(others, []), outs)


def give_arrived(facts, own, other, rows, half):
    def body(f, *refs):
        out_ref = refs[4]
        near = f[CORE] == f[X]
        edge = jnp.where(f[X] == 0, f[LAST], f[FIRST]) == 1
        for ref, here in zip(
            refs, (~near & edge, near & ~edge, near & edge, ~near & ~edge)
        ):

            @pl.when(here)
            def _():
                out_ref[...] = ref[:rows]

    return call(body, facts, own[1:] + other[1:], shape(rows, half))


def give(facts, blocks, start, stop, half):
    def body(f, up_0_ref, low_1_ref, out_ref):
        out_ref[...] = jnp.where(
            f[X] == 0, low_1_ref[start:stop], up_0_ref[start:stop]
        )

    return call(
        body, facts, [blocks[0], blocks[3]], shape(stop - start, half)
    )


def final_turn(f, own_ref, other_ref):
    rotation = jnp.where(f[CORE] == f[X], own_ref[...], other_ref[...])
    return split(swapped(f[X] == 1, rotation, 0))


def final_product(moved, native, turned):
    return dot3(lax.concatenate([moved, native], 1), turned)


def put_rows(copies, sems, source, target, here, there, value):
    rows = value.shape[0]
    source[here : here + rows] = value
    copy = pltpu.make_async_copy(
        source.at[here : here + rows],
        target.at[pl.ds(pl.multiple_of(there, 8), rows)],
        sems.at[len(copies)],
    )
    copies.append(copy)
    copy.start()


def finish_call(body, facts, inputs, outputs, outs, rows, vector_rows, size):
    vmem = pl.BlockSpec(memory_space=pltpu.VMEM)
    hbm = pl.BlockSpec(memory_space=pl.ANY)
    first = 1 + len(inputs)
    return pl.pallas_call(
        body,
        out_shape=outs,
        in_specs=[pl.BlockSpec(memory_space=pltpu.SMEM)]
        + [vmem] * len(inputs)
        + [hbm] * len(outputs),
        out_specs=(hbm, hbm, vmem)[: len(outs)],
        input_output_aliases={first + k: k for k in range(len(outputs))},
        cost_estimate=pl.CostEstimate(flops=1, transcendentals=0, bytes_accessed=1),
        scratch_shapes=[
            pltpu.VMEM((rows, size), jnp.float32),
            pltpu.VMEM((vector_rows, size), jnp.float32),
            pltpu.SemaphoreType.DMA((4,)),
        ],
        compiler_params=pltpu.CompilerParams(vmem_limit_bytes=24 << 20),
    )(facts, *inputs, *outputs)


def finish_kept(facts, packs, squares, blocks, native, got_top, part, half):
    size = 2 * half
    vector_rows = blocks[0].shape[0] - part
    top = got_top.shape[0]

    def body(f, own_ref, other_ref, *refs):
        x = f[X]
        turned = final_turn(f, own_ref, other_ref)
        native_ref, top_ref = refs[4:6]
        total = jnp.where(f[CORE] == x, refs[6][:1], refs[7][:1])
        out_ref, vectors_ref, singular_ref, out, vectors, sems = refs[8:]
        singular_ref[...] = jnp.sqrt(jnp.maximum(total, 0.0) + 1e-06)
        copies = []

        def kept(rows):
            up_0, low_0, up_1, low_1 = [r[rows] for r in refs[:4]]
            return final_product(
                jnp.where(x == 0, up_0, low_1),
                jnp.where(x == 0, low_0, up_1),
                turned,
            )

        def put(*args):
            put_rows(copies, sems, *args)

        middle = part // 2
        put(out, out_ref, 0, x * part, kept(slice(0, middle)))
        put(out, out_ref, middle, x * part + middle, kept(slice(middle, part)))
        value = final_product(top_ref[...], native_ref[:top], turned)
        put(out, out_ref, part, (1 - x) * part, value)
        put(vectors, vectors_ref, 0, x * vector_rows, kept(slice(part, None)))
        for copy in copies:
            copy.wait()

    outs = (shape(2 * part, size), shape(2 * vector_rows, size), shape(1, size))
    inputs = packs + blocks + [native, got_top] + squares
    return finish_call(
        body, facts, inputs, [], outs, part + top, vector_rows, size
    )


def finish_rest(facts, packs, outputs, native, got_rest, part, half):
    size = 2 * half
    vector_rows = native.shape[0] - part
    rest = got_rest.shape[0] - vector_rows
    top = part - rest

    def body(f, own_ref, other_ref, native_ref, rest_ref, *refs):
        x = f[X]
        turned = final_turn(f, own_ref, other_ref)
        out_ref, vectors_ref, out, vectors, sems = refs[2:]
        copies = []
        value = final_product(rest_ref[:rest], native_ref[top:part], turned)
        put_rows(copies, sems, out, out_ref, 0, (1 - x) * part + top, value)
        value = final_product(rest_ref[rest:], native_ref[part:], turned)
        put_rows(copies, sems, vectors, vectors_ref, 0, (1 - x) * vector_rows, value)
        for copy in copies:
            copy.wait()

    outs = (shape(2 * part, size), shape(2 * vector_rows, size))
    inputs = packs + [native, got_rest]
    return finish_call(
        body, facts, inputs, outputs, outs, rest, vector_rows, size
    )


def per_device(sector, block_label):
    local_rows, size = sector.shape
    half = size // 2
    part = local_rows // 2
    pairs = lax.axis_size("pair")
    row_count = lax.axis_size("row")
    vector_rows = pairs * size // row_count // 2
    pair_index = lax.axis_index("pair")
    row_index = lax.axis_index("row")
    x = pair_index % 2
    group = pair_index // 2
    core = row_index % 2

    def permute(block, route):
        moves = [
            (a * row_count + b, c * row_count + d) for (a, b), (c, d) in route
        ]
        return lax.ppermute(block, ("pair", "row"), moves)

    devices = [(p, r) for p in range(pairs) for r in range(row_count)]

    def exchange(block, over_pair, over_row):
        return permute(
            block, [((p ^ over_pair, r ^ over_row), (p, r)) for p, r in devices]
        )

    def shift(block, leftward):
        moves = []
        for p, r in devices:
            source = p + 2 if leftward(p, r) else p - 2
            if 0 <= source < pairs:
                moves.append(((source, r), (p, r)))
        return permute(block, moves)

    def pass_diagonal(block):
        moves = []
        for p, r in devices:
            other = p + 2 if r % 2 else p - 2
            inside = 0 <= other < pairs
            moves.append(((other, r ^ 1) if inside else (p, r), (p, r)))
        return permute(block, [((a, b), c) for (a, b), c in moves])

    def first_diagonal(block, leaves):
        moves = []
        for p, r in devices:
            c, even = r % 2, p - p % 2
            if leaves:
                source = even - 1 if c == 0 else even + 2
                if not 0 <= source < pairs:
                    source = even + c
            else:
                source = even + 1 - c
            moves.append(((source, r - c + p % 2), (p, r)))
        return permute(block, moves)

    def sum_rows(block):
        bit = 4
        while bit < row_count:
            block = block + exchange(block, 0, bit)
            bit *= 2
        return block

    names = jnp.arange(16, dtype=jnp.int32)
    facts = jnp.zeros((16,), jnp.int32)
    for name, value in (
        (X, x),
        (CORE, core),
        (FIRST, group == 0),
        (LAST, group == pairs // 2 - 1),
        (VROW, (row_index * 2 + x) * vector_rows),
        (EVEN, group % 2 == 0),
    ):
        facts = jnp.where(names == name, value.astype(jnp.int32), facts)
    labels = lax.dynamic_slice_in_dim(block_label, 4 * group, 4)
    facts = lax.dynamic_update_slice_in_dim(facts, labels, LABEL, 0)

    def together(*arrays):
        return lax.optimization_barrier(arrays)

    top_give, rest_give = give_rows(sector, part * 3 // 4)
    got_top = exchange(top_give, 1, 0)
    own = first_gram(sector, half)
    own = sum_rows(own + exchange(own, 0, 1))
    rotation, gram, rotation_half = first_rotation(facts, own, exchange(own, 0, 2), half)

    for sweep_round in range(ROUNDS - 1):
        last_move = sweep_round == ROUNDS - 2
        if sweep_round == 0:
            other_half = exchange(rotation_half, 1, 0)
            other_rotation = [other_half, exchange(other_half, 0, 1)]
            stay, leave = turn_rows(
                facts, [rotation], sector, vector_rows, half, True
            )
            leave, rest_give = together(leave, rest_give)
            got_rest = exchange(rest_give, 1, 0)
            own = [stay, leave, shift(leave, lambda p, r: p % 2 == 0)]
            others = []
            for got, below in ((got_top, 0), (got_rest, vector_rows)):
                stay, leave = turn_rows(facts, other_rotation, got, below, half, False)
                others.append([stay, leave, shift(leave, lambda p, r: p % 2 == 1)])
            leave, stay = turned_gram(facts, gram, rotation, X)
            diagonals = [first_diagonal(leave, True), first_diagonal(stay, False)]
            *grams, up_0, low_0, up_1, low_1 = cross_gram(
                facts, own, others, X, part, half
            )
        else:
            other_rotation = exchange(rotation, 0, 1)
            stay, leave = turn(facts, rotation, blocks, True)
            own = [stay, leave, shift(leave, lambda p, r: r % 2 == 0)]
            stay, leave, *native = turn(
                facts, other_rotation, blocks, False, stay if last_move else None
            )
            others = [[stay, leave, shift(leave, lambda p, r: r % 2 == 1)]]
            leave, stay = turned_gram(facts, gram, rotation, CORE)
            diagonals = [pass_diagonal(leave), exchange(stay, 0, 1)]
            if last_move:
                native = exchange(native[0], 1, 0)
                top = part * 5 // 8
                top_give = give_arrived(facts, own, others[0], top, half)
                own[2], others[0][2], top_give, *diagonals = together(
                    own[2], others[0][2], top_give, *diagonals
                )
                got_top = exchange(top_give, 1, 0)
            *grams, up_0, low_0, up_1, low_1 = cross_gram(
                facts, own, others, CORE, part, half
            )
        blocks = [up_0, low_0, up_1, low_1]
        if last_move:
            grams[1], native = together(grams[1], native)
        else:
            grams[1], *diagonals = together(grams[1], *diagonals)
        own = sum_rows(grams[0] + exchange(grams[1], 0, 1))
        parts = [own, exchange(own, 0, 2), exchange(own, 1, 0), exchange(own, 1, 2)]
        if last_move:
            rest_give = give(facts, blocks, top, part + vector_rows, half)
            *parts, got_top, rest_give = together(*parts, got_top, rest_give)
            got_rest = exchange(rest_give, 1, 0)
        rotation, gram = later_rotation(facts, parts, diagonals, half)
    packs = [rotation, exchange(rotation, 0, 1)]
    squares = squares_of(facts, gram, rotation)
    squares = [squares, exchange(squares, 0, 1)]
    *outputs, singular = finish_kept(
        facts, packs, squares, blocks, native, got_top, part, half
    )
    rotated, vectors_out = finish_rest(
        facts, packs, outputs, native, got_rest, part, half
    )
    return rotated, vectors_out, singular.reshape(size)


def solution(mesh):
    placed = (P("row", "pair"), P())
    return jax.shard_map(
        per_device,
        mesh=mesh,
        in_specs=placed,
        out_specs=(P("row", "pair"), P("row", "pair"), P("pair")),
        check_vma=False,
    )
```
